32 devices in a mesh: dp: 8 (over y, x, core), mp: 4 (over z).
Axes of the slice: x: 2, y: 2, z: 4, core: 2. Of those that a mesh axis runs over, the one named last changes fastest.
Arguments:
- caption_tokens: bfloat16 [784, 16, 768], P('dp'), may hold values from -6 to 6
- image_tokens: bfloat16 [224, 50, 768], P(('dp', 'mp')), may hold values from -6 to 6
- image_attend: bfloat16 [3, 768, 768], replicated, may hold values from -0.21875 to 0.21875
- image_output: bfloat16 [768, 768], replicated, may hold values from -0.4375 to 0.4375
- image_expand: bfloat16 [768, 3072], replicated, may hold values from -0.21875 to 0.21875
- image_reduce: bfloat16 [3072, 768], replicated, may hold values from -0.109375 to 0.109375
- image_gains: float32 [2, 768], replicated, may hold values from 0.1 to 1.9
- caption_attend: bfloat16 [3, 768, 768], P(None, None, 'mp'), may hold values from -0.21875 to 0.21875
- attend_bias: float32 [2, 768], P(None, 'mp'), may hold values from -3 to 3
- caption_output: bfloat16 [768, 768], P('mp'), may hold values from -0.4375 to 0.4375
- output_bias: float32 [768], replicated, may hold values from -1 to 1
- caption_expand: bfloat16 [768, 3072], P(None, 'mp'), may hold values from -0.21875 to 0.21875
- expand_bias: float32 [3072], P('mp'), may hold values from -3 to 3
- caption_reduce: bfloat16 [3072, 768], P('mp'), may hold values from -0.109375 to 0.109375
- reduce_bias: float32 [768], replicated, may hold values from -1 to 1
- norm_gains: float32 [2, 768], replicated, may hold values from 0.1 to 1.9
- norm_shifts: float32 [2, 768], replicated, may hold values from -2 to 2
- log_scale: float32 [1], replicated, may hold values from 3.6 to 4.4
- caption_image: int32 [784], P('dp'), may hold values from 0 to 223, as said below
Outputs:
- contrast_loss: float32 [1], replicated
- gradient_tokens: float32 [784, 16, 768], P('dp')
- gradient_attend: float32 [3, 768, 768], P(None, None, 'mp')
- gradient_attend_bias: float32 [2, 768], P(None, 'mp')
- gradient_output: float32 [768, 768], P('mp')
- gradient_output_bias: float32 [768], replicated
- gradient_expand: float32 [768, 3072], P(None, 'mp')
- gradient_expand_bias: float32 [3072], P('mp')
- gradient_reduce: float32 [3072, 768], P('mp')
- gradient_reduce_bias: float32 [768], replicated
- gradient_gains: float32 [2, 768], replicated
- gradient_shifts: float32 [2, 768], replicated
- gradient_log_scale: float32 [1], replicated
The draws below stay inside these ranges and needn't reach their ends.
Inputs may be any that keep to these rules, and one draw needn't show every extreme that they name: `caption_image`: every image is named by at least one and at most five captions.
All inputs are finite; a program needn't handle non-finite values.
Results may differ from the reference program's by a relative error of at most 0.014.
Values may be sent and summed in bfloat16 or wider, within the bound.
A program may use at most 128 MiB of HBM per device.

```python
import jax
import jax.numpy as jnp
from jax import lax

D = 768
HEADS = 12
HEAD_DIM = 64
FF = 3072
TXT_LEN = 16
IMG_LEN = 50
IMG_DEV = 7
CAP_DEV = 98
IMAGES = 224
CAPTIONS = 784
N_DP = 8
N_MP = 4


def draw_caption_image(key, part):
    quarter = IMAGES // 4
    first_key, second_key, order_key, shuffle_key = jax.random.split(key, 4)
    lower_pair = jax.random.randint(first_key, (quarter,), 1, 6).astype(jnp.int32)
    upper_pair = jax.random.randint(second_key, (quarter,), 3, 6).astype(jnp.int32)
    lower_pair = lower_pair.at[0].set(1)
    upper_pair = upper_pair.at[0].set(5)
    counts = jnp.stack([lower_pair, 6 - lower_pair, upper_pair, 8 - upper_pair], axis=1).reshape(IMAGES)
    counts = counts[jax.random.permutation(order_key, IMAGES)]
    owners = jnp.repeat(jnp.arange(IMAGES, dtype=jnp.int32), counts, total_repeat_length=CAPTIONS)
    return jax.random.permutation(shuffle_key, owners).astype(jnp.int32)


def steps_of(rng, dims, cuts, low, top_value):
    level = 1.0
    for axis_at, shards_of in cuts:
        heights = jax.random.uniform(jax.random.fold_in(jax.random.fold_in(rng, 6), axis_at), (shards_of,), jnp.float32, low / len(cuts), top_value / len(cuts))
        level = level * jnp.repeat(jnp.exp(heights), dims[axis_at] // shards_of).reshape((-1,) + (1,) * (len(dims) - 1 - axis_at))
    return level


def bell_draw(stream_key, extent, deviation, limit, pieces=(), kind=jnp.bfloat16):
    values = jax.random.normal(stream_key, extent, jnp.float32) * deviation
    if len(pieces) > 0:
        values = steps_of(stream_key, extent, pieces, -0.22, 0.18) * values
    return jnp.clip(values, min=-limit, max=limit).astype(kind)


def setup_inputs(seed: int = 0) -> dict:
    key_of = jax.random.split(jax.random.key(seed), 20)
    return {
        "caption_tokens": bell_draw(key_of[0], (CAPTIONS, TXT_LEN, D), 1.0, 6.0, ((0, 8),)),
        "image_tokens": bell_draw(key_of[1], (IMAGES, IMG_LEN, D), 1.0, 6.0, ((0, 32),)),
        "image_attend": bell_draw(key_of[2], (3, D, D), D ** -0.5, 0.21875),
        "image_output": bell_draw(key_of[3], (D, D), (D // 4) ** -0.5, 0.4375),
        "image_expand": bell_draw(key_of[4], (D, FF), D ** -0.5, 0.21875),
        "image_reduce": bell_draw(key_of[5], (FF, D), FF ** -0.5, 0.109375),
        "image_gains": jnp.clip(1.0 + 0.18 * jax.random.normal(key_of[6], (2, D), jnp.float32), 0.1, 1.9),
        "caption_attend": bell_draw(key_of[7], (3, D, D), D ** -0.5, 0.21875, ((2, 4),)),
        "attend_bias": bell_draw(key_of[8], (2, D), 0.5, 3.0, ((1, 4),), jnp.float32),
        "caption_output": bell_draw(key_of[9], (D, D), (D // 4) ** -0.5, 0.4375, ((0, 4),)),
        "output_bias": bell_draw(key_of[10], (D,), 0.15, 1.0, (), jnp.float32),
        "caption_expand": bell_draw(key_of[11], (D, FF), D ** -0.5, 0.21875, ((1, 4),)),
        "expand_bias": bell_draw(key_of[12], (FF,), 0.5, 3.0, ((0, 4),), jnp.float32),
        "caption_reduce": bell_draw(key_of[13], (FF, D), FF ** -0.5, 0.109375, ((0, 4),)),
        "reduce_bias": bell_draw(key_of[14], (D,), 0.15, 1.0, (), jnp.float32),
        "norm_gains": jnp.clip(1.0 + 0.18 * jax.random.normal(key_of[15], (2, D), jnp.float32), 0.1, 1.9),
        "norm_shifts": bell_draw(key_of[16], (2, D), 0.3, 2.0, (), jnp.float32),
        "log_scale": jnp.clip(jax.random.uniform(key_of[17], (1,), jnp.float32, 3.6, 4.4), 3.6, 4.4),
        "caption_image": draw_caption_image(jax.random.fold_in(key_of[19], 71), 0),
    }


@jax.custom_vjp
def low(v):
    return lax.optimization_barrier(v.astype(jnp.bfloat16)).astype(jnp.float32)

@jax.custom_vjp
def low_back(v):
    return v

def low_keep(v):
    return (low(v), None)

def low_pass(kept, grad):
    return (grad,)

def back_keep(v):
    return (v, None)

def back_low(kept, grad):
    return (low(grad),)
low.defvjp(low_keep, low_pass)
low_back.defvjp(back_keep, back_low)

def product(left_side, right_side):
    return jnp.dot(left_side, right_side, precision=lax.Precision.HIGHEST, preferred_element_type=jnp.float32)

def contract(formula, left_side, right_side):
    return jnp.einsum(formula, left_side, right_side, precision=lax.Precision.HIGHEST, preferred_element_type=jnp.float32)

def norm_rows(values, gains, shifts):
    centred = values - lax.optimization_barrier(jnp.mean(values, axis=-1, keepdims=True))
    variance = lax.optimization_barrier(jnp.mean(centred * centred, axis=-1, keepdims=True))
    return centred * lax.rsqrt(variance + 1e-06) * gains + shifts

def softmax_last(logits):
    highest = lax.optimization_barrier(jnp.max(logits, axis=-1, keepdims=True))
    expos = jnp.exp(logits - highest)
    return expos / lax.optimization_barrier(jnp.sum(expos, axis=-1, keepdims=True))

def unit_rows(pooled):
    return pooled * lax.rsqrt(lax.optimization_barrier(jnp.sum(pooled * pooled, axis=-1, keepdims=True)) + 1e-06)

def image_block(tokens, image_attend, image_output, image_expand, image_reduce, image_gains):
    group_size = tokens.shape[0]
    heads_shape = (group_size, IMG_LEN, HEADS, HEAD_DIM)
    flattened = tokens.reshape(group_size * IMG_LEN, D)
    normed = low(norm_rows(flattened, image_gains[0], 0.0))
    queries = low(product(normed, image_attend[0])).reshape(heads_shape)
    keyset = low(product(normed, image_attend[1])).reshape(heads_shape)
    valueset = low(product(normed, image_attend[2])).reshape(heads_shape)
    weights = low(softmax_last(contract('bqhd,bkhd->bhqk', queries, keyset) * HEAD_DIM ** (-0.5)))
    mixture = low(contract('bhqk,bkhd->bqhd', weights, valueset).reshape(group_size * IMG_LEN, D))
    residual = flattened + product(mixture, image_output)
    normed_two = low(norm_rows(residual, image_gains[1], 0.0))
    activated = low(jax.nn.gelu(product(normed_two, image_expand), approximate=True))
    outputs = residual + product(activated, image_reduce)
    return low(unit_rows(lax.optimization_barrier(jnp.mean(outputs.reshape(group_size, IMG_LEN, D), axis=1))))

def caption_block(tokens, params):
    attend, attend_bias, output_weight, output_bias, expand, expand_bias, reduce_weight, reduce_bias, norm_gains, norm_shifts, log_scale = params
    group_size = tokens.shape[0]
    heads_shape = (group_size, TXT_LEN, HEADS, HEAD_DIM)
    flattened = tokens.reshape(group_size * TXT_LEN, D)
    normed = low(norm_rows(flattened, norm_gains[0], norm_shifts[0]))
    queries = low(low_back(product(normed, attend[0]) + attend_bias[0])).reshape(heads_shape)
    keyset = low(low_back(product(normed, attend[1]))).reshape(heads_shape)
    valueset = low(low_back(product(normed, attend[2]) + attend_bias[1])).reshape(heads_shape)
    logits = low_back(contract('bqhd,bkhd->bhqk', queries, keyset) * HEAD_DIM ** (-0.5))
    weights = low(softmax_last(logits))
    mixture = low(low_back(contract('bhqk,bkhd->bqhd', weights, valueset).reshape(group_size * TXT_LEN, D)))
    residual = flattened + (low_back(product(mixture, output_weight)) + output_bias)
    normed_two = low(norm_rows(residual, norm_gains[1], norm_shifts[1]))
    hidden = low_back(product(normed_two, expand) + expand_bias)
    activated = low(jax.nn.gelu(hidden, approximate=True))
    outputs = residual + (low_back(product(activated, reduce_weight)) + reduce_bias)
    return unit_rows(lax.optimization_barrier(jnp.mean(outputs.reshape(group_size, TXT_LEN, D), axis=1)))

def objective(params, caption_all, image_embed, caption_image):
    blocks = caption_all.reshape(N_DP, CAP_DEV, TXT_LEN, D)
    embed = lax.map(jax.checkpoint(lambda group_tokens: caption_block(group_tokens, params)), blocks).reshape(CAPTIONS, D)
    embed_low = low(embed)
    cosine = low_back(product(embed_low, image_embed.T))
    scores = jnp.exp(params[10][0]) * cosine
    matches = (caption_image[:, None] == jnp.arange(IMAGES, dtype=jnp.int32)[None, :]).astype(jnp.float32)
    row_top = lax.optimization_barrier(jnp.max(scores, axis=1, keepdims=True))
    row_lse = row_top[:, 0] + jnp.log(lax.optimization_barrier(jnp.sum(jnp.exp(scores - row_top), axis=1)))
    column_top = lax.optimization_barrier(jnp.max(scores, axis=0, keepdims=True))
    column_lse = column_top[0] + jnp.log(lax.optimization_barrier(jnp.sum(jnp.exp(scores - column_top), axis=0)))
    row_positive = lax.optimization_barrier(jnp.sum(scores * matches, axis=1))
    column_positive = lax.optimization_barrier(jnp.sum(scores * matches, axis=0))
    counts = lax.optimization_barrier(jnp.sum(matches, axis=0))
    loss_value = 0.5 * (jnp.sum(row_lse - row_positive) / CAPTIONS + jnp.sum(column_lse - column_positive / counts) / IMAGES)
    return (CAPTIONS * loss_value, loss_value)

def reference(caption_tokens, image_tokens, image_attend, image_output, image_expand, image_reduce, image_gains, caption_attend, attend_bias, caption_output, output_bias, caption_expand, expand_bias, caption_reduce, reduce_bias, norm_gains, norm_shifts, log_scale, caption_image):
    frozen = (image_attend.astype(jnp.float32), image_output.astype(jnp.float32), image_expand.astype(jnp.float32), image_reduce.astype(jnp.float32), image_gains.astype(jnp.float32))
    image_groups = image_tokens.astype(jnp.float32).reshape(N_DP * N_MP, IMG_DEV, IMG_LEN, D)
    image_embed = lax.map(lambda group_tokens: image_block(group_tokens, frozen[0], frozen[1], frozen[2], frozen[3], frozen[4]), image_groups).reshape(IMAGES, D)
    params = (caption_attend.astype(jnp.float32), attend_bias.astype(jnp.float32), caption_output.astype(jnp.float32), output_bias.astype(jnp.float32), caption_expand.astype(jnp.float32), expand_bias.astype(jnp.float32), caption_reduce.astype(jnp.float32), reduce_bias.astype(jnp.float32), norm_gains.astype(jnp.float32), norm_shifts.astype(jnp.float32), log_scale.astype(jnp.float32))
    objective_value, pullback, loss_value = jax.vjp(lambda weights, tokens: objective(weights, tokens, image_embed, caption_image), params, caption_tokens.astype(jnp.float32), has_aux=True)
    gradients, gradient_tokens = pullback(jnp.ones((), jnp.float32))
    return (loss_value.reshape(1), gradient_tokens, gradients[0], gradients[1], gradients[2], gradients[3], gradients[4], gradients[5], gradients[6], gradients[7], gradients[8], gradients[9], gradients[10])
```

```python
from functools import partial

import jax
import jax.numpy as jnp
from jax import lax
from jax.sharding import PartitionSpec as P

HEAD_DIM = 64


def norm_rows(values, gains, shifts):
    centred = values - jnp.mean(values, axis=-1, keepdims=True)
    variance = jnp.mean(centred * centred, axis=-1, keepdims=True)
    return centred * lax.rsqrt(variance + 1e-06) * gains + shifts


def softmax_last(logits):
    highest = jnp.max(logits, axis=-1, keepdims=True)
    expos = jnp.exp(logits - highest)
    return expos / jnp.sum(expos, axis=-1, keepdims=True)


def unit_rows(pooled):
    return pooled * lax.rsqrt(jnp.sum(pooled * pooled, axis=-1, keepdims=True) + 1e-06)


def matmul(left_side, right_side):
    return jnp.dot(left_side, right_side, preferred_element_type=jnp.float32)


def contract_last(left_side, right_side):
    return lax.dot_general(
        left_side, right_side, (((1,), (1,)), ((), ())), preferred_element_type=jnp.float32
    )


def outer_sum(left_side, right_side):
    return lax.dot_general(
        left_side, right_side, (((0,), (0,)), ((), ())), preferred_element_type=jnp.float32
    )


def contract(formula, left_side, right_side):
    return jnp.einsum(formula, left_side, right_side, preferred_element_type=jnp.float32)


def image_block(tokens, image_attend, image_output, image_expand, image_reduce, image_gains):
    group_size, length, model_width = tokens.shape
    heads_count = model_width // HEAD_DIM
    heads_shape = (group_size, length, heads_count, HEAD_DIM)
    flattened = tokens.astype(jnp.float32).reshape(group_size * length, model_width)
    normed = norm_rows(flattened, image_gains[0], 0.0).astype(jnp.bfloat16)
    queries = matmul(normed, image_attend[0]).astype(jnp.bfloat16).reshape(heads_shape)
    keyset = matmul(normed, image_attend[1]).astype(jnp.bfloat16).reshape(heads_shape)
    valueset = matmul(normed, image_attend[2]).astype(jnp.bfloat16).reshape(heads_shape)
    weights = softmax_last(
        contract("bqhd,bkhd->bhqk", queries, keyset) * HEAD_DIM ** (-0.5)
    ).astype(jnp.bfloat16)
    mixture = (
        contract("bhqk,bkhd->bqhd", weights, valueset)
        .astype(jnp.bfloat16)
        .reshape(group_size * length, model_width)
    )
    residual = flattened + matmul(mixture, image_output)
    normed_two = norm_rows(residual, image_gains[1], 0.0).astype(jnp.bfloat16)
    activated = jax.nn.gelu(matmul(normed_two, image_expand), approximate=True).astype(jnp.bfloat16)
    activated_mean = jnp.mean(
        activated.astype(jnp.float32).reshape(group_size, length, activated.shape[1]), axis=1
    )
    residual_mean = jnp.mean(residual.reshape(group_size, length, model_width), axis=1)
    pooled = residual_mean + matmul(activated_mean.astype(jnp.bfloat16), image_reduce)
    return unit_rows(pooled).astype(jnp.bfloat16)


def local(
    caption_tokens,
    image_tokens,
    image_attend,
    image_output,
    image_expand,
    image_reduce,
    image_gains,
    caption_attend,
    attend_bias,
    caption_output,
    output_bias,
    caption_expand,
    expand_bias,
    caption_reduce,
    reduce_bias,
    norm_gains,
    norm_shifts,
    log_scale,
    caption_image,
):
    local_embed = image_block(
        image_tokens, image_attend, image_output, image_expand, image_reduce, image_gains
    )
    group_images = lax.all_gather(local_embed, "mp", axis=0, tiled=True)
    captions, length, model_width = caption_tokens.shape
    row_count = captions * length
    heads_local = caption_attend.shape[2] // HEAD_DIM
    head_scale = HEAD_DIM ** (-0.5)

    def split_heads(matrix):
        return matrix.reshape(captions, length, heads_local, HEAD_DIM)

    flattened = caption_tokens.astype(jnp.float32).reshape(row_count, model_width)
    normed, norm_back_one = jax.vjp(norm_rows, flattened, norm_gains[0], norm_shifts[0])
    normed_low = normed.astype(jnp.bfloat16)
    queries = (matmul(normed_low, caption_attend[0]) + attend_bias[0]).astype(jnp.bfloat16)
    keyset = matmul(normed_low, caption_attend[1]).astype(jnp.bfloat16)
    valueset = (matmul(normed_low, caption_attend[2]) + attend_bias[1]).astype(jnp.bfloat16)
    weights = softmax_last(
        contract("bqhd,bkhd->bhqk", split_heads(queries), split_heads(keyset)) * head_scale
    )
    weights_low = weights.astype(jnp.bfloat16)
    mixture = (
        contract("bhqk,bkhd->bqhd", weights_low, split_heads(valueset))
        .astype(jnp.bfloat16)
        .reshape(row_count, heads_local * HEAD_DIM)
    )
    attended = lax.psum(matmul(mixture, caption_output).astype(jnp.bfloat16), "mp").astype(
        jnp.float32
    )
    residual = flattened + (attended + output_bias)
    normed_two, norm_back_two = jax.vjp(norm_rows, residual, norm_gains[1], norm_shifts[1])
    normed_two_low = normed_two.astype(jnp.bfloat16)
    hidden = matmul(normed_two_low, caption_expand) + expand_bias
    activated, activation_back = jax.vjp(partial(jax.nn.gelu, approximate=True), hidden)
    activated_low = activated.astype(jnp.bfloat16)
    activated_mean = jnp.mean(
        activated_low.astype(jnp.float32).reshape(captions, length, activated.shape[1]), axis=1
    ).astype(jnp.bfloat16)
    reduced = lax.psum(matmul(activated_mean, caption_reduce).astype(jnp.bfloat16), "mp").astype(
        jnp.float32
    )
    pooled = jnp.mean(residual.reshape(captions, length, model_width), axis=1) + (
        reduced + reduce_bias
    )
    embed, unit_back = jax.vjp(unit_rows, pooled)
    embed_low = embed.astype(jnp.bfloat16)
    scaling = jnp.exp(log_scale[0])
    devices_data = lax.axis_size("dp")
    total_captions = captions * devices_data
    total_images = group_images.shape[0] * devices_data
    portion = lax.all_gather(group_images, "dp", axis=0, tiled=True)
    row_top = jnp.full((captions,), -1e30, jnp.float32)
    portion_rows = portion.shape[0]
    scores = scaling * contract_last(embed_low, portion)
    matches = (caption_image[:, None] == lax.iota(jnp.int32, portion_rows)[None, :]).astype(
        jnp.float32
    )
    new_top = jnp.maximum(row_top, jnp.max(scores, axis=1))
    row_total = jnp.sum(jnp.exp(scores - new_top[:, None]), axis=1)
    row_positive = jnp.sum(scores * matches, axis=1)
    portion_top = jnp.max(scores, axis=0)
    column_top = portion_top
    column_total = jnp.sum(jnp.exp(scores - portion_top[None, :]), axis=0)
    column_positive = jnp.sum(scores * matches, axis=0)
    column_count = jnp.sum(matches, axis=0)
    everything = lax.all_gather(
        jnp.stack([column_top, column_total, column_positive, column_count]), "dp"
    )
    column_top = jnp.max(everything[:, 0], axis=0)
    column_total = jnp.sum(everything[:, 1] * jnp.exp(everything[:, 0] - column_top[None]), axis=0)
    column_positive = jnp.sum(everything[:, 2], axis=0)
    column_count = jnp.sum(everything[:, 3], axis=0)
    statistics = (new_top, row_total, row_positive)
    row_lse = statistics[0] + jnp.log(statistics[1])
    column_lse = column_top + jnp.log(column_total)
    column_inverse = 1.0 / column_count
    row_part = jnp.sum(row_lse - statistics[2])
    column_part = jnp.sum(column_lse - column_positive / column_count)
    image_weight = 0.5 * total_captions / total_images
    grad_scores = 0.5 * (jnp.exp(scores - row_lse[:, None]) - matches) + image_weight * (
        jnp.exp(scores - column_lse[None, :]) - matches * column_inverse[None, :]
    )
    grad_scale = jnp.sum(grad_scores * scores)
    grad_cosine = (scaling * grad_scores).astype(jnp.bfloat16)
    grad_embed = matmul(grad_cosine, portion)
    grad_pooled = unit_back(grad_embed)[0]
    grad_rows = jnp.broadcast_to(
        grad_pooled[:, None, :] * (1.0 / length), (captions, length, model_width)
    ).reshape(row_count, model_width)
    gradient_reduce_bias = jnp.sum(grad_pooled, axis=0)
    grad_pooled_low = grad_pooled.astype(jnp.bfloat16)
    gradient_reduce = outer_sum(activated_mean, grad_pooled_low)
    grad_activated = jnp.broadcast_to(
        (contract_last(grad_pooled_low, caption_reduce) * (1.0 / length))[:, None, :],
        (captions, length, caption_reduce.shape[0]),
    ).reshape(row_count, caption_reduce.shape[0])
    grad_hidden = activation_back(grad_activated)[0].astype(jnp.bfloat16)
    gradient_expand_bias = jnp.sum(grad_hidden.astype(jnp.float32), axis=0)
    gradient_expand = outer_sum(normed_two_low, grad_hidden)
    grad_normed_two = lax.psum(
        contract_last(grad_hidden, caption_expand).astype(jnp.bfloat16), "mp"
    ).astype(jnp.float32)
    grad_from_norm, gain_second, shift_second = norm_back_two(grad_normed_two)
    grad_residual = grad_rows + grad_from_norm
    grad_residual_low = grad_residual.astype(jnp.bfloat16)
    gradient_output_bias = jnp.sum(grad_residual, axis=0)
    gradient_output = outer_sum(mixture, grad_residual_low)
    grad_mixture = split_heads(
        contract_last(grad_residual_low, caption_output).astype(jnp.bfloat16)
    )
    grad_probs = contract("bqhd,bkhd->bhqk", grad_mixture, split_heads(valueset))
    grad_valueset = (
        contract("bhqk,bqhd->bkhd", weights_low, grad_mixture)
        .astype(jnp.bfloat16)
        .reshape(row_count, heads_local * HEAD_DIM)
    )
    grad_logits = (
        weights * (grad_probs - jnp.sum(grad_probs * weights, axis=-1, keepdims=True))
    ).astype(jnp.bfloat16)
    grad_queries = (
        (contract("bhqk,bkhd->bqhd", grad_logits, split_heads(keyset)) * head_scale)
        .astype(jnp.bfloat16)
        .reshape(row_count, heads_local * HEAD_DIM)
    )
    grad_keyset = (
        (contract("bhqk,bqhd->bkhd", grad_logits, split_heads(queries)) * head_scale)
        .astype(jnp.bfloat16)
        .reshape(row_count, heads_local * HEAD_DIM)
    )
    gradient_attend = jnp.stack(
        [
            outer_sum(normed_low, grad_queries),
            outer_sum(normed_low, grad_keyset),
            outer_sum(normed_low, grad_valueset),
        ]
    )
    gradient_attend_bias = jnp.stack(
        [
            jnp.sum(grad_queries.astype(jnp.float32), axis=0),
            jnp.sum(grad_valueset.astype(jnp.float32), axis=0),
        ]
    )
    partial_normed = (
        contract_last(grad_queries, caption_attend[0])
        + contract_last(grad_keyset, caption_attend[1])
        + contract_last(grad_valueset, caption_attend[2])
    )
    grad_normed = lax.psum(partial_normed.astype(jnp.bfloat16), "mp").astype(jnp.float32)
    grad_from_first, gain_first, shift_first = norm_back_one(grad_normed)
    gradient_tokens = (grad_residual + grad_from_first).reshape(captions, length, model_width)
    large = lax.psum(
        [
            part.astype(jnp.bfloat16)
            for part in (gradient_attend, gradient_output, gradient_expand, gradient_reduce)
        ],
        "dp",
    )
    large = [part.astype(jnp.float32) for part in large]
    small = lax.psum(
        (
            gradient_attend_bias,
            gradient_output_bias,
            gradient_expand_bias,
            gradient_reduce_bias,
            jnp.stack([gain_first, gain_second]),
            jnp.stack([shift_first, shift_second]),
            grad_scale,
            row_part,
        ),
        "dp",
    )
    summed = (
        large[0],
        small[0],
        large[1],
        small[1],
        large[2],
        small[2],
        large[3],
        small[3],
        small[4],
        small[5],
        small[6],
        small[7],
    )
    contrast_loss = (0.5 * (summed[11] / total_captions + column_part / total_images)).reshape(1)
    return (
        contrast_loss,
        gradient_tokens,
        summed[0],
        summed[1],
        summed[2],
        summed[3],
        summed[4],
        summed[5],
        summed[6],
        summed[7],
        summed[8],
        summed[9],
        summed[10].reshape(1),
    )


def solution(mesh):
    in_specs = (
        P("dp", None, None),
        P(("dp", "mp"), None, None),
        P(),
        P(),
        P(),
        P(),
        P(),
        P(None, None, "mp"),
        P(None, "mp"),
        P("mp", None),
        P(),
        P(None, "mp"),
        P("mp"),
        P("mp", None),
        P(),
        P(),
        P(),
        P(),
        P("dp"),
    )
    out_specs = (
        P(),
        P("dp", None, None),
        P(None, None, "mp"),
        P(None, "mp"),
        P("mp", None),
        P(),
        P(None, "mp"),
        P("mp"),
        P("mp", None),
        P(),
        P(),
        P(),
        P(),
    )
    return jax.shard_map(local, mesh=mesh, in_specs=in_specs, out_specs=out_specs, check_vma=False)
```

```python
import functools

import jax
import jax.numpy as jnp
from jax import lax
from jax.experimental import pallas as pl
from jax.experimental.pallas import tpu as pltpu
from jax.sharding import PartitionSpec as P

HEAD_DIM = 64
LEN = 16
PIECE = 48
BLOCK = 112
F32 = jnp.float32
LOW = jnp.bfloat16
FAR = -1e30
GELU_A = 0.7978845608028654
GELU_B = 0.044715


def dot(a, b):
    return lax.dot_general(a, b, (((1,), (0,)), ((), ())), preferred_element_type=F32)


def dot_nt(a, b):
    return lax.dot_general(a, b, (((1,), (1,)), ((), ())), preferred_element_type=F32)


def dot_tn(a, b):
    return lax.dot_general(a, b, (((0,), (0,)), ((), ())), preferred_element_type=F32)


def iota(shape, axis):
    return lax.broadcasted_iota(jnp.int32, shape, axis)


def standard(x):
    width = x.shape[-1]
    centred = x - jnp.sum(x, axis=-1, keepdims=True) * (1.0 / width)
    variance = jnp.sum(centred * centred, axis=-1, keepdims=True) * (1.0 / width)
    scale = lax.rsqrt(variance + 1e-6)
    return centred * scale, scale


def gelu_parts(h):
    square = h * h
    t = jnp.tanh(GELU_A * h * (1.0 + GELU_B * square))
    half = 0.5 * (1.0 + t)
    slope = half + 0.5 * h * (1.0 - t * t) * (GELU_A * (1.0 + 3.0 * GELU_B * square))
    return h * half, slope


def sum8(x):
    return x[0:8] + x[8:16]


def body(
    n_dp,
    n_mp,
    tok_in,
    imt,
    ia_in,
    io_in,
    ie_in,
    ir_in,
    wao_in,
    we_in,
    wr_in,
    par,
    cap,
    red,
    gt,
    sgo,
    W,
    IW,
    TOK,
    N1,
    QKV,
    PR,
    MIX,
    RES,
    N2,
    GP,
    PA,
    ACC,
    GRL,
    GT,
    IP,
    EMB,
    MSG,
    STATS,
    SB,
    HM3,
    BM,
    HM4,
    POOL,
    EL,
    GPL,
    GA,
    RCORE,
    RB1,
    RB2,
    RZ,
    XR,
    XST,
    SG,
    SGR,
    gz_s,
    gz_r,
    ga_s,
    ga_r,
    loc_sem,
    iw_sem,
    tok_sem,
    sb_s,
    sb_r,
    emb_s,
    emb_r,
    st_s,
    st_r,
    stx_s,
    stx_r,
    rs_s,
    rs_r,
    ag_s,
    ag_r,
    xr_s,
    xr_r,
    sg_s,
    sg_r,
    gt_s,
    gt_r,
    out_sem,
):
    d = lax.axis_index("dp")
    m = lax.axis_index("mp")
    n_all = n_dp * n_mp
    me = d * n_mp + m
    bits = n_dp.bit_length() - 1
    extra = bits - 3
    images, image_len = imt.shape[0], imt.shape[1]
    rows = TOK.shape[0] * LEN
    n_cap = TOK.shape[0]
    n_blocks = rows // BLOCK
    width = RES.shape[1]
    shard = QKV.shape[3]
    image_rows = images * 64
    t_all = EMB.shape[0] * 8
    total_images = images * n_all
    total_captions = n_cap * 2 * n_dp

    def bit(v, b):
        return lax.rem(v // (1 << b), 2)

    def flip(v, b):
        return v + (1 - 2 * bit(v, b)) * (1 << b)

    cb, xb, yb = bit(d, 0), bit(d, 1), bit(d, 2)
    half = lax.rem(m, 2)
    pair = flip(m, 0)
    p_a = cb * 4 + yb * 2 + xb
    p_b = 8 + cb * 4 + xb * 2 + yb
    core_dev = (flip(d, 0), m)
    x_dev = (flip(d, 1), m)
    y_dev = (flip(d, 2), m)
    pair_dev = (d, pair)
    sends = []

    def remote(src, dst, ss, rs, dev):
        copy = pltpu.make_async_remote_copy(
            src_ref=src,
            dst_ref=dst,
            send_sem=ss,
            recv_sem=rs,
            device_id=dev,
            device_id_type=pl.DeviceIdType.MESH,
        )
        copy.start()
        sends.append(copy)
        return copy

    def local(src, dst, sem):
        copy = pltpu.make_async_copy(src, dst, sem)
        copy.start()
        return copy

    barrier = pltpu.get_barrier_semaphore()

    def greet(k, carry):
        q = lax.rem(me + k, n_all)
        pl.semaphore_signal(
            barrier,
            inc=1,
            device_id=(q // n_mp, lax.rem(q, n_mp)),
            device_id_type=pl.DeviceIdType.MESH,
        )
        return carry

    lax.fori_loop(1, n_all, greet, 0)

    image_loads = {}

    def load_image(i):
        if i < 3:
            src, slot = ia_in.at[i], i
        elif i == 3:
            src, slot = io_in, 3
        elif i < 8:
            src, slot = ie_in.at[:, :, pl.ds((i - 4) * width, width)], i
        else:
            src, slot = ir_in.at[i - 8], i - 8
        image_loads[i] = local(src, IW.at[slot], iw_sem.at[i])

    for i in range(8):
        load_image(i)
    tok_copy = local(tok_in.at[pl.ds(half * n_cap, n_cap)], TOK, tok_sem)
    sources = (wao_in, we_in, wr_in)
    own_loads = [local(sources[g], W.at[g, m], loc_sem.at[g]) for g in range(3)]

    pl.semaphore_wait(barrier, n_all - 1)

    hops = (1, 3, 2)
    zc, ac = {}, {}

    def gather_z(g):
        for k in hops:
            dev = (d, lax.rem(m + k, n_mp))
            for ab, p in ((0, p_a), (1, p_b)):
                zc[g, k, ab] = remote(
                    sources[g].at[pl.ds(p, 1)],
                    W.at[g, m, pl.ds(p, 1)],
                    gz_s.at[g, k - 1, ab],
                    gz_r.at[g, k - 1, ab],
                    dev,
                )

    def spread(at, stage, ss, rs):
        if stage == 0:
            pieces = ((p_a, 1, x_dev), (p_b, 1, y_dev))
        elif stage == 1:
            pieces = ((cb * 4 + yb * 2, 2, y_dev), (8 + cb * 4 + xb * 2, 2, x_dev))
        else:
            pieces = ((cb * 4, 4, core_dev), (8 + cb * 4, 4, core_dev))
        return [
            remote(at(p, n), at(p, n), ss.at[stage, ab], rs.at[stage, ab], dev)
            for ab, (p, n, dev) in enumerate(pieces)
        ]

    def gather_start(g, stage):
        for k in hops:
            source = lax.rem(m + n_mp - k, n_mp)
            if stage == 0:
                for ab in range(2):
                    zc[g, k, ab].wait_recv()
            else:
                for copy in ac[g, stage - 1, k]:
                    copy.wait_recv()
            ac[g, stage, k] = spread(
                lambda p, n: W.at[g, source, pl.ds(p, n)],
                stage,
                ga_s.at[g, k - 1],
                ga_r.at[g, k - 1],
            )

    def gather_end(g):
        for k in hops:
            for copy in ac[g, 2, k]:
                copy.wait_recv()
        own_loads[g].wait()

    gather_z(0)
    sb_copies = []
    for k in hops:
        sb_copies.append(
            remote(
                par.at[pl.ds(8, 8)],
                SB.at[m],
                sb_s.at[k - 1],
                sb_r.at[k - 1],
                (d, lax.rem(m + k, n_mp)),
            )
        )
    SB[m] = par[8:16]

    HM3[...] = jnp.where(
        iota((3 * BLOCK, shard), 0) // BLOCK == iota((3 * BLOCK, shard), 1) // HEAD_DIM, 1.0, 0.0
    ).astype(LOW)
    BM[...] = jnp.where(
        lax.rem(iota((3 * BLOCK, BLOCK), 0), BLOCK) // LEN == iota((3 * BLOCK, BLOCK), 1) // LEN,
        0.0,
        FAR,
    )
    HM4[...] = jnp.where(
        iota((256, 256), 0) // 64 == iota((256, 256), 1) // HEAD_DIM, 1.0, 0.0
    ).astype(LOW)
    POOL[...] = jnp.where(iota(POOL.shape, 1) // LEN == iota(POOL.shape, 0), 1.0, 0.0).astype(LOW)

    RES[pl.ds(0, image_rows), :] = jnp.zeros((image_rows, width), F32)
    GP[3, pl.ds(0, image_rows), :] = jnp.zeros((image_rows, width), LOW)
    gain_one = par[0:1]
    gain_two = par[1:2]

    def image_norm(i, carry):
        x = imt[i].astype(F32)
        at = pl.multiple_of(i * 64, 64)
        RES[pl.ds(at, image_len), :] = x
        GP[3, pl.ds(at, image_len), :] = (standard(x)[0] * gain_one).astype(LOW)
        return carry

    lax.fori_loop(0, images, image_norm, 0)
    for i in range(3):
        image_loads[i].wait()

    def image_qkv(j, carry):
        GP[j, pl.ds(0, image_rows), :] = dot(
            GP[3, pl.ds(0, image_rows), :], IW[j].reshape(width, width)
        ).astype(LOW)
        return carry

    lax.fori_loop(0, 3, image_qkv, 0)
    for i in range(8, 11):
        load_image(i)
    gather_start(0, 0)
    gather_z(1)

    key_valid = jnp.where(iota((256, 64), 1) < image_len, 0.0, FAR)
    lane_head = iota((64, 256), 1) // HEAD_DIM

    def image_attention(i, carry):
        at = pl.multiple_of(i * 64, 64)
        for n in range(width // 256):
            lanes = slice(256 * n, 256 * n + 256)
            q = GP[0, pl.ds(at, 64), lanes]
            k = GP[1, pl.ds(at, 64), lanes]
            v = GP[2, pl.ds(at, 64), lanes]
            logits = dot_nt(jnp.concatenate([q] * 4, axis=0) * HM4[...], k) * 0.125 + key_valid
            expos = jnp.exp(logits - jnp.max(logits, axis=-1, keepdims=True))
            probs = (expos * (1.0 / jnp.sum(expos, axis=-1, keepdims=True))).astype(LOW)
            o = dot(probs, v)
            mix = jnp.where(
                lane_head < 2,
                jnp.where(lane_head == 0, o[0:64], o[64:128]),
                jnp.where(lane_head == 2, o[128:192], o[192:256]),
            )
            N2[pl.ds(at, 64), lanes] = mix.astype(LOW)
        return carry

    lax.fori_loop(0, images, image_attention, 0)
    gather_start(0, 1)
    image_loads[3].wait()

    def image_out(n, carry):
        lanes = pl.ds(pl.multiple_of(n * 256, 256), 256)
        RES[pl.ds(0, image_rows), lanes] += dot(
            N2[pl.ds(0, image_rows), :], IW[3, :, :, lanes].reshape(width, 256)
        )
        return carry

    lax.fori_loop(0, width // 256, image_out, 0)
    load_image(11)

    def image_norm_two(t, carry):
        at = pl.ds(pl.multiple_of(t * 16, 16), 16)
        GP[3, at, :] = (standard(RES[at, :])[0] * gain_two).astype(LOW)
        return carry

    lax.fori_loop(0, image_rows // 16, image_norm_two, 0, unroll=4)
    IP[...] = jnp.zeros_like(IP)
    for i in range(images):
        IP[i : i + 1, :] = jnp.sum(RES[64 * i : 64 * i + image_len, :], axis=0, keepdims=True) * (
            1.0 / image_len
        )
    image_pool = jnp.where(
        (iota((16, image_rows), 1) // 64 == iota((16, image_rows), 0))
        & (lax.rem(iota((16, image_rows), 1), 64) < image_len),
        1.0,
        0.0,
    ).astype(LOW)
    for i in range(4, 12):
        image_loads[i].wait()

    def image_feed(u, carry):
        ACC[pl.ds(0, image_rows), :] = dot(
            GP[3, pl.ds(0, image_rows), :], IW[4 + u].reshape(width, width)
        )

        def activate(t, inner):
            at = pl.ds(pl.multiple_of(t * 16, 16), 16)
            h = ACC[at, :]
            act = 0.5 * h * (1.0 + jnp.tanh(GELU_A * h * (1.0 + GELU_B * h * h)))
            N2[at, :] = act.astype(LOW)
            return inner

        lax.fori_loop(0, image_rows // 16, activate, 0, unroll=4)
        pooled = (dot(image_pool, N2[pl.ds(0, image_rows), :]) * (1.0 / image_len)).astype(LOW)
        IP[...] += dot(pooled, IW[u].reshape(width, width))
        return carry

    lax.fori_loop(0, 2, image_feed, 0)
    gather_start(0, 2)
    gather_start(1, 0)
    gather_z(2)
    lax.fori_loop(2, 4, image_feed, 0)
    pooled_image = IP[0:8]
    EMB[me] = (
        pooled_image
        * lax.rsqrt(jnp.sum(pooled_image * pooled_image, axis=-1, keepdims=True) + 1e-6)
    ).astype(LOW)

    def send_embed(k, carry):
        q = lax.rem(me + k, n_all)
        pltpu.make_async_remote_copy(
            src_ref=EMB.at[me],
            dst_ref=EMB.at[me],
            send_sem=emb_s,
            recv_sem=emb_r,
            device_id=(q // n_mp, lax.rem(q, n_mp)),
            device_id_type=pl.DeviceIdType.MESH,
        ).start()
        return carry

    lax.fori_loop(1, n_all, send_embed, 0)

    tok_copy.wait()
    g1, g2 = par[4:5], par[5:6]
    b1, b2 = par[6:7], par[7:8]

    def norm_one(t, carry):
        at = pl.ds(pl.multiple_of(t * LEN, LEN), LEN)
        N1[at, :] = (standard(TOK[t].astype(F32))[0] * g1 + b1).astype(LOW)
        return carry

    lax.fori_loop(0, n_cap, norm_one, 0, unroll=7)
    for copy in sb_copies:
        copy.wait_recv()
    gather_end(0)

    def project(t, carry):
        s, j = t // 3, lax.rem(t, 3)
        weight = W[0, s, pl.ds(4 * j, 4)].reshape(shard, width)
        QKV[j, s] = (dot_nt(N1[...], weight) + SB[s, pl.ds(j, 1), 0:shard]).astype(LOW)
        return carry

    lax.fori_loop(0, 3 * n_mp, project, 0)
    gather_start(1, 1)
    lane_three = iota((BLOCK, shard), 1) // HEAD_DIM

    def join_heads(o):
        return jnp.where(
            lane_three == 0,
            o[0:BLOCK],
            jnp.where(lane_three == 1, o[BLOCK : 2 * BLOCK], o[2 * BLOCK : 3 * BLOCK]),
        )

    def attention(b, carry):
        at = pl.ds(pl.multiple_of(b * BLOCK, 16), BLOCK)
        for s in range(n_mp):
            q = jnp.concatenate([QKV[0, s, at, :]] * 3, axis=0) * HM3[...]
            logits = dot_nt(q, QKV[1, s, at, :]) * 0.125 + BM[...]
            expos = jnp.exp(logits - jnp.max(logits, axis=-1, keepdims=True))
            probs = (expos * (1.0 / jnp.sum(expos, axis=-1, keepdims=True))).astype(LOW)
            PR[s, b] = probs
            MIX[s, at, :] = join_heads(dot(probs, QKV[2, s, at, :])).astype(LOW)
        return carry

    lax.fori_loop(0, n_blocks, attention, 0)
    gather_start(1, 2)
    gather_start(2, 0)

    def attend_out(n, carry):
        lanes = pl.ds(pl.multiple_of(n * 256, 256), 256)
        total = dot(MIX[0], W[0, 0, pl.ds(12, 4), :, lanes].reshape(shard, 256))
        for s in range(1, n_mp):
            total += dot(MIX[s], W[0, s, pl.ds(12, 4), :, lanes].reshape(shard, 256))
        ACC[:, lanes] = total
        return carry

    lax.fori_loop(0, width // 256, attend_out, 0)
    out_bias = par[2:3]

    def norm_two(t, carry):
        at = pl.ds(pl.multiple_of(t * LEN, LEN), LEN)
        x = TOK[t].astype(F32) + (ACC[at, :] + out_bias)
        RES[at, :] = x
        N2[at, :] = (standard(x)[0] * g2 + b2).astype(LOW)
        return carry

    lax.fori_loop(0, n_cap, norm_two, 0, unroll=7)
    gather_end(1)
    gather_start(2, 1)

    def feed(s, carry):
        ACC[...] = dot(N2[...], W[1, s].reshape(width, width))
        bias = SB[s, 3:4, :]

        def activate(t, inner):
            at = pl.ds(pl.multiple_of(t * LEN, LEN), LEN)
            act, slope = gelu_parts(ACC[at, :] + bias)
            GT[at, :] = act.astype(LOW)
            GP[s, at, :] = slope.astype(LOW)
            return inner

        lax.fori_loop(0, n_cap, activate, 0, unroll=7)
        PA[s] = (dot(POOL[...], GT[...]) * (1.0 / LEN)).astype(LOW)
        return carry

    lax.fori_loop(0, n_mp, feed, 0)
    gather_start(2, 2)

    def pool_residual(n, carry):
        lanes = pl.ds(pl.multiple_of(n * 128, 128), 128)
        res = RES[:, lanes]
        res_high = res.astype(LOW)
        res_low = (res - res_high.astype(F32)).astype(LOW)
        EL[:, lanes] = (dot(POOL[...], res_high) + dot(POOL[...], res_low)) * (1.0 / LEN)
        return carry

    lax.fori_loop(0, width // 128, pool_residual, 0)
    pooled = EL[...] + par[3:4]
    gather_end(2)
    for s in range(n_mp):
        pooled += dot(PA[s], W[2, s].reshape(width, width))
    inverse = lax.rsqrt(jnp.sum(pooled * pooled, axis=-1, keepdims=True) + 1e-6)
    embed = pooled * inverse
    EL[...] = embed

    pltpu.make_async_copy(EMB.at[pl.ds(0, n_all - 1)], EMB.at[pl.ds(0, n_all - 1)], emb_r).wait()
    group = min(n_all, 32)

    def embeds(c):
        part = EMB[c * group : c * group + group].astype(F32)
        return part.reshape(group * 8, width).astype(LOW)

    scaling = jnp.exp(par[12:13, 0:1])
    embed_low = embed.astype(LOW)
    scores = scaling * jnp.concatenate(
        [dot_nt(embed_low, embeds(c)) for c in range(n_all // group)], axis=1
    )
    cap_rows = scores.shape[0]
    column = iota((cap_rows, t_all), 1)
    col_ok = lax.rem(column, 8) < images
    row_ok = iota((cap_rows, t_all), 0) < n_cap
    image_id = (column // 8) * images + lax.rem(column, 8)
    matches = jnp.where((cap[half] == image_id) & col_ok & row_ok, 1.0, 0.0)
    by_row = jnp.where(col_ok, scores, FAR)
    row_top = jnp.max(by_row, axis=1, keepdims=True)
    row_lse = row_top + jnp.log(jnp.sum(jnp.exp(by_row - row_top), axis=1, keepdims=True))
    row_positive = jnp.sum(scores * matches, axis=1, keepdims=True)
    row_part = jnp.sum(
        jnp.where(iota((cap_rows, 1), 0) < n_cap, row_lse - row_positive, 0.0), axis=0, keepdims=True
    )
    by_column = jnp.where(row_ok, scores, FAR)
    top = jnp.max(by_column, axis=0, keepdims=True)
    MSG[...] = jnp.zeros_like(MSG)
    MSG[0:1, :] = top
    MSG[1:2, :] = jnp.sum(jnp.exp(by_column - top), axis=0, keepdims=True)
    MSG[2:3, :] = jnp.sum(scores * matches, axis=0, keepdims=True)
    MSG[3:4, :] = jnp.sum(matches, axis=0, keepdims=True)
    MSG[4:5, :] = jnp.broadcast_to(row_part, (1, t_all))
    low = lax.rem(d, 8)
    slot = low * 2 + half
    STATS[slot] = MSG[...]

    def send_stats(k, carry):
        q = lax.rem(slot + k, 16)
        pltpu.make_async_remote_copy(
            src_ref=MSG,
            dst_ref=STATS.at[slot],
            send_sem=st_s,
            recv_sem=st_r,
            device_id=(d - low + q // 2, m - half + lax.rem(q, 2)),
            device_id_type=pl.DeviceIdType.MESH,
        ).start()
        return carry

    lax.fori_loop(1, 16, send_stats, 0)
    pltpu.make_async_copy(STATS.at[pl.ds(0, 15)], STATS.at[pl.ds(0, 15)], st_r).wait()
    top = jnp.max(STATS[:, 0, :], axis=0, keepdims=True)
    total = jnp.sum(STATS[:, 1, :] * jnp.exp(STATS[:, 0, :] - top), axis=0, keepdims=True)
    positive = jnp.sum(STATS[:, 2, :], axis=0, keepdims=True)
    count = jnp.sum(STATS[:, 3, :], axis=0, keepdims=True)
    row_sum = jnp.sum(STATS[:, 4, :], axis=0, keepdims=True)
    for x in range(extra):
        XST[0, x] = jnp.concatenate(
            [top, total, positive, count, row_sum, jnp.zeros((3, t_all), F32)], axis=0
        )
        remote(
            XST.at[0, x], XST.at[1, x], stx_s.at[x], stx_r.at[x], (flip(d, 3 + x), m)
        ).wait_recv()
        other = XST[1, x]
        joined = jnp.maximum(top, other[0:1])
        total = total * jnp.exp(top - joined) + other[1:2] * jnp.exp(other[0:1] - joined)
        top = joined
        positive = positive + other[2:3]
        count = count + other[3:4]
        row_sum = row_sum + other[4:5]
    ok = col_ok[0:1]
    count = jnp.where(ok, count, 1.0)
    col_lse = top + jnp.log(total)
    column_part = jnp.sum(
        jnp.where(ok, col_lse - positive / count, 0.0), axis=1, keepdims=True
    )
    loss = 0.5 * (row_sum[:, 0:1] * (1.0 / total_captions) + column_part * (1.0 / total_images))
    weight = 0.5 * total_captions / total_images
    grad_scores = 0.5 * (jnp.exp(by_row - row_lse) - matches) + weight * (
        jnp.exp(by_column - col_lse) - matches * (1.0 / count)
    )
    grad_scores = jnp.where(col_ok & row_ok, grad_scores, 0.0)
    grad_log = jnp.sum(
        jnp.sum(grad_scores * scores, axis=1, keepdims=True), axis=0, keepdims=True
    )
    embed = EL[...]
    grad_cosine = (scaling * grad_scores).astype(LOW)
    grad_embed = dot(grad_cosine[:, 0 : group * 8], embeds(0))
    for c in range(1, n_all // group):
        grad_embed += dot(grad_cosine[:, c * group * 8 : (c + 1) * group * 8], embeds(c))
    grad_pooled = (
        grad_embed - embed * jnp.sum(embed * grad_embed, axis=-1, keepdims=True)
    ) * inverse
    SG[0] = jnp.zeros(SG.shape[1:], F32)
    SG[0, 13:14, :] = jnp.sum(grad_pooled, axis=0, keepdims=True)
    SG[0, 18:19, :] = jnp.broadcast_to(grad_log, (1, width))
    GPL[0] = grad_pooled.astype(LOW)
    grad_rows = grad_pooled * (1.0 / LEN)
    EL[...] = grad_rows
    GPL[1] = grad_rows.astype(LOW)

    def part(g, i):
        return IW.at[2 * g + i]

    places = (4, 7, 6)

    def whole(g):
        return IW.at[places[g]]

    def settle(copies):
        for copy in copies:
            copy.wait_send()
        sends[:] = [other for other in sends if all(other is not copy for copy in copies)]

    def add_pieces(g, i, p, n, read):
        for r in range(n):
            IW[2 * g + i, p + r] = IW[2 * g + i, p + r] + read(r)

    state = {}
    stores = []

    def reduce_step(g, step):
        if step == 0:
            if g == 0:
                settle([copy for old in range(4) for copy in state[2, old]])
            copies = []
            for i in range(2):
                for ab in range(2):
                    p = 8 * ab + 4 * (1 - cb)
                    copies.append(
                        remote(
                            part(g, i).at[pl.ds(p, 4)],
                            RCORE.at[g % 2, i, ab],
                            rs_s.at[g, 0, 2 * i + ab],
                            rs_r.at[g, 0, 2 * i + ab],
                            core_dev,
                        )
                    )
            state[g, 0] = copies
        elif step == 1:
            for copy in state[g, 0]:
                copy.wait_recv()
            for i in range(2):
                for ab in range(2):
                    add_pieces(
                        g, i, 8 * ab + 4 * cb, 4, lambda r, i=i, ab=ab: RCORE[g % 2, i, ab, r]
                    )
            copies = []
            for i in range(2):
                for ab, b, dev in ((0, yb, y_dev), (1, xb, x_dev)):
                    p = 8 * ab + 4 * cb + 2 * (1 - b)
                    copies.append(
                        remote(
                            part(g, i).at[pl.ds(p, 2)],
                            RB1.at[g % 2, i, ab],
                            rs_s.at[g, 1, 2 * i + ab],
                            rs_r.at[g, 1, 2 * i + ab],
                            dev,
                        )
                    )
            state[g, 1] = copies
        elif step == 2:
            for copy in state[g, 1]:
                copy.wait_recv()
            for i in range(2):
                for ab, b in ((0, yb), (1, xb)):
                    add_pieces(
                        g,
                        i,
                        8 * ab + 4 * cb + 2 * b,
                        2,
                        lambda r, i=i, ab=ab: RB1[g % 2, i, ab, r],
                    )
            copies = []
            for i in range(2):
                for ab, b, c, dev in ((0, yb, xb, x_dev), (1, xb, yb, y_dev)):
                    p = 8 * ab + 4 * cb + 2 * b + 1 - c
                    copies.append(
                        remote(
                            part(g, i).at[pl.ds(p, 1)],
                            RB2.at[g % 2, i, ab],
                            rs_s.at[g, 2, 2 * i + ab],
                            rs_r.at[g, 2, 2 * i + ab],
                            dev,
                        )
                    )
            state[g, 2] = copies
        elif step == 3:
            for copy in state[g, 2]:
                copy.wait_recv()
            for i in range(2):
                for ab, p in ((0, p_a), (1, p_b)):
                    add_pieces(g, i, p, 1, lambda r, i=i, ab=ab: RB2[g % 2, i, ab, r])
            state[g, 3] = [
                remote(
                    part(g, 1).at[pl.ds(p, 1)],
                    RZ.at[g, ab],
                    rs_s.at[g, 3, ab],
                    rs_r.at[g, 3, ab],
                    pair_dev,
                )
                for ab, p in ((0, p_a), (1, p_b))
            ]
        elif step == 4:
            for copy in state[g, 3]:
                copy.wait_recv()
            for ab, p in ((0, p_a), (1, p_b)):
                IW[places[g], p] = IW[2 * g, p] + RZ[g, ab, 0]
            for x in range(extra):
                copies = [
                    remote(
                        whole(g).at[pl.ds(p, 1)],
                        XR.at[g % 2, x, ab],
                        xr_s.at[g, x, ab],
                        xr_r.at[g, x, ab],
                        (flip(d, 3 + x), m),
                    )
                    for ab, p in ((0, p_a), (1, p_b))
                ]
                for copy in copies:
                    copy.wait_recv()
                settle(copies)
                for ab, p in ((0, p_a), (1, p_b)):
                    IW[places[g], p] = IW[places[g], p] + XR[g % 2, x, ab, 0]
            state[g, 4] = spread(
                lambda p, n: whole(g).at[pl.ds(p, n)], 0, ag_s.at[g], ag_r.at[g]
            )
        elif step in (5, 6):
            for copy in state[g, step - 1]:
                copy.wait_recv()
            state[g, step] = spread(
                lambda p, n: whole(g).at[pl.ds(p, n)], step - 4, ag_s.at[g], ag_r.at[g]
            )
        else:
            for copy in state[g, 6]:
                copy.wait_recv()
            stores.append(local(whole(g), red.at[g], out_sem.at[g]))

    shards = (m, pair)
    for i in range(2):
        IW[4 + i] = dot_tn(PA[shards[i]], GPL[0]).astype(LOW).reshape(16, PIECE, width)
    reduce_step(2, 0)

    def grad_activation(s, carry):
        GA[s] = dot_nt(GPL[1], W[2, s].reshape(width, width))
        return carry

    lax.fori_loop(0, n_mp, grad_activation, 0)
    reduce_step(2, 1)
    ones = jnp.ones((16, rows), LOW)

    def grad_hidden(s, carry):
        def scale(t, inner):
            at = pl.ds(pl.multiple_of(t * LEN, LEN), LEN)
            GP[s, at, :] = (GP[s, at, :].astype(F32) * GA[s, pl.ds(t, 1), :]).astype(LOW)
            return inner

        lax.fori_loop(0, n_cap, scale, 0, unroll=7)
        SG[0, pl.ds(8 + s, 1), :] = dot(ones, GP[s])[0:1]
        return carry

    lax.fori_loop(0, n_mp, grad_hidden, 0)
    reduce_step(2, 2)

    def expand_gradient(i, carry):
        s = m + i * (pair - m)
        IW[2 + i] = dot_tn(N2[...], GP[s]).astype(LOW).reshape(16, PIECE, width)
        return carry

    lax.fori_loop(0, 2, expand_gradient, 0)
    reduce_step(1, 0)
    reduce_step(2, 3)

    def grad_norm_two(n, carry):
        p = pl.ds(8 * n, 8)
        total = dot_nt(GP[0], W[1, 0, p].reshape(8 * PIECE, width))
        for s in range(1, n_mp):
            total += dot_nt(GP[s], W[1, s, p].reshape(8 * PIECE, width))
        ACC[:, pl.ds(pl.multiple_of(n * 384, 128), 384)] = total
        return carry

    lax.fori_loop(0, 2, grad_norm_two, 0)
    reduce_step(1, 1)
    reduce_step(2, 4)

    def norm_back(e, gain, x):
        xhat, scale = standard(x)
        eg = e * gain
        c1 = jnp.sum(eg, axis=-1, keepdims=True) * (1.0 / width)
        c2 = jnp.sum(eg * xhat, axis=-1, keepdims=True) * (1.0 / width)
        return (eg - c1 - xhat * c2) * scale, sum8(e * xhat), sum8(e)

    zero8 = jnp.zeros((8, width), F32)

    def back_two(t, carry):
        at = pl.ds(pl.multiple_of(t * LEN, LEN), LEN)
        dv, dg, db = norm_back(ACC[at, :], g2, RES[at, :])
        g = EL[pl.ds(t, 1), :] + dv
        RES[at, :] = g
        GRL[at, :] = g.astype(LOW)
        return carry[0] + dg, carry[1] + db, carry[2] + sum8(g)

    dg, db, do = lax.fori_loop(0, n_cap, back_two, (zero8, zero8, zero8), unroll=7)
    SG[0, 15:16, :] = jnp.sum(dg, axis=0, keepdims=True)
    SG[0, 17:18, :] = jnp.sum(db, axis=0, keepdims=True)
    SG[0, 12:13, :] = jnp.sum(do, axis=0, keepdims=True)

    for i in range(2):
        IW[i, pl.ds(12, 4)] = dot_tn(MIX[shards[i]], GRL[...]).astype(LOW).reshape(4, PIECE, width)
    reduce_step(1, 2)
    reduce_step(2, 5)

    def grad_mixture(s, carry):
        MIX[s] = dot_nt(GRL[...], W[0, s, pl.ds(12, 4)].reshape(shard, width)).astype(LOW)
        return carry

    lax.fori_loop(0, n_mp, grad_mixture, 0)
    reduce_step(2, 6)

    def attention_back(b, carry):
        at = pl.ds(pl.multiple_of(b * BLOCK, 16), BLOCK)
        for s in range(n_mp):
            q = jnp.concatenate([QKV[0, s, at, :]] * 3, axis=0) * HM3[...]
            g = jnp.concatenate([MIX[s, at, :]] * 3, axis=0) * HM3[...]
            k = QKV[1, s, at, :]
            v = QKV[2, s, at, :]
            low_probs = PR[s, b]
            probs = low_probs.astype(F32)
            grad_probs = dot_nt(g, v)
            inner = jnp.sum(grad_probs * probs, axis=-1, keepdims=True)
            grad_logits = (probs * (grad_probs - inner)).astype(LOW)
            QKV[2, s, at, :] = dot_tn(low_probs, g).astype(LOW)
            QKV[0, s, at, :] = (join_heads(dot(grad_logits, k)) * 0.125).astype(LOW)
            QKV[1, s, at, :] = (dot_tn(grad_logits, q) * 0.125).astype(LOW)
        return carry

    lax.fori_loop(0, n_blocks, attention_back, 0)
    reduce_step(1, 3)

    def grad_norm_one(n, carry):
        lanes = pl.ds(pl.multiple_of(n * 256, 256), 256)
        total = None
        for s in range(n_mp):
            for j in range(3):
                term = dot(QKV[j, s], W[0, s, pl.ds(4 * j, 4), :, lanes].reshape(shard, 256))
                total = term if total is None else total + term
        ACC[:, lanes] = total
        return carry

    lax.fori_loop(0, width // 256, grad_norm_one, 0)
    reduce_step(1, 4)

    def back_one(t, carry):
        at = pl.ds(pl.multiple_of(t * LEN, LEN), LEN)
        dv, dg, db = norm_back(ACC[at, :], g1, TOK[t].astype(F32))
        GT[at, :] = (RES[at, :] + dv).astype(LOW)
        return carry[0] + dg, carry[1] + db

    dg, db = lax.fori_loop(0, n_cap, back_one, (zero8, zero8), unroll=7)
    SG[0, 14:15, :] = jnp.sum(dg, axis=0, keepdims=True)
    SG[0, 16:17, :] = jnp.sum(db, axis=0, keepdims=True)
    gt_copy = remote(GT, gt.at[half], gt_s, gt_r, pair_dev)
    stores.append(local(GT, gt.at[half], out_sem.at[3]))

    def attend_gradient(t, carry):
        i, j = t // 3, lax.rem(t, 3)
        s = m + i * (pair - m)
        IW[i, pl.ds(4 * j, 4)] = dot_tn(QKV[j, s], N1[...]).astype(LOW).reshape(4, PIECE, width)
        return carry

    lax.fori_loop(0, 6, attend_gradient, 0)
    reduce_step(0, 0)

    def bias_gradient(s, carry):
        SG[0, pl.ds(s, 1), 0:shard] = dot(ones, QKV[0, s])[0:1]
        SG[0, pl.ds(4 + s, 1), 0:shard] = dot(ones, QKV[2, s])[0:1]
        return carry

    lax.fori_loop(0, n_mp, bias_gradient, 0)
    reduce_step(1, 5)

    small_devs = [core_dev, y_dev, x_dev, pair_dev] + [(flip(d, 3 + x), m) for x in range(extra)]
    small = {}

    def small_start(i):
        small[i] = remote(SG.at[i], SGR.at[i], sg_s.at[i], sg_r.at[i], small_devs[i])

    def small_end(i):
        small[i].wait_recv()
        SG[i + 1] = SG[i] + SGR[i]

    small_start(0)
    reduce_step(0, 1)
    small_end(0)
    small_start(1)
    reduce_step(1, 6)
    reduce_step(0, 2)
    small_end(1)
    small_start(2)
    reduce_step(0, 3)
    small_end(2)
    small_start(3)
    reduce_step(0, 4)
    small_end(3)
    for i in range(4, 4 + extra):
        small_start(i)
        small_end(i)
    reduce_step(0, 5)
    reduce_step(0, 6)
    last = SG.shape[0] - 1
    sgo[...] = jnp.zeros_like(sgo)
    sgo[0:1, :] = SG[last, pl.ds(m, 1), :]
    sgo[1:2, :] = SG[last, pl.ds(4 + m, 1), :]
    sgo[2:3, :] = SG[last, pl.ds(8 + m, 1), :]
    sgo[3:10, :] = SG[last, 12:19, :]
    sgo[10:11, :] = jnp.broadcast_to(loss, (1, width))
    for g in range(3):
        reduce_step(g, 7)
    gt_copy.wait_recv()
    pltpu.make_async_copy(EMB.at[pl.ds(0, n_all - 1)], EMB.at[pl.ds(0, n_all - 1)], emb_s).wait()
    pltpu.make_async_copy(STATS.at[pl.ds(0, 15)], STATS.at[pl.ds(0, 15)], st_s).wait()
    for copy in sends:
        copy.wait_send()
    for copy in stores:
        copy.wait()


def local_step(
    n_dp,
    n_mp,
    caption_tokens,
    image_tokens,
    image_attend,
    image_output,
    image_expand,
    image_reduce,
    image_gains,
    caption_attend,
    attend_bias,
    caption_output,
    output_bias,
    caption_expand,
    expand_bias,
    caption_reduce,
    reduce_bias,
    norm_gains,
    norm_shifts,
    log_scale,
    caption_image,
):
    captions, length, width = caption_tokens.shape
    images, image_len, _ = image_tokens.shape
    shard = caption_attend.shape[2]
    units = caption_expand.shape[1]
    n_cap = captions // 2
    rows = n_cap * length
    n_blocks = rows // BLOCK
    n_all = n_dp * n_mp
    t_all = n_all * 8
    extra = n_dp.bit_length() - 1 - 3
    assert length == LEN and units == width and shard * n_mp == width and width == 16 * PIECE

    def pieces(a):
        return a.reshape(a.shape[:-2] + (16, PIECE, a.shape[-1]))

    wao = pieces(
        jnp.concatenate(
            [jnp.swapaxes(caption_attend, 1, 2).reshape(3 * shard, width), caption_output], axis=0
        )
    )

    def row(a):
        return jnp.pad(a.reshape(1, -1), ((0, 0), (0, width - a.size)))

    zero_row = jnp.zeros((1, width), F32)
    par = jnp.concatenate(
        [
            image_gains,
            row(output_bias),
            row(reduce_bias),
            norm_gains,
            norm_shifts,
            row(attend_bias[0]),
            zero_row,
            row(attend_bias[1]),
            row(expand_bias),
            row(log_scale),
            zero_row,
            zero_row,
            zero_row,
        ],
        axis=0,
    )
    cap = jnp.pad(
        caption_image.reshape(2, n_cap, 1), ((0, 0), (0, 64 - n_cap), (0, 0)), constant_values=-1
    )
    any_space = pl.BlockSpec(memory_space=pl.ANY)
    vmem = pl.BlockSpec(memory_space=pltpu.VMEM)
    nx = max(extra, 1)
    dma = pltpu.SemaphoreType.DMA
    scratch = [
        pltpu.VMEM((3, n_mp, 16, PIECE, width), LOW),
        pltpu.VMEM((8, 16, PIECE, width), LOW),
        pltpu.VMEM((n_cap, length, width), LOW),
        pltpu.VMEM((rows, width), LOW),
        pltpu.VMEM((3, n_mp, rows, shard), LOW),
        pltpu.VMEM((n_mp, n_blocks, 3 * BLOCK, BLOCK), LOW),
        pltpu.VMEM((n_mp, rows, shard), LOW),
        pltpu.VMEM((rows, width), F32),
        pltpu.VMEM((rows, width), LOW),
        pltpu.VMEM((n_mp, rows, width), LOW),
        pltpu.VMEM((n_mp, 64, width), LOW),
        pltpu.VMEM((rows, width), F32),
        pltpu.VMEM((rows, width), LOW),
        pltpu.VMEM((rows, width), LOW),
        pltpu.VMEM((16, width), F32),
        pltpu.VMEM((n_all, 8, width), LOW),
        pltpu.VMEM((8, t_all), F32),
        pltpu.VMEM((16, 8, t_all), F32),
        pltpu.VMEM((n_mp, 8, width), F32),
        pltpu.VMEM((3 * BLOCK, shard), LOW),
        pltpu.VMEM((3 * BLOCK, BLOCK), F32),
        pltpu.VMEM((256, 256), LOW),
        pltpu.VMEM((64, rows), LOW),
        pltpu.VMEM((64, width), F32),
        pltpu.VMEM((2, 64, width), LOW),
        pltpu.VMEM((n_mp, 64, width), F32),
        pltpu.VMEM((2, 2, 2, 4, PIECE, width), LOW),
        pltpu.VMEM((2, 2, 2, 2, PIECE, width), LOW),
        pltpu.VMEM((2, 2, 2, 1, PIECE, width), LOW),
        pltpu.VMEM((3, 2, 1, PIECE, width), LOW),
        pltpu.VMEM((2, nx, 2, 1, PIECE, width), LOW),
        pltpu.VMEM((2, nx, 8, t_all), F32),
        pltpu.VMEM((5 + extra, 24, width), F32),
        pltpu.VMEM((4 + extra, 24, width), F32),
        dma((3, 3, 2)),
        dma((3, 3, 2)),
        dma((3, 3, 3, 2)),
        dma((3, 3, 3, 2)),
        dma((3,)),
        dma((12,)),
        dma,
        dma((3,)),
        dma((3,)),
        dma,
        dma,
        dma,
        dma,
        dma((nx,)),
        dma((nx,)),
        dma((3, 4, 4)),
        dma((3, 4, 4)),
        dma((3, 3, 2)),
        dma((3, 3, 2)),
        dma((3, nx, 2)),
        dma((3, nx, 2)),
        dma((4 + extra,)),
        dma((4 + extra,)),
        dma,
        dma,
        dma((4,)),
    ]
    red, gt, sgo = pl.pallas_call(
        functools.partial(body, n_dp, n_mp),
        out_shape=(
            jax.ShapeDtypeStruct((3, 16, PIECE, width), LOW),
            jax.ShapeDtypeStruct((2, rows, width), LOW),
            jax.ShapeDtypeStruct((16, width), F32),
        ),
        in_specs=[any_space, vmem] + [any_space] * 7 + [vmem, vmem],
        out_specs=(any_space, any_space, vmem),
        scratch_shapes=scratch,
        compiler_params=pltpu.CompilerParams(
            collective_id=0, has_side_effects=True, vmem_limit_bytes=66_000_000
        ),
        name="step",
    )(
        caption_tokens,
        image_tokens,
        pieces(image_attend),
        pieces(image_output),
        pieces(image_expand),
        image_reduce.reshape(-1, 16, PIECE, width),
        wao,
        pieces(caption_expand),
        pieces(caption_reduce),
        par,
        cap,
    )
    red = red.astype(F32).reshape(3, width, width)
    gradient_attend = jnp.swapaxes(red[0, : 3 * shard].reshape(3, shard, width), 1, 2)
    return (
        sgo[10, 0:1],
        gt.astype(F32).reshape(captions, length, width),
        gradient_attend,
        sgo[0:2, :shard],
        red[0, 3 * shard :],
        sgo[3],
        red[1],
        sgo[2],
        red[2],
        sgo[4],
        sgo[5:7],
        sgo[7:9],
        sgo[9, 0:1],
    )


def solution(mesh):
    in_specs = (
        P("dp", None, None),
        P(("dp", "mp"), None, None),
        P(),
        P(),
        P(),
        P(),
        P(),
        P(None, None, "mp"),
        P(None, "mp"),
        P("mp", None),
        P(),
        P(None, "mp"),
        P("mp"),
        P("mp", None),
        P(),
        P(),
        P(),
        P(),
        P("dp"),
    )
    out_specs = (
        P(),
        P("dp", None, None),
        P(None, None, "mp"),
        P(None, "mp"),
        P("mp", None),
        P(),
        P(None, "mp"),
        P("mp"),
        P("mp", None),
        P(),
        P(),
        P(),
        P(),
    )
    step = functools.partial(local_step, mesh.shape["dp"], mesh.shape["mp"])
    return jax.shard_map(step, mesh=mesh, in_specs=in_specs, out_specs=out_specs, check_vma=False)
```

```python
import functools

import jax
import jax.numpy as jnp
from jax import lax
from jax.experimental import pallas as pl
from jax.experimental.pallas import tpu as pltpu
from jax.sharding import PartitionSpec as P

HEAD_DIM = 64
LEN = 16
PIECE = 48
BLOCK = 112
F32 = jnp.float32
LOW = jnp.bfloat16
FAR = -1e30
GELU_A = 0.7978845608028654
GELU_B = 0.044715


def dot(a, b):
    return lax.dot_general(a, b, (((1,), (0,)), ((), ())), preferred_element_type=F32)


def dot_nt(a, b):
    return lax.dot_general(a, b, (((1,), (1,)), ((), ())), preferred_element_type=F32)


def dot_tn(a, b):
    return lax.dot_general(a, b, (((0,), (0,)), ((), ())), preferred_element_type=F32)


def iota(shape, axis):
    return lax.broadcasted_iota(jnp.int32, shape, axis)


def standard(x):
    width = x.shape[-1]
    centred = x - jnp.sum(x, axis=-1, keepdims=True) * (1.0 / width)
    variance = jnp.sum(centred * centred, axis=-1, keepdims=True) * (1.0 / width)
    scale = lax.rsqrt(variance + 1e-6)
    return centred * scale, scale


def gelu_parts(h):
    square = h * h
    t = jnp.tanh(GELU_A * h * (1.0 + GELU_B * square))
    half = 0.5 * (1.0 + t)
    slope = half + 0.5 * h * (1.0 - t * t) * (GELU_A * (1.0 + 3.0 * GELU_B * square))
    return h * half, slope


def sum8(x):
    return x[0:8] + x[8:16]


def body(
    n_dp,
    n_mp,
    tok_in,
    imt,
    ia_in,
    io_in,
    ie_in,
    ir_in,
    ca_in,
    co_in,
    we_in,
    wr_in,
    image_gains,
    attend_bias,
    output_bias,
    expand_bias,
    reduce_bias,
    norm_gains,
    norm_shifts,
    log_scale,
    cap,
    red,
    gt,
    sgo,
    W,
    IW,
    TOK,
    N1,
    QKV,
    PR,
    MIX,
    RES,
    N2,
    GP,
    PA,
    ACC,
    GRL,
    GT,
    IP,
    EMB,
    MSG,
    STATS,
    SBL,
    SB,
    HM3,
    BM,
    HM4,
    POOL,
    EL,
    GPL,
    GA,
    RCORE,
    RB1,
    RB2,
    RZ,
    XR,
    XST,
    SG,
    SGR,
    gz_s,
    gz_r,
    ga_s,
    ga_r,
    loc_sem,
    ca_sem,
    iw_sem,
    tok_sem,
    sb_s,
    sb_r,
    emb_s,
    emb_r,
    st_s,
    st_r,
    stx_s,
    stx_r,
    rs_s,
    rs_r,
    ag_s,
    ag_r,
    xr_s,
    xr_r,
    sg_s,
    sg_r,
    gt_s,
    gt_r,
    out_sem,
):
    d = lax.axis_index("dp")
    m = lax.axis_index("mp")
    n_all = n_dp * n_mp
    me = d * n_mp + m
    bits = n_dp.bit_length() - 1
    extra = bits - 3
    images, image_len = imt.shape[0], imt.shape[1]
    rows = TOK.shape[0] * LEN
    n_cap = TOK.shape[0]
    n_blocks = rows // BLOCK
    width = RES.shape[1]
    shard = QKV.shape[3]
    image_rows = images * 64
    t_all = EMB.shape[0] * 8
    total_images = images * n_all
    total_captions = n_cap * 2 * n_dp

    def bit(v, b):
        return lax.rem(v // (1 << b), 2)

    def flip(v, b):
        return v + (1 - 2 * bit(v, b)) * (1 << b)

    cb, xb, yb = bit(d, 0), bit(d, 1), bit(d, 2)
    half = lax.rem(m, 2)
    pair = flip(m, 0)
    p_a = cb * 4 + yb * 2 + xb
    p_b = 8 + cb * 4 + xb * 2 + yb
    core_dev = (flip(d, 0), m)
    x_dev = (flip(d, 1), m)
    y_dev = (flip(d, 2), m)
    pair_dev = (d, pair)
    sends = []

    def remote(src, dst, ss, rs, dev):
        copy = pltpu.make_async_remote_copy(
            src_ref=src,
            dst_ref=dst,
            send_sem=ss,
            recv_sem=rs,
            device_id=dev,
            device_id_type=pl.DeviceIdType.MESH,
        )
        copy.start()
        sends.append(copy)
        return copy

    def local(src, dst, sem):
        copy = pltpu.make_async_copy(src, dst, sem)
        copy.start()
        return copy

    barrier = pltpu.get_barrier_semaphore()

    def greet(k, carry):
        q = lax.rem(me + k, n_all)
        pl.semaphore_signal(
            barrier,
            inc=1,
            device_id=(q // n_mp, lax.rem(q, n_mp)),
            device_id_type=pl.DeviceIdType.MESH,
        )
        return carry

    lax.fori_loop(1, n_all, greet, 0)

    image_loads = {}

    def load_image(i):
        if i < 3:
            src, slot = ia_in.at[i], i
        elif i == 3:
            src, slot = io_in, 3
        elif i < 8:
            src, slot = ie_in.at[:, pl.ds((i - 4) * width, width)], i
        else:
            src, slot = ir_in.at[pl.ds((i - 8) * width, width)], i - 8
        image_loads[i] = local(src, IW.at[slot], iw_sem.at[i])

    ca_copies = [
        local(ca_in.at[j], W.at[0, m, pl.ds(shard * j, shard)], ca_sem.at[j]) for j in range(3)
    ]
    own_loads = [local(co_in, W.at[0, m, pl.ds(3 * shard, shard)], loc_sem.at[0])]
    SBL[...] = jnp.zeros_like(SBL)
    SBL[0:1, 0:shard] = attend_bias[0:1, :]
    SBL[2:3, 0:shard] = attend_bias[1:2, :]
    SBL[3:4, :] = expand_bias[...].reshape(1, width)
    SB[m] = SBL[...]
    for copy in ca_copies + own_loads[0:1]:
        copy.wait()
    pl.semaphore_wait(barrier, n_all - 1)

    hops = (1, 2, 3)

    def partner(k):
        other = flip(m, 0) if k % 2 else m
        return flip(other, 1) if k >= 2 else other

    zc, ac = {}, {}
    sources = (W.at[0, m], we_in, wr_in)

    def span(p, n):
        return pl.ds(pl.multiple_of(p * PIECE, 16), n * PIECE)

    def gather_z(g):
        for k in hops:
            dev = (d, partner(k))
            for ab, p in ((0, p_a), (1, p_b)):
                zc[g, k, ab] = remote(
                    sources[g].at[span(p, 1)],
                    W.at[g, m, span(p, 1)],
                    gz_s.at[g, k - 1, ab],
                    gz_r.at[g, k - 1, ab],
                    dev,
                )

    def spread(at, stage, ab, ss, rs):
        if stage == 0:
            p, n, dev = ((p_a, 1, x_dev), (p_b, 1, y_dev))[ab]
        elif stage == 1:
            p, n, dev = ((cb * 4 + yb * 2, 2, y_dev), (8 + cb * 4 + xb * 2, 2, x_dev))[ab]
        else:
            p, n, dev = 8 * ab + cb * 4, 4, core_dev
        return remote(at(p, n), at(p, n), ss.at[stage, ab], rs.at[stage, ab], dev)

    def gather_start(g, stage):
        for k in hops:
            source = partner(k)
            for ab in range(2):
                (zc[g, k, ab] if stage == 0 else ac[g, stage - 1, k, ab]).wait_recv()
                ac[g, stage, k, ab] = spread(
                    lambda p, n: W.at[g, source, span(p, n)],
                    stage,
                    ab,
                    ga_s.at[g, k - 1],
                    ga_r.at[g, k - 1],
                )

    def gather_end(g):
        for k in hops:
            for ab in range(2):
                ac[g, 2, k, ab].wait_recv()
        if g > 0:
            own_loads[g].wait()

    gather_z(0)
    sb_copies = []
    for k in hops:
        sb_copies.append(
            remote(
                SBL,
                SB.at[m],
                sb_s.at[k - 1],
                sb_r.at[k - 1],
                (d, partner(k)),
            )
        )
    for i in range(3):
        load_image(i)
    tok_copy = local(tok_in.at[pl.ds(half * n_cap, n_cap)], TOK, tok_sem)
    for i in range(3, 8):
        load_image(i)
    own_loads.append(local(we_in, W.at[1, m], loc_sem.at[1]))
    own_loads.append(local(wr_in, W.at[2, m], loc_sem.at[2]))
    row_block = iota((BLOCK, BLOCK), 0) >> 4
    near = jnp.where(row_block == (iota((BLOCK, BLOCK), 1) >> 4), 0.0, FAR)
    lane_shard = iota((BLOCK, shard), 1) >> 6
    for h in range(3):
        at = slice(h * BLOCK, (h + 1) * BLOCK)
        HM3[at, :] = jnp.where(lane_shard == h, 1.0, 0.0).astype(LOW)
        BM[at, :] = near
    lane_four = iota((64, 256), 1) >> 6
    for h in range(4):
        HM4[64 * h : 64 * h + 64, :] = jnp.where(lane_four == h, 1.0, 0.0).astype(LOW)
    POOL[...] = jnp.where((iota(POOL.shape, 1) >> 4) == iota(POOL.shape, 0), 1.0, 0.0).astype(LOW)
    RES[pl.ds(0, image_rows), :] = jnp.zeros((image_rows, width), F32)
    GP[3, pl.ds(0, image_rows), :] = jnp.zeros((image_rows, width), LOW)
    gain_one = image_gains[0:1, :]
    gain_two = image_gains[1:2, :]

    def image_norm(i, carry):
        x = imt[i].astype(F32)
        at = pl.multiple_of(i * 64, 64)
        RES[pl.ds(at, image_len), :] = x
        GP[3, pl.ds(at, image_len), :] = (standard(x)[0] * gain_one).astype(LOW)
        return carry

    lax.fori_loop(0, images, image_norm, 0)
    for i in range(3):
        image_loads[i].wait()

    def image_qkv(j, carry):
        GP[j, pl.ds(0, image_rows), :] = dot(
            GP[3, pl.ds(0, image_rows), :], IW[j]
        ).astype(LOW)
        return carry

    lax.fori_loop(0, 3, image_qkv, 0)
    for i in range(8, 11):
        load_image(i)
    gather_start(0, 0)
    gather_z(1)

    key_valid = jnp.where(iota((256, 64), 1) < image_len, 0.0, FAR)
    lane_head = iota((64, 256), 1) >> 6

    def image_attention(i, carry):
        at = pl.multiple_of(i * 64, 64)
        for n in range(width // 256):
            lanes = slice(256 * n, 256 * n + 256)
            q = GP[0, pl.ds(at, 64), lanes]
            k = GP[1, pl.ds(at, 64), lanes]
            v = GP[2, pl.ds(at, 64), lanes]
            logits = dot_nt(jnp.concatenate([q] * 4, axis=0) * HM4[...], k) * 0.125 + key_valid
            expos = jnp.exp(logits - jnp.max(logits, axis=-1, keepdims=True))
            probs = (expos * (1.0 / jnp.sum(expos, axis=-1, keepdims=True))).astype(LOW)
            o = dot(probs, v)
            mix = jnp.where(
                lane_head < 2,
                jnp.where(lane_head == 0, o[0:64], o[64:128]),
                jnp.where(lane_head == 2, o[128:192], o[192:256]),
            )
            N2[pl.ds(at, 64), lanes] = mix.astype(LOW)
        return carry

    lax.fori_loop(0, images, image_attention, 0)
    gather_start(0, 1)
    image_loads[3].wait()

    def image_out(n, carry):
        lanes = pl.ds(pl.multiple_of(n * 256, 256), 256)
        RES[pl.ds(0, image_rows), lanes] += dot(
            N2[pl.ds(0, image_rows), :], IW[3, :, lanes]
        )
        return carry

    lax.fori_loop(0, width // 256, image_out, 0)
    load_image(11)

    def image_norm_two(t, carry):
        at = pl.ds(pl.multiple_of(t * 16, 16), 16)
        GP[3, at, :] = (standard(RES[at, :])[0] * gain_two).astype(LOW)
        return carry

    lax.fori_loop(0, image_rows // 16, image_norm_two, 0, unroll=4)
    IP[...] = jnp.zeros_like(IP)
    for i in range(images):
        IP[i : i + 1, :] = jnp.sum(RES[64 * i : 64 * i + image_len, :], axis=0, keepdims=True) * (
            1.0 / image_len
        )
    image_pool = jnp.where(
        ((iota((16, image_rows), 1) >> 6) == iota((16, image_rows), 0))
        & ((iota((16, image_rows), 1) & 63) < image_len),
        1.0,
        0.0,
    ).astype(LOW)
    for i in range(4, 12):
        image_loads[i].wait()

    def image_feed(u, carry):
        ACC[pl.ds(0, image_rows), :] = dot(
            GP[3, pl.ds(0, image_rows), :], IW[4 + u]
        )

        def activate(t, inner):
            at = pl.ds(pl.multiple_of(t * 16, 16), 16)
            h = ACC[at, :]
            act = 0.5 * h * (1.0 + jnp.tanh(GELU_A * h * (1.0 + GELU_B * h * h)))
            N2[at, :] = act.astype(LOW)
            return inner

        lax.fori_loop(0, image_rows // 16, activate, 0, unroll=4)
        pooled = (dot(image_pool, N2[pl.ds(0, image_rows), :]) * (1.0 / image_len)).astype(LOW)
        IP[...] += dot(pooled, IW[u])
        return carry

    lax.fori_loop(0, 2, image_feed, 0)
    gather_start(1, 0)
    gather_z(2)
    gather_start(0, 2)
    lax.fori_loop(2, 4, image_feed, 0)
    pooled_image = IP[0:8]
    EMB[me] = (
        pooled_image
        * lax.rsqrt(jnp.sum(pooled_image * pooled_image, axis=-1, keepdims=True) + 1e-6)
    ).astype(LOW)

    def send_embed(k, carry):
        q = lax.rem(me + k, n_all)
        pltpu.make_async_remote_copy(
            src_ref=EMB.at[me],
            dst_ref=EMB.at[me],
            send_sem=emb_s,
            recv_sem=emb_r,
            device_id=(q // n_mp, lax.rem(q, n_mp)),
            device_id_type=pl.DeviceIdType.MESH,
        ).start()
        return carry

    lax.fori_loop(1, n_all, send_embed, 0)

    tok_copy.wait()
    g1, g2 = norm_gains[0:1, :], norm_gains[1:2, :]
    b1, b2 = norm_shifts[0:1, :], norm_shifts[1:2, :]

    def norm_one(t, carry):
        at = pl.ds(pl.multiple_of(t * LEN, LEN), LEN)
        N1[at, :] = (standard(TOK[t].astype(F32))[0] * g1 + b1).astype(LOW)
        return carry

    lax.fori_loop(0, n_cap, norm_one, 0, unroll=7)
    for copy in sb_copies:
        copy.wait_recv()
    gather_end(0)

    def project(t, carry):
        s, j = t // 3, lax.rem(t, 3)
        weight = W[0, s, pl.ds(pl.multiple_of(shard * j, 16), shard), :]
        QKV[j, s] = (dot_nt(N1[...], weight) + SB[s, pl.ds(j, 1), 0:shard]).astype(LOW)
        return carry

    gather_start(1, 1)
    lax.fori_loop(0, 3 * n_mp, project, 0)
    gather_start(2, 0)
    lane_three = iota((BLOCK, shard), 1) >> 6

    def join_heads(o):
        return jnp.where(
            lane_three == 0,
            o[0:BLOCK],
            jnp.where(lane_three == 1, o[BLOCK : 2 * BLOCK], o[2 * BLOCK : 3 * BLOCK]),
        )

    def attention(b, carry):
        at = pl.ds(pl.multiple_of(b * BLOCK, 16), BLOCK)
        loaded = [[QKV[j, s, at, :] for j in range(3)] for s in range(n_mp)]
        heads, mask = HM3[...], BM[...]
        every = []
        for q, k, v in loaded:
            logits = dot_nt(jnp.concatenate([q] * 3, axis=0) * heads, k) * 0.125 + mask
            expos = jnp.exp(logits - jnp.max(logits, axis=-1, keepdims=True))
            probs = (expos * (1.0 / jnp.sum(expos, axis=-1, keepdims=True))).astype(LOW)
            every.append((probs, join_heads(dot(probs, v)).astype(LOW)))
        for s, (probs, mixed) in enumerate(every):
            PR[s, b] = probs
            MIX[s, at, :] = mixed
        return carry

    lax.fori_loop(0, n_blocks // 2, attention, 0)
    gather_start(1, 2)
    lax.fori_loop(n_blocks // 2, n_blocks, attention, 0)
    gather_start(2, 1)

    def attend_out(n, carry):
        lanes = pl.ds(pl.multiple_of(n * 256, 256), 256)
        total = dot(MIX[0], W[0, 0, pl.ds(3 * shard, shard), lanes])
        for s in range(1, n_mp):
            total += dot(MIX[s], W[0, s, pl.ds(3 * shard, shard), lanes])
        ACC[:, lanes] = total
        return carry

    lax.fori_loop(0, width // 256, attend_out, 0)
    out_bias = output_bias[...].reshape(1, width)

    def norm_two(t, carry):
        at = pl.ds(pl.multiple_of(t * LEN, LEN), LEN)
        x = TOK[t].astype(F32) + (ACC[at, :] + out_bias)
        RES[at, :] = x
        N2[at, :] = (standard(x)[0] * g2 + b2).astype(LOW)
        return carry

    lax.fori_loop(0, n_cap, norm_two, 0, unroll=7)
    gather_end(1)

    def feed(s, carry):
        ACC[...] = dot(N2[...], W[1, s])
        bias = SB[s, 3:4, :]

        def activate(t, inner):
            at = pl.ds(pl.multiple_of(t * LEN, LEN), LEN)
            act, slope = gelu_parts(ACC[at, :] + bias)
            GT[at, :] = act.astype(LOW)
            GP[s, at, :] = slope.astype(LOW)
            return inner

        lax.fori_loop(0, n_cap, activate, 0, unroll=7)
        PA[s] = (dot(POOL[...], GT[...]) * (1.0 / LEN)).astype(LOW)
        return carry

    lax.fori_loop(0, 2, feed, 0)
    gather_start(2, 2)
    lax.fori_loop(2, n_mp, feed, 0)

    def pool_residual(n, carry):
        lanes = pl.ds(pl.multiple_of(n * 128, 128), 128)
        res = RES[:, lanes]
        res_high = res.astype(LOW)
        res_low = (res - res_high.astype(F32)).astype(LOW)
        EL[:, lanes] = (dot(POOL[...], res_high) + dot(POOL[...], res_low)) * (1.0 / LEN)
        return carry

    lax.fori_loop(0, width // 128, pool_residual, 0)
    pooled = EL[...] + reduce_bias[...].reshape(1, width)
    gather_end(2)
    for s in range(n_mp):
        pooled += dot(PA[s], W[2, s])
    inverse = lax.rsqrt(jnp.sum(pooled * pooled, axis=-1, keepdims=True) + 1e-6)
    embed = pooled * inverse
    EL[...] = embed

    pltpu.make_async_copy(EMB.at[pl.ds(0, n_all - 1)], EMB.at[pl.ds(0, n_all - 1)], emb_r).wait()
    group = min(n_all, 32)

    def embeds(c):
        part = EMB[c * group : c * group + group].astype(F32)
        return part.reshape(group * 8, width).astype(LOW)

    scaling = jnp.exp(log_scale[...].reshape(1, 1))
    embed_low = embed.astype(LOW)
    scores = scaling * jnp.concatenate(
        [dot_nt(embed_low, embeds(c)) for c in range(n_all // group)], axis=1
    )
    cap_rows = scores.shape[0]
    column = iota((cap_rows, t_all), 1)
    col_ok = (column & 7) < images
    row_ok = iota((cap_rows, t_all), 0) < n_cap
    image_id = (column >> 3) * images + (column & 7)
    cap_wide = jnp.broadcast_to(cap[...].reshape(1, 2 * n_cap).astype(F32), (cap_rows, 2 * n_cap))
    mine = iota((cap_rows, 2 * n_cap), 1) == iota((cap_rows, 2 * n_cap), 0) + half * n_cap
    cap_column = jnp.sum(jnp.where(mine, cap_wide, 0.0), axis=1, keepdims=True)
    matches = jnp.where((cap_column == image_id.astype(F32)) & col_ok & row_ok, 1.0, 0.0)
    by_row = jnp.where(col_ok, scores, FAR)
    row_top = jnp.max(by_row, axis=1, keepdims=True)
    row_lse = row_top + jnp.log(jnp.sum(jnp.exp(by_row - row_top), axis=1, keepdims=True))
    row_positive = jnp.sum(scores * matches, axis=1, keepdims=True)
    row_part = jnp.sum(
        jnp.where(iota((cap_rows, 1), 0) < n_cap, row_lse - row_positive, 0.0), axis=0, keepdims=True
    )
    by_column = jnp.where(row_ok, scores, FAR)
    top = jnp.max(by_column, axis=0, keepdims=True)
    MSG[...] = jnp.zeros_like(MSG)
    MSG[0:1, :] = top
    MSG[1:2, :] = jnp.sum(jnp.exp(by_column - top), axis=0, keepdims=True)
    MSG[2:3, :] = jnp.sum(scores * matches, axis=0, keepdims=True)
    MSG[3:4, :] = jnp.sum(matches, axis=0, keepdims=True)
    MSG[4:5, :] = jnp.broadcast_to(row_part, (1, t_all))
    low = lax.rem(d, 8)
    slot = low * 2 + half
    STATS[slot] = MSG[...]

    def send_stats(k, carry):
        q = lax.rem(slot + k, 16)
        pltpu.make_async_remote_copy(
            src_ref=MSG,
            dst_ref=STATS.at[slot],
            send_sem=st_s,
            recv_sem=st_r,
            device_id=(d - low + q // 2, m - half + lax.rem(q, 2)),
            device_id_type=pl.DeviceIdType.MESH,
        ).start()
        return carry

    lax.fori_loop(1, 16, send_stats, 0)
    pltpu.make_async_copy(STATS.at[pl.ds(0, 15)], STATS.at[pl.ds(0, 15)], st_r).wait()
    top = jnp.max(STATS[:, 0, :], axis=0, keepdims=True)
    total = jnp.sum(STATS[:, 1, :] * jnp.exp(STATS[:, 0, :] - top), axis=0, keepdims=True)
    positive = jnp.sum(STATS[:, 2, :], axis=0, keepdims=True)
    count = jnp.sum(STATS[:, 3, :], axis=0, keepdims=True)
    row_sum = jnp.sum(STATS[:, 4, :], axis=0, keepdims=True)
    for x in range(extra):
        XST[0, x] = jnp.concatenate(
            [top, total, positive, count, row_sum, jnp.zeros((3, t_all), F32)], axis=0
        )
        remote(
            XST.at[0, x], XST.at[1, x], stx_s.at[x], stx_r.at[x], (flip(d, 3 + x), m)
        ).wait_recv()
        other = XST[1, x]
        joined = jnp.maximum(top, other[0:1])
        total = total * jnp.exp(top - joined) + other[1:2] * jnp.exp(other[0:1] - joined)
        top = joined
        positive = positive + other[2:3]
        count = count + other[3:4]
        row_sum = row_sum + other[4:5]
    ok = col_ok[0:1]
    count = jnp.where(ok, count, 1.0)
    col_lse = top + jnp.log(total)
    column_part = jnp.sum(
        jnp.where(ok, col_lse - positive / count, 0.0), axis=1, keepdims=True
    )
    loss = 0.5 * (row_sum[:, 0:1] * (1.0 / total_captions) + column_part * (1.0 / total_images))
    weight = 0.5 * total_captions / total_images
    grad_scores = 0.5 * (jnp.exp(by_row - row_lse) - matches) + weight * (
        jnp.exp(by_column - col_lse) - matches * (1.0 / count)
    )
    grad_scores = jnp.where(col_ok & row_ok, grad_scores, 0.0)
    grad_log = jnp.sum(
        jnp.sum(grad_scores * scores, axis=1, keepdims=True), axis=0, keepdims=True
    )
    embed = EL[...]
    grad_cosine = (scaling * grad_scores).astype(LOW)
    grad_embed = dot(grad_cosine[:, 0 : group * 8], embeds(0))
    for c in range(1, n_all // group):
        grad_embed += dot(grad_cosine[:, c * group * 8 : (c + 1) * group * 8], embeds(c))
    grad_pooled = (
        grad_embed - embed * jnp.sum(embed * grad_embed, axis=-1, keepdims=True)
    ) * inverse
    SG[0] = jnp.zeros(SG.shape[1:], F32)
    SG[0, 13:14, :] = jnp.sum(grad_pooled, axis=0, keepdims=True)
    SG[0, 18:19, :] = jnp.broadcast_to(grad_log, (1, width))
    GPL[0] = grad_pooled.astype(LOW)
    grad_rows = grad_pooled * (1.0 / LEN)
    EL[...] = grad_rows
    GPL[1] = grad_rows.astype(LOW)

    def part(g, i):
        return IW.at[2 * g + i]

    places = (4, 7, 6)

    def whole(g):
        return IW.at[places[g]]

    def settle(copies):
        for copy in copies:
            copy.wait_send()
        sends[:] = [other for other in sends if all(other is not copy for copy in copies)]

    state = {}
    stores = []
    axis_one = ((yb, y_dev), (xb, x_dev))
    axis_two = ((xb, x_dev), (yb, y_dev))
    own = (p_a, p_b)

    def scatter(g, stage, i, ab):
        bit_one, dev_one = axis_one[ab]
        bit_two, dev_two = axis_two[ab]
        run = 8 * ab + 4 * cb + 2 * bit_one
        if stage == 0:
            p, n, dst, dev = 8 * ab + 4 * (1 - cb), 4, RCORE.at[g % 2, i, ab], core_dev
        elif stage == 1:
            p, n, dst, dev = 8 * ab + 4 * cb + 2 * (1 - bit_one), 2, RB1.at[g % 2, i, ab], dev_one
        elif stage == 2:
            p, n, dst, dev = run + 1 - bit_two, 1, RB2.at[g % 2, i, ab], dev_two
        else:
            p, n, dst, dev = own[ab], 1, RZ.at[g, ab], pair_dev
        k = 2 * i + ab
        state[g, stage, i, ab] = remote(
            part(g, i).at[span(p, n)], dst, rs_s.at[g, stage, k], rs_r.at[g, stage, k], dev
        )

    def add_in(g, stage, i, ab):
        state[g, stage, i, ab].wait_recv()
        run = 8 * ab + 4 * cb
        if stage == 0:
            at, got = span(run, 4), RCORE[g % 2, i, ab]
        elif stage == 1:
            at, got = span(run + 2 * axis_one[ab][0], 2), RB1[g % 2, i, ab]
        else:
            at, got = span(own[ab], 1), RB2[g % 2, i, ab]
        IW[2 * g + i, at, :] = IW[2 * g + i, at, :] + got

    def gather_back(g, stage, ab):
        state[g, "gather", stage, ab] = spread(
            lambda p, n: whole(g).at[span(p, n)], stage, ab, ag_s.at[g], ag_r.at[g]
        )

    def reduce_start(g, ab):
        if g == 0:
            settle([state.pop((2, a, i, ab)) for a in range(4) for i in range(2) if (2, a, i, ab) in state])
        for i in (1, 0):
            scatter(g, 0, i, ab)

    def reduce_step(g, step):
        if step == 0:
            for ab in range(2):
                reduce_start(g, ab)
        elif step < 4:
            for i in (1, 0):
                for ab in range(2):
                    add_in(g, step - 1, i, ab)
                    if step < 3 or i == 1:
                        scatter(g, step, i, ab)
        elif step == 4:
            for ab in range(2):
                state[g, 3, 1, ab].wait_recv()
                at = span(own[ab], 1)
                IW[places[g], at, :] = IW[2 * g, at, :] + RZ[g, ab]
                for x in range(extra):
                    copy = remote(
                        whole(g).at[at],
                        XR.at[g % 2, x, ab],
                        xr_s.at[g, x, ab],
                        xr_r.at[g, x, ab],
                        (flip(d, 3 + x), m),
                    )
                    copy.wait_recv()
                    settle([copy])
                    IW[places[g], at, :] = IW[places[g], at, :] + XR[g % 2, x, ab]
                gather_back(g, 0, ab)
        elif step < 7:
            for ab in range(2):
                state[g, "gather", step - 5, ab].wait_recv()
                gather_back(g, step - 4, ab)
        else:
            for ab in range(2):
                state[g, "gather", 2, ab].wait_recv()
            stores.append(local(whole(g), red.at[g], out_sem.at[g]))

    shards = (m, pair)
    for i in range(2):
        IW[4 + i] = dot_tn(PA[shards[i]], GPL[0]).astype(LOW)
    reduce_step(2, 0)

    def grad_activation(s, carry):
        GA[s] = dot_nt(GPL[1], W[2, s])
        return carry

    lax.fori_loop(0, n_mp, grad_activation, 0)
    reduce_step(2, 1)
    ones = jnp.ones((16, rows), LOW)

    def grad_hidden(s, carry):
        def scale(t, inner):
            at = pl.ds(pl.multiple_of(t * LEN, LEN), LEN)
            GP[s, at, :] = (GP[s, at, :].astype(F32) * GA[s, pl.ds(t, 1), :]).astype(LOW)
            return inner

        lax.fori_loop(0, n_cap, scale, 0, unroll=7)
        SG[0, pl.ds(8 + s, 1), :] = dot(ones, GP[s])[0:1]
        return carry

    lax.fori_loop(0, n_mp, grad_hidden, 0)
    reduce_step(2, 2)

    def expand_gradient(i, carry):
        s = m + i * (pair - m)
        IW[2 + i] = dot_tn(N2[...], GP[s]).astype(LOW)
        return carry

    lax.fori_loop(0, 2, expand_gradient, 0)
    reduce_step(1, 0)
    reduce_step(2, 3)

    def grad_norm_two(n, carry):
        p = pl.ds(pl.multiple_of(n * 384, 128), 384)
        total = dot_nt(GP[0], W[1, 0, p, :])
        for s in range(1, n_mp):
            total += dot_nt(GP[s], W[1, s, p, :])
        ACC[:, pl.ds(pl.multiple_of(n * 384, 128), 384)] = total
        return carry

    lax.fori_loop(0, 2, grad_norm_two, 0)
    reduce_step(1, 1)
    reduce_step(2, 4)

    def norm_back(e, gain, x):
        xhat, scale = standard(x)
        eg = e * gain
        c1 = jnp.sum(eg, axis=-1, keepdims=True) * (1.0 / width)
        c2 = jnp.sum(eg * xhat, axis=-1, keepdims=True) * (1.0 / width)
        return (eg - c1 - xhat * c2) * scale, sum8(e * xhat), sum8(e)

    zero8 = jnp.zeros((8, width), F32)

    def back_two(t, carry):
        dg, db, do = carry
        found = []
        for u in range(7):
            at = pl.ds(pl.multiple_of((7 * t + u) * LEN, LEN), LEN)
            dv, one, two = norm_back(ACC[at, :], g2, RES[at, :])
            g = EL[pl.ds(7 * t + u, 1), :] + dv
            found.append((at, g))
            dg, db, do = dg + one, db + two, do + sum8(g)
        for at, g in found:
            RES[at, :] = g
            GRL[at, :] = g.astype(LOW)
        return dg, db, do

    dg, db, do = lax.fori_loop(0, n_cap // 7, back_two, (zero8, zero8, zero8))
    SG[0, 15:16, :] = jnp.sum(dg, axis=0, keepdims=True)
    SG[0, 17:18, :] = jnp.sum(db, axis=0, keepdims=True)
    SG[0, 12:13, :] = jnp.sum(do, axis=0, keepdims=True)

    for i in range(2):
        IW[i, 3 * shard : 4 * shard, :] = dot_tn(MIX[shards[i]], GRL[...]).astype(LOW)
    reduce_step(1, 2)
    reduce_step(2, 5)

    def grad_mixture(s, carry):
        MIX[s] = dot_nt(GRL[...], W[0, s, pl.ds(3 * shard, shard), :]).astype(LOW)
        return carry

    lax.fori_loop(0, n_mp, grad_mixture, 0)
    reduce_step(2, 6)

    def attention_back(b, carry):
        at = pl.ds(pl.multiple_of(b * BLOCK, 16), BLOCK)
        loaded = [
            [QKV[j, s, at, :] for j in range(3)] + [MIX[s, at, :], PR[s, b]] for s in range(n_mp)
        ]
        heads = HM3[...]
        every = []
        for q, k, v, g, low_probs in loaded:
            q = jnp.concatenate([q] * 3, axis=0) * heads
            g = jnp.concatenate([g] * 3, axis=0) * heads
            probs = low_probs.astype(F32)
            grad_probs = dot_nt(g, v)
            inner = jnp.sum(grad_probs * probs, axis=-1, keepdims=True)
            grad_logits = (probs * (grad_probs - inner)).astype(LOW)
            every.append(
                (
                    (join_heads(dot(grad_logits, k)) * 0.125).astype(LOW),
                    (dot_tn(grad_logits, q) * 0.125).astype(LOW),
                    dot_tn(low_probs, g).astype(LOW),
                )
            )
        for s, grads in enumerate(every):
            for j in range(3):
                QKV[j, s, at, :] = grads[j]
        return carry

    def attend_gradient(j):
        def one(i, carry):
            s = m + i * (pair - m)
            IW[i, shard * j : shard * (j + 1), :] = dot_tn(QKV[j, s], N1[...]).astype(LOW)
            return carry

        lax.fori_loop(0, 2, one, 0)

    small_gain, small_shift = zero8, zero8
    gt_copies = []
    cuts = (0, 4, n_blocks)
    for r in range(2):
        lax.fori_loop(cuts[r], cuts[r + 1], attention_back, 0)
        reduce_step(1, 3 + r)
        if r == 1:
            attend_gradient(2)
            reduce_start(0, 1)
            attend_gradient(0)
            attend_gradient(1)
            reduce_start(0, 0)
        first, last = cuts[r] * (BLOCK // LEN), cuts[r + 1] * (BLOCK // LEN)
        stripe = pl.ds(first * LEN, (last - first) * LEN)

        def grad_norm_one(n, carry):
            lanes = pl.ds(pl.multiple_of(n * 256, 256), 256)
            total = None
            for s in range(n_mp):
                for j in range(3):
                    term = dot(
                        QKV[j, s, stripe, :],
                        W[0, s, pl.ds(shard * j, shard), lanes],
                    )
                    total = term if total is None else total + term
            ACC[stripe, lanes] = total
            return carry

        lax.fori_loop(0, width // 256, grad_norm_one, 0)
        if r == 1:
            reduce_step(0, 1)

        def back_one(t, carry):
            at = pl.ds(pl.multiple_of(t * LEN, LEN), LEN)
            dv, dg, db = norm_back(ACC[at, :], g1, TOK[t].astype(F32))
            GT[at, :] = (RES[at, :] + dv).astype(LOW)
            return carry[0] + dg, carry[1] + db

        small_gain, small_shift = lax.fori_loop(
            first, last, back_one, (small_gain, small_shift), unroll=7
        )
        gt_copies.append(
            remote(GT.at[stripe], gt.at[half, stripe], gt_s.at[r], gt_r.at[r], pair_dev)
        )
    stores.append(local(GT, gt.at[half], out_sem.at[3]))
    reduce_step(0, 2)
    SG[0, 14:15, :] = jnp.sum(small_gain, axis=0, keepdims=True)
    SG[0, 16:17, :] = jnp.sum(small_shift, axis=0, keepdims=True)

    def bias_gradient(s, carry):
        SG[0, pl.ds(s, 1), 0:shard] = dot(ones, QKV[0, s])[0:1]
        SG[0, pl.ds(4 + s, 1), 0:shard] = dot(ones, QKV[2, s])[0:1]
        return carry

    lax.fori_loop(0, n_mp, bias_gradient, 0)
    small_devs = [core_dev, y_dev, x_dev, pair_dev] + [(flip(d, 3 + x), m) for x in range(extra)]
    small = {}

    def small_start(i):
        small[i] = remote(SG.at[i], SGR.at[i], sg_s.at[i], sg_r.at[i], small_devs[i])

    def small_end(i):
        small[i].wait_recv()
        SG[i + 1] = SG[i] + SGR[i]

    small_start(0)
    reduce_step(1, 5)
    small_end(0)
    small_start(1)
    reduce_step(0, 3)
    small_end(1)
    small_start(2)
    reduce_step(1, 6)
    small_end(2)
    small_start(3)
    reduce_step(2, 7)
    reduce_step(0, 4)
    small_end(3)
    for i in range(4, 4 + extra):
        small_start(i)
        small_end(i)
    reduce_step(0, 5)
    reduce_step(1, 7)
    reduce_step(0, 6)
    last = SG.shape[0] - 1
    sgo[...] = jnp.zeros_like(sgo)
    sgo[0:1, :] = SG[last, pl.ds(m, 1), :]
    sgo[1:2, :] = SG[last, pl.ds(4 + m, 1), :]
    sgo[2:3, :] = SG[last, pl.ds(8 + m, 1), :]
    sgo[3:10, :] = SG[last, 12:19, :]
    sgo[10:11, :] = jnp.broadcast_to(loss, (1, width))
    reduce_step(0, 7)
    for copy in gt_copies:
        copy.wait_recv()
    pltpu.make_async_copy(EMB.at[pl.ds(0, n_all - 1)], EMB.at[pl.ds(0, n_all - 1)], emb_s).wait()
    pltpu.make_async_copy(STATS.at[pl.ds(0, 15)], STATS.at[pl.ds(0, 15)], st_s).wait()
    for copy in sends:
        copy.wait_send()
    for copy in stores:
        copy.wait()


def local_step(
    n_dp,
    n_mp,
    caption_tokens,
    image_tokens,
    image_attend,
    image_output,
    image_expand,
    image_reduce,
    image_gains,
    caption_attend,
    attend_bias,
    caption_output,
    output_bias,
    caption_expand,
    expand_bias,
    caption_reduce,
    reduce_bias,
    norm_gains,
    norm_shifts,
    log_scale,
    caption_image,
):
    captions, length, width = caption_tokens.shape
    images, image_len, _ = image_tokens.shape
    shard = caption_attend.shape[2]
    units = caption_expand.shape[1]
    n_cap = captions // 2
    rows = n_cap * length
    n_blocks = rows // BLOCK
    n_all = n_dp * n_mp
    t_all = n_all * 8
    extra = n_dp.bit_length() - 1 - 3
    assert length == LEN and units == width and shard * n_mp == width and width == 16 * PIECE

    any_space = pl.BlockSpec(memory_space=pl.ANY)
    vmem = pl.BlockSpec(memory_space=pltpu.VMEM)
    nx = max(extra, 1)
    dma = pltpu.SemaphoreType.DMA
    scratch = [
        pltpu.VMEM((3, n_mp, width, width), LOW),
        pltpu.VMEM((8, width, width), LOW),
        pltpu.VMEM((n_cap, length, width), LOW),
        pltpu.VMEM((rows, width), LOW),
        pltpu.VMEM((3, n_mp, rows, shard), LOW),
        pltpu.VMEM((n_mp, n_blocks, 3 * BLOCK, BLOCK), LOW),
        pltpu.VMEM((n_mp, rows, shard), LOW),
        pltpu.VMEM((rows, width), F32),
        pltpu.VMEM((rows, width), LOW),
        pltpu.VMEM((n_mp, rows, width), LOW),
        pltpu.VMEM((n_mp, 64, width), LOW),
        pltpu.VMEM((rows, width), F32),
        pltpu.VMEM((rows, width), LOW),
        pltpu.VMEM((rows, width), LOW),
        pltpu.VMEM((16, width), F32),
        pltpu.VMEM((n_all, 8, width), LOW),
        pltpu.VMEM((8, t_all), F32),
        pltpu.VMEM((16, 8, t_all), F32),
        pltpu.VMEM((8, width), F32),
        pltpu.VMEM((n_mp, 8, width), F32),
        pltpu.VMEM((3 * BLOCK, shard), LOW),
        pltpu.VMEM((3 * BLOCK, BLOCK), F32),
        pltpu.VMEM((256, 256), LOW),
        pltpu.VMEM((64, rows), LOW),
        pltpu.VMEM((64, width), F32),
        pltpu.VMEM((2, 64, width), LOW),
        pltpu.VMEM((n_mp, 64, width), F32),
        pltpu.VMEM((2, 2, 2, 4 * PIECE, width), LOW),
        pltpu.VMEM((2, 2, 2, 2 * PIECE, width), LOW),
        pltpu.VMEM((2, 2, 2, PIECE, width), LOW),
        pltpu.VMEM((3, 2, PIECE, width), LOW),
        pltpu.VMEM((2, nx, 2, PIECE, width), LOW),
        pltpu.VMEM((2, nx, 8, t_all), F32),
        pltpu.VMEM((5 + extra, 24, width), F32),
        pltpu.VMEM((4 + extra, 24, width), F32),
        dma((3, 3, 2)),
        dma((3, 3, 2)),
        dma((3, 3, 3, 2)),
        dma((3, 3, 3, 2)),
        dma((3,)),
        dma((3,)),
        dma((12,)),
        dma,
        dma((3,)),
        dma((3,)),
        dma,
        dma,
        dma,
        dma,
        dma((nx,)),
        dma((nx,)),
        dma((3, 4, 4)),
        dma((3, 4, 4)),
        dma((3, 3, 2)),
        dma((3, 3, 2)),
        dma((3, nx, 2)),
        dma((3, nx, 2)),
        dma((4 + extra,)),
        dma((4 + extra,)),
        dma((2,)),
        dma((2,)),
        dma((4,)),
    ]
    red, gt, sgo = pl.pallas_call(
        functools.partial(body, n_dp, n_mp),
        out_shape=(
            jax.ShapeDtypeStruct((3, width, width), LOW),
            jax.ShapeDtypeStruct((2, rows, width), LOW),
            jax.ShapeDtypeStruct((16, width), F32),
        ),
        in_specs=[any_space, vmem] + [any_space] * 8 + [vmem] * 9,
        out_specs=(any_space, any_space, vmem),
        scratch_shapes=scratch,
        compiler_params=pltpu.CompilerParams(
            collective_id=0, has_side_effects=True, vmem_limit_bytes=66_000_000
        ),
        name="step",
    )(
        caption_tokens,
        image_tokens,
        image_attend,
        image_output,
        image_expand,
        image_reduce,
        jnp.swapaxes(caption_attend, 1, 2),
        caption_output,
        caption_expand,
        caption_reduce,
        image_gains,
        attend_bias,
        output_bias,
        expand_bias,
        reduce_bias,
        norm_gains,
        norm_shifts,
        log_scale,
        caption_image,
    )
    shapes = (
        (1,),
        (captions, length, width),
        (3, shard, width),
        (2, shard),
        (shard, width),
        (width,),
        (width, units),
        (units,),
        (units, width),
        (width,),
        (2, width),
        (2, width),
        (1,),
    )
    large = (1, 2, 4, 6, 8)
    parts = 7
    grads = pl.pallas_call(
        finish,
        out_shape=tuple(jax.ShapeDtypeStruct(shape, F32) for shape in shapes),
        in_specs=[any_space, any_space, vmem],
        out_specs=tuple(any_space if i in large else vmem for i in range(len(shapes))),
        scratch_shapes=[
            pltpu.VMEM((captions, length, width), LOW),
            pltpu.VMEM((captions, length, width), F32),
            pltpu.VMEM((3, width, width), LOW),
            pltpu.VMEM((3, width, width), F32),
            pltpu.VMEM((3, shard, width), F32),
            dma((parts,)),
            dma((parts,)),
            dma((3,)),
            dma((6,)),
        ],
        compiler_params=pltpu.CompilerParams(vmem_limit_bytes=64_000_000),
        name="finish",
    )(red, gt.reshape(captions, length, width), sgo)
    return (*grads[:2], jnp.swapaxes(grads[2], 1, 2), *grads[3:])


def finish(
    red,
    gt,
    small,
    loss,
    tokens,
    attend,
    attend_bias,
    output,
    output_bias,
    expand,
    expand_bias,
    reduce,
    reduce_bias,
    gains,
    shifts,
    log_scale,
    GT,
    TOKENS,
    RED,
    WIDE,
    ATTEND,
    gt_in,
    gt_out,
    red_in,
    red_out,
):
    def copy(src, dst, sem):
        made = pltpu.make_async_copy(src, dst, sem)
        made.start()
        return made

    parts = gt_in.shape[0]
    size = GT.shape[0] // parts
    width = GT.shape[2]
    shard = ATTEND.shape[1]
    order = (0, 1, 2)
    weights = {g: copy(red.at[g], RED.at[g], red_in.at[g]) for g in order}
    pieces = [
        copy(gt.at[pl.ds(i * size, size)], GT.at[pl.ds(i * size, size)], gt_in.at[i])
        for i in range(parts)
    ]
    written = []
    loss[...] = small[10:11, 0:1].reshape(1)
    attend_bias[...] = small[0:2, 0:shard]
    expand_bias[...] = small[2:3, :].reshape(width)
    output_bias[...] = small[3:4, :].reshape(width)
    reduce_bias[...] = small[4:5, :].reshape(width)
    gains[...] = small[5:7, :]
    shifts[...] = small[7:9, :]
    log_scale[...] = small[9:10, 0:1].reshape(1)
    for g in order:
        weights[g].wait()
        if g == 0:
            for j in range(3):
                ATTEND[j] = RED[0, shard * j : shard * (j + 1), :].astype(F32)
                written.append(copy(ATTEND.at[j], attend.at[j], red_out.at[j]))
            WIDE[0, 3 * shard :, :] = RED[0, 3 * shard :, :].astype(F32)
            written.append(copy(WIDE.at[0, pl.ds(3 * shard, shard)], output, red_out.at[3]))
        else:

            def widen(t, carry):
                at = pl.ds(pl.multiple_of(t * 96, 96), 96)
                WIDE[g, at, :] = RED[g, at, :].astype(F32)
                return carry

            lax.fori_loop(0, width // 96, widen, 0)
            written.append(copy(WIDE.at[g], (expand, reduce)[g - 1], red_out.at[3 + g]))
    for i in range(parts):
        pieces[i].wait()
        at = slice(i * size, i * size + size)
        TOKENS[at] = GT[at].astype(F32)
        written.append(
            copy(
                TOKENS.at[pl.ds(i * size, size)], tokens.at[pl.ds(i * size, size)], gt_out.at[i]
            )
        )
    for made in written:
        made.wait()


def solution(mesh):
    in_specs = (
        P("dp", None, None),
        P(("dp", "mp"), None, None),
        P(),
        P(),
        P(),
        P(),
        P(),
        P(None, None, "mp"),
        P(None, "mp"),
        P("mp", None),
        P(),
        P(None, "mp"),
        P("mp"),
        P("mp", None),
        P(),
        P(),
        P(),
        P(),
        P("dp"),
    )
    out_specs = (
        P(),
        P("dp", None, None),
        P(None, None, "mp"),
        P(None, "mp"),
        P("mp", None),
        P(),
        P(None, "mp"),
        P("mp"),
        P("mp", None),
        P(),
        P(),
        P(),
        P(),
    )
    step = functools.partial(local_step, mesh.shape["dp"], mesh.shape["mp"])
    return jax.shard_map(step, mesh=mesh, in_specs=in_specs, out_specs=out_specs, check_vma=False)
```

```python
import functools

import jax
import jax.numpy as jnp
from jax import lax
from jax.experimental import pallas as pl
from jax.experimental.pallas import tpu as pltpu
from jax.sharding import PartitionSpec as P

HEAD_DIM = 64
LEN = 16
PIECE = 48
BLOCK = 112
F32 = jnp.float32
LOW = jnp.bfloat16
FAR = -1e30
ALL_HOPS = (1, 2, 3)
RPLAN = {
    0: ((2, 0),),
    2: ((2, 1),),
    4: ((1, 0),),
    6: ((2, 2), (1, 1)),
    8: ((2, 3),),
    10: ((1, 2), (2, 4)),
    12: ((1, 3), (2, 5)),
    15: ((1, 4), (2, 6)),
    16: ((0, 1),),
    22: ((0, 2),),
    23: ((1, 5), (0, 3)),
    24: ((1, 6),),
    25: ((2, 7), (0, 4)),
    26: ((1, 7), (0, 5)),
    27: ((0, 6),),
    28: ((0, 7),),
}
PLAN = {
    1: ((0, 0, (1,)),),
    2: ((0, 0, (2, 3)), (1, -1, ()),),
    3: ((0, 1, (1, 2)),),
    5: ((0, 1, (3,)),),
    6: ((0, 2, (1, 2)),),
    7: ((0, 2, (3,)), (1, 0, ALL_HOPS), (2, -1, ()),),
    10: ((1, 1, ALL_HOPS),),
    12: ((2, 0, ALL_HOPS),),
    13: ((1, 2, ALL_HOPS),),
    15: ((2, 1, ALL_HOPS),),
    17: ((2, 2, ALL_HOPS),),
}
GELU_A = 0.7978845608028654
GELU_B = 0.044715


def dot(a, b):
    return lax.dot_general(a, b, (((1,), (0,)), ((), ())), preferred_element_type=F32)


def dot_nt(a, b):
    return lax.dot_general(a, b, (((1,), (1,)), ((), ())), preferred_element_type=F32)


def dot_tn(a, b):
    return lax.dot_general(a, b, (((0,), (0,)), ((), ())), preferred_element_type=F32)


def iota(shape, axis):
    return lax.broadcasted_iota(jnp.int32, shape, axis)


def standard(x):
    width = x.shape[-1]
    centred = x - jnp.sum(x, axis=-1, keepdims=True) * (1.0 / width)
    variance = jnp.sum(centred * centred, axis=-1, keepdims=True) * (1.0 / width)
    scale = lax.rsqrt(variance + 1e-6)
    return centred * scale, scale


def gelu_parts(h):
    square = h * h
    t = jnp.tanh(GELU_A * h * (1.0 + GELU_B * square))
    half = 0.5 * (1.0 + t)
    slope = half + 0.5 * h * (1.0 - t * t) * (GELU_A * (1.0 + 3.0 * GELU_B * square))
    return h * half, slope


def sum8(x):
    return x[0:8] + x[8:16]


def body(
    n_dp,
    n_mp,
    tok_in,
    imt,
    ia_in,
    io_in,
    ie_in,
    ir_in,
    ca_in,
    co_in,
    we_in,
    wr_in,
    image_gains,
    attend_bias,
    output_bias,
    expand_bias,
    reduce_bias,
    norm_gains,
    norm_shifts,
    log_scale,
    cap,
    red,
    gt,
    sgo,
    W,
    IW,
    TOK,
    N1,
    QKV,
    PR,
    MIX,
    RES,
    N2,
    GP,
    PA,
    ACC,
    GRL,
    GT,
    IP,
    EMB,
    MSG,
    STATS,
    SBL,
    SB,
    HM3,
    BM,
    HM4,
    POOL,
    EL,
    GPL,
    GA,
    RCORE,
    RB1,
    RB2,
    RZ,
    XR,
    XST,
    SG,
    SGR,
    gz_s,
    gz_r,
    ga_s,
    ga_r,
    loc_sem,
    ca_sem,
    iw_sem,
    tok_sem,
    sb_s,
    sb_r,
    emb_s,
    emb_r,
    st_s,
    st_r,
    stx_s,
    stx_r,
    rs_s,
    rs_r,
    ag_s,
    ag_r,
    xr_s,
    xr_r,
    sg_s,
    sg_r,
    gt_s,
    gt_r,
    out_sem,
):
    d = lax.axis_index("dp")
    m = lax.axis_index("mp")
    n_all = n_dp * n_mp
    me = d * n_mp + m
    bits = n_dp.bit_length() - 1
    extra = bits - 3
    images, image_len = imt.shape[0], imt.shape[1]
    rows = TOK.shape[0] * LEN
    n_cap = TOK.shape[0]
    n_blocks = rows // BLOCK
    width = RES.shape[1]
    shard = QKV.shape[3]
    image_rows = images * 64
    t_all = EMB.shape[0] * 8
    total_images = images * n_all
    total_captions = n_cap * 2 * n_dp

    def bit(v, b):
        return lax.rem(v // (1 << b), 2)

    def flip(v, b):
        return v + (1 - 2 * bit(v, b)) * (1 << b)

    cb, xb, yb = bit(d, 0), bit(d, 1), bit(d, 2)
    half = lax.rem(m, 2)
    pair = flip(m, 0)
    p_a = cb * 4 + yb * 2 + xb
    p_b = 8 + cb * 4 + xb * 2 + yb
    core_dev = (flip(d, 0), m)
    x_dev = (flip(d, 1), m)
    y_dev = (flip(d, 2), m)
    pair_dev = (d, pair)
    sends = []

    def remote(src, dst, ss, rs, dev):
        copy = pltpu.make_async_remote_copy(
            src_ref=src,
            dst_ref=dst,
            send_sem=ss,
            recv_sem=rs,
            device_id=dev,
            device_id_type=pl.DeviceIdType.MESH,
        )
        copy.start()
        sends.append(copy)
        return copy

    def local(src, dst, sem):
        copy = pltpu.make_async_copy(src, dst, sem)
        copy.start()
        return copy

    barrier = pltpu.get_barrier_semaphore()

    def greet(k, carry):
        q = lax.rem(me + k, n_all)
        pl.semaphore_signal(
            barrier,
            inc=1,
            device_id=(q // n_mp, lax.rem(q, n_mp)),
            device_id_type=pl.DeviceIdType.MESH,
        )
        return carry

    lax.fori_loop(1, n_all, greet, 0)

    image_loads = {}

    def load_image(i):
        if i < 3:
            src, slot = ia_in.at[i], i
        elif i == 3:
            src, slot = io_in, 3
        elif i < 8:
            src, slot = ie_in.at[:, pl.ds((i - 4) * width, width)], i
        else:
            src, slot = ir_in.at[pl.ds((i - 8) * width, width)], i - 8
        image_loads[i] = local(src, IW.at[slot], iw_sem.at[i])

    ca_copies = [
        local(ca_in.at[j], W.at[0, m, pl.ds(shard * j, shard)], ca_sem.at[j]) for j in range(3)
    ]
    own_loads = [local(co_in, W.at[0, m, pl.ds(3 * shard, shard)], loc_sem.at[0])]
    SBL[...] = jnp.zeros_like(SBL)
    SBL[0:1, 0:shard] = attend_bias[0:1, :]
    SBL[2:3, 0:shard] = attend_bias[1:2, :]
    SBL[3:4, :] = expand_bias[...].reshape(1, width)
    SB[m] = SBL[...]
    for copy in ca_copies + own_loads[0:1]:
        copy.wait()
    pl.semaphore_wait(barrier, n_all - 1)

    hops = (1, 2, 3)

    def partner(k):
        other = flip(m, 0) if k % 2 else m
        return flip(other, 1) if k >= 2 else other

    zc, ac = {}, {}
    sources = (W.at[0, m], we_in, wr_in)

    def span(p, n):
        return pl.ds(pl.multiple_of(p * PIECE, 16), n * PIECE)

    def gather_z(g):
        for k in hops:
            dev = (d, partner(k))
            for ab, p in ((0, p_a), (1, p_b)):
                zc[g, k, ab] = remote(
                    sources[g].at[span(p, 1)],
                    W.at[g, m, span(p, 1)],
                    gz_s.at[g, k - 1, ab],
                    gz_r.at[g, k - 1, ab],
                    dev,
                )

    def spread(at, stage, ab, ss, rs):
        if stage == 0:
            p, n, dev = ((p_a, 1, x_dev), (p_b, 1, y_dev))[ab]
        elif stage == 1:
            p, n, dev = ((cb * 4 + yb * 2, 2, y_dev), (8 + cb * 4 + xb * 2, 2, x_dev))[ab]
        else:
            p, n, dev = 8 * ab + cb * 4, 4, core_dev
        return remote(at(p, n), at(p, n), ss.at[stage, ab], rs.at[stage, ab], dev)

    def gather_start(g, stage, ks=(1, 2, 3)):
        for k in ks:
            source = partner(k)
            for ab in range(2):
                (zc[g, k, ab] if stage == 0 else ac[g, stage - 1, k, ab]).wait_recv()
                ac[g, stage, k, ab] = spread(
                    lambda p, n: W.at[g, source, span(p, n)],
                    stage,
                    ab,
                    ga_s.at[g, k - 1],
                    ga_r.at[g, k - 1],
                )

    def gather_end(g):
        for k in hops:
            for ab in range(2):
                ac[g, 2, k, ab].wait_recv()
        if g > 0:
            own_loads[g].wait()

    def tick(place):
        for g, stage, ks in PLAN.get(place, ()):
            if stage < 0:
                gather_z(g)
            else:
                gather_start(g, stage, ks)

    gather_z(0)
    sb_copies = []
    for k in hops:
        sb_copies.append(
            remote(
                SBL,
                SB.at[m],
                sb_s.at[k - 1],
                sb_r.at[k - 1],
                (d, partner(k)),
            )
        )
    for i in range(3):
        load_image(i)
    tok_copy = local(tok_in.at[pl.ds(half * n_cap, n_cap)], TOK, tok_sem)
    for i in range(3, 8):
        load_image(i)
    own_loads.append(local(we_in, W.at[1, m], loc_sem.at[1]))
    own_loads.append(local(wr_in, W.at[2, m], loc_sem.at[2]))
    row_block = iota((BLOCK, BLOCK), 0) >> 4
    near = jnp.where(row_block == (iota((BLOCK, BLOCK), 1) >> 4), 0.0, FAR)
    lane_shard = iota((BLOCK, shard), 1) >> 6
    for h in range(3):
        at = slice(h * BLOCK, (h + 1) * BLOCK)
        HM3[at, :] = jnp.where(lane_shard == h, 1.0, 0.0).astype(LOW)
        BM[at, :] = near
    lane_four = iota((64, 256), 1) >> 6
    for h in range(4):
        HM4[64 * h : 64 * h + 64, :] = jnp.where(lane_four == h, 1.0, 0.0).astype(LOW)
    POOL[...] = jnp.where((iota(POOL.shape, 1) >> 4) == iota(POOL.shape, 0), 1.0, 0.0).astype(LOW)
    RES[pl.ds(0, image_rows), :] = jnp.zeros((image_rows, width), F32)
    GP[3, pl.ds(0, image_rows), :] = jnp.zeros((image_rows, width), LOW)
    gain_one = image_gains[0:1, :]
    gain_two = image_gains[1:2, :]

    def image_norm(i, carry):
        x = imt[i].astype(F32)
        at = pl.multiple_of(i * 64, 64)
        RES[pl.ds(at, image_len), :] = x
        GP[3, pl.ds(at, image_len), :] = (standard(x)[0] * gain_one).astype(LOW)
        return carry

    lax.fori_loop(0, images, image_norm, 0)
    for i in range(3):
        image_loads[i].wait()

    def image_qkv(j, carry):
        GP[j, pl.ds(0, image_rows), :] = dot(
            GP[3, pl.ds(0, image_rows), :], IW[j]
        ).astype(LOW)
        return carry

    lax.fori_loop(0, 3, image_qkv, 0)
    for i in range(8, 11):
        load_image(i)
    tick(1)

    key_valid = jnp.where(iota((256, 64), 1) < image_len, 0.0, FAR)
    lane_head = iota((64, 256), 1) >> 6

    def image_attention(i, carry):
        at = pl.multiple_of(i * 64, 64)
        for n in range(width // 256):
            lanes = slice(256 * n, 256 * n + 256)
            q = GP[0, pl.ds(at, 64), lanes]
            k = GP[1, pl.ds(at, 64), lanes]
            v = GP[2, pl.ds(at, 64), lanes]
            logits = dot_nt(jnp.concatenate([q] * 4, axis=0) * HM4[...], k) * 0.125 + key_valid
            expos = jnp.exp(logits - jnp.max(logits, axis=-1, keepdims=True))
            probs = (expos * (1.0 / jnp.sum(expos, axis=-1, keepdims=True))).astype(LOW)
            o = dot(probs, v)
            mix = jnp.where(
                lane_head < 2,
                jnp.where(lane_head == 0, o[0:64], o[64:128]),
                jnp.where(lane_head == 2, o[128:192], o[192:256]),
            )
            N2[pl.ds(at, 64), lanes] = mix.astype(LOW)
        return carry

    lax.fori_loop(0, images, image_attention, 0)
    tick(2)
    image_loads[3].wait()

    def image_out(n, carry):
        lanes = pl.ds(pl.multiple_of(n * 256, 256), 256)
        RES[pl.ds(0, image_rows), lanes] += dot(
            N2[pl.ds(0, image_rows), :], IW[3, :, lanes]
        )
        return carry

    lax.fori_loop(0, width // 256, image_out, 0)
    load_image(11)

    def image_norm_two(t, carry):
        at = pl.ds(pl.multiple_of(t * 16, 16), 16)
        GP[3, at, :] = (standard(RES[at, :])[0] * gain_two).astype(LOW)
        return carry

    lax.fori_loop(0, image_rows // 16, image_norm_two, 0, unroll=4)
    IP[...] = jnp.zeros_like(IP)
    for i in range(images):
        IP[i : i + 1, :] = jnp.sum(RES[64 * i : 64 * i + image_len, :], axis=0, keepdims=True) * (
            1.0 / image_len
        )
    image_pool = jnp.where(
        ((iota((16, image_rows), 1) >> 6) == iota((16, image_rows), 0))
        & ((iota((16, image_rows), 1) & 63) < image_len),
        1.0,
        0.0,
    ).astype(LOW)
    for i in range(4, 12):
        image_loads[i].wait()

    def image_feed(u, carry):
        ACC[pl.ds(0, image_rows), :] = dot(
            GP[3, pl.ds(0, image_rows), :], IW[4 + u]
        )

        def activate(t, inner):
            at = pl.ds(pl.multiple_of(t * 16, 16), 16)
            h = ACC[at, :]
            act = 0.5 * h * (1.0 + jnp.tanh(GELU_A * h * (1.0 + GELU_B * h * h)))
            N2[at, :] = act.astype(LOW)
            return inner

        lax.fori_loop(0, image_rows // 16, activate, 0, unroll=4)
        pooled = (dot(image_pool, N2[pl.ds(0, image_rows), :]) * (1.0 / image_len)).astype(LOW)
        IP[...] += dot(pooled, IW[u])
        return carry

    tick(3)
    lax.fori_loop(0, 1, image_feed, 0)
    tick(4)
    lax.fori_loop(1, 2, image_feed, 0)
    tick(5)
    lax.fori_loop(2, 3, image_feed, 0)
    tick(6)
    lax.fori_loop(3, 4, image_feed, 0)
    tick(7)
    pooled_image = IP[0:8]
    EMB[me] = (
        pooled_image
        * lax.rsqrt(jnp.sum(pooled_image * pooled_image, axis=-1, keepdims=True) + 1e-6)
    ).astype(LOW)

    def send_embed(k, carry):
        q = lax.rem(me + k, n_all)
        pltpu.make_async_remote_copy(
            src_ref=EMB.at[me],
            dst_ref=EMB.at[me],
            send_sem=emb_s,
            recv_sem=emb_r,
            device_id=(q // n_mp, lax.rem(q, n_mp)),
            device_id_type=pl.DeviceIdType.MESH,
        ).start()
        return carry

    lax.fori_loop(1, n_all, send_embed, 0)

    tok_copy.wait()
    g1, g2 = norm_gains[0:1, :], norm_gains[1:2, :]
    b1, b2 = norm_shifts[0:1, :], norm_shifts[1:2, :]

    def norm_one(t, carry):
        at = pl.ds(pl.multiple_of(t * LEN, LEN), LEN)
        N1[at, :] = (standard(TOK[t].astype(F32))[0] * g1 + b1).astype(LOW)
        return carry

    lax.fori_loop(0, n_cap, norm_one, 0, unroll=7)
    tick(8)
    for copy in sb_copies:
        copy.wait_recv()
    gather_end(0)

    def project(t, carry):
        s, j = t // 3, lax.rem(t, 3)
        weight = W[0, s, pl.ds(pl.multiple_of(shard * j, 16), shard), :]
        QKV[j, s] = (dot_nt(N1[...], weight) + SB[s, pl.ds(j, 1), 0:shard]).astype(LOW)
        return carry

    tick(9)
    lax.fori_loop(0, 6, project, 0)
    tick(10)
    lax.fori_loop(6, 3 * n_mp, project, 0)
    tick(11)
    lane_three = iota((BLOCK, shard), 1) >> 6

    def join_heads(o):
        return jnp.where(
            lane_three == 0,
            o[0:BLOCK],
            jnp.where(lane_three == 1, o[BLOCK : 2 * BLOCK], o[2 * BLOCK : 3 * BLOCK]),
        )

    def attention(b, carry):
        at = pl.ds(pl.multiple_of(b * BLOCK, 16), BLOCK)
        loaded = [[QKV[j, s, at, :] for j in range(3)] for s in range(n_mp)]
        heads, mask = HM3[...], BM[...]
        every = []
        for q, k, v in loaded:
            logits = dot_nt(jnp.concatenate([q] * 3, axis=0) * heads, k) * 0.125 + mask
            expos = jnp.exp(logits - jnp.max(logits, axis=-1, keepdims=True))
            probs = (expos * (1.0 / jnp.sum(expos, axis=-1, keepdims=True))).astype(LOW)
            every.append((probs, join_heads(dot(probs, v)).astype(LOW)))
        for s, (probs, mixed) in enumerate(every):
            PR[s, b] = probs
            MIX[s, at, :] = mixed
        return carry

    lax.fori_loop(0, 2, attention, 0)
    tick(12)
    lax.fori_loop(2, 4, attention, 0)
    tick(13)
    lax.fori_loop(4, n_blocks, attention, 0)
    tick(14)

    def attend_out(n, carry):
        lanes = pl.ds(pl.multiple_of(n * 256, 256), 256)
        total = dot(MIX[0], W[0, 0, pl.ds(3 * shard, shard), lanes])
        for s in range(1, n_mp):
            total += dot(MIX[s], W[0, s, pl.ds(3 * shard, shard), lanes])
        ACC[:, lanes] = total
        return carry

    lax.fori_loop(0, width // 256, attend_out, 0)
    out_bias = output_bias[...].reshape(1, width)

    def norm_two(t, carry):
        at = pl.ds(pl.multiple_of(t * LEN, LEN), LEN)
        x = TOK[t].astype(F32) + (ACC[at, :] + out_bias)
        RES[at, :] = x
        N2[at, :] = (standard(x)[0] * g2 + b2).astype(LOW)
        return carry

    lax.fori_loop(0, n_cap, norm_two, 0, unroll=7)
    tick(15)
    gather_end(1)

    def feed(s, carry):
        ACC[...] = dot(N2[...], W[1, s])
        bias = SB[s, 3:4, :]

        def activate(t, inner):
            at = pl.ds(pl.multiple_of(t * LEN, LEN), LEN)
            act, slope = gelu_parts(ACC[at, :] + bias)
            GT[at, :] = act.astype(LOW)
            GP[s, at, :] = slope.astype(LOW)
            return inner

        lax.fori_loop(0, n_cap, activate, 0, unroll=7)
        PA[s] = (dot(POOL[...], GT[...]) * (1.0 / LEN)).astype(LOW)
        return carry

    lax.fori_loop(0, 1, feed, 0)
    tick(16)
    lax.fori_loop(1, 2, feed, 0)
    tick(17)
    lax.fori_loop(2, 3, feed, 0)
    tick(18)
    lax.fori_loop(3, n_mp, feed, 0)
    tick(19)

    def pool_residual(n, carry):
        lanes = pl.ds(pl.multiple_of(n * 128, 128), 128)
        res = RES[:, lanes]
        res_high = res.astype(LOW)
        res_low = (res - res_high.astype(F32)).astype(LOW)
        EL[:, lanes] = (dot(POOL[...], res_high) + dot(POOL[...], res_low)) * (1.0 / LEN)
        return carry

    lax.fori_loop(0, width // 128, pool_residual, 0)
    pooled = EL[...] + reduce_bias[...].reshape(1, width)
    gather_end(2)
    for s in range(n_mp):
        pooled += dot(PA[s], W[2, s])
    inverse = lax.rsqrt(jnp.sum(pooled * pooled, axis=-1, keepdims=True) + 1e-6)
    embed = pooled * inverse
    EL[...] = embed

    pltpu.make_async_copy(EMB.at[pl.ds(0, n_all - 1)], EMB.at[pl.ds(0, n_all - 1)], emb_r).wait()
    group = min(n_all, 32)

    def embeds(c):
        part = EMB[c * group : c * group + group].astype(F32)
        return part.reshape(group * 8, width).astype(LOW)

    scaling = jnp.exp(log_scale[...].reshape(1, 1))
    embed_low = embed.astype(LOW)
    scores = scaling * jnp.concatenate(
        [dot_nt(embed_low, embeds(c)) for c in range(n_all // group)], axis=1
    )
    cap_rows = scores.shape[0]
    column = iota((cap_rows, t_all), 1)
    col_ok = (column & 7) < images
    row_ok = iota((cap_rows, t_all), 0) < n_cap
    image_id = (column >> 3) * images + (column & 7)
    cap_wide = jnp.broadcast_to(cap[...].reshape(1, 2 * n_cap).astype(F32), (cap_rows, 2 * n_cap))
    mine = iota((cap_rows, 2 * n_cap), 1) == iota((cap_rows, 2 * n_cap), 0) + half * n_cap
    cap_column = jnp.sum(jnp.where(mine, cap_wide, 0.0), axis=1, keepdims=True)
    matches = jnp.where((cap_column == image_id.astype(F32)) & col_ok & row_ok, 1.0, 0.0)
    by_row = jnp.where(col_ok, scores, FAR)
    row_top = jnp.max(by_row, axis=1, keepdims=True)
    row_lse = row_top + jnp.log(jnp.sum(jnp.exp(by_row - row_top), axis=1, keepdims=True))
    row_positive = jnp.sum(scores * matches, axis=1, keepdims=True)
    row_part = jnp.sum(
        jnp.where(iota((cap_rows, 1), 0) < n_cap, row_lse - row_positive, 0.0), axis=0, keepdims=True
    )
    by_column = jnp.where(row_ok, scores, FAR)
    top = jnp.max(by_column, axis=0, keepdims=True)
    MSG[...] = jnp.zeros_like(MSG)
    MSG[0:1, :] = top
    MSG[1:2, :] = jnp.sum(jnp.exp(by_column - top), axis=0, keepdims=True)
    MSG[2:3, :] = jnp.sum(scores * matches, axis=0, keepdims=True)
    MSG[3:4, :] = jnp.sum(matches, axis=0, keepdims=True)
    MSG[4:5, :] = jnp.broadcast_to(row_part, (1, t_all))
    low = lax.rem(d, 8)
    slot = low * 2 + half
    STATS[slot] = MSG[...]

    def send_stats(k, carry):
        q = lax.rem(slot + k, 16)
        pltpu.make_async_remote_copy(
            src_ref=MSG,
            dst_ref=STATS.at[slot],
            send_sem=st_s,
            recv_sem=st_r,
            device_id=(d - low + q // 2, m - half + lax.rem(q, 2)),
            device_id_type=pl.DeviceIdType.MESH,
        ).start()
        return carry

    lax.fori_loop(1, 16, send_stats, 0)
    pltpu.make_async_copy(STATS.at[pl.ds(0, 15)], STATS.at[pl.ds(0, 15)], st_r).wait()
    top = jnp.max(STATS[:, 0, :], axis=0, keepdims=True)
    total = jnp.sum(STATS[:, 1, :] * jnp.exp(STATS[:, 0, :] - top), axis=0, keepdims=True)
    positive = jnp.sum(STATS[:, 2, :], axis=0, keepdims=True)
    count = jnp.sum(STATS[:, 3, :], axis=0, keepdims=True)
    row_sum = jnp.sum(STATS[:, 4, :], axis=0, keepdims=True)
    for x in range(extra):
        XST[0, x] = jnp.concatenate(
            [top, total, positive, count, row_sum, jnp.zeros((3, t_all), F32)], axis=0
        )
        remote(
            XST.at[0, x], XST.at[1, x], stx_s.at[x], stx_r.at[x], (flip(d, 3 + x), m)
        ).wait_recv()
        other = XST[1, x]
        joined = jnp.maximum(top, other[0:1])
        total = total * jnp.exp(top - joined) + other[1:2] * jnp.exp(other[0:1] - joined)
        top = joined
        positive = positive + other[2:3]
        count = count + other[3:4]
        row_sum = row_sum + other[4:5]
    ok = col_ok[0:1]
    count = jnp.where(ok, count, 1.0)
    col_lse = top + jnp.log(total)
    column_part = jnp.sum(
        jnp.where(ok, col_lse - positive / count, 0.0), axis=1, keepdims=True
    )
    loss = 0.5 * (row_sum[:, 0:1] * (1.0 / total_captions) + column_part * (1.0 / total_images))
    weight = 0.5 * total_captions / total_images
    grad_scores = 0.5 * (jnp.exp(by_row - row_lse) - matches) + weight * (
        jnp.exp(by_column - col_lse) - matches * (1.0 / count)
    )
    grad_scores = jnp.where(col_ok & row_ok, grad_scores, 0.0)
    grad_log = jnp.sum(
        jnp.sum(grad_scores * scores, axis=1, keepdims=True), axis=0, keepdims=True
    )
    embed = EL[...]
    grad_cosine = (scaling * grad_scores).astype(LOW)
    grad_embed = dot(grad_cosine[:, 0 : group * 8], embeds(0))
    for c in range(1, n_all // group):
        grad_embed += dot(grad_cosine[:, c * group * 8 : (c + 1) * group * 8], embeds(c))
    grad_pooled = (
        grad_embed - embed * jnp.sum(embed * grad_embed, axis=-1, keepdims=True)
    ) * inverse
    SG[0] = jnp.zeros(SG.shape[1:], F32)
    SG[0, 13:14, :] = jnp.sum(grad_pooled, axis=0, keepdims=True)
    SG[0, 18:19, :] = jnp.broadcast_to(grad_log, (1, width))
    GPL[0] = grad_pooled.astype(LOW)
    grad_rows = grad_pooled * (1.0 / LEN)
    EL[...] = grad_rows
    GPL[1] = grad_rows.astype(LOW)

    def part(g, i):
        return IW.at[2 * g + i]

    places = (4, 7, 6)

    def whole(g):
        return IW.at[places[g]]

    def settle(copies):
        for copy in copies:
            copy.wait_send()
        sends[:] = [other for other in sends if all(other is not copy for copy in copies)]

    state = {}
    stores = []
    axis_one = ((yb, y_dev), (xb, x_dev))
    axis_two = ((xb, x_dev), (yb, y_dev))
    own = (p_a, p_b)

    def scatter(g, stage, i, ab):
        bit_one, dev_one = axis_one[ab]
        bit_two, dev_two = axis_two[ab]
        run = 8 * ab + 4 * cb + 2 * bit_one
        if stage == 0:
            p, n, dst, dev = 8 * ab + 4 * (1 - cb), 4, RCORE.at[g % 2, i, ab], core_dev
        elif stage == 1:
            p, n, dst, dev = 8 * ab + 4 * cb + 2 * (1 - bit_one), 2, RB1.at[g % 2, i, ab], dev_one
        elif stage == 2:
            p, n, dst, dev = run + 1 - bit_two, 1, RB2.at[g % 2, i, ab], dev_two
        else:
            p, n, dst, dev = own[ab], 1, RZ.at[g, ab], pair_dev
        k = 2 * i + ab
        state[g, stage, i, ab] = remote(
            part(g, i).at[span(p, n)], dst, rs_s.at[g, stage, k], rs_r.at[g, stage, k], dev
        )

    def add_in(g, stage, i, ab):
        state[g, stage, i, ab].wait_recv()
        run = 8 * ab + 4 * cb
        if stage == 0:
            at, got = span(run, 4), RCORE[g % 2, i, ab]
        elif stage == 1:
            at, got = span(run + 2 * axis_one[ab][0], 2), RB1[g % 2, i, ab]
        else:
            at, got = span(own[ab], 1), RB2[g % 2, i, ab]
        IW[2 * g + i, at, :] = IW[2 * g + i, at, :] + got

    def gather_back(g, stage, ab):
        state[g, "gather", stage, ab] = spread(
            lambda p, n: whole(g).at[span(p, n)], stage, ab, ag_s.at[g], ag_r.at[g]
        )

    def reduce_start(g, ab):
        if g == 0:
            settle([state.pop((2, a, i, ab)) for a in range(4) for i in range(2) if (2, a, i, ab) in state])
        for i in (1, 0):
            scatter(g, 0, i, ab)

    def reduce_step(g, step):
        if step == 0:
            for ab in range(2):
                reduce_start(g, ab)
        elif step < 4:
            for i in (1, 0):
                for ab in range(2):
                    add_in(g, step - 1, i, ab)
                    if step < 3 or i == 1:
                        scatter(g, step, i, ab)
        elif step == 4:
            for ab in range(2):
                state[g, 3, 1, ab].wait_recv()
                at = span(own[ab], 1)
                IW[places[g], at, :] = IW[2 * g, at, :] + RZ[g, ab]
                for x in range(extra):
                    copy = remote(
                        whole(g).at[at],
                        XR.at[g % 2, x, ab],
                        xr_s.at[g, x, ab],
                        xr_r.at[g, x, ab],
                        (flip(d, 3 + x), m),
                    )
                    copy.wait_recv()
                    settle([copy])
                    IW[places[g], at, :] = IW[places[g], at, :] + XR[g % 2, x, ab]
                gather_back(g, 0, ab)
        elif step < 7:
            for ab in range(2):
                state[g, "gather", step - 5, ab].wait_recv()
                gather_back(g, step - 4, ab)
        else:
            for ab in range(2):
                state[g, "gather", 2, ab].wait_recv()
            stores.append(local(whole(g), red.at[g], out_sem.at[g]))

    def back_tick(place):
        for g, step in RPLAN.get(place, ()):
            reduce_step(g, step)

    shards = (m, pair)
    for i in range(2):
        IW[4 + i] = dot_tn(PA[shards[i]], GPL[0]).astype(LOW)

    back_tick(0)

    def grad_activation(s, carry):
        GA[s] = dot_nt(GPL[1], W[2, s])
        return carry

    lax.fori_loop(0, n_mp, grad_activation, 0)
    back_tick(1)
    ones = jnp.ones((16, rows), LOW)

    def grad_hidden(s, carry):
        def scale(t, inner):
            at = pl.ds(pl.multiple_of(t * LEN, LEN), LEN)
            GP[s, at, :] = (GP[s, at, :].astype(F32) * GA[s, pl.ds(t, 1), :]).astype(LOW)
            return inner

        lax.fori_loop(0, n_cap, scale, 0, unroll=7)
        SG[0, pl.ds(8 + s, 1), :] = dot(ones, GP[s])[0:1]
        return carry

    lax.fori_loop(0, 2, grad_hidden, 0)
    back_tick(2)
    lax.fori_loop(2, n_mp, grad_hidden, 0)
    back_tick(3)

    def expand_gradient(i, carry):
        s = m + i * (pair - m)
        IW[2 + i] = dot_tn(N2[...], GP[s]).astype(LOW)
        return carry

    lax.fori_loop(0, 2, expand_gradient, 0)
    back_tick(4)

    def grad_norm_two(n, carry):
        p = pl.ds(pl.multiple_of(n * 384, 128), 384)
        total = dot_nt(GP[0], W[1, 0, p, :])
        for s in range(1, n_mp):
            total += dot_nt(GP[s], W[1, s, p, :])
        ACC[:, pl.ds(pl.multiple_of(n * 384, 128), 384)] = total
        return carry

    lax.fori_loop(0, 1, grad_norm_two, 0)
    back_tick(5)
    lax.fori_loop(1, 2, grad_norm_two, 0)
    back_tick(6)

    def norm_back(e, gain, x):
        xhat, scale = standard(x)
        eg = e * gain
        c1 = jnp.sum(eg, axis=-1, keepdims=True) * (1.0 / width)
        c2 = jnp.sum(eg * xhat, axis=-1, keepdims=True) * (1.0 / width)
        return (eg - c1 - xhat * c2) * scale, sum8(e * xhat), sum8(e)

    zero8 = jnp.zeros((8, width), F32)

    def back_two(t, carry):
        dg, db, do = carry
        found = []
        for u in range(7):
            at = pl.ds(pl.multiple_of((7 * t + u) * LEN, LEN), LEN)
            dv, one, two = norm_back(ACC[at, :], g2, RES[at, :])
            g = EL[pl.ds(7 * t + u, 1), :] + dv
            found.append((at, g))
            dg, db, do = dg + one, db + two, do + sum8(g)
        for at, g in found:
            RES[at, :] = g
            GRL[at, :] = g.astype(LOW)
        return dg, db, do

    dg, db, do = lax.fori_loop(0, n_cap // 7, back_two, (zero8, zero8, zero8))
    SG[0, 15:16, :] = jnp.sum(dg, axis=0, keepdims=True)
    SG[0, 17:18, :] = jnp.sum(db, axis=0, keepdims=True)
    SG[0, 12:13, :] = jnp.sum(do, axis=0, keepdims=True)

    back_tick(7)
    for i in range(2):
        IW[i, 3 * shard : 4 * shard, :] = dot_tn(MIX[shards[i]], GRL[...]).astype(LOW)

    def grad_mixture(s, carry):
        MIX[s] = dot_nt(GRL[...], W[0, s, pl.ds(3 * shard, shard), :]).astype(LOW)
        return carry

    lax.fori_loop(0, n_mp, grad_mixture, 0)
    back_tick(8)

    def attention_back(b, carry):
        at = pl.ds(pl.multiple_of(b * BLOCK, 16), BLOCK)
        loaded = [
            [QKV[j, s, at, :] for j in range(3)] + [MIX[s, at, :], PR[s, b]] for s in range(n_mp)
        ]
        heads = HM3[...]
        every = []
        for q, k, v, g, low_probs in loaded:
            q = jnp.concatenate([q] * 3, axis=0) * heads
            g = jnp.concatenate([g] * 3, axis=0) * heads
            probs = low_probs.astype(F32)
            grad_probs = dot_nt(g, v)
            inner = jnp.sum(grad_probs * probs, axis=-1, keepdims=True)
            grad_logits = (probs * (grad_probs - inner)).astype(LOW)
            every.append(
                (
                    (join_heads(dot(grad_logits, k)) * 0.125).astype(LOW),
                    (dot_tn(grad_logits, q) * 0.125).astype(LOW),
                    dot_tn(low_probs, g).astype(LOW),
                )
            )
        for s, grads in enumerate(every):
            for j in range(3):
                QKV[j, s, at, :] = grads[j]
        return carry

    def attend_gradient(j):
        def one(i, carry):
            s = m + i * (pair - m)
            IW[i, shard * j : shard * (j + 1), :] = dot_tn(QKV[j, s], N1[...]).astype(LOW)
            return carry

        lax.fori_loop(0, 2, one, 0)

    small_gain, small_shift = zero8, zero8
    gt_copies = []
    cuts = (0, 4, n_blocks)
    for r in range(2):
        middle = (cuts[r] + cuts[r + 1]) // 2
        lax.fori_loop(cuts[r], middle, attention_back, 0)
        back_tick(9 + 5 * r)
        lax.fori_loop(middle, cuts[r + 1], attention_back, 0)
        back_tick(10 + 5 * r)
        if r == 1:
            attend_gradient(2)
            reduce_start(0, 1)
            attend_gradient(0)
            attend_gradient(1)
            reduce_start(0, 0)
            back_tick(20)
        first, last = cuts[r] * (BLOCK // LEN), cuts[r + 1] * (BLOCK // LEN)
        stripe = pl.ds(first * LEN, (last - first) * LEN)

        def grad_norm_one(n, carry):
            lanes = pl.ds(pl.multiple_of(n * 256, 256), 256)
            total = None
            for s in range(n_mp):
                for j in range(3):
                    term = dot(
                        QKV[j, s, stripe, :],
                        W[0, s, pl.ds(shard * j, shard), lanes],
                    )
                    total = term if total is None else total + term
            ACC[stripe, lanes] = total
            return carry

        lax.fori_loop(0, width // 256, grad_norm_one, 0)
        back_tick(11 + 5 * r)
        def back_one(t, carry):
            at = pl.ds(pl.multiple_of(t * LEN, LEN), LEN)
            dv, dg, db = norm_back(ACC[at, :], g1, TOK[t].astype(F32))
            GT[at, :] = (RES[at, :] + dv).astype(LOW)
            return carry[0] + dg, carry[1] + db

        small_gain, small_shift = lax.fori_loop(
            first, last, back_one, (small_gain, small_shift), unroll=7
        )
        back_tick(12 + 5 * r)
        gt_copies.append(
            remote(GT.at[stripe], gt.at[half, stripe], gt_s.at[r], gt_r.at[r], pair_dev)
        )
    back_tick(21)
    stores.append(local(GT, gt.at[half], out_sem.at[3]))
    SG[0, 14:15, :] = jnp.sum(small_gain, axis=0, keepdims=True)
    SG[0, 16:17, :] = jnp.sum(small_shift, axis=0, keepdims=True)

    def bias_gradient(s, carry):
        SG[0, pl.ds(s, 1), 0:shard] = dot(ones, QKV[0, s])[0:1]
        SG[0, pl.ds(4 + s, 1), 0:shard] = dot(ones, QKV[2, s])[0:1]
        return carry

    lax.fori_loop(0, n_mp, bias_gradient, 0)
    small_devs = [core_dev, y_dev, x_dev, pair_dev] + [(flip(d, 3 + x), m) for x in range(extra)]
    small = {}

    def small_start(i):
        small[i] = remote(SG.at[i], SGR.at[i], sg_s.at[i], sg_r.at[i], small_devs[i])

    def small_end(i):
        small[i].wait_recv()
        SG[i + 1] = SG[i] + SGR[i]

    back_tick(22)
    small_start(0)
    back_tick(23)
    small_end(0)
    small_start(1)
    back_tick(24)
    small_end(1)
    small_start(2)
    back_tick(25)
    small_end(2)
    small_start(3)
    back_tick(26)
    small_end(3)
    for i in range(4, 4 + extra):
        small_start(i)
        small_end(i)
    back_tick(27)
    last = SG.shape[0] - 1
    sgo[...] = jnp.zeros_like(sgo)
    sgo[0:1, :] = SG[last, pl.ds(m, 1), :]
    sgo[1:2, :] = SG[last, pl.ds(4 + m, 1), :]
    sgo[2:3, :] = SG[last, pl.ds(8 + m, 1), :]
    sgo[3:10, :] = SG[last, 12:19, :]
    sgo[10:11, :] = jnp.broadcast_to(loss, (1, width))
    back_tick(28)
    for copy in gt_copies:
        copy.wait_recv()
    pltpu.make_async_copy(EMB.at[pl.ds(0, n_all - 1)], EMB.at[pl.ds(0, n_all - 1)], emb_s).wait()
    pltpu.make_async_copy(STATS.at[pl.ds(0, 15)], STATS.at[pl.ds(0, 15)], st_s).wait()
    for copy in sends:
        copy.wait_send()
    for copy in stores:
        copy.wait()


def local_step(
    n_dp,
    n_mp,
    caption_tokens,
    image_tokens,
    image_attend,
    image_output,
    image_expand,
    image_reduce,
    image_gains,
    caption_attend,
    attend_bias,
    caption_output,
    output_bias,
    caption_expand,
    expand_bias,
    caption_reduce,
    reduce_bias,
    norm_gains,
    norm_shifts,
    log_scale,
    caption_image,
):
    captions, length, width = caption_tokens.shape
    images, image_len, _ = image_tokens.shape
    shard = caption_attend.shape[2]
    units = caption_expand.shape[1]
    n_cap = captions // 2
    rows = n_cap * length
    n_blocks = rows // BLOCK
    n_all = n_dp * n_mp
    t_all = n_all * 8
    extra = n_dp.bit_length() - 1 - 3
    assert length == LEN and units == width and shard * n_mp == width and width == 16 * PIECE

    any_space = pl.BlockSpec(memory_space=pl.ANY)
    vmem = pl.BlockSpec(memory_space=pltpu.VMEM)
    nx = max(extra, 1)
    dma = pltpu.SemaphoreType.DMA
    scratch = [
        pltpu.VMEM((3, n_mp, width, width), LOW),
        pltpu.VMEM((8, width, width), LOW),
        pltpu.VMEM((n_cap, length, width), LOW),
        pltpu.VMEM((rows, width), LOW),
        pltpu.VMEM((3, n_mp, rows, shard), LOW),
        pltpu.VMEM((n_mp, n_blocks, 3 * BLOCK, BLOCK), LOW),
        pltpu.VMEM((n_mp, rows, shard), LOW),
        pltpu.VMEM((rows, width), F32),
        pltpu.VMEM((rows, width), LOW),
        pltpu.VMEM((n_mp, rows, width), LOW),
        pltpu.VMEM((n_mp, 64, width), LOW),
        pltpu.VMEM((rows, width), F32),
        pltpu.VMEM((rows, width), LOW),
        pltpu.VMEM((rows, width), LOW),
        pltpu.VMEM((16, width), F32),
        pltpu.VMEM((n_all, 8, width), LOW),
        pltpu.VMEM((8, t_all), F32),
        pltpu.VMEM((16, 8, t_all), F32),
        pltpu.VMEM((8, width), F32),
        pltpu.VMEM((n_mp, 8, width), F32),
        pltpu.VMEM((3 * BLOCK, shard), LOW),
        pltpu.VMEM((3 * BLOCK, BLOCK), F32),
        pltpu.VMEM((256, 256), LOW),
        pltpu.VMEM((64, rows), LOW),
        pltpu.VMEM((64, width), F32),
        pltpu.VMEM((2, 64, width), LOW),
        pltpu.VMEM((n_mp, 64, width), F32),
        pltpu.VMEM((2, 2, 2, 4 * PIECE, width), LOW),
        pltpu.VMEM((2, 2, 2, 2 * PIECE, width), LOW),
        pltpu.VMEM((2, 2, 2, PIECE, width), LOW),
        pltpu.VMEM((3, 2, PIECE, width), LOW),
        pltpu.VMEM((2, nx, 2, PIECE, width), LOW),
        pltpu.VMEM((2, nx, 8, t_all), F32),
        pltpu.VMEM((5 + extra, 24, width), F32),
        pltpu.VMEM((4 + extra, 24, width), F32),
        dma((3, 3, 2)),
        dma((3, 3, 2)),
        dma((3, 3, 3, 2)),
        dma((3, 3, 3, 2)),
        dma((3,)),
        dma((3,)),
        dma((12,)),
        dma,
        dma((3,)),
        dma((3,)),
        dma,
        dma,
        dma,
        dma,
        dma((nx,)),
        dma((nx,)),
        dma((3, 4, 4)),
        dma((3, 4, 4)),
        dma((3, 3, 2)),
        dma((3, 3, 2)),
        dma((3, nx, 2)),
        dma((3, nx, 2)),
        dma((4 + extra,)),
        dma((4 + extra,)),
        dma((2,)),
        dma((2,)),
        dma((4,)),
    ]
    red, gt, sgo = pl.pallas_call(
        functools.partial(body, n_dp, n_mp),
        out_shape=(
            jax.ShapeDtypeStruct((3, width, width), LOW),
            jax.ShapeDtypeStruct((2, rows, width), LOW),
            jax.ShapeDtypeStruct((16, width), F32),
        ),
        in_specs=[any_space, vmem] + [any_space] * 8 + [vmem] * 9,
        out_specs=(any_space, any_space, vmem),
        scratch_shapes=scratch,
        compiler_params=pltpu.CompilerParams(
            collective_id=0, has_side_effects=True, vmem_limit_bytes=66_000_000
        ),
        name="step",
    )(
        caption_tokens,
        image_tokens,
        image_attend,
        image_output,
        image_expand,
        image_reduce,
        jnp.swapaxes(caption_attend, 1, 2),
        caption_output,
        caption_expand,
        caption_reduce,
        image_gains,
        attend_bias,
        output_bias,
        expand_bias,
        reduce_bias,
        norm_gains,
        norm_shifts,
        log_scale,
        caption_image,
    )
    shapes = (
        (1,),
        (captions, length, width),
        (3, shard, width),
        (2, shard),
        (shard, width),
        (width,),
        (width, units),
        (units,),
        (units, width),
        (width,),
        (2, width),
        (2, width),
        (1,),
    )
    large = (1, 2, 4, 6, 8)
    parts = 7
    grads = pl.pallas_call(
        finish,
        out_shape=tuple(jax.ShapeDtypeStruct(shape, F32) for shape in shapes),
        in_specs=[any_space, any_space, vmem],
        out_specs=tuple(any_space if i in large else vmem for i in range(len(shapes))),
        scratch_shapes=[
            pltpu.VMEM((captions, length, width), LOW),
            pltpu.VMEM((captions, length, width), F32),
            pltpu.VMEM((3, width, width), LOW),
            pltpu.VMEM((3, width, width), F32),
            pltpu.VMEM((3, shard, width), F32),
            dma((parts,)),
            dma((parts,)),
            dma((3,)),
            dma((6,)),
        ],
        compiler_params=pltpu.CompilerParams(vmem_limit_bytes=64_000_000),
        name="finish",
    )(red, gt.reshape(captions, length, width), sgo)
    return (*grads[:2], jnp.swapaxes(grads[2], 1, 2), *grads[3:])


def finish(
    red,
    gt,
    small,
    loss,
    tokens,
    attend,
    attend_bias,
    output,
    output_bias,
    expand,
    expand_bias,
    reduce,
    reduce_bias,
    gains,
    shifts,
    log_scale,
    GT,
    TOKENS,
    RED,
    WIDE,
    ATTEND,
    gt_in,
    gt_out,
    red_in,
    red_out,
):
    def copy(src, dst, sem):
        made = pltpu.make_async_copy(src, dst, sem)
        made.start()
        return made

    parts = gt_in.shape[0]
    size = GT.shape[0] // parts
    width = GT.shape[2]
    shard = ATTEND.shape[1]
    order = (0, 1, 2)
    weights = {g: copy(red.at[g], RED.at[g], red_in.at[g]) for g in order}
    pieces = [
        copy(gt.at[pl.ds(i * size, size)], GT.at[pl.ds(i * size, size)], gt_in.at[i])
        for i in range(parts)
    ]
    written = []
    loss[...] = small[10:11, 0:1].reshape(1)
    attend_bias[...] = small[0:2, 0:shard]
    expand_bias[...] = small[2:3, :].reshape(width)
    output_bias[...] = small[3:4, :].reshape(width)
    reduce_bias[...] = small[4:5, :].reshape(width)
    gains[...] = small[5:7, :]
    shifts[...] = small[7:9, :]
    log_scale[...] = small[9:10, 0:1].reshape(1)
    for g in order:
        weights[g].wait()
        if g == 0:
            for j in range(3):
                ATTEND[j] = RED[0, shard * j : shard * (j + 1), :].astype(F32)
                written.append(copy(ATTEND.at[j], attend.at[j], red_out.at[j]))
            WIDE[0, 3 * shard :, :] = RED[0, 3 * shard :, :].astype(F32)
            written.append(copy(WIDE.at[0, pl.ds(3 * shard, shard)], output, red_out.at[3]))
        else:

            def widen(t, carry):
                at = pl.ds(pl.multiple_of(t * 96, 96), 96)
                WIDE[g, at, :] = RED[g, at, :].astype(F32)
                return carry

            lax.fori_loop(0, width // 96, widen, 0)
            written.append(copy(WIDE.at[g], (expand, reduce)[g - 1], red_out.at[3 + g]))
    for i in range(parts):
        pieces[i].wait()
        at = slice(i * size, i * size + size)
        TOKENS[at] = GT[at].astype(F32)
        written.append(
            copy(
                TOKENS.at[pl.ds(i * size, size)], tokens.at[pl.ds(i * size, size)], gt_out.at[i]
            )
        )
    for made in written:
        made.wait()


def solution(mesh):
    in_specs = (
        P("dp", None, None),
        P(("dp", "mp"), None, None),
        P(),
        P(),
        P(),
        P(),
        P(),
        P(None, None, "mp"),
        P(None, "mp"),
        P("mp", None),
        P(),
        P(None, "mp"),
        P("mp"),
        P("mp", None),
        P(),
        P(),
        P(),
        P(),
        P("dp"),
    )
    out_specs = (
        P(),
        P("dp", None, None),
        P(None, None, "mp"),
        P(None, "mp"),
        P("mp", None),
        P(),
        P(None, "mp"),
        P("mp"),
        P("mp", None),
        P(),
        P(),
        P(),
        P(),
    )
    step = functools.partial(local_step, mesh.shape["dp"], mesh.shape["mp"])
    return jax.shard_map(step, mesh=mesh, in_specs=in_specs, out_specs=out_specs, check_vma=False)
```

```python
import functools

import jax
import jax.numpy as jnp
from jax import lax
from jax.experimental import pallas as pl
from jax.experimental.pallas import tpu as pltpu
from jax.sharding import PartitionSpec as P

HEAD_DIM = 64
LEN = 16
PIECE = 48
BLOCK = 112
F32 = jnp.float32
LOW = jnp.bfloat16
FAR = -1e30
ALL_HOPS = (1, 2, 3)
RPLAN = {
    0: ((2, 0),),
    2: ((2, 1),),
    4: ((1, 0),),
    6: ((2, 2), (1, 1),),
    8: ((2, 3),),
    9: ((2, 4),),
    12: ((1, 2),),
    10: ((1, 3), (2, 5),),
    11: ((2, 6),),
    17: ((0, 1),),
    21: ((0, 2),),
    22: ((1, 4), (0, 3),),
    23: ((1, 5),),
    24: ((0, 4), (1, 6),),
    25: ((0, 5), (2, 7),),
    26: ((1, 7),),
    27: ((0, 6),),
    28: ((0, 7),),
}
PLAN = {
    1: ((0, 0, (1,)),),
    2: ((0, 0, (2, 3)), (1, -1, (1,)), (2, -1, (1,)),),
    3: ((0, 1, (1, 2)), (1, -1, (2, 3)), (2, -1, (2, 3)),),
    5: ((0, 1, (3,)),),
    6: ((0, 2, (1, 2)),),
    7: ((0, 2, (3,)), (1, 0, (1,)), (2, 0, (1,)),),
    10: ((1, 1, (1,)), (2, 1, (1,)),),
    12: ((1, 2, (1,)), (2, 2, (1,)),),
    13: ((1, 0, (2, 3)),),
    14: ((1, 1, (2, 3)), (2, 0, (2, 3)),),
    16: ((1, 2, (2, 3)),),
    17: ((2, 1, (2, 3)),),
    19: ((2, 2, (2, 3)),),
}
GELU_A = 0.7978845608028654
GELU_B = 0.044715


def dot(a, b):
    return lax.dot_general(a, b, (((1,), (0,)), ((), ())), preferred_element_type=F32)


def dot_nt(a, b):
    return lax.dot_general(a, b, (((1,), (1,)), ((), ())), preferred_element_type=F32)


def dot_tn(a, b):
    return lax.dot_general(a, b, (((0,), (0,)), ((), ())), preferred_element_type=F32)


def iota(shape, axis):
    return lax.broadcasted_iota(jnp.int32, shape, axis)


def standard(x):
    width = x.shape[-1]
    centred = x - jnp.sum(x, axis=-1, keepdims=True) * (1.0 / width)
    variance = jnp.sum(centred * centred, axis=-1, keepdims=True) * (1.0 / width)
    scale = lax.rsqrt(variance + 1e-6)
    return centred * scale, scale


def gelu_parts(h):
    square = h * h
    t = jnp.tanh(GELU_A * h * (1.0 + GELU_B * square))
    half = 0.5 * (1.0 + t)
    slope = half + 0.5 * h * (1.0 - t * t) * (GELU_A * (1.0 + 3.0 * GELU_B * square))
    return h * half, slope


def sum8(x):
    return x[0:8] + x[8:16]


def body(
    n_dp,
    n_mp,
    tok_in,
    imt,
    ia_in,
    io_in,
    ie_in,
    ir_in,
    ca_in,
    co_in,
    we_in,
    wr_in,
    image_gains,
    attend_bias,
    output_bias,
    expand_bias,
    reduce_bias,
    norm_gains,
    norm_shifts,
    log_scale,
    cap,
    red,
    gt,
    sgo,
    W,
    IW,
    TOK,
    N1,
    QKV,
    PR,
    MIX,
    RES,
    N2,
    GP,
    PA,
    PB,
    ACC,
    GRL,
    GT,
    IP,
    EMB,
    MSG,
    STATS,
    SBL,
    SB,
    HM3,
    BM,
    HM4,
    POOL,
    EL,
    GPL,
    GA,
    RCORE,
    RB1,
    RB2,
    RZ,
    XR,
    XST,
    SG,
    SGR,
    gz_s,
    gz_r,
    ga_s,
    ga_r,
    loc_sem,
    ca_sem,
    iw_sem,
    tok_sem,
    sb_s,
    sb_r,
    emb_s,
    emb_r,
    st_s,
    st_r,
    stx_s,
    stx_r,
    rs_s,
    rs_r,
    ag_s,
    ag_r,
    xr_s,
    xr_r,
    sg_s,
    sg_r,
    gt_s,
    gt_r,
    out_sem,
    pb_s,
    pb_r,
):
    d = lax.axis_index("dp")
    m = lax.axis_index("mp")
    n_all = n_dp * n_mp
    me = d * n_mp + m
    bits = n_dp.bit_length() - 1
    extra = bits - 3
    images, image_len = imt.shape[0], imt.shape[1]
    rows = TOK.shape[0] * LEN
    n_cap = TOK.shape[0]
    n_blocks = rows // BLOCK
    width = RES.shape[1]
    shard = QKV.shape[3]
    image_rows = images * 64
    t_all = EMB.shape[0] * 8
    total_images = images * n_all
    total_captions = n_cap * 2 * n_dp

    def bit(v, b):
        return lax.rem(v // (1 << b), 2)

    def flip(v, b):
        return v + (1 - 2 * bit(v, b)) * (1 << b)

    cb, xb, yb = bit(d, 0), bit(d, 1), bit(d, 2)
    half = lax.rem(m, 2)
    pair = flip(m, 0)
    p_a = cb * 4 + yb * 2 + xb
    p_b = 8 + cb * 4 + xb * 2 + yb
    core_dev = (flip(d, 0), m)
    x_dev = (flip(d, 1), m)
    y_dev = (flip(d, 2), m)
    pair_dev = (d, pair)
    sends = []

    def remote(src, dst, ss, rs, dev):
        copy = pltpu.make_async_remote_copy(
            src_ref=src,
            dst_ref=dst,
            send_sem=ss,
            recv_sem=rs,
            device_id=dev,
            device_id_type=pl.DeviceIdType.MESH,
        )
        copy.start()
        sends.append(copy)
        return copy

    def local(src, dst, sem):
        copy = pltpu.make_async_copy(src, dst, sem)
        copy.start()
        return copy

    barrier = pltpu.get_barrier_semaphore()

    low = lax.rem(d, 8)
    slot = low * 2 + half

    def near_device(k):
        q = lax.rem(slot + k, 16)
        return (d - low + q // 2, m - half + lax.rem(q, 2))

    def greet(k, carry):
        pl.semaphore_signal(
            barrier, inc=1, device_id=near_device(k), device_id_type=pl.DeviceIdType.MESH
        )
        return carry

    far = flip(m, 1)
    far_pair = flip(pair, 1)
    others = [(d, far), (d, far_pair)] + [(flip(d, 3 + x), m) for x in range(extra)]
    for dev in others:
        pl.semaphore_signal(barrier, inc=1, device_id=dev, device_id_type=pl.DeviceIdType.MESH)
    lax.fori_loop(1, 16, greet, 0)

    image_loads = {}

    def load_image(i):
        if i < 3:
            src, slot = ia_in.at[i], i
        elif i == 3:
            src, slot = io_in, 3
        elif i < 8:
            src, slot = ie_in.at[:, pl.ds((i - 4) * width, width)], i
        else:
            src, slot = ir_in.at[pl.ds((i - 8) * width, width)], i - 8
        image_loads[i] = local(src, IW.at[slot], iw_sem.at[i])

    ca_copies = [
        local(ca_in.at[j], W.at[0, m, pl.ds(shard * j, shard)], ca_sem.at[j]) for j in range(3)
    ]
    own_loads = [local(co_in, W.at[0, m, pl.ds(3 * shard, shard)], loc_sem.at[0])]
    SBL[...] = jnp.zeros_like(SBL)
    SBL[0:1, 0:shard] = attend_bias[0:1, :]
    SBL[2:3, 0:shard] = attend_bias[1:2, :]
    SBL[3:4, :] = expand_bias[...].reshape(1, width)
    SB[m] = SBL[...]
    for copy in ca_copies + own_loads[0:1]:
        copy.wait()
    pl.semaphore_wait(barrier, 15 + len(others))

    hops = (1, 2, 3)

    def partner(k):
        other = flip(m, 0) if k % 2 else m
        return flip(other, 1) if k >= 2 else other

    zc, ac = {}, {}
    sources = (W.at[0, m], we_in, wr_in)

    def span(p, n):
        return pl.ds(pl.multiple_of(p * PIECE, 16), n * PIECE)

    def gather_z(g, ks=(1, 2, 3)):
        for k in ks:
            dev = (d, partner(k))
            for ab, p in ((0, p_a), (1, p_b)):
                zc[g, k, ab] = remote(
                    sources[g].at[span(p, 1)],
                    W.at[g, m, span(p, 1)],
                    gz_s.at[g, k - 1, ab],
                    gz_r.at[g, k - 1, ab],
                    dev,
                )

    def spread(at, stage, ab, ss, rs):
        if stage == 0:
            p, n, dev = ((p_a, 1, x_dev), (p_b, 1, y_dev))[ab]
        elif stage == 1:
            p, n, dev = ((cb * 4 + yb * 2, 2, y_dev), (8 + cb * 4 + xb * 2, 2, x_dev))[ab]
        else:
            p, n, dev = 8 * ab + cb * 4, 4, core_dev
        return remote(at(p, n), at(p, n), ss.at[stage, ab], rs.at[stage, ab], dev)

    def gather_start(g, stage, ks=(1, 2, 3)):
        for k in ks:
            source = partner(k)
            for ab in range(2):
                (zc[g, k, ab] if stage == 0 else ac[g, stage - 1, k, ab]).wait_recv()
                ac[g, stage, k, ab] = spread(
                    lambda p, n: W.at[g, source, span(p, n)],
                    stage,
                    ab,
                    ga_s.at[g, k - 1],
                    ga_r.at[g, k - 1],
                )

    def gather_end(g, ks=(1, 2, 3)):
        for k in ks:
            for ab in range(2):
                ac[g, 2, k, ab].wait_recv()
        if g > 0 and 1 in ks:
            own_loads[g].wait()

    def tick(place):
        for g, stage, ks in PLAN.get(place, ()):
            if stage < 0:
                gather_z(g, ks)
            else:
                gather_start(g, stage, ks)

    gather_z(0)
    sb_copies = []
    for k in hops:
        sb_copies.append(
            remote(
                SBL,
                SB.at[m],
                sb_s.at[k - 1],
                sb_r.at[k - 1],
                (d, partner(k)),
            )
        )
    for i in range(3):
        load_image(i)
    tok_copy = local(tok_in.at[pl.ds(half * n_cap, n_cap)], TOK, tok_sem)
    for i in range(3, 8):
        load_image(i)
    own_loads.append(local(we_in, W.at[1, m], loc_sem.at[1]))
    own_loads.append(local(wr_in, W.at[2, m], loc_sem.at[2]))
    query = iota((BLOCK, 3 * BLOCK), 1)
    query = query - jnp.where(query >= 2 * BLOCK, 2 * BLOCK, jnp.where(query >= BLOCK, BLOCK, 0))
    BM[...] = jnp.where((iota((BLOCK, 3 * BLOCK), 0) >> 4) == (query >> 4), 0.0, FAR)
    lane_shard = iota((BLOCK, shard), 1) >> 6
    for h in range(3):
        at = slice(h * BLOCK, (h + 1) * BLOCK)
        HM3[at, :] = jnp.where(lane_shard == h, 1.0, 0.0).astype(LOW)
    lane_four = iota((64, 256), 1) >> 6
    for h in range(4):
        HM4[64 * h : 64 * h + 64, :] = jnp.where(lane_four == h, 1.0, 0.0).astype(LOW)
    POOL[...] = jnp.where((iota(POOL.shape, 1) >> 4) == iota(POOL.shape, 0), 1.0, 0.0).astype(LOW)
    RES[pl.ds(0, image_rows), :] = jnp.zeros((image_rows, width), F32)
    GP[3, pl.ds(0, image_rows), :] = jnp.zeros((image_rows, width), LOW)
    gain_one = image_gains[0:1, :]
    gain_two = image_gains[1:2, :]

    def image_norm(i, carry):
        x = imt[i].astype(F32)
        at = pl.multiple_of(i * 64, 64)
        RES[pl.ds(at, image_len), :] = x
        GP[3, pl.ds(at, image_len), :] = (standard(x)[0] * gain_one).astype(LOW)
        return carry

    lax.fori_loop(0, images, image_norm, 0)
    for i in range(3):
        image_loads[i].wait()

    def image_qkv(j, carry):
        GP[j, pl.ds(0, image_rows), :] = dot(
            GP[3, pl.ds(0, image_rows), :], IW[j]
        ).astype(LOW)
        return carry

    lax.fori_loop(0, 3, image_qkv, 0)
    for i in range(8, 11):
        load_image(i)
    tick(1)

    key_valid = jnp.where(iota((256, 64), 1) < image_len, 0.0, FAR)
    lane_head = iota((64, 256), 1) >> 6

    def image_attention(i, carry):
        at = pl.multiple_of(i * 64, 64)
        for n in range(width // 256):
            lanes = slice(256 * n, 256 * n + 256)
            q = GP[0, pl.ds(at, 64), lanes]
            k = GP[1, pl.ds(at, 64), lanes]
            v = GP[2, pl.ds(at, 64), lanes]
            logits = dot_nt(jnp.concatenate([q] * 4, axis=0) * HM4[...], k) * 0.125 + key_valid
            expos = jnp.exp(logits - jnp.max(logits, axis=-1, keepdims=True))
            probs = (expos * (1.0 / jnp.sum(expos, axis=-1, keepdims=True))).astype(LOW)
            o = dot(probs, v)
            mix = jnp.where(
                lane_head < 2,
                jnp.where(lane_head == 0, o[0:64], o[64:128]),
                jnp.where(lane_head == 2, o[128:192], o[192:256]),
            )
            N2[pl.ds(at, 64), lanes] = mix.astype(LOW)
        return carry

    lax.fori_loop(0, images, image_attention, 0)
    tick(2)
    image_loads[3].wait()

    def image_out(n, carry):
        lanes = pl.ds(pl.multiple_of(n * 256, 256), 256)
        RES[pl.ds(0, image_rows), lanes] += dot(
            N2[pl.ds(0, image_rows), :], IW[3, :, lanes]
        )
        return carry

    lax.fori_loop(0, width // 256, image_out, 0)
    load_image(11)

    def image_norm_two(t, carry):
        at = pl.ds(pl.multiple_of(t * 16, 16), 16)
        GP[3, at, :] = (standard(RES[at, :])[0] * gain_two).astype(LOW)
        return carry

    lax.fori_loop(0, image_rows // 16, image_norm_two, 0, unroll=4)
    IP[...] = jnp.zeros_like(IP)
    for i in range(images):
        IP[i : i + 1, :] = jnp.sum(RES[64 * i : 64 * i + image_len, :], axis=0, keepdims=True) * (
            1.0 / image_len
        )
    image_pool = jnp.where(
        ((iota((16, image_rows), 1) >> 6) == iota((16, image_rows), 0))
        & ((iota((16, image_rows), 1) & 63) < image_len),
        1.0,
        0.0,
    ).astype(LOW)
    for i in range(4, 12):
        image_loads[i].wait()

    def image_feed(u, carry):
        ACC[pl.ds(0, image_rows), :] = dot(
            GP[3, pl.ds(0, image_rows), :], IW[4 + u]
        )

        def activate(t, inner):
            at = pl.ds(pl.multiple_of(t * 16, 16), 16)
            h = ACC[at, :]
            act = 0.5 * h * (1.0 + jnp.tanh(GELU_A * h * (1.0 + GELU_B * h * h)))
            N2[at, :] = act.astype(LOW)
            return inner

        lax.fori_loop(0, image_rows // 16, activate, 0, unroll=4)
        pooled = (dot(image_pool, N2[pl.ds(0, image_rows), :]) * (1.0 / image_len)).astype(LOW)
        IP[...] += dot(pooled, IW[u])
        return carry

    tick(3)
    lax.fori_loop(0, 1, image_feed, 0)
    tick(4)
    lax.fori_loop(1, 2, image_feed, 0)
    tick(5)
    lax.fori_loop(2, 3, image_feed, 0)
    tick(6)
    lax.fori_loop(3, 4, image_feed, 0)
    tick(7)
    pooled_image = IP[0:8]
    EMB[me] = (
        pooled_image
        * lax.rsqrt(jnp.sum(pooled_image * pooled_image, axis=-1, keepdims=True) + 1e-6)
    ).astype(LOW)

    shown = {}

    def show(stage, first, n, dev, at):
        run = EMB.at[pl.ds(first * n_mp, n * n_mp)]
        shown.setdefault(stage, []).append(
            remote(run, run, emb_s.at[at], emb_r.at[at], dev)
        )

    def show_embeds(stage):
        for copy in shown.get(stage - 1, ()):
            copy.wait_recv()
        if stage == 0:
            for k in hops:
                run = EMB.at[me]
                shown.setdefault(0, []).append(
                    remote(run, run, emb_s.at[k - 1], emb_r.at[k - 1], (d, partner(k)))
                )
        elif stage == 1:
            show(1, d, 1, x_dev, 3)
        elif stage == 2:
            for x in range(2):
                show(2, d + 2 * (x - xb), 1, y_dev, 4 + x)
        elif stage == 3:
            for q in range(4):
                show(3, d - low + cb + 2 * q, 1, core_dev, 6 + q)
        else:
            for x in range(extra):
                run = 8 << x
                first = d - lax.rem(d, run)
                show(4 + x, first, run, (flip(d, 3 + x), m), 10 + x)
                for copy in shown[4 + x]:
                    copy.wait_recv()

    show_embeds(0)

    tok_copy.wait()
    g1, g2 = norm_gains[0:1, :], norm_gains[1:2, :]
    b1, b2 = norm_shifts[0:1, :], norm_shifts[1:2, :]

    def norm_one(t, carry):
        at = pl.ds(pl.multiple_of(t * LEN, LEN), LEN)
        N1[at, :] = (standard(TOK[t].astype(F32))[0] * g1 + b1).astype(LOW)
        return carry

    lax.fori_loop(0, n_cap, norm_one, 0, unroll=7)
    tick(8)
    for copy in sb_copies:
        copy.wait_recv()
    gather_end(0)

    def project(t, carry):
        s, j = t // 3, lax.rem(t, 3)
        weight = W[0, s, pl.ds(pl.multiple_of(shard * j, 16), shard), :]
        QKV[j, s] = (dot_nt(N1[...], weight) + SB[s, pl.ds(j, 1), 0:shard]).astype(LOW)
        return carry

    tick(9)
    lax.fori_loop(0, 6, project, 0)
    tick(10)
    lax.fori_loop(6, 3 * n_mp, project, 0)
    tick(11)
    lane_three = iota((BLOCK, shard), 1) >> 6

    def join_heads(o):
        return jnp.where(
            lane_three == 0,
            o[0:BLOCK],
            jnp.where(lane_three == 1, o[BLOCK : 2 * BLOCK], o[2 * BLOCK : 3 * BLOCK]),
        )

    def attention(b, carry):
        at = pl.ds(pl.multiple_of(b * BLOCK, 16), BLOCK)
        loaded = [[QKV[j, s, at, :] for j in range(3)] for s in range(n_mp)]
        heads, mask = HM3[...], BM[...]
        every = []
        for q, k, v in loaded:
            logits = dot_nt(k, jnp.concatenate([q] * 3, axis=0) * heads) * 0.125 + mask
            expos = jnp.exp(logits - jnp.max(logits, axis=0, keepdims=True))
            probs = (expos * (1.0 / jnp.sum(expos, axis=0, keepdims=True))).astype(LOW)
            every.append((probs, join_heads(dot_tn(probs, v)).astype(LOW)))
        for s, (probs, mixed) in enumerate(every):
            PR[s, b] = probs
            MIX[s, at, :] = mixed
        return carry

    lax.fori_loop(0, 2, attention, 0)
    tick(12)
    lax.fori_loop(2, 4, attention, 0)
    tick(13)
    lax.fori_loop(4, n_blocks, attention, 0)
    tick(14)

    def attend_out(n, carry):
        lanes = pl.ds(pl.multiple_of(n * 256, 256), 256)
        total = dot(MIX[0], W[0, 0, pl.ds(3 * shard, shard), lanes])
        for s in range(1, n_mp):
            total += dot(MIX[s], W[0, s, pl.ds(3 * shard, shard), lanes])
        ACC[:, lanes] = total
        return carry

    lax.fori_loop(0, width // 256, attend_out, 0)
    out_bias = output_bias[...].reshape(1, width)

    def norm_two(t, carry):
        at = pl.ds(pl.multiple_of(t * LEN, LEN), LEN)
        x = TOK[t].astype(F32) + (ACC[at, :] + out_bias)
        RES[at, :] = x
        N2[at, :] = (standard(x)[0] * g2 + b2).astype(LOW)
        return carry

    lax.fori_loop(0, n_cap, norm_two, 0, unroll=7)
    tick(15)
    show_embeds(1)
    gather_end(1, (1,))

    def feed_one(s):
        ACC[...] = dot(N2[...], W[1, s])
        bias = SB[s, 3:4, :]

        def activate(t, inner):
            at = pl.ds(pl.multiple_of(t * LEN, LEN), LEN)
            act, slope = gelu_parts(ACC[at, :] + bias)
            GT[at, :] = act.astype(LOW)
            GP[s, at, :] = slope.astype(LOW)
            return inner

        lax.fori_loop(0, n_cap, activate, 0, unroll=7)
        PA[s] = (dot(POOL[...], GT[...]) * (1.0 / LEN)).astype(LOW)

    def feed_near(i, carry):
        feed_one(m + i * (pair - m))
        return carry

    def feed_far(i, carry):
        feed_one(far + i * (far_pair - far))
        return carry

    lax.fori_loop(0, 1, feed_near, 0)
    tick(16)
    show_embeds(2)
    lax.fori_loop(1, 2, feed_near, 0)
    tick(17)
    show_embeds(3)
    def pool_residual(n, carry):
        lanes = pl.ds(pl.multiple_of(n * 128, 128), 128)
        res = RES[:, lanes]
        res_high = res.astype(LOW)
        res_low = (res - res_high.astype(F32)).astype(LOW)
        EL[:, lanes] = (dot(POOL[...], res_high) + dot(POOL[...], res_low)) * (1.0 / LEN)
        return carry

    lax.fori_loop(0, width // 128, pool_residual, 0)
    pooled = EL[...] + reduce_bias[...].reshape(1, width)
    gather_end(2, (1,))
    PB[0] = (dot(PA[m], W[2, m]) + dot(PA[pair], W[2, pair])).astype(LOW)
    pooled_copy = remote(PB.at[0], PB.at[1], pb_s, pb_r, (d, far))
    tick(18)
    pooled_copy.wait_recv()
    pooled += PB[0].astype(F32) + PB[1].astype(F32)
    inverse = lax.rsqrt(jnp.sum(pooled * pooled, axis=-1, keepdims=True) + 1e-6)
    embed = pooled * inverse
    EL[...] = embed

    show_embeds(4)
    group = min(n_all, 32)

    def embeds(c):
        part = EMB[c * group : c * group + group].astype(F32)
        return part.reshape(group * 8, width).astype(LOW)

    scaling = jnp.exp(log_scale[...].reshape(1, 1))
    embed_low = embed.astype(LOW)
    scores = scaling * jnp.concatenate(
        [dot_nt(embed_low, embeds(c)) for c in range(n_all // group)], axis=1
    )
    cap_rows = scores.shape[0]
    column = iota((cap_rows, t_all), 1)
    col_ok = (column & 7) < images
    row_ok = iota((cap_rows, t_all), 0) < n_cap
    image_id = (column >> 3) * images + (column & 7)
    cap_wide = jnp.broadcast_to(cap[...].reshape(1, 2 * n_cap).astype(F32), (cap_rows, 2 * n_cap))
    mine = iota((cap_rows, 2 * n_cap), 1) == iota((cap_rows, 2 * n_cap), 0) + half * n_cap
    cap_column = jnp.sum(jnp.where(mine, cap_wide, 0.0), axis=1, keepdims=True)
    matches = jnp.where((cap_column == image_id.astype(F32)) & col_ok & row_ok, 1.0, 0.0)
    by_row = jnp.where(col_ok, scores, FAR)
    row_top = jnp.max(by_row, axis=1, keepdims=True)
    row_lse = row_top + jnp.log(jnp.sum(jnp.exp(by_row - row_top), axis=1, keepdims=True))
    row_positive = jnp.sum(scores * matches, axis=1, keepdims=True)
    row_part = jnp.sum(
        jnp.where(iota((cap_rows, 1), 0) < n_cap, row_lse - row_positive, 0.0), axis=0, keepdims=True
    )
    by_column = jnp.where(row_ok, scores, FAR)
    top = jnp.max(by_column, axis=0, keepdims=True)
    MSG[...] = jnp.zeros_like(MSG)
    MSG[0:1, :] = top
    MSG[1:2, :] = jnp.sum(jnp.exp(by_column - top), axis=0, keepdims=True)
    MSG[2:3, :] = jnp.sum(scores * matches, axis=0, keepdims=True)
    MSG[3:4, :] = jnp.sum(matches, axis=0, keepdims=True)
    MSG[4:5, :] = jnp.broadcast_to(row_part, (1, t_all))
    STATS[slot] = MSG[...]

    def send_stats(k, carry):
        pltpu.make_async_remote_copy(
            src_ref=MSG,
            dst_ref=STATS.at[slot],
            send_sem=st_s,
            recv_sem=st_r,
            device_id=near_device(k),
            device_id_type=pl.DeviceIdType.MESH,
        ).start()
        return carry

    lax.fori_loop(1, 16, send_stats, 0)
    tick(19)
    gather_end(1, (2, 3))
    lax.fori_loop(0, 1, feed_far, 0)
    tick(20)
    lax.fori_loop(1, 2, feed_far, 0)
    gather_end(2, (2, 3))
    pltpu.make_async_copy(STATS.at[pl.ds(0, 15)], STATS.at[pl.ds(0, 15)], st_r).wait()
    top = jnp.max(STATS[:, 0, :], axis=0, keepdims=True)
    total = jnp.sum(STATS[:, 1, :] * jnp.exp(STATS[:, 0, :] - top), axis=0, keepdims=True)
    positive = jnp.sum(STATS[:, 2, :], axis=0, keepdims=True)
    count = jnp.sum(STATS[:, 3, :], axis=0, keepdims=True)
    row_sum = jnp.sum(STATS[:, 4, :], axis=0, keepdims=True)
    for x in range(extra):
        XST[0, x] = jnp.concatenate(
            [top, total, positive, count, row_sum, jnp.zeros((3, t_all), F32)], axis=0
        )
        remote(
            XST.at[0, x], XST.at[1, x], stx_s.at[x], stx_r.at[x], (flip(d, 3 + x), m)
        ).wait_recv()
        other = XST[1, x]
        joined = jnp.maximum(top, other[0:1])
        total = total * jnp.exp(top - joined) + other[1:2] * jnp.exp(other[0:1] - joined)
        top = joined
        positive = positive + other[2:3]
        count = count + other[3:4]
        row_sum = row_sum + other[4:5]
    ok = col_ok[0:1]
    count = jnp.where(ok, count, 1.0)
    col_lse = top + jnp.log(total)
    column_part = jnp.sum(
        jnp.where(ok, col_lse - positive / count, 0.0), axis=1, keepdims=True
    )
    loss = 0.5 * (row_sum[:, 0:1] * (1.0 / total_captions) + column_part * (1.0 / total_images))
    weight = 0.5 * total_captions / total_images
    grad_scores = 0.5 * (jnp.exp(by_row - row_lse) - matches) + weight * (
        jnp.exp(by_column - col_lse) - matches * (1.0 / count)
    )
    grad_scores = jnp.where(col_ok & row_ok, grad_scores, 0.0)
    grad_log = jnp.sum(
        jnp.sum(grad_scores * scores, axis=1, keepdims=True), axis=0, keepdims=True
    )
    embed = EL[...]
    grad_cosine = (scaling * grad_scores).astype(LOW)
    grad_embed = dot(grad_cosine[:, 0 : group * 8], embeds(0))
    for c in range(1, n_all // group):
        grad_embed += dot(grad_cosine[:, c * group * 8 : (c + 1) * group * 8], embeds(c))
    grad_pooled = (
        grad_embed - embed * jnp.sum(embed * grad_embed, axis=-1, keepdims=True)
    ) * inverse
    SG[0] = jnp.zeros(SG.shape[1:], F32)
    SG[0, 13:14, :] = jnp.sum(grad_pooled, axis=0, keepdims=True)
    SG[0, 18:19, :] = jnp.broadcast_to(grad_log, (1, width))
    GPL[0] = grad_pooled.astype(LOW)
    grad_rows = grad_pooled * (1.0 / LEN)
    EL[...] = grad_rows
    GPL[1] = grad_rows.astype(LOW)

    def part(g, i):
        return IW.at[2 * g + i]

    places = (4, 7, 6)

    def whole(g):
        return IW.at[places[g]]

    def settle(copies):
        for copy in copies:
            copy.wait_send()
        sends[:] = [other for other in sends if all(other is not copy for copy in copies)]

    state = {}
    stores = []
    axis_one = ((yb, y_dev), (xb, x_dev))
    axis_two = ((xb, x_dev), (yb, y_dev))
    own = (p_a, p_b)

    def scatter(g, stage, i, ab):
        bit_one, dev_one = axis_one[ab]
        bit_two, dev_two = axis_two[ab]
        run = 8 * ab + 4 * cb + 2 * bit_one
        if stage == 0:
            p, n, dst, dev = 8 * ab + 4 * (1 - cb), 4, RCORE.at[g % 2, i, ab], core_dev
        elif stage == 1:
            p, n, dst, dev = 8 * ab + 4 * cb + 2 * (1 - bit_one), 2, RB1.at[g % 2, i, ab], dev_one
        elif stage == 2:
            p, n, dst, dev = run + 1 - bit_two, 1, RB2.at[g % 2, i, ab], dev_two
        else:
            p, n, dst, dev = own[ab], 1, RZ.at[g, ab], pair_dev
        k = 2 * i + ab
        state[g, stage, i, ab] = remote(
            part(g, i).at[span(p, n)], dst, rs_s.at[g, stage, k], rs_r.at[g, stage, k], dev
        )

    def add_in(g, stage, i, ab):
        state[g, stage, i, ab].wait_recv()
        run = 8 * ab + 4 * cb
        if stage == 0:
            at, got = span(run, 4), RCORE[g % 2, i, ab]
        elif stage == 1:
            at, got = span(run + 2 * axis_one[ab][0], 2), RB1[g % 2, i, ab]
        else:
            at, got = span(own[ab], 1), RB2[g % 2, i, ab]
        IW[2 * g + i, at, :] = IW[2 * g + i, at, :] + got

    def gather_back(g, stage, ab):
        state[g, "gather", stage, ab] = spread(
            lambda p, n: whole(g).at[span(p, n)], stage, ab, ag_s.at[g], ag_r.at[g]
        )

    def reduce_start(g, ab):
        if g == 0:
            settle([state.pop((2, a, i, ab)) for a in range(4) for i in range(2) if (2, a, i, ab) in state])
        for i in (1, 0):
            scatter(g, 0, i, ab)

    def reduce_step(g, step):
        if step == 0:
            for ab in range(2):
                reduce_start(g, ab)
        elif step < 4:
            for i in (1, 0):
                for ab in range(2):
                    add_in(g, step - 1, i, ab)
                    if step < 3 or i == 1:
                        scatter(g, step, i, ab)
        elif step == 4:
            for ab in range(2):
                state[g, 3, 1, ab].wait_recv()
                at = span(own[ab], 1)
                IW[places[g], at, :] = IW[2 * g, at, :] + RZ[g, ab]
                for x in range(extra):
                    copy = remote(
                        whole(g).at[at],
                        XR.at[g % 2, x, ab],
                        xr_s.at[g, x, ab],
                        xr_r.at[g, x, ab],
                        (flip(d, 3 + x), m),
                    )
                    copy.wait_recv()
                    settle([copy])
                    IW[places[g], at, :] = IW[places[g], at, :] + XR[g % 2, x, ab]
                gather_back(g, 0, ab)
        elif step < 7:
            for ab in range(2):
                state[g, "gather", step - 5, ab].wait_recv()
                gather_back(g, step - 4, ab)
        else:
            for ab in range(2):
                state[g, "gather", 2, ab].wait_recv()
            stores.append(local(whole(g), red.at[g], out_sem.at[g]))

    def back_tick(place):
        for g, step in RPLAN.get(place, ()):
            reduce_step(g, step)

    shards = (m, pair)
    for i in range(2):
        IW[4 + i] = dot_tn(PA[shards[i]], GPL[0]).astype(LOW)

    back_tick(0)

    def grad_activation(s, carry):
        GA[s] = dot_nt(GPL[1], W[2, s])
        return carry

    lax.fori_loop(0, n_mp, grad_activation, 0)
    back_tick(1)
    ones = jnp.ones((16, rows), LOW)

    def grad_hidden(s, carry):
        def scale(t, inner):
            at = pl.ds(pl.multiple_of(t * LEN, LEN), LEN)
            GP[s, at, :] = (GP[s, at, :].astype(F32) * GA[s, pl.ds(t, 1), :]).astype(LOW)
            return inner

        lax.fori_loop(0, n_cap, scale, 0, unroll=7)
        SG[0, pl.ds(8 + s, 1), :] = dot(ones, GP[s])[0:1]
        return carry

    lax.fori_loop(0, 2, grad_hidden, 0)
    back_tick(2)
    lax.fori_loop(2, n_mp, grad_hidden, 0)
    back_tick(3)

    def expand_gradient(i, carry):
        s = m + i * (pair - m)
        IW[2 + i] = dot_tn(N2[...], GP[s]).astype(LOW)
        return carry

    lax.fori_loop(0, 2, expand_gradient, 0)
    back_tick(4)

    def grad_norm_two(n, carry):
        p = pl.ds(pl.multiple_of(n * 384, 128), 384)
        total = dot_nt(
            jnp.concatenate([GP[s] for s in range(n_mp)], axis=1),
            jnp.concatenate([W[1, s, p, :] for s in range(n_mp)], axis=1),
        )
        ACC[:, pl.ds(pl.multiple_of(n * 384, 128), 384)] = total
        return carry

    lax.fori_loop(0, 1, grad_norm_two, 0)
    back_tick(5)
    lax.fori_loop(1, 2, grad_norm_two, 0)
    back_tick(6)

    def norm_back(e, gain, x):
        xhat, scale = standard(x)
        eg = e * gain
        c1 = jnp.sum(eg, axis=-1, keepdims=True) * (1.0 / width)
        c2 = jnp.sum(eg * xhat, axis=-1, keepdims=True) * (1.0 / width)
        return (eg - c1 - xhat * c2) * scale, sum8(e * xhat), sum8(e)

    zero8 = jnp.zeros((8, width), F32)

    def back_two(t, carry):
        dg, db, do = carry
        found = []
        for u in range(7):
            at = pl.ds(pl.multiple_of((7 * t + u) * LEN, LEN), LEN)
            dv, one, two = norm_back(ACC[at, :], g2, RES[at, :])
            g = EL[pl.ds(7 * t + u, 1), :] + dv
            found.append((at, g))
            dg, db, do = dg + one, db + two, do + sum8(g)
        for at, g in found:
            RES[at, :] = g
            GRL[at, :] = g.astype(LOW)
        return dg, db, do

    dg, db, do = lax.fori_loop(0, n_cap // 7, back_two, (zero8, zero8, zero8))
    SG[0, 15:16, :] = jnp.sum(dg, axis=0, keepdims=True)
    SG[0, 17:18, :] = jnp.sum(db, axis=0, keepdims=True)
    SG[0, 12:13, :] = jnp.sum(do, axis=0, keepdims=True)

    back_tick(7)
    for i in range(2):
        IW[i, 3 * shard : 4 * shard, :] = dot_tn(MIX[shards[i]], GRL[...]).astype(LOW)

    def grad_mixture(s, carry):
        MIX[s] = dot_nt(GRL[...], W[0, s, pl.ds(3 * shard, shard), :]).astype(LOW)
        return carry

    lax.fori_loop(0, n_mp, grad_mixture, 0)
    back_tick(8)

    def attention_back(b, carry):
        at = pl.ds(pl.multiple_of(b * BLOCK, 16), BLOCK)
        loaded = [
            [QKV[j, s, at, :] for j in range(3)] + [MIX[s, at, :], PR[s, b]] for s in range(n_mp)
        ]
        heads = HM3[...]
        every = []
        for q, k, v, g, low_probs in loaded:
            q = jnp.concatenate([q] * 3, axis=0) * heads
            g = jnp.concatenate([g] * 3, axis=0) * heads
            probs = low_probs.astype(F32)
            grad_probs = dot_nt(v, g)
            inner = jnp.sum(grad_probs * probs, axis=0, keepdims=True)
            grad_logits = (probs * (grad_probs - inner)).astype(LOW)
            every.append(
                (
                    (join_heads(dot_tn(grad_logits, k)) * 0.125).astype(LOW),
                    (dot(grad_logits, q) * 0.125).astype(LOW),
                    dot(low_probs, g).astype(LOW),
                )
            )
        for s, grads in enumerate(every):
            for j in range(3):
                QKV[j, s, at, :] = grads[j]
        return carry

    def attend_gradient(j):
        def one(i, carry):
            s = m + i * (pair - m)
            IW[i, shard * j : shard * (j + 1), :] = dot_tn(QKV[j, s], N1[...]).astype(LOW)
            return carry

        lax.fori_loop(0, 2, one, 0)

    small_gain, small_shift = zero8, zero8
    gt_copies = []
    cuts = (0, 3, 5, n_blocks)
    for r in range(3):
        lax.fori_loop(cuts[r], cuts[r + 1], attention_back, 0)
        back_tick(9 + r)
        if r == 2:
            attend_gradient(2)
            reduce_start(0, 1)
            attend_gradient(0)
            attend_gradient(1)
            reduce_start(0, 0)
            back_tick(20)
        first, last = cuts[r] * (BLOCK // LEN), cuts[r + 1] * (BLOCK // LEN)
        stripe = pl.ds(first * LEN, (last - first) * LEN)

        def grad_norm_one(n, carry):
            lanes = pl.ds(pl.multiple_of(n * 256, 256), 256)
            total = None
            for s in range(n_mp):
                for j in range(3):
                    term = dot(
                        QKV[j, s, stripe, :],
                        W[0, s, pl.ds(shard * j, shard), lanes],
                    )
                    total = term if total is None else total + term
            ACC[stripe, lanes] = total
            return carry

        lax.fori_loop(0, width // 256, grad_norm_one, 0)
        back_tick(12 + r)
        def back_one(t, carry):
            at = pl.ds(pl.multiple_of(t * LEN, LEN), LEN)
            dv, dg, db = norm_back(ACC[at, :], g1, TOK[t].astype(F32))
            GT[at, :] = (RES[at, :] + dv).astype(LOW)
            return carry[0] + dg, carry[1] + db

        small_gain, small_shift = lax.fori_loop(
            first, last, back_one, (small_gain, small_shift), unroll=7
        )
        back_tick(15 + r)
        gt_copies.append(
            remote(GT.at[stripe], gt.at[half, stripe], gt_s.at[r], gt_r.at[r], pair_dev)
        )
    back_tick(21)
    stores.append(local(GT, gt.at[half], out_sem.at[3]))
    SG[0, 14:15, :] = jnp.sum(small_gain, axis=0, keepdims=True)
    SG[0, 16:17, :] = jnp.sum(small_shift, axis=0, keepdims=True)

    def bias_gradient(s, carry):
        SG[0, pl.ds(s, 1), 0:shard] = dot(ones, QKV[0, s])[0:1]
        SG[0, pl.ds(4 + s, 1), 0:shard] = dot(ones, QKV[2, s])[0:1]
        return carry

    lax.fori_loop(0, n_mp, bias_gradient, 0)
    small_devs = [core_dev, y_dev, x_dev, pair_dev] + [(flip(d, 3 + x), m) for x in range(extra)]
    small = {}

    def small_start(i):
        small[i] = remote(SG.at[i], SGR.at[i], sg_s.at[i], sg_r.at[i], small_devs[i])

    def small_end(i):
        small[i].wait_recv()
        SG[i + 1] = SG[i] + SGR[i]

    back_tick(22)
    small_start(0)
    back_tick(23)
    small_end(0)
    small_start(1)
    back_tick(24)
    small_end(1)
    small_start(2)
    back_tick(25)
    small_end(2)
    small_start(3)
    back_tick(26)
    small_end(3)
    for i in range(4, 4 + extra):
        small_start(i)
        small_end(i)
    back_tick(27)
    last = SG.shape[0] - 1
    sgo[...] = jnp.zeros_like(sgo)
    sgo[0:1, :] = SG[last, pl.ds(m, 1), :]
    sgo[1:2, :] = SG[last, pl.ds(4 + m, 1), :]
    sgo[2:3, :] = SG[last, pl.ds(8 + m, 1), :]
    sgo[3:10, :] = SG[last, 12:19, :]
    sgo[10:11, :] = jnp.broadcast_to(loss, (1, width))
    back_tick(28)
    for copy in gt_copies:
        copy.wait_recv()
    pltpu.make_async_copy(STATS.at[pl.ds(0, 15)], STATS.at[pl.ds(0, 15)], st_s).wait()
    for copy in sends:
        copy.wait_send()
    for copy in stores:
        copy.wait()


def local_step(
    n_dp,
    n_mp,
    caption_tokens,
    image_tokens,
    image_attend,
    image_output,
    image_expand,
    image_reduce,
    image_gains,
    caption_attend,
    attend_bias,
    caption_output,
    output_bias,
    caption_expand,
    expand_bias,
    caption_reduce,
    reduce_bias,
    norm_gains,
    norm_shifts,
    log_scale,
    caption_image,
):
    captions, length, width = caption_tokens.shape
    images, image_len, _ = image_tokens.shape
    shard = caption_attend.shape[2]
    units = caption_expand.shape[1]
    n_cap = captions // 2
    rows = n_cap * length
    n_blocks = rows // BLOCK
    n_all = n_dp * n_mp
    t_all = n_all * 8
    extra = n_dp.bit_length() - 1 - 3
    assert length == LEN and units == width and shard * n_mp == width and width == 16 * PIECE

    any_space = pl.BlockSpec(memory_space=pl.ANY)
    vmem = pl.BlockSpec(memory_space=pltpu.VMEM)
    nx = max(extra, 1)
    dma = pltpu.SemaphoreType.DMA
    scratch = [
        pltpu.VMEM((3, n_mp, width, width), LOW),
        pltpu.VMEM((8, width, width), LOW),
        pltpu.VMEM((n_cap, length, width), LOW),
        pltpu.VMEM((rows, width), LOW),
        pltpu.VMEM((3, n_mp, rows, shard), LOW),
        pltpu.VMEM((n_mp, n_blocks, BLOCK, 3 * BLOCK), LOW),
        pltpu.VMEM((n_mp, rows, shard), LOW),
        pltpu.VMEM((rows, width), F32),
        pltpu.VMEM((rows, width), LOW),
        pltpu.VMEM((n_mp, rows, width), LOW),
        pltpu.VMEM((n_mp, 64, width), LOW),
        pltpu.VMEM((2, 64, width), LOW),
        pltpu.VMEM((rows, width), F32),
        pltpu.VMEM((rows, width), LOW),
        pltpu.VMEM((rows, width), LOW),
        pltpu.VMEM((16, width), F32),
        pltpu.VMEM((n_all, 8, width), LOW),
        pltpu.VMEM((8, t_all), F32),
        pltpu.VMEM((16, 8, t_all), F32),
        pltpu.VMEM((8, width), F32),
        pltpu.VMEM((n_mp, 8, width), F32),
        pltpu.VMEM((3 * BLOCK, shard), LOW),
        pltpu.VMEM((BLOCK, 3 * BLOCK), F32),
        pltpu.VMEM((256, 256), LOW),
        pltpu.VMEM((64, rows), LOW),
        pltpu.VMEM((64, width), F32),
        pltpu.VMEM((2, 64, width), LOW),
        pltpu.VMEM((n_mp, 64, width), F32),
        pltpu.VMEM((2, 2, 2, 4 * PIECE, width), LOW),
        pltpu.VMEM((2, 2, 2, 2 * PIECE, width), LOW),
        pltpu.VMEM((2, 2, 2, PIECE, width), LOW),
        pltpu.VMEM((3, 2, PIECE, width), LOW),
        pltpu.VMEM((2, nx, 2, PIECE, width), LOW),
        pltpu.VMEM((2, nx, 8, t_all), F32),
        pltpu.VMEM((5 + extra, 24, width), F32),
        pltpu.VMEM((4 + extra, 24, width), F32),
        dma((3, 3, 2)),
        dma((3, 3, 2)),
        dma((3, 3, 3, 2)),
        dma((3, 3, 3, 2)),
        dma((3,)),
        dma((3,)),
        dma((12,)),
        dma,
        dma((3,)),
        dma((3,)),
        dma((10 + nx,)),
        dma((10 + nx,)),
        dma,
        dma,
        dma((nx,)),
        dma((nx,)),
        dma((3, 4, 4)),
        dma((3, 4, 4)),
        dma((3, 3, 2)),
        dma((3, 3, 2)),
        dma((3, nx, 2)),
        dma((3, nx, 2)),
        dma((4 + extra,)),
        dma((4 + extra,)),
        dma((3,)),
        dma((3,)),
        dma((4,)),
        dma,
        dma,
    ]
    red, gt, sgo = pl.pallas_call(
        functools.partial(body, n_dp, n_mp),
        out_shape=(
            jax.ShapeDtypeStruct((3, width, width), LOW),
            jax.ShapeDtypeStruct((2, rows, width), LOW),
            jax.ShapeDtypeStruct((16, width), F32),
        ),
        in_specs=[any_space, vmem] + [any_space] * 8 + [vmem] * 9,
        out_specs=(any_space, any_space, vmem),
        scratch_shapes=scratch,
        compiler_params=pltpu.CompilerParams(
            collective_id=0, has_side_effects=True, vmem_limit_bytes=66_000_000
        ),
        name="step",
    )(
        caption_tokens,
        image_tokens,
        image_attend,
        image_output,
        image_expand,
        image_reduce,
        jnp.swapaxes(caption_attend, 1, 2),
        caption_output,
        caption_expand,
        caption_reduce,
        image_gains,
        attend_bias,
        output_bias,
        expand_bias,
        reduce_bias,
        norm_gains,
        norm_shifts,
        log_scale,
        caption_image,
    )
    shapes = (
        (1,),
        (captions, length, width),
        (3, shard, width),
        (2, shard),
        (shard, width),
        (width,),
        (width, units),
        (units,),
        (units, width),
        (width,),
        (2, width),
        (2, width),
        (1,),
    )
    large = (1, 2, 4, 6, 8)
    parts = 7
    grads = pl.pallas_call(
        finish,
        out_shape=tuple(jax.ShapeDtypeStruct(shape, F32) for shape in shapes),
        in_specs=[any_space, any_space, vmem],
        out_specs=tuple(any_space if i in large else vmem for i in range(len(shapes))),
        scratch_shapes=[
            pltpu.VMEM((captions, length, width), LOW),
            pltpu.VMEM((captions, length, width), F32),
            pltpu.VMEM((3, width, width), LOW),
            pltpu.VMEM((3, width, width), F32),
            pltpu.VMEM((3, shard, width), F32),
            dma((parts,)),
            dma((parts,)),
            dma((3,)),
            dma((6,)),
        ],
        compiler_params=pltpu.CompilerParams(vmem_limit_bytes=64_000_000),
        name="finish",
    )(red, gt.reshape(captions, length, width), sgo)
    return (*grads[:2], jnp.swapaxes(grads[2], 1, 2), *grads[3:])


def finish(
    red,
    gt,
    small,
    loss,
    tokens,
    attend,
    attend_bias,
    output,
    output_bias,
    expand,
    expand_bias,
    reduce,
    reduce_bias,
    gains,
    shifts,
    log_scale,
    GT,
    TOKENS,
    RED,
    WIDE,
    ATTEND,
    gt_in,
    gt_out,
    red_in,
    red_out,
):
    def copy(src, dst, sem):
        made = pltpu.make_async_copy(src, dst, sem)
        made.start()
        return made

    parts = gt_in.shape[0]
    size = GT.shape[0] // parts
    width = GT.shape[2]
    shard = ATTEND.shape[1]
    order = (0, 1, 2)
    weights = {g: copy(red.at[g], RED.at[g], red_in.at[g]) for g in order}
    pieces = [
        copy(gt.at[pl.ds(i * size, size)], GT.at[pl.ds(i * size, size)], gt_in.at[i])
        for i in range(parts)
    ]
    written = []
    loss[...] = small[10:11, 0:1].reshape(1)
    attend_bias[...] = small[0:2, 0:shard]
    expand_bias[...] = small[2:3, :].reshape(width)
    output_bias[...] = small[3:4, :].reshape(width)
    reduce_bias[...] = small[4:5, :].reshape(width)
    gains[...] = small[5:7, :]
    shifts[...] = small[7:9, :]
    log_scale[...] = small[9:10, 0:1].reshape(1)
    for g in order:
        weights[g].wait()
        if g == 0:
            for j in range(3):
                ATTEND[j] = RED[0, shard * j : shard * (j + 1), :].astype(F32)
                written.append(copy(ATTEND.at[j], attend.at[j], red_out.at[j]))
            WIDE[0, 3 * shard :, :] = RED[0, 3 * shard :, :].astype(F32)
            written.append(copy(WIDE.at[0, pl.ds(3 * shard, shard)], output, red_out.at[3]))
        else:

            def widen(t, carry):
                at = pl.ds(pl.multiple_of(t * 96, 96), 96)
                WIDE[g, at, :] = RED[g, at, :].astype(F32)
                return carry

            lax.fori_loop(0, width // 96, widen, 0)
            written.append(copy(WIDE.at[g], (expand, reduce)[g - 1], red_out.at[3 + g]))
    for i in range(parts):
        pieces[i].wait()
        at = slice(i * size, i * size + size)
        TOKENS[at] = GT[at].astype(F32)
        written.append(
            copy(
                TOKENS.at[pl.ds(i * size, size)], tokens.at[pl.ds(i * size, size)], gt_out.at[i]
            )
        )
    for made in written:
        made.wait()


def solution(mesh):
    in_specs = (
        P("dp", None, None),
        P(("dp", "mp"), None, None),
        P(),
        P(),
        P(),
        P(),
        P(),
        P(None, None, "mp"),
        P(None, "mp"),
        P("mp", None),
        P(),
        P(None, "mp"),
        P("mp"),
        P("mp", None),
        P(),
        P(),
        P(),
        P(),
        P("dp"),
    )
    out_specs = (
        P(),
        P("dp", None, None),
        P(None, None, "mp"),
        P(None, "mp"),
        P("mp", None),
        P(),
        P(None, "mp"),
        P("mp"),
        P("mp", None),
        P(),
        P(),
        P(),
        P(),
    )
    step = functools.partial(local_step, mesh.shape["dp"], mesh.shape["mp"])
    return jax.shard_map(step, mesh=mesh, in_specs=in_specs, out_specs=out_specs, check_vma=False)
```

```python
import functools

import jax
import jax.numpy as jnp
from jax import lax
from jax.experimental import pallas as pl
from jax.experimental.pallas import tpu as pltpu
from jax.sharding import PartitionSpec as P

HEAD_DIM = 64
LEN = 16
PIECE = 48
BLOCK = 112
F32 = jnp.float32
LOW = jnp.bfloat16
FAR = -1e30
ALL_HOPS = (1, 2, 3)
RPLAN = {
    0: ((2, 0),),
    2: ((2, 1),),
    4: ((1, 0),),
    5: ((2, 2), (1, 1),),
    6: ((2, 3),),
    8: ((2, 4),),
    9: ((1, 2),),
    20: ((1, 3),),
    10: ((0, 1),),
    15: ((1, 4),),
    13: ((2, 5),),
    11: ((0, 2),),
    16: ((0, 3),),
    17: ((2, 6),),
    18: ((1, 5),),
    21: ((0, 4),),
    22: ((1, 6), (2, 7),),
    23: ((0, 5),),
    25: ((1, 7),),
    26: ((0, 6),),
    28: ((0, 7),),
}
PLAN = {
    1: ((0, 0, (1,)),),
    2: ((0, 0, (2, 3)), (1, -1, (1,)), (2, -1, (1,)),),
    3: ((0, 1, (1, 2)), (1, -1, (2, 3)), (2, -1, (2, 3)),),
    4: ((0, 2, (1,)),),
    5: ((0, 1, (3,)),),
    7: ((0, 2, (2,)), (0, 2, (3,)), (1, 0, (1,)), (2, 0, (1,)),),
    10: ((1, 1, (1,)), (2, 1, (1,)),),
    12: ((1, 2, (1,)), (2, 2, (1,)),),
    13: ((1, 0, (2, 3)),),
    14: ((1, 1, (2, 3)),),
    16: ((1, 2, (2, 3)),),
    17: ((2, 0, (2, 3)),),
    20: ((2, 1, (2, 3)),),
    22: ((2, 2, (2, 3)),),
}
GELU_A = 0.7978845608028654
GELU_B = 0.044715


def dot(a, b):
    return lax.dot_general(a, b, (((1,), (0,)), ((), ())), preferred_element_type=F32)


def dot_nt(a, b):
    return lax.dot_general(a, b, (((1,), (1,)), ((), ())), preferred_element_type=F32)


def dot_tn(a, b):
    return lax.dot_general(a, b, (((0,), (0,)), ((), ())), preferred_element_type=F32)


def iota(shape, axis):
    return lax.broadcasted_iota(jnp.int32, shape, axis)


def standard(x):
    width = x.shape[-1]
    centred = x - jnp.sum(x, axis=-1, keepdims=True) * (1.0 / width)
    variance = jnp.sum(centred * centred, axis=-1, keepdims=True) * (1.0 / width)
    scale = lax.rsqrt(variance + 1e-6)
    return centred * scale, scale


def gelu_parts(h):
    square = h * h
    t = jnp.tanh(GELU_A * h * (1.0 + GELU_B * square))
    half = 0.5 * (1.0 + t)
    slope = half + 0.5 * h * (1.0 - t * t) * (GELU_A * (1.0 + 3.0 * GELU_B * square))
    return h * half, slope


def sum8(x):
    return x[0:8] + x[8:16]


def body(
    n_dp,
    n_mp,
    tok_in,
    imt_in,
    ia_in,
    io_in,
    ie_in,
    ir_in,
    ca_in,
    co_in,
    we_in,
    wr_in,
    image_gains,
    attend_bias,
    output_bias,
    expand_bias,
    reduce_bias,
    norm_gains,
    norm_shifts,
    log_scale,
    cap,
    red,
    gt,
    sgo,
    W,
    IW,
    TOK,
    imt,
    N1,
    QKV,
    PR,
    MIX,
    RES,
    N2,
    GP,
    PA,
    PB,
    ACC,
    GRL,
    GT,
    IP,
    EMB,
    MSG,
    STATS,
    SBL,
    SB,
    HM3,
    BM,
    HM4,
    POOL,
    EL,
    GPL,
    GA,
    RCORE,
    RB1,
    RB2,
    RZ,
    XR,
    XST,
    SG,
    SGR,
    gz_s,
    gz_r,
    ga_s,
    ga_r,
    loc_sem,
    ca_sem,
    iw_sem,
    imt_sem,
    tok_sem,
    sb_s,
    sb_r,
    emb_s,
    emb_r,
    st_s,
    st_r,
    stx_s,
    stx_r,
    rs_s,
    rs_r,
    ag_s,
    ag_r,
    xr_s,
    xr_r,
    sg_s,
    sg_r,
    gt_s,
    gt_r,
    out_sem,
    pb_s,
    pb_r,
):
    d = lax.axis_index("dp")
    m = lax.axis_index("mp")
    n_all = n_dp * n_mp
    me = d * n_mp + m
    bits = n_dp.bit_length() - 1
    extra = bits - 3
    images, image_len = imt.shape[0], imt.shape[1]
    rows = TOK.shape[0] * LEN
    n_cap = TOK.shape[0]
    n_blocks = rows // BLOCK
    width = RES.shape[1]
    shard = QKV.shape[3]
    image_rows = images * 64
    t_all = EMB.shape[0] * 8
    total_images = images * n_all
    total_captions = n_cap * 2 * n_dp

    def bit(v, b):
        return lax.rem(v // (1 << b), 2)

    def flip(v, b):
        return v + (1 - 2 * bit(v, b)) * (1 << b)

    cb, xb, yb = bit(d, 0), bit(d, 1), bit(d, 2)
    half = lax.rem(m, 2)
    pair = flip(m, 0)
    p_a = cb * 4 + yb * 2 + xb
    p_b = 8 + cb * 4 + xb * 2 + yb
    core_dev = (flip(d, 0), m)
    x_dev = (flip(d, 1), m)
    y_dev = (flip(d, 2), m)
    pair_dev = (d, pair)
    sends = []

    def remote(src, dst, ss, rs, dev):
        copy = pltpu.make_async_remote_copy(
            src_ref=src,
            dst_ref=dst,
            send_sem=ss,
            recv_sem=rs,
            device_id=dev,
            device_id_type=pl.DeviceIdType.MESH,
        )
        copy.start()
        sends.append(copy)
        return copy

    def local(src, dst, sem):
        copy = pltpu.make_async_copy(src, dst, sem)
        copy.start()
        return copy

    barrier = pltpu.get_barrier_semaphore()

    low = lax.rem(d, 8)
    slot = low * 2 + half

    def near_device(k):
        q = lax.rem(slot + k, 16)
        return (d - low + q // 2, m - half + lax.rem(q, 2))

    def greet(k, carry):
        pl.semaphore_signal(
            barrier, inc=1, device_id=near_device(k), device_id_type=pl.DeviceIdType.MESH
        )
        return carry

    far = flip(m, 1)
    far_pair = flip(pair, 1)
    others = [(d, far), (d, far_pair)] + [(flip(d, 3 + x), m) for x in range(extra)]
    for dev in others:
        pl.semaphore_signal(barrier, inc=1, device_id=dev, device_id_type=pl.DeviceIdType.MESH)
    lax.fori_loop(1, 16, greet, 0)

    image_loads = {}

    def load_image(i):
        if i < 3:
            src, slot = ia_in.at[i], i
        elif i == 3:
            src, slot = io_in, 3
        elif i < 8:
            src, slot = ie_in.at[:, pl.ds((i - 4) * width, width)], i
        else:
            src, slot = ir_in.at[pl.ds((i - 8) * width, width)], i - 8
        image_loads[i] = local(src, IW.at[slot], iw_sem.at[i])

    ca_copies = [
        local(ca_in.at[j], W.at[0, m, pl.ds(shard * j, shard)], ca_sem.at[j]) for j in range(3)
    ]
    own_loads = [local(co_in, W.at[0, m, pl.ds(3 * shard, shard)], loc_sem.at[0])]
    SBL[...] = jnp.zeros_like(SBL)
    SBL[0:1, 0:shard] = attend_bias[0:1, :]
    SBL[2:3, 0:shard] = attend_bias[1:2, :]
    SBL[3:4, :] = expand_bias[...].reshape(1, width)
    SB[m] = SBL[...]
    for copy in ca_copies + own_loads[0:1]:
        copy.wait()
    pl.semaphore_wait(barrier, 15 + len(others))

    hops = (1, 2, 3)

    def partner(k):
        other = flip(m, 0) if k % 2 else m
        return flip(other, 1) if k >= 2 else other

    zc, ac = {}, {}
    sources = (W.at[0, m], we_in, wr_in)

    def span(p, n):
        return pl.ds(pl.multiple_of(p * PIECE, 16), n * PIECE)

    def gather_z(g, ks=(1, 2, 3)):
        for k in ks:
            dev = (d, partner(k))
            for ab, p in ((0, p_a), (1, p_b)):
                zc[g, k, ab] = remote(
                    sources[g].at[span(p, 1)],
                    W.at[g, m, span(p, 1)],
                    gz_s.at[g, k - 1, ab],
                    gz_r.at[g, k - 1, ab],
                    dev,
                )

    def spread(at, stage, ab, ss, rs):
        if stage == 0:
            p, n, dev = ((p_a, 1, x_dev), (p_b, 1, y_dev))[ab]
        elif stage == 1:
            p, n, dev = ((cb * 4 + yb * 2, 2, y_dev), (8 + cb * 4 + xb * 2, 2, x_dev))[ab]
        else:
            p, n, dev = 8 * ab + cb * 4, 4, core_dev
        return remote(at(p, n), at(p, n), ss.at[stage, ab], rs.at[stage, ab], dev)

    def gather_start(g, stage, ks=(1, 2, 3)):
        for k in ks:
            source = partner(k)
            for ab in range(2):
                (zc[g, k, ab] if stage == 0 else ac[g, stage - 1, k, ab]).wait_recv()
                ac[g, stage, k, ab] = spread(
                    lambda p, n: W.at[g, source, span(p, n)],
                    stage,
                    ab,
                    ga_s.at[g, k - 1],
                    ga_r.at[g, k - 1],
                )

    def gather_end(g, ks=(1, 2, 3)):
        for k in ks:
            for ab in range(2):
                ac[g, 2, k, ab].wait_recv()
        if g > 0 and 1 in ks:
            own_loads[g].wait()

    def tick(place):
        for g, stage, ks in PLAN.get(place, ()):
            if stage < 0:
                gather_z(g, ks)
            else:
                gather_start(g, stage, ks)

    gather_z(0)
    sb_copies = []
    for k in hops:
        sb_copies.append(
            remote(
                SBL,
                SB.at[m],
                sb_s.at[k - 1],
                sb_r.at[k - 1],
                (d, partner(k)),
            )
        )
    imt_copy = local(imt_in, imt, imt_sem)
    for i in range(3):
        load_image(i)
    tok_copy = local(tok_in.at[pl.ds(half * n_cap, n_cap)], TOK, tok_sem)
    for i in range(3, 8):
        load_image(i)
    own_loads.append(local(we_in, W.at[1, m], loc_sem.at[1]))
    own_loads.append(local(wr_in, W.at[2, m], loc_sem.at[2]))
    query = iota((BLOCK, 3 * BLOCK), 1)
    query = query - jnp.where(query >= 2 * BLOCK, 2 * BLOCK, jnp.where(query >= BLOCK, BLOCK, 0))
    BM[...] = jnp.where((iota((BLOCK, 3 * BLOCK), 0) >> 4) == (query >> 4), 0.0, FAR)
    lane_shard = iota((BLOCK, shard), 1) >> 6
    for h in range(3):
        at = slice(h * BLOCK, (h + 1) * BLOCK)
        HM3[at, :] = jnp.where(lane_shard == h, 1.0, 0.0).astype(LOW)
    lane_four = iota((64, 256), 1) >> 6
    for h in range(4):
        HM4[64 * h : 64 * h + 64, :] = jnp.where(lane_four == h, 1.0, 0.0).astype(LOW)
    POOL[...] = jnp.where((iota(POOL.shape, 1) >> 4) == iota(POOL.shape, 0), 1.0, 0.0).astype(LOW)
    RES[pl.ds(0, image_rows), :] = jnp.zeros((image_rows, width), F32)
    GP[3, pl.ds(0, image_rows), :] = jnp.zeros((image_rows, width), LOW)
    gain_one = image_gains[0:1, :]
    gain_two = image_gains[1:2, :]

    def image_norm(i, carry):
        x = imt[i].astype(F32)
        at = pl.multiple_of(i * 64, 64)
        RES[pl.ds(at, image_len), :] = x
        GP[3, pl.ds(at, image_len), :] = (standard(x)[0] * gain_one).astype(LOW)
        return carry

    imt_copy.wait()
    lax.fori_loop(0, images, image_norm, 0)
    for i in range(3):
        image_loads[i].wait()

    def image_qkv(j, carry):
        GP[j, pl.ds(0, image_rows), :] = dot(
            GP[3, pl.ds(0, image_rows), :], IW[j]
        ).astype(LOW)
        return carry

    lax.fori_loop(0, 3, image_qkv, 0)
    for i in range(8, 11):
        load_image(i)
    tick(1)

    key_valid = jnp.where(iota((256, 64), 1) < image_len, 0.0, FAR)
    lane_head = iota((64, 256), 1) >> 6

    def image_attention(i, carry):
        at = pl.multiple_of(i * 64, 64)
        for n in range(width // 256):
            lanes = slice(256 * n, 256 * n + 256)
            q = GP[0, pl.ds(at, 64), lanes]
            k = GP[1, pl.ds(at, 64), lanes]
            v = GP[2, pl.ds(at, 64), lanes]
            logits = dot_nt(jnp.concatenate([q] * 4, axis=0) * HM4[...], k) * 0.125 + key_valid
            expos = jnp.exp(logits - jnp.max(logits, axis=-1, keepdims=True))
            probs = (expos * (1.0 / jnp.sum(expos, axis=-1, keepdims=True))).astype(LOW)
            o = dot(probs, v)
            mix = jnp.where(
                lane_head < 2,
                jnp.where(lane_head == 0, o[0:64], o[64:128]),
                jnp.where(lane_head == 2, o[128:192], o[192:256]),
            )
            N2[pl.ds(at, 64), lanes] = mix.astype(LOW)
        return carry

    lax.fori_loop(0, images, image_attention, 0)
    tick(2)
    image_loads[3].wait()

    def image_out(n, carry):
        lanes = pl.ds(pl.multiple_of(n * 256, 256), 256)
        RES[pl.ds(0, image_rows), lanes] += dot(
            N2[pl.ds(0, image_rows), :], IW[3, :, lanes]
        )
        return carry

    lax.fori_loop(0, width // 256, image_out, 0)
    load_image(11)

    def image_norm_two(t, carry):
        at = pl.ds(pl.multiple_of(t * 16, 16), 16)
        GP[3, at, :] = (standard(RES[at, :])[0] * gain_two).astype(LOW)
        return carry

    lax.fori_loop(0, image_rows // 16, image_norm_two, 0, unroll=4)
    IP[...] = jnp.zeros_like(IP)
    for i in range(images):
        IP[i : i + 1, :] = jnp.sum(RES[64 * i : 64 * i + image_len, :], axis=0, keepdims=True) * (
            1.0 / image_len
        )
    image_pool = jnp.where(
        ((iota((16, image_rows), 1) >> 6) == iota((16, image_rows), 0))
        & ((iota((16, image_rows), 1) & 63) < image_len),
        1.0,
        0.0,
    ).astype(LOW)
    for i in range(4, 12):
        image_loads[i].wait()

    def image_feed(u, carry):
        ACC[pl.ds(0, image_rows), :] = dot(
            GP[3, pl.ds(0, image_rows), :], IW[4 + u]
        )

        def activate(t, inner):
            at = pl.ds(pl.multiple_of(t * 16, 16), 16)
            h = ACC[at, :]
            act = 0.5 * h * (1.0 + jnp.tanh(GELU_A * h * (1.0 + GELU_B * h * h)))
            N2[at, :] = act.astype(LOW)
            return inner

        lax.fori_loop(0, image_rows // 16, activate, 0, unroll=4)
        pooled = (dot(image_pool, N2[pl.ds(0, image_rows), :]) * (1.0 / image_len)).astype(LOW)
        IP[...] += dot(pooled, IW[u])
        return carry

    tick(3)
    lax.fori_loop(0, 1, image_feed, 0)
    tick(4)
    lax.fori_loop(1, 2, image_feed, 0)
    tick(5)
    lax.fori_loop(2, 3, image_feed, 0)
    tick(6)
    lax.fori_loop(3, 4, image_feed, 0)
    tick(7)
    pooled_image = IP[0:8]
    EMB[me] = (
        pooled_image
        * lax.rsqrt(jnp.sum(pooled_image * pooled_image, axis=-1, keepdims=True) + 1e-6)
    ).astype(LOW)

    shown = {}

    def show(stage, first, n, dev, at):
        run = EMB.at[pl.ds(first * n_mp, n * n_mp)]
        shown.setdefault(stage, []).append(
            remote(run, run, emb_s.at[at], emb_r.at[at], dev)
        )

    def show_embeds(stage):
        for copy in shown.get(stage - 1, ()):
            copy.wait_recv()
        if stage == 0:
            for k in hops:
                run = EMB.at[me]
                shown.setdefault(0, []).append(
                    remote(run, run, emb_s.at[k - 1], emb_r.at[k - 1], (d, partner(k)))
                )
        elif stage == 1:
            show(1, d, 1, x_dev, 3)
        elif stage == 2:
            for x in range(2):
                show(2, d + 2 * (x - xb), 1, y_dev, 4 + x)
        elif stage == 3:
            for q in range(4):
                show(3, d - low + cb + 2 * q, 1, core_dev, 6 + q)
        else:
            for x in range(extra):
                run = 8 << x
                first = d - lax.rem(d, run)
                show(4 + x, first, run, (flip(d, 3 + x), m), 10 + x)
                for copy in shown[4 + x]:
                    copy.wait_recv()

    show_embeds(0)

    tok_copy.wait()
    g1, g2 = norm_gains[0:1, :], norm_gains[1:2, :]
    b1, b2 = norm_shifts[0:1, :], norm_shifts[1:2, :]

    def norm_one(t, carry):
        at = pl.ds(pl.multiple_of(t * LEN, LEN), LEN)
        N1[at, :] = (standard(TOK[t].astype(F32))[0] * g1 + b1).astype(LOW)
        return carry

    lax.fori_loop(0, n_cap, norm_one, 0, unroll=7)
    tick(8)
    for copy in sb_copies:
        copy.wait_recv()
    gather_end(0, (1,))

    def project(near, distant):
        def one(t, carry):
            s, j = near + (t // 3) * (distant - near), lax.rem(t, 3)
            weight = W[0, s, pl.ds(pl.multiple_of(shard * j, 16), shard), :]
            QKV[j, s] = (dot_nt(N1[...], weight) + SB[s, pl.ds(j, 1), 0:shard]).astype(LOW)
            return carry

        lax.fori_loop(0, 6, one, 0)

    tick(9)
    project(m, pair)
    tick(10)
    gather_end(0, (2, 3))
    project(far, far_pair)
    tick(11)
    lane_three = iota((BLOCK, shard), 1) >> 6

    def join_heads(o):
        return jnp.where(
            lane_three == 0,
            o[0:BLOCK],
            jnp.where(lane_three == 1, o[BLOCK : 2 * BLOCK], o[2 * BLOCK : 3 * BLOCK]),
        )

    def attention(b, carry):
        at = pl.ds(pl.multiple_of(b * BLOCK, 16), BLOCK)
        loaded = [[QKV[j, s, at, :] for j in range(3)] for s in range(n_mp)]
        heads, mask = HM3[...], BM[...]
        every = []
        for q, k, v in loaded:
            logits = dot_nt(k, jnp.concatenate([q] * 3, axis=0) * heads) * 0.125 + mask
            expos = jnp.exp(logits - jnp.max(logits, axis=0, keepdims=True))
            probs = (expos * (1.0 / jnp.sum(expos, axis=0, keepdims=True))).astype(LOW)
            every.append((probs, join_heads(dot_tn(probs, v)).astype(LOW)))
        for s, (probs, mixed) in enumerate(every):
            PR[s, b] = probs
            MIX[s, at, :] = mixed
        return carry

    lax.fori_loop(0, 2, attention, 0)
    tick(12)
    lax.fori_loop(2, 4, attention, 0)
    tick(13)
    lax.fori_loop(4, n_blocks, attention, 0)
    tick(14)

    def attend_out(n, carry):
        lanes = pl.ds(pl.multiple_of(n * 256, 256), 256)
        total = dot(MIX[0], W[0, 0, pl.ds(3 * shard, shard), lanes])
        for s in range(1, n_mp):
            total += dot(MIX[s], W[0, s, pl.ds(3 * shard, shard), lanes])
        ACC[:, lanes] = total
        return carry

    lax.fori_loop(0, width // 256, attend_out, 0)
    out_bias = output_bias[...].reshape(1, width)

    def norm_two(t, carry):
        at = pl.ds(pl.multiple_of(t * LEN, LEN), LEN)
        x = TOK[t].astype(F32) + (ACC[at, :] + out_bias)
        RES[at, :] = x
        N2[at, :] = (standard(x)[0] * g2 + b2).astype(LOW)
        return carry

    lax.fori_loop(0, n_cap, norm_two, 0, unroll=7)
    tick(15)
    show_embeds(1)
    gather_end(1, (1,))

    def feed_one(s):
        ACC[...] = dot(N2[...], W[1, s])
        bias = SB[s, 3:4, :]

        def activate(t, inner):
            at = pl.ds(pl.multiple_of(t * LEN, LEN), LEN)
            act, slope = gelu_parts(ACC[at, :] + bias)
            GT[at, :] = act.astype(LOW)
            GP[s, at, :] = slope.astype(LOW)
            return inner

        lax.fori_loop(0, n_cap, activate, 0, unroll=7)
        PA[s] = (dot(POOL[...], GT[...]) * (1.0 / LEN)).astype(LOW)

    def feed_near(i, carry):
        feed_one(m + i * (pair - m))
        return carry

    def feed_far(i, carry):
        feed_one(far + i * (far_pair - far))
        return carry

    lax.fori_loop(0, 1, feed_near, 0)
    tick(16)
    show_embeds(2)
    lax.fori_loop(1, 2, feed_near, 0)
    tick(17)
    show_embeds(3)
    gather_end(2, (1,))
    PB[0] = (dot(PA[m], W[2, m]) + dot(PA[pair], W[2, pair])).astype(LOW)
    pooled_copy = remote(PB.at[0], PB.at[1], pb_s, pb_r, (d, far))
    tick(18)

    def pool_residual(n, carry):
        lanes = pl.ds(pl.multiple_of(n * 128, 128), 128)
        res = RES[:, lanes]
        res_high = res.astype(LOW)
        res_low = (res - res_high.astype(F32)).astype(LOW)
        EL[:, lanes] = (dot(POOL[...], res_high) + dot(POOL[...], res_low)) * (1.0 / LEN)
        return carry

    lax.fori_loop(0, width // 128, pool_residual, 0)
    pooled = EL[...] + reduce_bias[...].reshape(1, width)
    pooled_copy.wait_recv()
    pooled += PB[0].astype(F32) + PB[1].astype(F32)
    inverse = lax.rsqrt(jnp.sum(pooled * pooled, axis=-1, keepdims=True) + 1e-6)
    embed = pooled * inverse
    EL[...] = embed

    show_embeds(4)
    group = min(n_all, 32)

    def embeds(c):
        part = EMB[c * group : c * group + group].astype(F32)
        return part.reshape(group * 8, width).astype(LOW)

    scaling = jnp.exp(log_scale[...].reshape(1, 1))
    embed_low = embed.astype(LOW)
    scores = scaling * jnp.concatenate(
        [dot_nt(embed_low, embeds(c)) for c in range(n_all // group)], axis=1
    )
    cap_rows = scores.shape[0]
    column = iota((cap_rows, t_all), 1)
    col_ok = (column & 7) < images
    row_ok = iota((cap_rows, t_all), 0) < n_cap
    image_id = (column >> 3) * images + (column & 7)
    cap_wide = jnp.broadcast_to(cap[...].reshape(1, 2 * n_cap).astype(F32), (cap_rows, 2 * n_cap))
    mine = iota((cap_rows, 2 * n_cap), 1) == iota((cap_rows, 2 * n_cap), 0) + half * n_cap
    cap_column = jnp.sum(jnp.where(mine, cap_wide, 0.0), axis=1, keepdims=True)
    matches = jnp.where((cap_column == image_id.astype(F32)) & col_ok & row_ok, 1.0, 0.0)
    by_row = jnp.where(col_ok, scores, FAR)
    row_top = jnp.max(by_row, axis=1, keepdims=True)
    row_lse = row_top + jnp.log(jnp.sum(jnp.exp(by_row - row_top), axis=1, keepdims=True))
    row_positive = jnp.sum(scores * matches, axis=1, keepdims=True)
    row_part = jnp.sum(
        jnp.where(iota((cap_rows, 1), 0) < n_cap, row_lse - row_positive, 0.0), axis=0, keepdims=True
    )
    by_column = jnp.where(row_ok, scores, FAR)
    top = jnp.max(by_column, axis=0, keepdims=True)
    MSG[...] = jnp.zeros_like(MSG)
    MSG[0:1, :] = top
    MSG[1:2, :] = jnp.sum(jnp.exp(by_column - top), axis=0, keepdims=True)
    MSG[2:3, :] = jnp.sum(scores * matches, axis=0, keepdims=True)
    MSG[3:4, :] = jnp.sum(matches, axis=0, keepdims=True)
    MSG[4:5, :] = jnp.broadcast_to(row_part, (1, t_all))
    STATS[slot] = MSG[...]

    def send_stats(k, carry):
        pltpu.make_async_remote_copy(
            src_ref=MSG,
            dst_ref=STATS.at[slot],
            send_sem=st_s,
            recv_sem=st_r,
            device_id=near_device(k),
            device_id_type=pl.DeviceIdType.MESH,
        ).start()
        return carry

    lax.fori_loop(1, 16, send_stats, 0)
    tick(19)
    gather_end(1, (2, 3))
    lax.fori_loop(0, 1, feed_far, 0)
    tick(20)
    lax.fori_loop(1, 2, feed_far, 0)
    pltpu.make_async_copy(STATS.at[pl.ds(0, 15)], STATS.at[pl.ds(0, 15)], st_r).wait()
    top = jnp.max(STATS[:, 0, :], axis=0, keepdims=True)
    total = jnp.sum(STATS[:, 1, :] * jnp.exp(STATS[:, 0, :] - top), axis=0, keepdims=True)
    positive = jnp.sum(STATS[:, 2, :], axis=0, keepdims=True)
    count = jnp.sum(STATS[:, 3, :], axis=0, keepdims=True)
    row_sum = jnp.sum(STATS[:, 4, :], axis=0, keepdims=True)
    for x in range(extra):
        XST[0, x] = jnp.concatenate(
            [top, total, positive, count, row_sum, jnp.zeros((3, t_all), F32)], axis=0
        )
        remote(
            XST.at[0, x], XST.at[1, x], stx_s.at[x], stx_r.at[x], (flip(d, 3 + x), m)
        ).wait_recv()
        other = XST[1, x]
        joined = jnp.maximum(top, other[0:1])
        total = total * jnp.exp(top - joined) + other[1:2] * jnp.exp(other[0:1] - joined)
        top = joined
        positive = positive + other[2:3]
        count = count + other[3:4]
        row_sum = row_sum + other[4:5]
    ok = col_ok[0:1]
    count = jnp.where(ok, count, 1.0)
    col_lse = top + jnp.log(total)
    column_part = jnp.sum(
        jnp.where(ok, col_lse - positive / count, 0.0), axis=1, keepdims=True
    )
    loss = 0.5 * (row_sum[:, 0:1] * (1.0 / total_captions) + column_part * (1.0 / total_images))
    weight = 0.5 * total_captions / total_images
    grad_scores = 0.5 * (jnp.exp(by_row - row_lse) - matches) + weight * (
        jnp.exp(by_column - col_lse) - matches * (1.0 / count)
    )
    grad_scores = jnp.where(col_ok & row_ok, grad_scores, 0.0)
    grad_log = jnp.sum(
        jnp.sum(grad_scores * scores, axis=1, keepdims=True), axis=0, keepdims=True
    )
    embed = EL[...]
    grad_cosine = (scaling * grad_scores).astype(LOW)
    grad_embed = dot(grad_cosine[:, 0 : group * 8], embeds(0))
    for c in range(1, n_all // group):
        grad_embed += dot(grad_cosine[:, c * group * 8 : (c + 1) * group * 8], embeds(c))
    grad_pooled = (
        grad_embed - embed * jnp.sum(embed * grad_embed, axis=-1, keepdims=True)
    ) * inverse
    SG[0] = jnp.zeros(SG.shape[1:], F32)
    SG[0, 13:14, :] = jnp.sum(grad_pooled, axis=0, keepdims=True)
    SG[0, 18:19, :] = jnp.broadcast_to(grad_log, (1, width))
    GPL[0] = grad_pooled.astype(LOW)
    grad_rows = grad_pooled * (1.0 / LEN)
    EL[...] = grad_rows
    GPL[1] = grad_rows.astype(LOW)

    def part(g, i):
        return IW.at[2 * g + i]

    places = (4, 7, 6)

    def whole(g):
        return IW.at[places[g]]

    def settle(copies):
        for copy in copies:
            copy.wait_send()
        sends[:] = [other for other in sends if all(other is not copy for copy in copies)]

    state = {}
    stores = []
    axis_one = ((yb, y_dev), (xb, x_dev))
    axis_two = ((xb, x_dev), (yb, y_dev))
    own = (p_a, p_b)

    def scatter(g, stage, i, ab):
        bit_one, dev_one = axis_one[ab]
        bit_two, dev_two = axis_two[ab]
        run = 8 * ab + 4 * cb + 2 * bit_one
        if stage == 0:
            p, n, dst, dev = 8 * ab + 4 * (1 - cb), 4, RCORE.at[g % 2, i, ab], core_dev
        elif stage == 1:
            p, n, dst, dev = 8 * ab + 4 * cb + 2 * (1 - bit_one), 2, RB1.at[g % 2, i, ab], dev_one
        elif stage == 2:
            p, n, dst, dev = run + 1 - bit_two, 1, RB2.at[g % 2, i, ab], dev_two
        else:
            p, n, dst, dev = own[ab], 1, RZ.at[g, ab], pair_dev
        k = 2 * i + ab
        state[g, stage, i, ab] = remote(
            part(g, i).at[span(p, n)], dst, rs_s.at[g, stage, k], rs_r.at[g, stage, k], dev
        )

    def add_in(g, stage, i, ab):
        state[g, stage, i, ab].wait_recv()
        run = 8 * ab + 4 * cb
        if stage == 0:
            at, got = span(run, 4), RCORE[g % 2, i, ab]
        elif stage == 1:
            at, got = span(run + 2 * axis_one[ab][0], 2), RB1[g % 2, i, ab]
        else:
            at, got = span(own[ab], 1), RB2[g % 2, i, ab]
        IW[2 * g + i, at, :] = IW[2 * g + i, at, :] + got

    def pass_on(g, ab, k, across_one, across_two, dev):
        bit_one = axis_one[ab][0] + across_one * (1 - 2 * axis_one[ab][0])
        bit_two = axis_two[ab][0] + across_two * (1 - 2 * axis_two[ab][0])
        run = whole(g).at[span(8 * ab + 4 * cb + 2 * bit_one + bit_two, 1)]
        state[g, "back", k, ab] = remote(run, run, ag_s.at[g, k, ab], ag_r.at[g, k, ab], dev)

    def gather_back(g, stage, ab):
        dev_one, dev_two = axis_one[ab][1], axis_two[ab][1]
        if stage == 0:
            pass_on(g, ab, 0, 0, 0, dev_two)
            pass_on(g, ab, 1, 0, 0, dev_one)
            pass_on(g, ab, 2, 0, 0, core_dev)
        elif stage == 1:
            state[g, "back", 0, ab].wait_recv()
            pass_on(g, ab, 3, 0, 1, dev_one)
            pass_on(g, ab, 4, 0, 1, core_dev)
        elif stage == 2:
            state[g, "back", 1, ab].wait_recv()
            pass_on(g, ab, 5, 1, 0, core_dev)
            state[g, "back", 3, ab].wait_recv()
            pass_on(g, ab, 6, 1, 1, core_dev)
        else:
            for k in (2, 4, 5, 6):
                state[g, "back", k, ab].wait_recv()

    def reduce_start(g, ab):
        if g == 0:
            settle([state.pop((2, a, i, ab)) for a in range(4) for i in range(2) if (2, a, i, ab) in state])
        for i in (1, 0):
            scatter(g, 0, i, ab)

    def reduce_step(g, step, half_of=None):
        if step == 0:
            for ab in range(2):
                reduce_start(g, ab)
        elif step < 4:
            halves = (half_of,) if half_of is not None else (0, 1)
            for i in (1, 0):
                for ab in halves:
                    add_in(g, step - 1, i, ab)
                    if step < 3 or i == 1:
                        scatter(g, step, i, ab)
        elif step == 4:
            for ab in range(2):
                state[g, 3, 1, ab].wait_recv()
                at = span(own[ab], 1)
                IW[places[g], at, :] = IW[2 * g, at, :] + RZ[g, ab]
                for x in range(extra):
                    copy = remote(
                        whole(g).at[at],
                        XR.at[g % 2, x, ab],
                        xr_s.at[g, x, ab],
                        xr_r.at[g, x, ab],
                        (flip(d, 3 + x), m),
                    )
                    copy.wait_recv()
                    settle([copy])
                    IW[places[g], at, :] = IW[places[g], at, :] + XR[g % 2, x, ab]
                gather_back(g, 0, ab)
        elif step < 7:
            for ab in range(2):
                gather_back(g, step - 4, ab)
        else:
            for ab in range(2):
                gather_back(g, 3, ab)
            stores.append(local(whole(g), red.at[g], out_sem.at[g]))

    def back_tick(place):
        for entry in RPLAN.get(place, ()):
            reduce_step(*entry)

    shards = (m, pair)
    for i in range(2):
        IW[4 + i] = dot_tn(PA[shards[i]], GPL[0]).astype(LOW)

    back_tick(0)

    def grad_activation(near, distant):
        for s in (near, distant):
            GA[s] = dot_nt(GPL[1], W[2, s])

    ones = jnp.ones((16, rows), LOW)

    def grad_hidden(near, distant):
        def one(k, carry):
            s = near + k * (distant - near)

            def scale(t, inner):
                at = pl.ds(pl.multiple_of(t * LEN, LEN), LEN)
                GP[s, at, :] = (GP[s, at, :].astype(F32) * GA[s, pl.ds(t, 1), :]).astype(LOW)
                return inner

            lax.fori_loop(0, n_cap, scale, 0, unroll=7)
            SG[0, pl.ds(8 + s, 1), :] = dot(ones, GP[s])[0:1]
            return carry

        lax.fori_loop(0, 2, one, 0)

    grad_activation(m, pair)
    back_tick(1)
    tick(21)
    grad_hidden(m, pair)
    back_tick(2)
    tick(22)

    def expand_gradient(i, carry):
        s = m + i * (pair - m)
        IW[2 + i] = dot_tn(N2[...], GP[s]).astype(LOW)
        return carry

    lax.fori_loop(0, 2, expand_gradient, 0)
    back_tick(4)
    tick(23)
    gather_end(2, (2, 3))
    grad_activation(far, far_pair)
    back_tick(3)
    grad_hidden(far, far_pair)
    back_tick(5)

    def grad_norm_two(n, carry):
        p = pl.ds(pl.multiple_of(n * 384, 128), 384)
        total = dot_nt(
            jnp.concatenate([GP[s] for s in range(n_mp)], axis=1),
            jnp.concatenate([W[1, s, p, :] for s in range(n_mp)], axis=1),
        )
        ACC[:, pl.ds(pl.multiple_of(n * 384, 128), 384)] = total
        return carry

    lax.fori_loop(0, 2, grad_norm_two, 0)
    back_tick(6)

    def norm_back(e, gain, x):
        xhat, scale = standard(x)
        eg = e * gain
        c1 = jnp.sum(eg, axis=-1, keepdims=True) * (1.0 / width)
        c2 = jnp.sum(eg * xhat, axis=-1, keepdims=True) * (1.0 / width)
        return (eg - c1 - xhat * c2) * scale, sum8(e * xhat), sum8(e)

    zero8 = jnp.zeros((8, width), F32)

    def back_two(t, carry):
        dg, db, do = carry
        found = []
        for u in range(7):
            at = pl.ds(pl.multiple_of((7 * t + u) * LEN, LEN), LEN)
            dv, one, two = norm_back(ACC[at, :], g2, RES[at, :])
            g = EL[pl.ds(7 * t + u, 1), :] + dv
            found.append((at, g))
            dg, db, do = dg + one, db + two, do + sum8(g)
        for at, g in found:
            RES[at, :] = g
            GRL[at, :] = g.astype(LOW)
        return dg, db, do

    dg, db, do = lax.fori_loop(0, n_cap // 7, back_two, (zero8, zero8, zero8))
    SG[0, 15:16, :] = jnp.sum(dg, axis=0, keepdims=True)
    SG[0, 17:18, :] = jnp.sum(db, axis=0, keepdims=True)
    SG[0, 12:13, :] = jnp.sum(do, axis=0, keepdims=True)

    back_tick(7)
    for i in range(2):
        IW[i, 3 * shard : 4 * shard, :] = dot_tn(MIX[shards[i]], GRL[...]).astype(LOW)

    def grad_mixture(s, carry):
        MIX[s] = dot_nt(GRL[...], W[0, s, pl.ds(3 * shard, shard), :]).astype(LOW)
        return carry

    lax.fori_loop(0, n_mp, grad_mixture, 0)
    back_tick(8)

    def attention_back(places):
        loaded = []
        for b, s in places:
            at = pl.ds(pl.multiple_of(b * BLOCK, 16), BLOCK)
            loaded.append([QKV[j, s, at, :] for j in range(3)] + [MIX[s, at, :], PR[s, b]])
        heads = HM3[...]
        every = []
        for q, k, v, g, low_probs in loaded:
            q = jnp.concatenate([q] * 3, axis=0) * heads
            g = jnp.concatenate([g] * 3, axis=0) * heads
            probs = low_probs.astype(F32)
            grad_probs = dot_nt(v, g)
            inner = jnp.sum(grad_probs * probs, axis=0, keepdims=True)
            grad_logits = (probs * (grad_probs - inner)).astype(LOW)
            every.append(
                (
                    (join_heads(dot_tn(grad_logits, k)) * 0.125).astype(LOW),
                    (dot(grad_logits, q) * 0.125).astype(LOW),
                    dot(low_probs, g).astype(LOW),
                )
            )
        for (b, s), grads in zip(places, every):
            at = pl.ds(pl.multiple_of(b * BLOCK, 16), BLOCK)
            for j in range(3):
                QKV[j, s, at, :] = grads[j]

    def attention_back_run(first, count, shards):
        def two(t, carry):
            b = first + 2 * t
            attention_back([(b + x, s) for x in range(2) for s in shards])
            return carry

        lax.fori_loop(0, count // 2, two, 0)
        if count % 2:
            attention_back([(first + count - 1, s) for s in shards])

    def attend_gradient(j):
        def one(i, carry):
            s = m + i * (pair - m)
            IW[i, shard * j : shard * (j + 1), :] = dot_tn(QKV[j, s], N1[...]).astype(LOW)
            return carry

        lax.fori_loop(0, 2, one, 0)

    small_devs = [core_dev, y_dev, x_dev, pair_dev] + [(flip(d, 3 + x), m) for x in range(extra)]
    small = {}

    def small_start(i):
        small[i] = remote(SG.at[i], SGR.at[i], sg_s.at[i], sg_r.at[i], small_devs[i])

    def small_end(i):
        small[i].wait_recv()
        SG[i + 1] = SG[i] + SGR[i]

    small_gain, small_shift = zero8, zero8
    gt_copies = []
    cuts = (0, 4, n_blocks)
    attention_back_run(0, n_blocks, (m, pair))
    back_tick(9)
    attend_gradient(2)
    reduce_start(0, 1)
    attend_gradient(0)
    attend_gradient(1)
    reduce_start(0, 0)
    back_tick(20)
    for r in range(2):
        attention_back_run(cuts[r], cuts[r + 1] - cuts[r], (far, far_pair))
        back_tick(10 + r)
        first, last = cuts[r] * (BLOCK // LEN), cuts[r + 1] * (BLOCK // LEN)
        stripe = pl.ds(first * LEN, (last - first) * LEN)

        def grad_norm_one(n, carry):
            lanes = pl.ds(pl.multiple_of(n * 256, 256), 256)
            total = None
            for s in range(n_mp):
                for j in range(3):
                    term = dot(
                        QKV[j, s, stripe, :],
                        W[0, s, pl.ds(shard * j, shard), lanes],
                    )
                    total = term if total is None else total + term
            ACC[stripe, lanes] = total
            return carry

        lax.fori_loop(0, width // 256, grad_norm_one, 0)
        back_tick(12 + r)
        def back_one(t, carry):
            at = pl.ds(pl.multiple_of(t * LEN, LEN), LEN)
            dv, dg, db = norm_back(ACC[at, :], g1, TOK[t].astype(F32))
            GT[at, :] = (RES[at, :] + dv).astype(LOW)
            return carry[0] + dg, carry[1] + db

        small_gain, small_shift = lax.fori_loop(
            first, last, back_one, (small_gain, small_shift), unroll=7
        )
        if r == 1:
            SG[0, 14:15, :] = jnp.sum(small_gain, axis=0, keepdims=True)
            SG[0, 16:17, :] = jnp.sum(small_shift, axis=0, keepdims=True)

            def bias_gradient(s, carry):
                SG[0, pl.ds(s, 1), 0:shard] = dot(ones, QKV[0, s])[0:1]
                SG[0, pl.ds(4 + s, 1), 0:shard] = dot(ones, QKV[2, s])[0:1]
                return carry

            lax.fori_loop(0, n_mp, bias_gradient, 0)
            small_start(0)
            back_tick(16)
            small_end(0)
            small_start(1)
            back_tick(17)
            small_end(1)
            small_start(2)
            back_tick(18)
            small_end(2)
            small_start(3)
        else:
            back_tick(15)
        gt_copies.append(
            remote(GT.at[stripe], gt.at[half, stripe], gt_s.at[r], gt_r.at[r], pair_dev)
        )
    stores.append(local(GT, gt.at[half], out_sem.at[3]))
    back_tick(21)
    small_end(3)
    for i in range(4, 4 + extra):
        small_start(i)
        small_end(i)
    for place in range(22, 28):
        back_tick(place)
    last = SG.shape[0] - 1
    sgo[...] = jnp.zeros_like(sgo)
    sgo[0:1, :] = SG[last, pl.ds(m, 1), :]
    sgo[1:2, :] = SG[last, pl.ds(4 + m, 1), :]
    sgo[2:3, :] = SG[last, pl.ds(8 + m, 1), :]
    sgo[3:10, :] = SG[last, 12:19, :]
    sgo[10:11, :] = jnp.broadcast_to(loss, (1, width))
    back_tick(28)
    for copy in gt_copies:
        copy.wait_recv()
    pltpu.make_async_copy(STATS.at[pl.ds(0, 15)], STATS.at[pl.ds(0, 15)], st_s).wait()
    for copy in sends:
        copy.wait_send()
    for copy in stores:
        copy.wait()


def local_step(
    n_dp,
    n_mp,
    caption_tokens,
    image_tokens,
    image_attend,
    image_output,
    image_expand,
    image_reduce,
    image_gains,
    caption_attend,
    attend_bias,
    caption_output,
    output_bias,
    caption_expand,
    expand_bias,
    caption_reduce,
    reduce_bias,
    norm_gains,
    norm_shifts,
    log_scale,
    caption_image,
):
    captions, length, width = caption_tokens.shape
    images, image_len, _ = image_tokens.shape
    shard = caption_attend.shape[2]
    units = caption_expand.shape[1]
    n_cap = captions // 2
    rows = n_cap * length
    n_blocks = rows // BLOCK
    n_all = n_dp * n_mp
    t_all = n_all * 8
    extra = n_dp.bit_length() - 1 - 3
    assert length == LEN and units == width and shard * n_mp == width and width == 16 * PIECE

    any_space = pl.BlockSpec(memory_space=pl.ANY)
    vmem = pl.BlockSpec(memory_space=pltpu.VMEM)
    nx = max(extra, 1)
    dma = pltpu.SemaphoreType.DMA
    scratch = [
        pltpu.VMEM((3, n_mp, width, width), LOW),
        pltpu.VMEM((8, width, width), LOW),
        pltpu.VMEM((n_cap, length, width), LOW),
        pltpu.VMEM((images, image_len, width), LOW),
        pltpu.VMEM((rows, width), LOW),
        pltpu.VMEM((3, n_mp, rows, shard), LOW),
        pltpu.VMEM((n_mp, n_blocks, BLOCK, 3 * BLOCK), LOW),
        pltpu.VMEM((n_mp, rows, shard), LOW),
        pltpu.VMEM((rows, width), F32),
        pltpu.VMEM((rows, width), LOW),
        pltpu.VMEM((n_mp, rows, width), LOW),
        pltpu.VMEM((n_mp, 64, width), LOW),
        pltpu.VMEM((2, 64, width), LOW),
        pltpu.VMEM((rows, width), F32),
        pltpu.VMEM((rows, width), LOW),
        pltpu.VMEM((rows, width), LOW),
        pltpu.VMEM((16, width), F32),
        pltpu.VMEM((n_all, 8, width), LOW),
        pltpu.VMEM((8, t_all), F32),
        pltpu.VMEM((16, 8, t_all), F32),
        pltpu.VMEM((8, width), F32),
        pltpu.VMEM((n_mp, 8, width), F32),
        pltpu.VMEM((3 * BLOCK, shard), LOW),
        pltpu.VMEM((BLOCK, 3 * BLOCK), F32),
        pltpu.VMEM((256, 256), LOW),
        pltpu.VMEM((64, rows), LOW),
        pltpu.VMEM((64, width), F32),
        pltpu.VMEM((2, 64, width), LOW),
        pltpu.VMEM((n_mp, 64, width), F32),
        pltpu.VMEM((2, 2, 2, 4 * PIECE, width), LOW),
        pltpu.VMEM((2, 2, 2, 2 * PIECE, width), LOW),
        pltpu.VMEM((2, 2, 2, PIECE, width), LOW),
        pltpu.VMEM((3, 2, PIECE, width), LOW),
        pltpu.VMEM((2, nx, 2, PIECE, width), LOW),
        pltpu.VMEM((2, nx, 8, t_all), F32),
        pltpu.VMEM((5 + extra, 24, width), F32),
        pltpu.VMEM((4 + extra, 24, width), F32),
        dma((3, 3, 2)),
        dma((3, 3, 2)),
        dma((3, 3, 3, 2)),
        dma((3, 3, 3, 2)),
        dma((3,)),
        dma((3,)),
        dma((12,)),
        dma,
        dma,
        dma((3,)),
        dma((3,)),
        dma((10 + nx,)),
        dma((10 + nx,)),
        dma,
        dma,
        dma((nx,)),
        dma((nx,)),
        dma((3, 4, 4)),
        dma((3, 4, 4)),
        dma((3, 7, 2)),
        dma((3, 7, 2)),
        dma((3, nx, 2)),
        dma((3, nx, 2)),
        dma((4 + extra,)),
        dma((4 + extra,)),
        dma((3,)),
        dma((3,)),
        dma((4,)),
        dma,
        dma,
    ]
    red, gt, sgo = pl.pallas_call(
        functools.partial(body, n_dp, n_mp),
        out_shape=(
            jax.ShapeDtypeStruct((3, width, width), LOW),
            jax.ShapeDtypeStruct((2, rows, width), LOW),
            jax.ShapeDtypeStruct((16, width), F32),
        ),
        in_specs=[any_space] * 10 + [vmem] * 9,
        out_specs=(any_space, any_space, vmem),
        scratch_shapes=scratch,
        compiler_params=pltpu.CompilerParams(
            collective_id=0, has_side_effects=True, vmem_limit_bytes=66_000_000
        ),
        name="step",
    )(
        caption_tokens,
        image_tokens,
        image_attend,
        image_output,
        image_expand,
        image_reduce,
        jnp.swapaxes(caption_attend, 1, 2),
        caption_output,
        caption_expand,
        caption_reduce,
        image_gains,
        attend_bias,
        output_bias,
        expand_bias,
        reduce_bias,
        norm_gains,
        norm_shifts,
        log_scale,
        caption_image,
    )
    shapes = (
        (1,),
        (captions, length, width),
        (3, shard, width),
        (2, shard),
        (shard, width),
        (width,),
        (width, units),
        (units,),
        (units, width),
        (width,),
        (2, width),
        (2, width),
        (1,),
    )
    large = (1, 2, 4, 6, 8)
    parts = 7
    grads = pl.pallas_call(
        finish,
        out_shape=tuple(jax.ShapeDtypeStruct(shape, F32) for shape in shapes),
        in_specs=[any_space, any_space, vmem],
        out_specs=tuple(any_space if i in large else vmem for i in range(len(shapes))),
        scratch_shapes=[
            pltpu.VMEM((captions, length, width), LOW),
            pltpu.VMEM((captions, length, width), F32),
            pltpu.VMEM((3, width, width), LOW),
            pltpu.VMEM((3, width, width), F32),
            pltpu.VMEM((3, shard, width), F32),
            dma((parts,)),
            dma((parts,)),
            dma((3,)),
            dma((6,)),
        ],
        compiler_params=pltpu.CompilerParams(vmem_limit_bytes=64_000_000),
        name="finish",
    )(red, gt.reshape(captions, length, width), sgo)
    return (*grads[:2], jnp.swapaxes(grads[2], 1, 2), *grads[3:])


def finish(
    red,
    gt,
    small,
    loss,
    tokens,
    attend,
    attend_bias,
    output,
    output_bias,
    expand,
    expand_bias,
    reduce,
    reduce_bias,
    gains,
    shifts,
    log_scale,
    GT,
    TOKENS,
    RED,
    WIDE,
    ATTEND,
    gt_in,
    gt_out,
    red_in,
    red_out,
):
    def copy(src, dst, sem):
        made = pltpu.make_async_copy(src, dst, sem)
        made.start()
        return made

    parts = gt_in.shape[0]
    size = GT.shape[0] // parts
    width = GT.shape[2]
    shard = ATTEND.shape[1]
    order = (0, 1, 2)
    weights = {g: copy(red.at[g], RED.at[g], red_in.at[g]) for g in order}
    pieces = [
        copy(gt.at[pl.ds(i * size, size)], GT.at[pl.ds(i * size, size)], gt_in.at[i])
        for i in range(parts)
    ]
    written = []
    loss[...] = small[10:11, 0:1].reshape(1)
    attend_bias[...] = small[0:2, 0:shard]
    expand_bias[...] = small[2:3, :].reshape(width)
    output_bias[...] = small[3:4, :].reshape(width)
    reduce_bias[...] = small[4:5, :].reshape(width)
    gains[...] = small[5:7, :]
    shifts[...] = small[7:9, :]
    log_scale[...] = small[9:10, 0:1].reshape(1)
    for g in order:
        weights[g].wait()
        if g == 0:
            for j in range(3):
                ATTEND[j] = RED[0, shard * j : shard * (j + 1), :].astype(F32)
                written.append(copy(ATTEND.at[j], attend.at[j], red_out.at[j]))
            WIDE[0, 3 * shard :, :] = RED[0, 3 * shard :, :].astype(F32)
            written.append(copy(WIDE.at[0, pl.ds(3 * shard, shard)], output, red_out.at[3]))
        else:

            def widen(t, carry):
                at = pl.ds(pl.multiple_of(t * 96, 96), 96)
                WIDE[g, at, :] = RED[g, at, :].astype(F32)
                return carry

            lax.fori_loop(0, width // 96, widen, 0)
            written.append(copy(WIDE.at[g], (expand, reduce)[g - 1], red_out.at[3 + g]))
    for i in range(parts):
        pieces[i].wait()
        at = slice(i * size, i * size + size)
        TOKENS[at] = GT[at].astype(F32)
        written.append(
            copy(
                TOKENS.at[pl.ds(i * size, size)], tokens.at[pl.ds(i * size, size)], gt_out.at[i]
            )
        )
    for made in written:
        made.wait()


def solution(mesh):
    in_specs = (
        P("dp", None, None),
        P(("dp", "mp"), None, None),
        P(),
        P(),
        P(),
        P(),
        P(),
        P(None, None, "mp"),
        P(None, "mp"),
        P("mp", None),
        P(),
        P(None, "mp"),
        P("mp"),
        P("mp", None),
        P(),
        P(),
        P(),
        P(),
        P("dp"),
    )
    out_specs = (
        P(),
        P("dp", None, None),
        P(None, None, "mp"),
        P(None, "mp"),
        P("mp", None),
        P(),
        P(None, "mp"),
        P("mp"),
        P("mp", None),
        P(),
        P(),
        P(),
        P(),
    )
    step = functools.partial(local_step, mesh.shape["dp"], mesh.shape["mp"])
    return jax.shard_map(step, mesh=mesh, in_specs=in_specs, out_specs=out_specs, check_vma=False)
```

```python
import functools

import jax
import jax.numpy as jnp
from jax import lax
from jax.experimental import pallas as pl
from jax.experimental.pallas import tpu as pltpu
from jax.sharding import PartitionSpec as P

HEAD_DIM = 64
LEN = 16
PIECE = 48
BLOCK = 112
F32 = jnp.float32
LOW = jnp.bfloat16
FAR = -1e30
ALL_HOPS = (1, 2, 3)
TILES = 7
RPLAN = {
    0: ((2, 0),),
    2: ((2, 1),),
    4: ((1, 0),),
    5: ((2, 2), (1, 1),),
    6: ((2, 3),),
    8: ((2, 4),),
    9: ((1, 2),),
    20: ((1, 3),),
    10: ((0, 1),),
    15: ((1, 4),),
    13: ((2, 5),),
    11: ((0, 2),),
    16: ((0, 3),),
    17: ((2, 6),),
    18: ((1, 5),),
    21: ((0, 4),),
    22: ((1, 6), (2, 7),),
    23: ((0, 5),),
    25: ((1, 7),),
    26: ((0, 6),),
    28: ((0, 7),),
}
PLAN = {
    1: ((0, 0, (1,)),),
    2: ((0, 0, (2, 3)), (1, -1, (1,)), (2, -1, (1,)),),
    3: ((0, 1, (1, 2)), (1, -1, (2, 3)), (2, -1, (2, 3)),),
    4: ((0, 2, (1,)),),
    5: ((0, 1, (3,)),),
    7: ((0, 2, (2,)), (0, 2, (3,)), (1, 0, (1,)), (2, 0, (1,)),),
    10: ((1, 1, (1,)), (2, 1, (1,)),),
    12: ((1, 2, (1,)), (2, 2, (1,)),),
    13: ((1, 0, (2, 3)),),
    14: ((1, 1, (2, 3)),),
    16: ((1, 2, (2, 3)),),
    17: ((2, 0, (2, 3)),),
    20: ((2, 1, (2, 3)),),
    22: ((2, 2, (2, 3)),),
}
GELU_A = 0.7978845608028654
GELU_B = 0.044715


def dot(a, b):
    return lax.dot_general(a, b, (((1,), (0,)), ((), ())), preferred_element_type=F32)


def dot_nt(a, b):
    return lax.dot_general(a, b, (((1,), (1,)), ((), ())), preferred_element_type=F32)


def dot_tn(a, b):
    return lax.dot_general(a, b, (((0,), (0,)), ((), ())), preferred_element_type=F32)


def iota(shape, axis):
    return lax.broadcasted_iota(jnp.int32, shape, axis)


def standard(x):
    width = x.shape[-1]
    centred = x - jnp.sum(x, axis=-1, keepdims=True) * (1.0 / width)
    variance = jnp.sum(centred * centred, axis=-1, keepdims=True) * (1.0 / width)
    scale = lax.rsqrt(variance + 1e-6)
    return centred * scale, scale


def gelu_parts(h):
    square = h * h
    p = 0.5 + 0.5 * jnp.tanh(h * (GELU_A + GELU_A * GELU_B * square))
    inner = h * (2.0 * GELU_A + 6.0 * GELU_A * GELU_B * square)
    return h * p, p * (1.0 + inner * (1.0 - p))


def sum8(x):
    return x[0:8] + x[8:16]


def body(
    n_dp,
    n_mp,
    tok_in,
    imt_in,
    ia_in,
    io_in,
    ie_in,
    ir_in,
    ca_in,
    co_in,
    we_in,
    wr_in,
    image_gains,
    attend_bias,
    output_bias,
    expand_bias,
    reduce_bias,
    norm_gains,
    norm_shifts,
    log_scale,
    cap,
    red,
    gt,
    sgo,
    W,
    IW,
    TOK,
    imt,
    N1,
    QKV,
    PR,
    MIX,
    RES,
    N2,
    GP,
    PA,
    PB,
    ACC,
    GRL,
    GT,
    IP,
    EMB,
    MSG,
    STATS,
    SBL,
    SB,
    HM3,
    BM,
    HM4,
    POOL,
    EL,
    GPL,
    GA,
    RCORE,
    RB1,
    RB2,
    RZ,
    XR,
    XST,
    SG,
    SGR,
    gz_s,
    gz_r,
    ga_s,
    ga_r,
    loc_sem,
    ca_sem,
    iw_sem,
    imt_sem,
    tok_sem,
    sb_s,
    sb_r,
    emb_s,
    emb_r,
    st_s,
    st_r,
    stx_s,
    stx_r,
    rs_s,
    rs_r,
    ag_s,
    ag_r,
    xr_s,
    xr_r,
    sg_s,
    sg_r,
    gt_s,
    gt_r,
    out_sem,
    pb_s,
    pb_r,
):
    d = lax.axis_index("dp")
    m = lax.axis_index("mp")
    n_all = n_dp * n_mp
    me = d * n_mp + m
    bits = n_dp.bit_length() - 1
    extra = bits - 3
    images, image_len = imt.shape[0], imt.shape[1]
    rows = TOK.shape[0] * LEN
    n_cap = TOK.shape[0]
    n_blocks = rows // BLOCK
    width = RES.shape[1]
    shard = QKV.shape[3]
    image_rows = images * 64
    t_all = EMB.shape[0] * 8
    total_images = images * n_all
    total_captions = n_cap * 2 * n_dp

    def bit(v, b):
        return lax.rem(v // (1 << b), 2)

    def flip(v, b):
        return v + (1 - 2 * bit(v, b)) * (1 << b)

    cb, xb, yb = bit(d, 0), bit(d, 1), bit(d, 2)
    half = lax.rem(m, 2)
    pair = flip(m, 0)
    p_a = cb * 4 + yb * 2 + xb
    p_b = 8 + cb * 4 + xb * 2 + yb
    core_dev = (flip(d, 0), m)
    x_dev = (flip(d, 1), m)
    y_dev = (flip(d, 2), m)
    pair_dev = (d, pair)
    sends = []

    def remote(src, dst, ss, rs, dev):
        copy = pltpu.make_async_remote_copy(
            src_ref=src,
            dst_ref=dst,
            send_sem=ss,
            recv_sem=rs,
            device_id=dev,
            device_id_type=pl.DeviceIdType.MESH,
        )
        copy.start()
        sends.append(copy)
        return copy

    def local(src, dst, sem):
        copy = pltpu.make_async_copy(src, dst, sem)
        copy.start()
        return copy

    barrier = pltpu.get_barrier_semaphore()

    low = lax.rem(d, 8)
    slot = low * 2 + half

    def near_device(k):
        q = lax.rem(slot + k, 16)
        return (d - low + q // 2, m - half + lax.rem(q, 2))

    def greet(k, carry):
        pl.semaphore_signal(
            barrier, inc=1, device_id=near_device(k), device_id_type=pl.DeviceIdType.MESH
        )
        return carry

    far = flip(m, 1)
    far_pair = flip(pair, 1)
    others = [(d, far), (d, far_pair)] + [(flip(d, 3 + x), m) for x in range(extra)]
    for dev in others:
        pl.semaphore_signal(barrier, inc=1, device_id=dev, device_id_type=pl.DeviceIdType.MESH)
    lax.fori_loop(1, 16, greet, 0)

    image_loads = {}

    def load_image(i):
        if i < 3:
            src, slot = ia_in.at[i], i
        elif i == 3:
            src, slot = io_in, 3
        elif i < 8:
            src, slot = ie_in.at[:, pl.ds((i - 4) * width, width)], i
        else:
            src, slot = ir_in.at[pl.ds((i - 8) * width, width)], i - 8
        image_loads[i] = local(src, IW.at[slot], iw_sem.at[i])

    ca_copies = [
        local(ca_in.at[j], W.at[0, m, pl.ds(shard * j, shard)], ca_sem.at[j]) for j in range(3)
    ]
    own_loads = [local(co_in, W.at[0, m, pl.ds(3 * shard, shard)], loc_sem.at[0])]
    SBL[...] = jnp.zeros_like(SBL)
    SBL[0:1, 0:shard] = attend_bias[0:1, :]
    SBL[2:3, 0:shard] = attend_bias[1:2, :]
    SBL[3:4, :] = expand_bias[...].reshape(1, width)
    SB[m] = SBL[...]
    for copy in ca_copies + own_loads[0:1]:
        copy.wait()
    pl.semaphore_wait(barrier, 15 + len(others))

    hops = (1, 2, 3)

    def partner(k):
        other = flip(m, 0) if k % 2 else m
        return flip(other, 1) if k >= 2 else other

    zc, ac = {}, {}
    sources = (W.at[0, m], we_in, wr_in)

    def span(p, n):
        return pl.ds(pl.multiple_of(p * PIECE, 16), n * PIECE)

    def gather_z(g, ks=(1, 2, 3)):
        for k in ks:
            dev = (d, partner(k))
            for ab, p in ((0, p_a), (1, p_b)):
                zc[g, k, ab] = remote(
                    sources[g].at[span(p, 1)],
                    W.at[g, m, span(p, 1)],
                    gz_s.at[g, k - 1, ab],
                    gz_r.at[g, k - 1, ab],
                    dev,
                )

    def spread(at, stage, ab, ss, rs):
        if stage == 0:
            p, n, dev = ((p_a, 1, x_dev), (p_b, 1, y_dev))[ab]
        elif stage == 1:
            p, n, dev = ((cb * 4 + yb * 2, 2, y_dev), (8 + cb * 4 + xb * 2, 2, x_dev))[ab]
        else:
            p, n, dev = 8 * ab + cb * 4, 4, core_dev
        return remote(at(p, n), at(p, n), ss.at[stage, ab], rs.at[stage, ab], dev)

    def gather_start(g, stage, ks=(1, 2, 3)):
        for k in ks:
            source = partner(k)
            for ab in range(2):
                (zc[g, k, ab] if stage == 0 else ac[g, stage - 1, k, ab]).wait_recv()
                ac[g, stage, k, ab] = spread(
                    lambda p, n: W.at[g, source, span(p, n)],
                    stage,
                    ab,
                    ga_s.at[g, k - 1],
                    ga_r.at[g, k - 1],
                )

    def gather_end(g, ks=(1, 2, 3)):
        for k in ks:
            for ab in range(2):
                ac[g, 2, k, ab].wait_recv()
        if g > 0 and 1 in ks:
            own_loads[g].wait()

    def tick(place):
        for g, stage, ks in PLAN.get(place, ()):
            if stage < 0:
                gather_z(g, ks)
            else:
                gather_start(g, stage, ks)

    gather_z(0)
    sb_copies = []
    for k in hops:
        sb_copies.append(
            remote(
                SBL,
                SB.at[m],
                sb_s.at[k - 1],
                sb_r.at[k - 1],
                (d, partner(k)),
            )
        )
    imt_copy = local(imt_in, imt, imt_sem)
    for i in range(3):
        load_image(i)
    tok_copy = local(tok_in.at[pl.ds(half * n_cap, n_cap)], TOK, tok_sem)
    for i in range(3, 8):
        load_image(i)
    own_loads.append(local(we_in, W.at[1, m], loc_sem.at[1]))
    own_loads.append(local(wr_in, W.at[2, m], loc_sem.at[2]))
    query = iota((BLOCK, 3 * BLOCK), 1)
    query = query - jnp.where(query >= 2 * BLOCK, 2 * BLOCK, jnp.where(query >= BLOCK, BLOCK, 0))
    BM[...] = jnp.where((iota((BLOCK, 3 * BLOCK), 0) >> 4) == (query >> 4), 0.0, FAR)
    lane_shard = iota((BLOCK, shard), 1) >> 6
    for h in range(3):
        at = slice(h * BLOCK, (h + 1) * BLOCK)
        HM3[at, :] = jnp.where(lane_shard == h, 1.0, 0.0).astype(LOW)
    lane_four = iota((64, 256), 1) >> 6
    for h in range(4):
        HM4[64 * h : 64 * h + 64, :] = jnp.where(lane_four == h, 1.0, 0.0).astype(LOW)
    POOL[...] = jnp.where((iota(POOL.shape, 1) >> 4) == iota(POOL.shape, 0), 1.0, 0.0).astype(LOW)
    RES[pl.ds(0, image_rows), :] = jnp.zeros((image_rows, width), F32)
    GP[3, pl.ds(0, image_rows), :] = jnp.zeros((image_rows, width), LOW)
    gain_one = image_gains[0:1, :]
    gain_two = image_gains[1:2, :]

    def image_norm(i, carry):
        x = imt[i].astype(F32)
        at = pl.multiple_of(i * 64, 64)
        RES[pl.ds(at, image_len), :] = x
        GP[3, pl.ds(at, image_len), :] = (standard(x)[0] * gain_one).astype(LOW)
        return carry

    imt_copy.wait()
    lax.fori_loop(0, images, image_norm, 0)
    for i in range(3):
        image_loads[i].wait()

    def image_qkv(j, carry):
        GP[j, pl.ds(0, image_rows), :] = dot(
            GP[3, pl.ds(0, image_rows), :], IW[j]
        ).astype(LOW)
        return carry

    lax.fori_loop(0, 3, image_qkv, 0)
    for i in range(8, 11):
        load_image(i)
    tick(1)

    key_valid = jnp.where(iota((256, 64), 1) < image_len, 0.0, FAR)
    lane_head = iota((64, 256), 1) >> 6

    def image_attention(i, carry):
        at = pl.multiple_of(i * 64, 64)
        for n in range(width // 256):
            lanes = slice(256 * n, 256 * n + 256)
            q = GP[0, pl.ds(at, 64), lanes]
            k = GP[1, pl.ds(at, 64), lanes]
            v = GP[2, pl.ds(at, 64), lanes]
            logits = dot_nt(jnp.concatenate([q] * 4, axis=0) * HM4[...], k) * 0.125 + key_valid
            expos = jnp.exp(logits - jnp.max(logits, axis=-1, keepdims=True))
            probs = (expos * (1.0 / jnp.sum(expos, axis=-1, keepdims=True))).astype(LOW)
            o = dot(probs, v)
            mix = jnp.where(
                lane_head < 2,
                jnp.where(lane_head == 0, o[0:64], o[64:128]),
                jnp.where(lane_head == 2, o[128:192], o[192:256]),
            )
            N2[pl.ds(at, 64), lanes] = mix.astype(LOW)
        return carry

    lax.fori_loop(0, images, image_attention, 0)
    tick(2)
    image_loads[3].wait()

    def image_out(n, carry):
        lanes = pl.ds(pl.multiple_of(n * 256, 256), 256)
        RES[pl.ds(0, image_rows), lanes] += dot(
            N2[pl.ds(0, image_rows), :], IW[3, :, lanes]
        )
        return carry

    lax.fori_loop(0, width // 256, image_out, 0)
    load_image(11)

    def image_norm_two(t, carry):
        at = pl.ds(pl.multiple_of(t * 16, 16), 16)
        GP[3, at, :] = (standard(RES[at, :])[0] * gain_two).astype(LOW)
        return carry

    lax.fori_loop(0, image_rows // 16, image_norm_two, 0, unroll=4)
    IP[...] = jnp.zeros_like(IP)
    for i in range(images):
        IP[i : i + 1, :] = jnp.sum(RES[64 * i : 64 * i + image_len, :], axis=0, keepdims=True) * (
            1.0 / image_len
        )
    image_pool = jnp.where(
        ((iota((16, image_rows), 1) >> 6) == iota((16, image_rows), 0))
        & ((iota((16, image_rows), 1) & 63) < image_len),
        1.0,
        0.0,
    ).astype(LOW)
    for i in range(4, 12):
        image_loads[i].wait()

    def image_feed(u, carry):
        ACC[pl.ds(0, image_rows), :] = dot(
            GP[3, pl.ds(0, image_rows), :], IW[4 + u]
        )

        def activate(t, inner):
            at = pl.ds(pl.multiple_of(t * 16, 16), 16)
            h = ACC[at, :]
            act = h * (0.5 + 0.5 * jnp.tanh(h * (GELU_A + GELU_A * GELU_B * (h * h))))
            N2[at, :] = act.astype(LOW)
            return inner

        lax.fori_loop(0, image_rows // 16, activate, 0, unroll=4)
        pooled = (dot(image_pool, N2[pl.ds(0, image_rows), :]) * (1.0 / image_len)).astype(LOW)
        IP[...] += dot(pooled, IW[u])
        return carry

    tick(3)
    lax.fori_loop(0, 1, image_feed, 0)
    tick(4)
    lax.fori_loop(1, 2, image_feed, 0)
    tick(5)
    lax.fori_loop(2, 3, image_feed, 0)
    tick(6)
    lax.fori_loop(3, 4, image_feed, 0)
    tick(7)
    pooled_image = IP[0:8]
    EMB[me] = (
        pooled_image
        * lax.rsqrt(jnp.sum(pooled_image * pooled_image, axis=-1, keepdims=True) + 1e-6)
    ).astype(LOW)

    shown = {}

    def show(stage, first, n, dev, at):
        run = EMB.at[pl.ds(first * n_mp, n * n_mp)]
        shown.setdefault(stage, []).append(
            remote(run, run, emb_s.at[at], emb_r.at[at], dev)
        )

    def show_embeds(stage):
        for copy in shown.get(stage - 1, ()):
            copy.wait_recv()
        if stage == 0:
            for k in hops:
                run = EMB.at[me]
                shown.setdefault(0, []).append(
                    remote(run, run, emb_s.at[k - 1], emb_r.at[k - 1], (d, partner(k)))
                )
        elif stage == 1:
            show(1, d, 1, x_dev, 3)
        elif stage == 2:
            for x in range(2):
                show(2, d + 2 * (x - xb), 1, y_dev, 4 + x)
        elif stage == 3:
            for q in range(4):
                show(3, d - low + cb + 2 * q, 1, core_dev, 6 + q)
        else:
            for x in range(extra):
                run = 8 << x
                first = d - lax.rem(d, run)
                show(4 + x, first, run, (flip(d, 3 + x), m), 10 + x)
                for copy in shown[4 + x]:
                    copy.wait_recv()

    show_embeds(0)

    tok_copy.wait()
    g1, g2 = norm_gains[0:1, :], norm_gains[1:2, :]
    b1, b2 = norm_shifts[0:1, :], norm_shifts[1:2, :]

    def norm_one(t, carry):
        at = pl.ds(pl.multiple_of(t * LEN, LEN), LEN)
        N1[at, :] = (standard(TOK[t].astype(F32))[0] * g1 + b1).astype(LOW)
        return carry

    lax.fori_loop(0, n_cap, norm_one, 0, unroll=7)
    tick(8)
    for copy in sb_copies:
        copy.wait_recv()
    gather_end(0, (1,))

    def project(near, distant):
        def one(t, carry):
            s, j = near + (t // 3) * (distant - near), lax.rem(t, 3)
            weight = W[0, s, pl.ds(pl.multiple_of(shard * j, 16), shard), :]
            QKV[j, s] = (dot_nt(N1[...], weight) + SB[s, pl.ds(j, 1), 0:shard]).astype(LOW)
            return carry

        lax.fori_loop(0, 6, one, 0)

    tick(9)
    project(m, pair)
    tick(10)
    gather_end(0, (2, 3))
    project(far, far_pair)
    tick(11)
    lane_three = iota((BLOCK, shard), 1) >> 6

    def join_heads(o):
        return jnp.where(
            lane_three == 0,
            o[0:BLOCK],
            jnp.where(lane_three == 1, o[BLOCK : 2 * BLOCK], o[2 * BLOCK : 3 * BLOCK]),
        )

    def attention(b, carry):
        at = pl.ds(pl.multiple_of(b * BLOCK, 16), BLOCK)
        loaded = [[QKV[j, s, at, :] for j in range(3)] for s in range(n_mp)]
        heads, mask = HM3[...], BM[...]
        every = []
        for q, k, v in loaded:
            logits = dot_nt(k, jnp.concatenate([q] * 3, axis=0) * heads) * 0.125 + mask
            expos = jnp.exp(logits - jnp.max(logits, axis=0, keepdims=True))
            probs = (expos * (1.0 / jnp.sum(expos, axis=0, keepdims=True))).astype(LOW)
            every.append((probs, join_heads(dot_tn(probs, v)).astype(LOW)))
        for s, (probs, mixed) in enumerate(every):
            PR[s, b] = probs
            MIX[s, at, :] = mixed
        return carry

    lax.fori_loop(0, 2, attention, 0)
    tick(12)
    lax.fori_loop(2, 4, attention, 0)
    tick(13)
    lax.fori_loop(4, n_blocks, attention, 0)
    tick(14)

    def attend_out(n, carry):
        lanes = pl.ds(pl.multiple_of(n * 256, 256), 256)
        total = dot(MIX[0], W[0, 0, pl.ds(3 * shard, shard), lanes])
        for s in range(1, n_mp):
            total += dot(MIX[s], W[0, s, pl.ds(3 * shard, shard), lanes])
        ACC[:, lanes] = total
        return carry

    lax.fori_loop(0, width // 256, attend_out, 0)
    out_bias = output_bias[...].reshape(1, width)

    def norm_two(t, carry):
        at = pl.ds(pl.multiple_of(t * LEN, LEN), LEN)
        x = TOK[t].astype(F32) + (ACC[at, :] + out_bias)
        RES[at, :] = x
        N2[at, :] = (standard(x)[0] * g2 + b2).astype(LOW)
        return carry

    lax.fori_loop(0, n_cap, norm_two, 0, unroll=7)
    tick(15)
    show_embeds(1)
    gather_end(1, (1,))

    def feed_one(s):
        bias = SB[s, 3:4, :]

        def tiles(t, carry):
            for x in range(TILES):
                first = pl.multiple_of((TILES * t + x) * BLOCK, 16)
                h = dot(N2[pl.ds(first, BLOCK), :], W[1, s])
                for u in range(BLOCK // LEN):
                    at = pl.ds(first + u * LEN, LEN)
                    act, slope = gelu_parts(h[u * LEN : (u + 1) * LEN] + bias)
                    GT[at, :] = act.astype(LOW)
                    GP[s, at, :] = slope.astype(LOW)
            return carry

        lax.fori_loop(0, n_blocks // TILES, tiles, 0)
        PA[s] = (dot(POOL[...], GT[...]) * (1.0 / LEN)).astype(LOW)

    def feed_near(i, carry):
        feed_one(m + i * (pair - m))
        return carry

    def feed_far(i, carry):
        feed_one(far + i * (far_pair - far))
        return carry

    lax.fori_loop(0, 1, feed_near, 0)
    tick(16)
    show_embeds(2)
    lax.fori_loop(1, 2, feed_near, 0)
    tick(17)
    show_embeds(3)
    gather_end(2, (1,))
    PB[0] = (dot(PA[m], W[2, m]) + dot(PA[pair], W[2, pair])).astype(LOW)
    pooled_copy = remote(PB.at[0], PB.at[1], pb_s, pb_r, (d, far))
    tick(18)

    def pool_residual(n, carry):
        lanes = pl.ds(pl.multiple_of(n * 128, 128), 128)
        res = RES[:, lanes]
        res_high = res.astype(LOW)
        res_low = (res - res_high.astype(F32)).astype(LOW)
        EL[:, lanes] = (dot(POOL[...], res_high) + dot(POOL[...], res_low)) * (1.0 / LEN)
        return carry

    lax.fori_loop(0, width // 128, pool_residual, 0)
    pooled = EL[...] + reduce_bias[...].reshape(1, width)
    pooled_copy.wait_recv()
    pooled += PB[0].astype(F32) + PB[1].astype(F32)
    inverse = lax.rsqrt(jnp.sum(pooled * pooled, axis=-1, keepdims=True) + 1e-6)
    embed = pooled * inverse
    EL[...] = embed

    show_embeds(4)
    group = min(n_all, 32)

    def embeds(c):
        part = EMB[c * group : c * group + group].astype(F32)
        return part.reshape(group * 8, width).astype(LOW)

    scaling = jnp.exp(log_scale[...].reshape(1, 1))
    embed_low = embed.astype(LOW)
    scores = scaling * jnp.concatenate(
        [dot_nt(embed_low, embeds(c)) for c in range(n_all // group)], axis=1
    )
    cap_rows = scores.shape[0]
    column = iota((cap_rows, t_all), 1)
    col_ok = (column & 7) < images
    row_ok = iota((cap_rows, t_all), 0) < n_cap
    image_id = (column >> 3) * images + (column & 7)
    cap_wide = jnp.broadcast_to(cap[...].reshape(1, 2 * n_cap).astype(F32), (cap_rows, 2 * n_cap))
    mine = iota((cap_rows, 2 * n_cap), 1) == iota((cap_rows, 2 * n_cap), 0) + half * n_cap
    cap_column = jnp.sum(jnp.where(mine, cap_wide, 0.0), axis=1, keepdims=True)
    matches = jnp.where((cap_column == image_id.astype(F32)) & col_ok & row_ok, 1.0, 0.0)
    by_row = jnp.where(col_ok, scores, FAR)
    row_top = jnp.max(by_row, axis=1, keepdims=True)
    row_lse = row_top + jnp.log(jnp.sum(jnp.exp(by_row - row_top), axis=1, keepdims=True))
    row_positive = jnp.sum(scores * matches, axis=1, keepdims=True)
    row_part = jnp.sum(
        jnp.where(iota((cap_rows, 1), 0) < n_cap, row_lse - row_positive, 0.0), axis=0, keepdims=True
    )
    by_column = jnp.where(row_ok, scores, FAR)
    top = jnp.max(by_column, axis=0, keepdims=True)
    MSG[...] = jnp.zeros_like(MSG)
    MSG[0:1, :] = top
    MSG[1:2, :] = jnp.sum(jnp.exp(by_column - top), axis=0, keepdims=True)
    MSG[2:3, :] = jnp.sum(scores * matches, axis=0, keepdims=True)
    MSG[3:4, :] = jnp.sum(matches, axis=0, keepdims=True)
    MSG[4:5, :] = jnp.broadcast_to(row_part, (1, t_all))
    STATS[slot] = MSG[...]

    def send_stats(k, carry):
        pltpu.make_async_remote_copy(
            src_ref=MSG,
            dst_ref=STATS.at[slot],
            send_sem=st_s,
            recv_sem=st_r,
            device_id=near_device(k),
            device_id_type=pl.DeviceIdType.MESH,
        ).start()
        return carry

    lax.fori_loop(1, 16, send_stats, 0)
    tick(19)
    gather_end(1, (2, 3))
    lax.fori_loop(0, 1, feed_far, 0)
    tick(20)
    lax.fori_loop(1, 2, feed_far, 0)
    pltpu.make_async_copy(STATS.at[pl.ds(0, 15)], STATS.at[pl.ds(0, 15)], st_r).wait()
    top = jnp.max(STATS[:, 0, :], axis=0, keepdims=True)
    total = jnp.sum(STATS[:, 1, :] * jnp.exp(STATS[:, 0, :] - top), axis=0, keepdims=True)
    positive = jnp.sum(STATS[:, 2, :], axis=0, keepdims=True)
    count = jnp.sum(STATS[:, 3, :], axis=0, keepdims=True)
    row_sum = jnp.sum(STATS[:, 4, :], axis=0, keepdims=True)
    for x in range(extra):
        XST[0, x] = jnp.concatenate(
            [top, total, positive, count, row_sum, jnp.zeros((3, t_all), F32)], axis=0
        )
        remote(
            XST.at[0, x], XST.at[1, x], stx_s.at[x], stx_r.at[x], (flip(d, 3 + x), m)
        ).wait_recv()
        other = XST[1, x]
        joined = jnp.maximum(top, other[0:1])
        total = total * jnp.exp(top - joined) + other[1:2] * jnp.exp(other[0:1] - joined)
        top = joined
        positive = positive + other[2:3]
        count = count + other[3:4]
        row_sum = row_sum + other[4:5]
    ok = col_ok[0:1]
    count = jnp.where(ok, count, 1.0)
    col_lse = top + jnp.log(total)
    column_part = jnp.sum(
        jnp.where(ok, col_lse - positive / count, 0.0), axis=1, keepdims=True
    )
    loss = 0.5 * (row_sum[:, 0:1] * (1.0 / total_captions) + column_part * (1.0 / total_images))
    weight = 0.5 * total_captions / total_images
    grad_scores = 0.5 * (jnp.exp(by_row - row_lse) - matches) + weight * (
        jnp.exp(by_column - col_lse) - matches * (1.0 / count)
    )
    grad_scores = jnp.where(col_ok & row_ok, grad_scores, 0.0)
    grad_log = jnp.sum(
        jnp.sum(grad_scores * scores, axis=1, keepdims=True), axis=0, keepdims=True
    )
    embed = EL[...]
    grad_cosine = (scaling * grad_scores).astype(LOW)
    grad_embed = dot(grad_cosine[:, 0 : group * 8], embeds(0))
    for c in range(1, n_all // group):
        grad_embed += dot(grad_cosine[:, c * group * 8 : (c + 1) * group * 8], embeds(c))
    grad_pooled = (
        grad_embed - embed * jnp.sum(embed * grad_embed, axis=-1, keepdims=True)
    ) * inverse
    SG[0] = jnp.zeros(SG.shape[1:], F32)
    SG[0, 13:14, :] = jnp.sum(grad_pooled, axis=0, keepdims=True)
    SG[0, 18:19, :] = jnp.broadcast_to(grad_log, (1, width))
    GPL[0] = grad_pooled.astype(LOW)
    grad_rows = grad_pooled * (1.0 / LEN)
    EL[...] = grad_rows
    GPL[1] = grad_rows.astype(LOW)

    def part(g, i):
        return IW.at[2 * g + i]

    places = (4, 7, 6)

    def whole(g):
        return IW.at[places[g]]

    def settle(copies):
        for copy in copies:
            copy.wait_send()
        sends[:] = [other for other in sends if all(other is not copy for copy in copies)]

    state = {}
    stores = []
    axis_one = ((yb, y_dev), (xb, x_dev))
    axis_two = ((xb, x_dev), (yb, y_dev))
    own = (p_a, p_b)

    def scatter(g, stage, i, ab):
        bit_one, dev_one = axis_one[ab]
        bit_two, dev_two = axis_two[ab]
        run = 8 * ab + 4 * cb + 2 * bit_one
        if stage == 0:
            p, n, dst, dev = 8 * ab + 4 * (1 - cb), 4, RCORE.at[g % 2, i, ab], core_dev
        elif stage == 1:
            p, n, dst, dev = 8 * ab + 4 * cb + 2 * (1 - bit_one), 2, RB1.at[g % 2, i, ab], dev_one
        elif stage == 2:
            p, n, dst, dev = run + 1 - bit_two, 1, RB2.at[g % 2, i, ab], dev_two
        else:
            p, n, dst, dev = own[ab], 1, RZ.at[g, ab], pair_dev
        k = 2 * i + ab
        state[g, stage, i, ab] = remote(
            part(g, i).at[span(p, n)], dst, rs_s.at[g, stage, k], rs_r.at[g, stage, k], dev
        )

    def add_in(g, stage, i, ab):
        state[g, stage, i, ab].wait_recv()
        run = 8 * ab + 4 * cb
        if stage == 0:
            at, got = span(run, 4), RCORE[g % 2, i, ab]
        elif stage == 1:
            at, got = span(run + 2 * axis_one[ab][0], 2), RB1[g % 2, i, ab]
        else:
            at, got = span(own[ab], 1), RB2[g % 2, i, ab]
        IW[2 * g + i, at, :] = IW[2 * g + i, at, :] + got

    def pass_on(g, ab, k, across_one, across_two, dev):
        bit_one = axis_one[ab][0] + across_one * (1 - 2 * axis_one[ab][0])
        bit_two = axis_two[ab][0] + across_two * (1 - 2 * axis_two[ab][0])
        run = whole(g).at[span(8 * ab + 4 * cb + 2 * bit_one + bit_two, 1)]
        state[g, "back", k, ab] = remote(run, run, ag_s.at[g, k, ab], ag_r.at[g, k, ab], dev)

    def gather_back(g, stage, ab):
        dev_one, dev_two = axis_one[ab][1], axis_two[ab][1]
        if stage == 0:
            pass_on(g, ab, 0, 0, 0, dev_two)
            pass_on(g, ab, 1, 0, 0, dev_one)
            pass_on(g, ab, 2, 0, 0, core_dev)
        elif stage == 1:
            state[g, "back", 0, ab].wait_recv()
            pass_on(g, ab, 3, 0, 1, dev_one)
            pass_on(g, ab, 4, 0, 1, core_dev)
        elif stage == 2:
            state[g, "back", 1, ab].wait_recv()
            pass_on(g, ab, 5, 1, 0, core_dev)
            state[g, "back", 3, ab].wait_recv()
            pass_on(g, ab, 6, 1, 1, core_dev)
        else:
            for k in (2, 4, 5, 6):
                state[g, "back", k, ab].wait_recv()

    def reduce_start(g, ab):
        if g == 0:
            settle([state.pop((2, a, i, ab)) for a in range(4) for i in range(2) if (2, a, i, ab) in state])
        for i in (1, 0):
            scatter(g, 0, i, ab)

    def reduce_step(g, step, half_of=None):
        if step == 0:
            for ab in range(2):
                reduce_start(g, ab)
        elif step < 4:
            halves = (half_of,) if half_of is not None else (0, 1)
            for i in (1, 0):
                for ab in halves:
                    add_in(g, step - 1, i, ab)
                    if step < 3 or i == 1:
                        scatter(g, step, i, ab)
        elif step == 4:
            for ab in range(2):
                state[g, 3, 1, ab].wait_recv()
                at = span(own[ab], 1)
                IW[places[g], at, :] = IW[2 * g, at, :] + RZ[g, ab]
                for x in range(extra):
                    copy = remote(
                        whole(g).at[at],
                        XR.at[g % 2, x, ab],
                        xr_s.at[g, x, ab],
                        xr_r.at[g, x, ab],
                        (flip(d, 3 + x), m),
                    )
                    copy.wait_recv()
                    settle([copy])
                    IW[places[g], at, :] = IW[places[g], at, :] + XR[g % 2, x, ab]
                gather_back(g, 0, ab)
        elif step < 7:
            for ab in range(2):
                gather_back(g, step - 4, ab)
        else:
            for ab in range(2):
                gather_back(g, 3, ab)
            stores.append(local(whole(g), red.at[g], out_sem.at[g]))

    def back_tick(place):
        for entry in RPLAN.get(place, ()):
            reduce_step(*entry)

    shards = (m, pair)
    for i in range(2):
        IW[4 + i] = dot_tn(PA[shards[i]], GPL[0]).astype(LOW)

    back_tick(0)

    def grad_activation(near, distant):
        for s in (near, distant):
            GA[s] = dot_nt(GPL[1], W[2, s])

    ones = jnp.ones((16, rows), LOW)

    def grad_hidden(near, distant):
        def one(k, carry):
            s = near + k * (distant - near)

            def scale(t, inner):
                at = pl.ds(pl.multiple_of(t * LEN, LEN), LEN)
                GP[s, at, :] = (GP[s, at, :].astype(F32) * GA[s, pl.ds(t, 1), :]).astype(LOW)
                return inner

            lax.fori_loop(0, n_cap, scale, 0, unroll=7)
            SG[0, pl.ds(8 + s, 1), :] = dot(ones, GP[s])[0:1]
            return carry

        lax.fori_loop(0, 2, one, 0)

    grad_activation(m, pair)
    back_tick(1)
    tick(21)
    grad_hidden(m, pair)
    back_tick(2)
    tick(22)

    def expand_gradient(i, carry):
        s = m + i * (pair - m)
        IW[2 + i] = dot_tn(N2[...], GP[s]).astype(LOW)
        return carry

    lax.fori_loop(0, 2, expand_gradient, 0)
    back_tick(4)
    tick(23)
    gather_end(2, (2, 3))
    grad_activation(far, far_pair)
    back_tick(3)
    grad_hidden(far, far_pair)
    back_tick(5)

    def grad_norm_two(n, carry):
        p = pl.ds(pl.multiple_of(n * 384, 128), 384)
        total = dot_nt(
            jnp.concatenate([GP[s] for s in range(n_mp)], axis=1),
            jnp.concatenate([W[1, s, p, :] for s in range(n_mp)], axis=1),
        )
        ACC[:, pl.ds(pl.multiple_of(n * 384, 128), 384)] = total
        return carry

    lax.fori_loop(0, 2, grad_norm_two, 0)
    back_tick(6)

    def norm_back(e, gain, x):
        xhat, scale = standard(x)
        eg = e * gain
        c1 = jnp.sum(eg, axis=-1, keepdims=True) * (1.0 / width)
        c2 = jnp.sum(eg * xhat, axis=-1, keepdims=True) * (1.0 / width)
        return (eg - c1 - xhat * c2) * scale, sum8(e * xhat), sum8(e)

    zero8 = jnp.zeros((8, width), F32)

    def back_two(t, carry):
        dg, db, do = carry
        found = []
        for u in range(7):
            at = pl.ds(pl.multiple_of((7 * t + u) * LEN, LEN), LEN)
            dv, one, two = norm_back(ACC[at, :], g2, RES[at, :])
            g = EL[pl.ds(7 * t + u, 1), :] + dv
            found.append((at, g))
            dg, db, do = dg + one, db + two, do + sum8(g)
        for at, g in found:
            RES[at, :] = g
            GRL[at, :] = g.astype(LOW)
        return dg, db, do

    dg, db, do = lax.fori_loop(0, n_cap // 7, back_two, (zero8, zero8, zero8))
    SG[0, 15:16, :] = jnp.sum(dg, axis=0, keepdims=True)
    SG[0, 17:18, :] = jnp.sum(db, axis=0, keepdims=True)
    SG[0, 12:13, :] = jnp.sum(do, axis=0, keepdims=True)

    back_tick(7)
    for i in range(2):
        IW[i, 3 * shard : 4 * shard, :] = dot_tn(MIX[shards[i]], GRL[...]).astype(LOW)

    def grad_mixture(s, carry):
        MIX[s] = dot_nt(GRL[...], W[0, s, pl.ds(3 * shard, shard), :]).astype(LOW)
        return carry

    lax.fori_loop(0, n_mp, grad_mixture, 0)
    back_tick(8)

    def attention_back(places):
        loaded = []
        for b, s in places:
            at = pl.ds(pl.multiple_of(b * BLOCK, 16), BLOCK)
            loaded.append([QKV[j, s, at, :] for j in range(3)] + [MIX[s, at, :], PR[s, b]])
        heads = HM3[...]
        every = []
        for q, k, v, g, low_probs in loaded:
            q = jnp.concatenate([q] * 3, axis=0) * heads
            g = jnp.concatenate([g] * 3, axis=0) * heads
            probs = low_probs.astype(F32)
            grad_probs = dot_nt(v, g)
            inner = jnp.sum(grad_probs * probs, axis=0, keepdims=True)
            grad_logits = (probs * (grad_probs - inner)).astype(LOW)
            every.append(
                (
                    (join_heads(dot_tn(grad_logits, k)) * 0.125).astype(LOW),
                    (dot(grad_logits, q) * 0.125).astype(LOW),
                    dot(low_probs, g).astype(LOW),
                )
            )
        for (b, s), grads in zip(places, every):
            at = pl.ds(pl.multiple_of(b * BLOCK, 16), BLOCK)
            for j in range(3):
                QKV[j, s, at, :] = grads[j]

    def attention_back_run(first, count, shards):
        def two(t, carry):
            b = first + 2 * t
            attention_back([(b + x, s) for x in range(2) for s in shards])
            return carry

        lax.fori_loop(0, count // 2, two, 0)
        if count % 2:
            attention_back([(first + count - 1, s) for s in shards])

    def attend_gradient(j):
        def one(i, carry):
            s = m + i * (pair - m)
            IW[i, shard * j : shard * (j + 1), :] = dot_tn(QKV[j, s], N1[...]).astype(LOW)
            return carry

        lax.fori_loop(0, 2, one, 0)

    small_devs = [core_dev, y_dev, x_dev, pair_dev] + [(flip(d, 3 + x), m) for x in range(extra)]
    small = {}

    def small_start(i):
        small[i] = remote(SG.at[i], SGR.at[i], sg_s.at[i], sg_r.at[i], small_devs[i])

    def small_end(i):
        small[i].wait_recv()
        SG[i + 1] = SG[i] + SGR[i]

    small_gain, small_shift = zero8, zero8
    gt_copies = []
    cuts = (0, 4, n_blocks)
    attention_back_run(0, n_blocks, (m, pair))
    back_tick(9)
    attend_gradient(2)
    reduce_start(0, 1)
    attend_gradient(0)
    attend_gradient(1)
    reduce_start(0, 0)
    back_tick(20)
    for r in range(2):
        attention_back_run(cuts[r], cuts[r + 1] - cuts[r], (far, far_pair))
        back_tick(10 + r)
        first, last = cuts[r] * (BLOCK // LEN), cuts[r + 1] * (BLOCK // LEN)
        stripe = pl.ds(first * LEN, (last - first) * LEN)

        def grad_norm_one(n, carry):
            lanes = pl.ds(pl.multiple_of(n * 256, 256), 256)
            total = None
            for s in range(n_mp):
                for j in range(3):
                    term = dot(
                        QKV[j, s, stripe, :],
                        W[0, s, pl.ds(shard * j, shard), lanes],
                    )
                    total = term if total is None else total + term
            ACC[stripe, lanes] = total
            return carry

        lax.fori_loop(0, width // 256, grad_norm_one, 0)
        back_tick(12 + r)
        def back_one(t, carry):
            at = pl.ds(pl.multiple_of(t * LEN, LEN), LEN)
            dv, dg, db = norm_back(ACC[at, :], g1, TOK[t].astype(F32))
            GT[at, :] = (RES[at, :] + dv).astype(LOW)
            return carry[0] + dg, carry[1] + db

        small_gain, small_shift = lax.fori_loop(
            first, last, back_one, (small_gain, small_shift), unroll=7
        )
        if r == 1:
            SG[0, 14:15, :] = jnp.sum(small_gain, axis=0, keepdims=True)
            SG[0, 16:17, :] = jnp.sum(small_shift, axis=0, keepdims=True)

            def bias_gradient(s, carry):
                SG[0, pl.ds(s, 1), 0:shard] = dot(ones, QKV[0, s])[0:1]
                SG[0, pl.ds(4 + s, 1), 0:shard] = dot(ones, QKV[2, s])[0:1]
                return carry

            lax.fori_loop(0, n_mp, bias_gradient, 0)
            small_start(0)
            back_tick(16)
            small_end(0)
            small_start(1)
            back_tick(17)
            small_end(1)
            small_start(2)
            back_tick(18)
            small_end(2)
            small_start(3)
        else:
            back_tick(15)
        gt_copies.append(
            remote(GT.at[stripe], gt.at[half, stripe], gt_s.at[r], gt_r.at[r], pair_dev)
        )
    stores.append(local(GT, gt.at[half], out_sem.at[3]))
    back_tick(21)
    small_end(3)
    for i in range(4, 4 + extra):
        small_start(i)
        small_end(i)
    for place in range(22, 28):
        back_tick(place)
    last = SG.shape[0] - 1
    sgo[...] = jnp.zeros_like(sgo)
    sgo[0:1, :] = SG[last, pl.ds(m, 1), :]
    sgo[1:2, :] = SG[last, pl.ds(4 + m, 1), :]
    sgo[2:3, :] = SG[last, pl.ds(8 + m, 1), :]
    sgo[3:10, :] = SG[last, 12:19, :]
    sgo[10:11, :] = jnp.broadcast_to(loss, (1, width))
    back_tick(28)
    for copy in gt_copies:
        copy.wait_recv()
    pltpu.make_async_copy(STATS.at[pl.ds(0, 15)], STATS.at[pl.ds(0, 15)], st_s).wait()
    for copy in sends:
        copy.wait_send()
    for copy in stores:
        copy.wait()


def local_step(
    n_dp,
    n_mp,
    caption_tokens,
    image_tokens,
    image_attend,
    image_output,
    image_expand,
    image_reduce,
    image_gains,
    caption_attend,
    attend_bias,
    caption_output,
    output_bias,
    caption_expand,
    expand_bias,
    caption_reduce,
    reduce_bias,
    norm_gains,
    norm_shifts,
    log_scale,
    caption_image,
):
    captions, length, width = caption_tokens.shape
    images, image_len, _ = image_tokens.shape
    shard = caption_attend.shape[2]
    units = caption_expand.shape[1]
    n_cap = captions // 2
    rows = n_cap * length
    n_blocks = rows // BLOCK
    n_all = n_dp * n_mp
    t_all = n_all * 8
    extra = n_dp.bit_length() - 1 - 3
    assert length == LEN and units == width and shard * n_mp == width and width == 16 * PIECE

    any_space = pl.BlockSpec(memory_space=pl.ANY)
    vmem = pl.BlockSpec(memory_space=pltpu.VMEM)
    nx = max(extra, 1)
    dma = pltpu.SemaphoreType.DMA
    scratch = [
        pltpu.VMEM((3, n_mp, width, width), LOW),
        pltpu.VMEM((8, width, width), LOW),
        pltpu.VMEM((n_cap, length, width), LOW),
        pltpu.VMEM((images, image_len, width), LOW),
        pltpu.VMEM((rows, width), LOW),
        pltpu.VMEM((3, n_mp, rows, shard), LOW),
        pltpu.VMEM((n_mp, n_blocks, BLOCK, 3 * BLOCK), LOW),
        pltpu.VMEM((n_mp, rows, shard), LOW),
        pltpu.VMEM((rows, width), F32),
        pltpu.VMEM((rows, width), LOW),
        pltpu.VMEM((n_mp, rows, width), LOW),
        pltpu.VMEM((n_mp, 64, width), LOW),
        pltpu.VMEM((2, 64, width), LOW),
        pltpu.VMEM((rows, width), F32),
        pltpu.VMEM((rows, width), LOW),
        pltpu.VMEM((rows, width), LOW),
        pltpu.VMEM((16, width), F32),
        pltpu.VMEM((n_all, 8, width), LOW),
        pltpu.VMEM((8, t_all), F32),
        pltpu.VMEM((16, 8, t_all), F32),
        pltpu.VMEM((8, width), F32),
        pltpu.VMEM((n_mp, 8, width), F32),
        pltpu.VMEM((3 * BLOCK, shard), LOW),
        pltpu.VMEM((BLOCK, 3 * BLOCK), F32),
        pltpu.VMEM((256, 256), LOW),
        pltpu.VMEM((64, rows), LOW),
        pltpu.VMEM((64, width), F32),
        pltpu.VMEM((2, 64, width), LOW),
        pltpu.VMEM((n_mp, 64, width), F32),
        pltpu.VMEM((2, 2, 2, 4 * PIECE, width), LOW),
        pltpu.VMEM((2, 2, 2, 2 * PIECE, width), LOW),
        pltpu.VMEM((2, 2, 2, PIECE, width), LOW),
        pltpu.VMEM((3, 2, PIECE, width), LOW),
        pltpu.VMEM((2, nx, 2, PIECE, width), LOW),
        pltpu.VMEM((2, nx, 8, t_all), F32),
        pltpu.VMEM((5 + extra, 24, width), F32),
        pltpu.VMEM((4 + extra, 24, width), F32),
        dma((3, 3, 2)),
        dma((3, 3, 2)),
        dma((3, 3, 3, 2)),
        dma((3, 3, 3, 2)),
        dma((3,)),
        dma((3,)),
        dma((12,)),
        dma,
        dma,
        dma((3,)),
        dma((3,)),
        dma((10 + nx,)),
        dma((10 + nx,)),
        dma,
        dma,
        dma((nx,)),
        dma((nx,)),
        dma((3, 4, 4)),
        dma((3, 4, 4)),
        dma((3, 7, 2)),
        dma((3, 7, 2)),
        dma((3, nx, 2)),
        dma((3, nx, 2)),
        dma((4 + extra,)),
        dma((4 + extra,)),
        dma((3,)),
        dma((3,)),
        dma((4,)),
        dma,
        dma,
    ]
    red, gt, sgo = pl.pallas_call(
        functools.partial(body, n_dp, n_mp),
        out_shape=(
            jax.ShapeDtypeStruct((3, width, width), LOW),
            jax.ShapeDtypeStruct((2, rows, width), LOW),
            jax.ShapeDtypeStruct((16, width), F32),
        ),
        in_specs=[any_space] * 10 + [vmem] * 9,
        out_specs=(any_space, any_space, vmem),
        scratch_shapes=scratch,
        compiler_params=pltpu.CompilerParams(
            collective_id=0, has_side_effects=True, vmem_limit_bytes=66_000_000
        ),
        name="step",
    )(
        caption_tokens,
        image_tokens,
        image_attend,
        image_output,
        image_expand,
        image_reduce,
        jnp.swapaxes(caption_attend, 1, 2),
        caption_output,
        caption_expand,
        caption_reduce,
        image_gains,
        attend_bias,
        output_bias,
        expand_bias,
        reduce_bias,
        norm_gains,
        norm_shifts,
        log_scale,
        caption_image,
    )
    shapes = (
        (1,),
        (captions, length, width),
        (3, shard, width),
        (2, shard),
        (shard, width),
        (width,),
        (width, units),
        (units,),
        (units, width),
        (width,),
        (2, width),
        (2, width),
        (1,),
    )
    large = (1, 2, 4, 6, 8)
    parts = 7
    grads = pl.pallas_call(
        finish,
        out_shape=tuple(jax.ShapeDtypeStruct(shape, F32) for shape in shapes),
        in_specs=[any_space, any_space, vmem],
        out_specs=tuple(any_space if i in large else vmem for i in range(len(shapes))),
        scratch_shapes=[
            pltpu.VMEM((captions, length, width), LOW),
            pltpu.VMEM((captions, length, width), F32),
            pltpu.VMEM((3, width, width), LOW),
            pltpu.VMEM((3, width, width), F32),
            pltpu.VMEM((3, shard, width), F32),
            dma((parts,)),
            dma((parts,)),
            dma((3,)),
            dma((6,)),
        ],
        compiler_params=pltpu.CompilerParams(vmem_limit_bytes=64_000_000),
        name="finish",
    )(red, gt.reshape(captions, length, width), sgo)
    return (*grads[:2], jnp.swapaxes(grads[2], 1, 2), *grads[3:])


def finish(
    red,
    gt,
    small,
    loss,
    tokens,
    attend,
    attend_bias,
    output,
    output_bias,
    expand,
    expand_bias,
    reduce,
    reduce_bias,
    gains,
    shifts,
    log_scale,
    GT,
    TOKENS,
    RED,
    WIDE,
    ATTEND,
    gt_in,
    gt_out,
    red_in,
    red_out,
):
    def copy(src, dst, sem):
        made = pltpu.make_async_copy(src, dst, sem)
        made.start()
        return made

    parts = gt_in.shape[0]
    size = GT.shape[0] // parts
    width = GT.shape[2]
    shard = ATTEND.shape[1]
    order = (0, 1, 2)
    weights = {g: copy(red.at[g], RED.at[g], red_in.at[g]) for g in order}
    pieces = [
        copy(gt.at[pl.ds(i * size, size)], GT.at[pl.ds(i * size, size)], gt_in.at[i])
        for i in range(parts)
    ]
    written = []
    loss[...] = small[10:11, 0:1].reshape(1)
    attend_bias[...] = small[0:2, 0:shard]
    expand_bias[...] = small[2:3, :].reshape(width)
    output_bias[...] = small[3:4, :].reshape(width)
    reduce_bias[...] = small[4:5, :].reshape(width)
    gains[...] = small[5:7, :]
    shifts[...] = small[7:9, :]
    log_scale[...] = small[9:10, 0:1].reshape(1)
    for g in order:
        weights[g].wait()
        if g == 0:
            for j in range(3):
                ATTEND[j] = RED[0, shard * j : shard * (j + 1), :].astype(F32)
                written.append(copy(ATTEND.at[j], attend.at[j], red_out.at[j]))
            WIDE[0, 3 * shard :, :] = RED[0, 3 * shard :, :].astype(F32)
            written.append(copy(WIDE.at[0, pl.ds(3 * shard, shard)], output, red_out.at[3]))
        else:

            def widen(t, carry):
                at = pl.ds(pl.multiple_of(t * 96, 96), 96)
                WIDE[g, at, :] = RED[g, at, :].astype(F32)
                return carry

            lax.fori_loop(0, width // 96, widen, 0)
            written.append(copy(WIDE.at[g], (expand, reduce)[g - 1], red_out.at[3 + g]))
    for i in range(parts):
        pieces[i].wait()
        at = slice(i * size, i * size + size)
        TOKENS[at] = GT[at].astype(F32)
        written.append(
            copy(
                TOKENS.at[pl.ds(i * size, size)], tokens.at[pl.ds(i * size, size)], gt_out.at[i]
            )
        )
    for made in written:
        made.wait()


def solution(mesh):
    in_specs = (
        P("dp", None, None),
        P(("dp", "mp"), None, None),
        P(),
        P(),
        P(),
        P(),
        P(),
        P(None, None, "mp"),
        P(None, "mp"),
        P("mp", None),
        P(),
        P(None, "mp"),
        P("mp"),
        P("mp", None),
        P(),
        P(),
        P(),
        P(),
        P("dp"),
    )
    out_specs = (
        P(),
        P("dp", None, None),
        P(None, None, "mp"),
        P(None, "mp"),
        P("mp", None),
        P(),
        P(None, "mp"),
        P("mp"),
        P("mp", None),
        P(),
        P(),
        P(),
        P(),
    )
    step = functools.partial(local_step, mesh.shape["dp"], mesh.shape["mp"])
    return jax.shard_map(step, mesh=mesh, in_specs=in_specs, out_specs=out_specs, check_vma=False)
```

```python
import functools

import jax
import jax.numpy as jnp
from jax import lax
from jax.experimental import pallas as pl
from jax.experimental.pallas import tpu as pltpu
from jax.sharding import PartitionSpec as P

HEAD_DIM = 64
LEN = 16
PIECE = 48
BLOCK = 112
F32 = jnp.float32
LOW = jnp.bfloat16
FAR = -1e30
ALL_HOPS = (1, 2, 3)
TILES = 7
RPLAN = {
    0: ((2, 0),),
    2: ((2, 1),),
    4: ((1, 0),),
    5: ((2, 2), (1, 1),),
    6: ((2, 3),),
    8: ((2, 4),),
    9: ((1, 2),),
    20: ((1, 3),),
    10: ((0, 1),),
    15: ((1, 4),),
    13: ((2, 5),),
    11: ((0, 2),),
    16: ((0, 3),),
    17: ((2, 6),),
    18: ((1, 5),),
    21: ((0, 4),),
    22: ((1, 6), (2, 7),),
    23: ((0, 5),),
    25: ((1, 7),),
    26: ((0, 6),),
    28: ((0, 7),),
}
PLAN = {
    1: ((0, 0, (1,)),),
    2: ((0, 0, (2, 3)), (1, -1, (1,)), (2, -1, (1,)),),
    3: ((0, 1, (1, 2)), (1, -1, (2, 3)), (2, -1, (2, 3)),),
    4: ((0, 2, (1,)),),
    5: ((0, 1, (3,)),),
    7: ((0, 2, (2,)), (0, 2, (3,)), (1, 0, (1,)), (2, 0, (1,)),),
    10: ((1, 1, (1,)), (2, 1, (1,)),),
    12: ((1, 2, (1,)), (2, 2, (1,)),),
    13: ((1, 0, (2, 3)),),
    14: ((1, 1, (2, 3)),),
    16: ((1, 2, (2, 3)),),
    17: ((2, 0, (2, 3)),),
    20: ((2, 1, (2, 3)),),
    22: ((2, 2, (2, 3)),),
}
GELU_A = 0.7978845608028654
GELU_B = 0.044715


def dot(a, b):
    return lax.dot_general(a, b, (((1,), (0,)), ((), ())), preferred_element_type=F32)


def dot_nt(a, b):
    return lax.dot_general(a, b, (((1,), (1,)), ((), ())), preferred_element_type=F32)


def dot_tn(a, b):
    return lax.dot_general(a, b, (((0,), (0,)), ((), ())), preferred_element_type=F32)


def iota(shape, axis):
    return lax.broadcasted_iota(jnp.int32, shape, axis)


def standard(x):
    width = x.shape[-1]
    centred = x - jnp.sum(x, axis=-1, keepdims=True) * (1.0 / width)
    variance = jnp.sum(centred * centred, axis=-1, keepdims=True) * (1.0 / width)
    scale = lax.rsqrt(variance + 1e-6)
    return centred * scale, scale


def gelu_parts(h):
    square = h * h
    p = 0.5 + 0.5 * jnp.tanh(h * (GELU_A + GELU_A * GELU_B * square))
    inner = h * (2.0 * GELU_A + 6.0 * GELU_A * GELU_B * square)
    return h * p, p * (1.0 + inner * (1.0 - p))


def sum8(x):
    return x[0:8] + x[8:16]


def body(
    n_dp,
    n_mp,
    tok_in,
    imt_in,
    ia_in,
    io_in,
    ie_in,
    ir_in,
    ca_in,
    co_in,
    we_in,
    wr_in,
    image_gains,
    attend_bias,
    output_bias,
    expand_bias,
    reduce_bias,
    norm_gains,
    norm_shifts,
    log_scale,
    cap,
    red,
    gt,
    sgo,
    W,
    IW,
    TOK,
    imt,
    N1,
    QKV,
    PR,
    MIX,
    RES,
    N2,
    GP,
    PA,
    PB,
    ACC,
    GRL,
    GT,
    IP,
    EMB,
    MSG,
    STATS,
    SBL,
    SB,
    HM3,
    BM,
    HM4,
    POOL,
    EL,
    GPL,
    GA,
    RCORE,
    RB1,
    RB2,
    RZ,
    XR,
    XST,
    SG,
    SGR,
    gz_s,
    gz_r,
    ga_s,
    ga_r,
    loc_sem,
    ca_sem,
    iw_sem,
    imt_sem,
    tok_sem,
    sb_s,
    sb_r,
    emb_s,
    emb_r,
    st_s,
    st_r,
    stx_s,
    stx_r,
    rs_s,
    rs_r,
    ag_s,
    ag_r,
    xr_s,
    xr_r,
    sg_s,
    sg_r,
    gt_s,
    gt_r,
    out_sem,
    pb_s,
    pb_r,
):
    d = lax.axis_index("dp")
    m = lax.axis_index("mp")
    n_all = n_dp * n_mp
    me = d * n_mp + m
    bits = n_dp.bit_length() - 1
    extra = bits - 3
    images, image_len = imt.shape[0], imt.shape[1]
    rows = TOK.shape[0] * LEN
    n_cap = TOK.shape[0]
    n_blocks = rows // BLOCK
    width = RES.shape[1]
    shard = QKV.shape[3]
    image_rows = images * 64
    t_all = EMB.shape[0] * 8
    total_images = images * n_all
    total_captions = n_cap * 2 * n_dp

    def bit(v, b):
        return lax.rem(v // (1 << b), 2)

    def flip(v, b):
        return v + (1 - 2 * bit(v, b)) * (1 << b)

    cb, xb, yb = bit(d, 0), bit(d, 1), bit(d, 2)
    half = lax.rem(m, 2)
    pair = flip(m, 0)
    p_a = cb * 4 + yb * 2 + xb
    p_b = 8 + cb * 4 + xb * 2 + yb
    core_dev = (flip(d, 0), m)
    x_dev = (flip(d, 1), m)
    y_dev = (flip(d, 2), m)
    pair_dev = (d, pair)
    sends = []

    def remote(src, dst, ss, rs, dev):
        copy = pltpu.make_async_remote_copy(
            src_ref=src,
            dst_ref=dst,
            send_sem=ss,
            recv_sem=rs,
            device_id=dev,
            device_id_type=pl.DeviceIdType.MESH,
        )
        copy.start()
        sends.append(copy)
        return copy

    def local(src, dst, sem):
        copy = pltpu.make_async_copy(src, dst, sem)
        copy.start()
        return copy

    barrier = pltpu.get_barrier_semaphore()

    low = lax.rem(d, 8)
    slot = low * 2 + half

    def near_device(k):
        q = lax.rem(slot + k, 16)
        return (d - low + q // 2, m - half + lax.rem(q, 2))

    def greet(k, carry):
        pl.semaphore_signal(
            barrier, inc=1, device_id=near_device(k), device_id_type=pl.DeviceIdType.MESH
        )
        return carry

    far = flip(m, 1)
    far_pair = flip(pair, 1)
    others = [(d, far), (d, far_pair)] + [(flip(d, 3 + x), m) for x in range(extra)]
    for dev in others:
        pl.semaphore_signal(barrier, inc=1, device_id=dev, device_id_type=pl.DeviceIdType.MESH)
    lax.fori_loop(1, 16, greet, 0)

    image_loads = {}

    def load_image(i):
        if i < 3:
            src, slot = ia_in.at[i], i
        elif i == 3:
            src, slot = io_in, 3
        elif i < 8:
            src, slot = ie_in.at[:, pl.ds((i - 4) * width, width)], i
        else:
            src, slot = ir_in.at[pl.ds((i - 8) * width, width)], i - 8
        image_loads[i] = local(src, IW.at[slot], iw_sem.at[i])

    ca_copies = [
        local(ca_in.at[j], W.at[0, m, pl.ds(shard * j, shard)], ca_sem.at[j]) for j in range(3)
    ]
    own_loads = [local(co_in, W.at[0, m, pl.ds(3 * shard, shard)], loc_sem.at[0])]
    SBL[...] = jnp.zeros_like(SBL)
    SBL[0:1, 0:shard] = attend_bias[0:1, :]
    SBL[2:3, 0:shard] = attend_bias[1:2, :]
    SBL[3:4, :] = expand_bias[...].reshape(1, width)
    SB[m] = SBL[...]
    for copy in ca_copies + own_loads[0:1]:
        copy.wait()
    pl.semaphore_wait(barrier, 15 + len(others))

    hops = (1, 2, 3)

    def partner(k):
        other = flip(m, 0) if k % 2 else m
        return flip(other, 1) if k >= 2 else other

    zc, ac = {}, {}
    sources = (W.at[0, m], we_in, wr_in)

    def span(p, n):
        return pl.ds(pl.multiple_of(p * PIECE, 16), n * PIECE)

    def gather_z(g, ks=(1, 2, 3)):
        for k in ks:
            dev = (d, partner(k))
            for ab, p in ((0, p_a), (1, p_b)):
                zc[g, k, ab] = remote(
                    sources[g].at[span(p, 1)],
                    W.at[g, m, span(p, 1)],
                    gz_s.at[g, k - 1, ab],
                    gz_r.at[g, k - 1, ab],
                    dev,
                )

    def spread(at, stage, ab, ss, rs):
        if stage == 0:
            p, n, dev = ((p_a, 1, x_dev), (p_b, 1, y_dev))[ab]
        elif stage == 1:
            p, n, dev = ((cb * 4 + yb * 2, 2, y_dev), (8 + cb * 4 + xb * 2, 2, x_dev))[ab]
        else:
            p, n, dev = 8 * ab + cb * 4, 4, core_dev
        return remote(at(p, n), at(p, n), ss.at[stage, ab], rs.at[stage, ab], dev)

    def gather_start(g, stage, ks=(1, 2, 3)):
        for k in ks:
            source = partner(k)
            for ab in range(2):
                (zc[g, k, ab] if stage == 0 else ac[g, stage - 1, k, ab]).wait_recv()
                ac[g, stage, k, ab] = spread(
                    lambda p, n: W.at[g, source, span(p, n)],
                    stage,
                    ab,
                    ga_s.at[g, k - 1],
                    ga_r.at[g, k - 1],
                )

    def gather_end(g, ks=(1, 2, 3)):
        for k in ks:
            for ab in range(2):
                ac[g, 2, k, ab].wait_recv()
        if g > 0 and 1 in ks:
            own_loads[g].wait()

    def tick(place):
        for g, stage, ks in PLAN.get(place, ()):
            if stage < 0:
                gather_z(g, ks)
            else:
                gather_start(g, stage, ks)

    gather_z(0)
    sb_copies = []
    for k in hops:
        sb_copies.append(
            remote(
                SBL,
                SB.at[m],
                sb_s.at[k - 1],
                sb_r.at[k - 1],
                (d, partner(k)),
            )
        )
    imt_copy = local(imt_in, imt, imt_sem)
    for i in range(3):
        load_image(i)
    tok_copy = local(tok_in.at[pl.ds(half * n_cap, n_cap)], TOK, tok_sem)
    for i in range(3, 8):
        load_image(i)
    own_loads.append(local(we_in, W.at[1, m], loc_sem.at[1]))
    own_loads.append(local(wr_in, W.at[2, m], loc_sem.at[2]))
    query = iota((BLOCK, 3 * BLOCK), 1)
    query = query - jnp.where(query >= 2 * BLOCK, 2 * BLOCK, jnp.where(query >= BLOCK, BLOCK, 0))
    BM[...] = jnp.where((iota((BLOCK, 3 * BLOCK), 0) >> 4) == (query >> 4), 0.0, FAR)
    lane_shard = iota((BLOCK, shard), 1) >> 6
    for h in range(3):
        at = slice(h * BLOCK, (h + 1) * BLOCK)
        HM3[at, :] = jnp.where(lane_shard == h, 1.0, 0.0).astype(LOW)
    lane_four = iota((64, 256), 1) >> 6
    for h in range(4):
        HM4[64 * h : 64 * h + 64, :] = jnp.where(lane_four == h, 1.0, 0.0).astype(LOW)
    POOL[...] = jnp.where((iota(POOL.shape, 1) >> 4) == iota(POOL.shape, 0), 1.0, 0.0).astype(LOW)
    RES[pl.ds(0, image_rows), :] = jnp.zeros((image_rows, width), F32)
    GP[3, pl.ds(0, image_rows), :] = jnp.zeros((image_rows, width), LOW)
    gain_one = image_gains[0:1, :]
    gain_two = image_gains[1:2, :]

    def image_norm(i, carry):
        x = imt[i].astype(F32)
        at = pl.multiple_of(i * 64, 64)
        RES[pl.ds(at, image_len), :] = x
        GP[3, pl.ds(at, image_len), :] = (standard(x)[0] * gain_one).astype(LOW)
        return carry

    imt_copy.wait()
    lax.fori_loop(0, images, image_norm, 0)
    for i in range(3):
        image_loads[i].wait()

    def image_qkv(j, carry):
        GP[j, pl.ds(0, image_rows), :] = dot(
            GP[3, pl.ds(0, image_rows), :], IW[j]
        ).astype(LOW)
        return carry

    lax.fori_loop(0, 3, image_qkv, 0)
    for i in range(8, 11):
        load_image(i)
    tick(1)

    key_valid = jnp.where(iota((256, 64), 1) < image_len, 0.0, FAR)
    lane_head = iota((64, 256), 1) >> 6

    def image_attention(i, carry):
        at = pl.multiple_of(i * 64, 64)
        for n in range(width // 256):
            lanes = slice(256 * n, 256 * n + 256)
            q = GP[0, pl.ds(at, 64), lanes]
            k = GP[1, pl.ds(at, 64), lanes]
            v = GP[2, pl.ds(at, 64), lanes]
            logits = dot_nt(jnp.concatenate([q] * 4, axis=0) * HM4[...], k) * 0.125 + key_valid
            expos = jnp.exp(logits - jnp.max(logits, axis=-1, keepdims=True))
            probs = (expos * (1.0 / jnp.sum(expos, axis=-1, keepdims=True))).astype(LOW)
            o = dot(probs, v)
            mix = jnp.where(
                lane_head < 2,
                jnp.where(lane_head == 0, o[0:64], o[64:128]),
                jnp.where(lane_head == 2, o[128:192], o[192:256]),
            )
            N2[pl.ds(at, 64), lanes] = mix.astype(LOW)
        return carry

    lax.fori_loop(0, images, image_attention, 0)
    tick(2)
    image_loads[3].wait()

    def image_out(n, carry):
        lanes = pl.ds(pl.multiple_of(n * 256, 256), 256)
        RES[pl.ds(0, image_rows), lanes] += dot(
            N2[pl.ds(0, image_rows), :], IW[3, :, lanes]
        )
        return carry

    lax.fori_loop(0, width // 256, image_out, 0)
    load_image(11)

    def image_norm_two(t, carry):
        at = pl.ds(pl.multiple_of(t * 16, 16), 16)
        GP[3, at, :] = (standard(RES[at, :])[0] * gain_two).astype(LOW)
        return carry

    lax.fori_loop(0, image_rows // 16, image_norm_two, 0, unroll=4)
    IP[...] = jnp.zeros_like(IP)
    for i in range(images):
        IP[i : i + 1, :] = jnp.sum(RES[64 * i : 64 * i + image_len, :], axis=0, keepdims=True) * (
            1.0 / image_len
        )
    image_pool = jnp.where(
        ((iota((16, image_rows), 1) >> 6) == iota((16, image_rows), 0))
        & ((iota((16, image_rows), 1) & 63) < image_len),
        1.0,
        0.0,
    ).astype(LOW)
    for i in range(4, 12):
        image_loads[i].wait()

    def image_feed(u, carry):
        ACC[pl.ds(0, image_rows), :] = dot(
            GP[3, pl.ds(0, image_rows), :], IW[4 + u]
        )

        def activate(t, inner):
            at = pl.ds(pl.multiple_of(t * 16, 16), 16)
            h = ACC[at, :]
            act = h * (0.5 + 0.5 * jnp.tanh(h * (GELU_A + GELU_A * GELU_B * (h * h))))
            N2[at, :] = act.astype(LOW)
            return inner

        lax.fori_loop(0, image_rows // 16, activate, 0, unroll=4)
        pooled = (dot(image_pool, N2[pl.ds(0, image_rows), :]) * (1.0 / image_len)).astype(LOW)
        IP[...] += dot(pooled, IW[u])
        return carry

    tick(3)
    lax.fori_loop(0, 1, image_feed, 0)
    tick(4)
    lax.fori_loop(1, 2, image_feed, 0)
    tick(5)
    lax.fori_loop(2, 3, image_feed, 0)
    tick(6)
    lax.fori_loop(3, 4, image_feed, 0)
    tick(7)
    pooled_image = IP[0:8]
    EMB[me] = (
        pooled_image
        * lax.rsqrt(jnp.sum(pooled_image * pooled_image, axis=-1, keepdims=True) + 1e-6)
    ).astype(LOW)

    shown = {}

    def show(stage, first, n, dev, at):
        run = EMB.at[pl.ds(first * n_mp, n * n_mp)]
        shown.setdefault(stage, []).append(
            remote(run, run, emb_s.at[at], emb_r.at[at], dev)
        )

    def show_embeds(stage):
        for copy in shown.get(stage - 1, ()):
            copy.wait_recv()
        if stage == 0:
            for k in hops:
                run = EMB.at[me]
                shown.setdefault(0, []).append(
                    remote(run, run, emb_s.at[k - 1], emb_r.at[k - 1], (d, partner(k)))
                )
        elif stage == 1:
            show(1, d, 1, x_dev, 3)
        elif stage == 2:
            for x in range(2):
                show(2, d + 2 * (x - xb), 1, y_dev, 4 + x)
        elif stage == 3:
            for q in range(4):
                show(3, d - low + cb + 2 * q, 1, core_dev, 6 + q)
        else:
            for x in range(extra):
                run = 8 << x
                first = d - lax.rem(d, run)
                show(4 + x, first, run, (flip(d, 3 + x), m), 10 + x)
                for copy in shown[4 + x]:
                    copy.wait_recv()

    show_embeds(0)

    tok_copy.wait()
    g1, g2 = norm_gains[0:1, :], norm_gains[1:2, :]
    b1, b2 = norm_shifts[0:1, :], norm_shifts[1:2, :]

    def norm_one(t, carry):
        at = pl.ds(pl.multiple_of(t * LEN, LEN), LEN)
        N1[at, :] = (standard(TOK[t].astype(F32))[0] * g1 + b1).astype(LOW)
        return carry

    lax.fori_loop(0, n_cap, norm_one, 0, unroll=7)
    tick(8)
    for copy in sb_copies:
        copy.wait_recv()
    gather_end(0, (1,))

    def project(near, distant):
        def one(t, carry):
            s, j = near + (t // 3) * (distant - near), lax.rem(t, 3)
            weight = W[0, s, pl.ds(pl.multiple_of(shard * j, 16), shard), :]
            QKV[j, s] = (dot_nt(N1[...], weight) + SB[s, pl.ds(j, 1), 0:shard]).astype(LOW)
            return carry

        lax.fori_loop(0, 6, one, 0)

    tick(9)
    project(m, pair)
    tick(10)
    gather_end(0, (2, 3))
    project(far, far_pair)
    tick(11)
    lane_three = iota((BLOCK, shard), 1) >> 6

    def join_heads(o):
        return jnp.where(
            lane_three == 0,
            o[0:BLOCK],
            jnp.where(lane_three == 1, o[BLOCK : 2 * BLOCK], o[2 * BLOCK : 3 * BLOCK]),
        )

    def attention(b, carry):
        at = pl.ds(pl.multiple_of(b * BLOCK, 16), BLOCK)
        loaded = [[QKV[j, s, at, :] for j in range(3)] for s in range(n_mp)]
        heads, mask = HM3[...], BM[...]
        every = []
        for q, k, v in loaded:
            logits = dot_nt(k, jnp.concatenate([q] * 3, axis=0) * heads) * 0.125 + mask
            expos = jnp.exp(logits - jnp.max(logits, axis=0, keepdims=True))
            probs = (expos * (1.0 / jnp.sum(expos, axis=0, keepdims=True))).astype(LOW)
            every.append((probs, join_heads(dot_tn(probs, v)).astype(LOW)))
        for s, (probs, mixed) in enumerate(every):
            PR[s, b] = probs
            MIX[s, at, :] = mixed
        return carry

    lax.fori_loop(0, 2, attention, 0)
    tick(12)
    lax.fori_loop(2, 4, attention, 0)
    tick(13)
    lax.fori_loop(4, n_blocks, attention, 0)
    tick(14)

    out_bias = output_bias[...].reshape(1, width)

    def attend_out(t, carry):
        start = pl.multiple_of(t * BLOCK, 16)
        rows_here = pl.ds(start, BLOCK)
        total = dot(MIX[0, rows_here, :], W[0, 0, pl.ds(3 * shard, shard), :])
        for s in range(1, n_mp):
            total += dot(MIX[s, rows_here, :], W[0, s, pl.ds(3 * shard, shard), :])
        for u in range(BLOCK // LEN):
            at = pl.ds(start + u * LEN, LEN)
            x = TOK[7 * t + u].astype(F32) + (total[u * LEN : (u + 1) * LEN] + out_bias)
            RES[at, :] = x
            N2[at, :] = (standard(x)[0] * g2 + b2).astype(LOW)
        return carry

    lax.fori_loop(0, n_blocks, attend_out, 0, unroll=True)
    tick(15)
    show_embeds(1)
    gather_end(1, (1,))

    def feed_one(s):
        bias = SB[s, 3:4, :]

        def tiles(t, carry):
            for x in range(TILES):
                first = pl.multiple_of((TILES * t + x) * BLOCK, 16)
                h = dot(N2[pl.ds(first, BLOCK), :], W[1, s])
                for u in range(BLOCK // LEN):
                    at = pl.ds(first + u * LEN, LEN)
                    act, slope = gelu_parts(h[u * LEN : (u + 1) * LEN] + bias)
                    GT[at, :] = act.astype(LOW)
                    GP[s, at, :] = slope.astype(LOW)
            return carry

        lax.fori_loop(0, n_blocks // TILES, tiles, 0)
        PA[s] = (dot(POOL[...], GT[...]) * (1.0 / LEN)).astype(LOW)

    def feed_near(i, carry):
        feed_one(m + i * (pair - m))
        return carry

    def feed_far(i, carry):
        feed_one(far + i * (far_pair - far))
        return carry

    lax.fori_loop(0, 1, feed_near, 0)
    tick(16)
    show_embeds(2)
    lax.fori_loop(1, 2, feed_near, 0)
    tick(17)
    show_embeds(3)
    gather_end(2, (1,))
    PB[0] = (dot(PA[m], W[2, m]) + dot(PA[pair], W[2, pair])).astype(LOW)
    pooled_copy = remote(PB.at[0], PB.at[1], pb_s, pb_r, (d, far))
    tick(18)

    def pool_residual(n, carry):
        lanes = pl.ds(pl.multiple_of(n * 128, 128), 128)
        res = RES[:, lanes]
        res_high = res.astype(LOW)
        res_low = (res - res_high.astype(F32)).astype(LOW)
        EL[:, lanes] = (dot(POOL[...], res_high) + dot(POOL[...], res_low)) * (1.0 / LEN)
        return carry

    lax.fori_loop(0, width // 128, pool_residual, 0)
    pooled = EL[...] + reduce_bias[...].reshape(1, width)
    pooled_copy.wait_recv()
    pooled += PB[0].astype(F32) + PB[1].astype(F32)
    inverse = lax.rsqrt(jnp.sum(pooled * pooled, axis=-1, keepdims=True) + 1e-6)
    embed = pooled * inverse
    EL[...] = embed

    show_embeds(4)
    group = min(n_all, 32)

    def embeds(c):
        part = EMB[c * group : c * group + group].astype(F32)
        return part.reshape(group * 8, width).astype(LOW)

    scaling = jnp.exp(log_scale[...].reshape(1, 1))
    embed_low = embed.astype(LOW)
    scores = scaling * jnp.concatenate(
        [dot_nt(embed_low, embeds(c)) for c in range(n_all // group)], axis=1
    )
    cap_rows = scores.shape[0]
    column = iota((cap_rows, t_all), 1)
    col_ok = (column & 7) < images
    row_ok = iota((cap_rows, t_all), 0) < n_cap
    image_id = (column >> 3) * images + (column & 7)
    cap_wide = jnp.broadcast_to(cap[...].reshape(1, 2 * n_cap).astype(F32), (cap_rows, 2 * n_cap))
    mine = iota((cap_rows, 2 * n_cap), 1) == iota((cap_rows, 2 * n_cap), 0) + half * n_cap
    cap_column = jnp.sum(jnp.where(mine, cap_wide, 0.0), axis=1, keepdims=True)
    matches = jnp.where((cap_column == image_id.astype(F32)) & col_ok & row_ok, 1.0, 0.0)
    by_row = jnp.where(col_ok, scores, FAR)
    row_top = jnp.max(by_row, axis=1, keepdims=True)
    row_lse = row_top + jnp.log(jnp.sum(jnp.exp(by_row - row_top), axis=1, keepdims=True))
    row_positive = jnp.sum(scores * matches, axis=1, keepdims=True)
    row_part = jnp.sum(
        jnp.where(iota((cap_rows, 1), 0) < n_cap, row_lse - row_positive, 0.0), axis=0, keepdims=True
    )
    by_column = jnp.where(row_ok, scores, FAR)
    top = jnp.max(by_column, axis=0, keepdims=True)
    MSG[...] = jnp.zeros_like(MSG)
    MSG[0:1, :] = top
    MSG[1:2, :] = jnp.sum(jnp.exp(by_column - top), axis=0, keepdims=True)
    MSG[2:3, :] = jnp.sum(scores * matches, axis=0, keepdims=True)
    MSG[3:4, :] = jnp.sum(matches, axis=0, keepdims=True)
    MSG[4:5, :] = jnp.broadcast_to(row_part, (1, t_all))
    STATS[slot] = MSG[...]

    def send_stats(k, carry):
        pltpu.make_async_remote_copy(
            src_ref=MSG,
            dst_ref=STATS.at[slot],
            send_sem=st_s,
            recv_sem=st_r,
            device_id=near_device(k),
            device_id_type=pl.DeviceIdType.MESH,
        ).start()
        return carry

    lax.fori_loop(1, 16, send_stats, 0)
    tick(19)
    gather_end(1, (2, 3))
    lax.fori_loop(0, 1, feed_far, 0)
    tick(20)
    lax.fori_loop(1, 2, feed_far, 0)
    pltpu.make_async_copy(STATS.at[pl.ds(0, 15)], STATS.at[pl.ds(0, 15)], st_r).wait()
    top = jnp.max(STATS[:, 0, :], axis=0, keepdims=True)
    total = jnp.sum(STATS[:, 1, :] * jnp.exp(STATS[:, 0, :] - top), axis=0, keepdims=True)
    positive = jnp.sum(STATS[:, 2, :], axis=0, keepdims=True)
    count = jnp.sum(STATS[:, 3, :], axis=0, keepdims=True)
    row_sum = jnp.sum(STATS[:, 4, :], axis=0, keepdims=True)
    for x in range(extra):
        XST[0, x] = jnp.concatenate(
            [top, total, positive, count, row_sum, jnp.zeros((3, t_all), F32)], axis=0
        )
        remote(
            XST.at[0, x], XST.at[1, x], stx_s.at[x], stx_r.at[x], (flip(d, 3 + x), m)
        ).wait_recv()
        other = XST[1, x]
        joined = jnp.maximum(top, other[0:1])
        total = total * jnp.exp(top - joined) + other[1:2] * jnp.exp(other[0:1] - joined)
        top = joined
        positive = positive + other[2:3]
        count = count + other[3:4]
        row_sum = row_sum + other[4:5]
    ok = col_ok[0:1]
    count = jnp.where(ok, count, 1.0)
    col_lse = top + jnp.log(total)
    column_part = jnp.sum(
        jnp.where(ok, col_lse - positive / count, 0.0), axis=1, keepdims=True
    )
    loss = 0.5 * (row_sum[:, 0:1] * (1.0 / total_captions) + column_part * (1.0 / total_images))
    weight = 0.5 * total_captions / total_images
    grad_scores = 0.5 * (jnp.exp(by_row - row_lse) - matches) + weight * (
        jnp.exp(by_column - col_lse) - matches * (1.0 / count)
    )
    grad_scores = jnp.where(col_ok & row_ok, grad_scores, 0.0)
    grad_log = jnp.sum(
        jnp.sum(grad_scores * scores, axis=1, keepdims=True), axis=0, keepdims=True
    )
    embed = EL[...]
    grad_cosine = (scaling * grad_scores).astype(LOW)
    grad_embed = dot(grad_cosine[:, 0 : group * 8], embeds(0))
    for c in range(1, n_all // group):
        grad_embed += dot(grad_cosine[:, c * group * 8 : (c + 1) * group * 8], embeds(c))
    grad_pooled = (
        grad_embed - embed * jnp.sum(embed * grad_embed, axis=-1, keepdims=True)
    ) * inverse
    SG[0] = jnp.zeros(SG.shape[1:], F32)
    SG[0, 13:14, :] = jnp.sum(grad_pooled, axis=0, keepdims=True)
    SG[0, 18:19, :] = jnp.broadcast_to(grad_log, (1, width))
    GPL[0] = grad_pooled.astype(LOW)
    grad_rows = grad_pooled * (1.0 / LEN)
    EL[...] = grad_rows
    GPL[1] = grad_rows.astype(LOW)

    def part(g, i):
        return IW.at[2 * g + i]

    places = (4, 7, 6)

    def whole(g):
        return IW.at[places[g]]

    def settle(copies):
        for copy in copies:
            copy.wait_send()
        sends[:] = [other for other in sends if all(other is not copy for copy in copies)]

    state = {}
    stores = []
    axis_one = ((yb, y_dev), (xb, x_dev))
    axis_two = ((xb, x_dev), (yb, y_dev))
    own = (p_a, p_b)

    def scatter(g, stage, i, ab):
        bit_one, dev_one = axis_one[ab]
        bit_two, dev_two = axis_two[ab]
        run = 8 * ab + 4 * cb + 2 * bit_one
        if stage == 0:
            p, n, dst, dev = 8 * ab + 4 * (1 - cb), 4, RCORE.at[g % 2, i, ab], core_dev
        elif stage == 1:
            p, n, dst, dev = 8 * ab + 4 * cb + 2 * (1 - bit_one), 2, RB1.at[g % 2, i, ab], dev_one
        elif stage == 2:
            p, n, dst, dev = run + 1 - bit_two, 1, RB2.at[g % 2, i, ab], dev_two
        else:
            p, n, dst, dev = own[ab], 1, RZ.at[g, ab], pair_dev
        k = 2 * i + ab
        state[g, stage, i, ab] = remote(
            part(g, i).at[span(p, n)], dst, rs_s.at[g, stage, k], rs_r.at[g, stage, k], dev
        )

    def add_in(g, stage, i, ab):
        state[g, stage, i, ab].wait_recv()
        run = 8 * ab + 4 * cb
        if stage == 0:
            at, got = span(run, 4), RCORE[g % 2, i, ab]
        elif stage == 1:
            at, got = span(run + 2 * axis_one[ab][0], 2), RB1[g % 2, i, ab]
        else:
            at, got = span(own[ab], 1), RB2[g % 2, i, ab]
        IW[2 * g + i, at, :] = IW[2 * g + i, at, :] + got

    def pass_on(g, ab, k, across_one, across_two, dev):
        bit_one = axis_one[ab][0] + across_one * (1 - 2 * axis_one[ab][0])
        bit_two = axis_two[ab][0] + across_two * (1 - 2 * axis_two[ab][0])
        run = whole(g).at[span(8 * ab + 4 * cb + 2 * bit_one + bit_two, 1)]
        state[g, "back", k, ab] = remote(run, run, ag_s.at[g, k, ab], ag_r.at[g, k, ab], dev)

    def gather_back(g, stage, ab):
        dev_one, dev_two = axis_one[ab][1], axis_two[ab][1]
        if stage == 0:
            pass_on(g, ab, 0, 0, 0, dev_two)
            pass_on(g, ab, 1, 0, 0, dev_one)
            pass_on(g, ab, 2, 0, 0, core_dev)
        elif stage == 1:
            state[g, "back", 0, ab].wait_recv()
            pass_on(g, ab, 3, 0, 1, dev_one)
            pass_on(g, ab, 4, 0, 1, core_dev)
        elif stage == 2:
            state[g, "back", 1, ab].wait_recv()
            pass_on(g, ab, 5, 1, 0, core_dev)
            state[g, "back", 3, ab].wait_recv()
            pass_on(g, ab, 6, 1, 1, core_dev)
        else:
            for k in (2, 4, 5, 6):
                state[g, "back", k, ab].wait_recv()

    def reduce_start(g, ab):
        if g == 0:
            settle([state.pop((2, a, i, ab)) for a in range(4) for i in range(2) if (2, a, i, ab) in state])
        for i in (1, 0):
            scatter(g, 0, i, ab)

    def reduce_step(g, step, half_of=None):
        if step == 0:
            for ab in range(2):
                reduce_start(g, ab)
        elif step < 4:
            halves = (half_of,) if half_of is not None else (0, 1)
            for i in (1, 0):
                for ab in halves:
                    add_in(g, step - 1, i, ab)
                    if step < 3 or i == 1:
                        scatter(g, step, i, ab)
        elif step == 4:
            for ab in range(2):
                state[g, 3, 1, ab].wait_recv()
                at = span(own[ab], 1)
                IW[places[g], at, :] = IW[2 * g, at, :] + RZ[g, ab]
                for x in range(extra):
                    copy = remote(
                        whole(g).at[at],
                        XR.at[g % 2, x, ab],
                        xr_s.at[g, x, ab],
                        xr_r.at[g, x, ab],
                        (flip(d, 3 + x), m),
                    )
                    copy.wait_recv()
                    settle([copy])
                    IW[places[g], at, :] = IW[places[g], at, :] + XR[g % 2, x, ab]
                gather_back(g, 0, ab)
        elif step < 7:
            for ab in range(2):
                gather_back(g, step - 4, ab)
        else:
            for ab in range(2):
                gather_back(g, 3, ab)
            stores.append(local(whole(g), red.at[g], out_sem.at[g]))

    def back_tick(place):
        for entry in RPLAN.get(place, ()):
            reduce_step(*entry)

    shards = (m, pair)
    for i in range(2):
        IW[4 + i] = dot_tn(PA[shards[i]], GPL[0]).astype(LOW)

    back_tick(0)

    def grad_activation(near, distant):
        for s in (near, distant):
            GA[s] = dot_nt(GPL[1], W[2, s])

    ones = jnp.ones((16, rows), LOW)

    def grad_hidden(near, distant):
        def one(k, carry):
            s = near + k * (distant - near)

            def scale(t, inner):
                at = pl.ds(pl.multiple_of(t * LEN, LEN), LEN)
                GP[s, at, :] = (GP[s, at, :].astype(F32) * GA[s, pl.ds(t, 1), :]).astype(LOW)
                return inner

            lax.fori_loop(0, n_cap, scale, 0, unroll=7)
            SG[0, pl.ds(8 + s, 1), :] = dot(ones, GP[s])[0:1]
            return carry

        lax.fori_loop(0, 2, one, 0)

    grad_activation(m, pair)
    back_tick(1)
    tick(21)
    grad_hidden(m, pair)
    back_tick(2)
    tick(22)

    def expand_gradient(i, carry):
        s = m + i * (pair - m)
        IW[2 + i] = dot_tn(N2[...], GP[s]).astype(LOW)
        return carry

    lax.fori_loop(0, 2, expand_gradient, 0)
    back_tick(4)
    tick(23)
    gather_end(2, (2, 3))
    grad_activation(far, far_pair)
    back_tick(3)
    grad_hidden(far, far_pair)
    back_tick(5)

    def grad_norm_two(n, carry):
        p = pl.ds(pl.multiple_of(n * 384, 128), 384)
        total = dot_nt(
            jnp.concatenate([GP[s] for s in range(n_mp)], axis=1),
            jnp.concatenate([W[1, s, p, :] for s in range(n_mp)], axis=1),
        )
        ACC[:, pl.ds(pl.multiple_of(n * 384, 128), 384)] = total
        return carry

    lax.fori_loop(0, 2, grad_norm_two, 0)
    back_tick(6)

    def norm_back(e, gain, x):
        xhat, scale = standard(x)
        eg = e * gain
        c1 = jnp.sum(eg, axis=-1, keepdims=True) * (1.0 / width)
        c2 = jnp.sum(eg * xhat, axis=-1, keepdims=True) * (1.0 / width)
        return (eg - c1 - xhat * c2) * scale, sum8(e * xhat), sum8(e)

    zero8 = jnp.zeros((8, width), F32)

    def back_two(t, carry):
        dg, db, do = carry
        found = []
        for u in range(7):
            at = pl.ds(pl.multiple_of((7 * t + u) * LEN, LEN), LEN)
            dv, one, two = norm_back(ACC[at, :], g2, RES[at, :])
            g = EL[pl.ds(7 * t + u, 1), :] + dv
            found.append((at, g))
            dg, db, do = dg + one, db + two, do + sum8(g)
        for at, g in found:
            RES[at, :] = g
            GRL[at, :] = g.astype(LOW)
        return dg, db, do

    dg, db, do = lax.fori_loop(0, n_cap // 7, back_two, (zero8, zero8, zero8))
    SG[0, 15:16, :] = jnp.sum(dg, axis=0, keepdims=True)
    SG[0, 17:18, :] = jnp.sum(db, axis=0, keepdims=True)
    SG[0, 12:13, :] = jnp.sum(do, axis=0, keepdims=True)

    back_tick(7)
    for i in range(2):
        IW[i, 3 * shard : 4 * shard, :] = dot_tn(MIX[shards[i]], GRL[...]).astype(LOW)

    def grad_mixture(s, carry):
        MIX[s] = dot_nt(GRL[...], W[0, s, pl.ds(3 * shard, shard), :]).astype(LOW)
        return carry

    lax.fori_loop(0, n_mp, grad_mixture, 0)
    back_tick(8)

    def attention_back(places):
        loaded = []
        for b, s in places:
            at = pl.ds(pl.multiple_of(b * BLOCK, 16), BLOCK)
            loaded.append([QKV[j, s, at, :] for j in range(3)] + [MIX[s, at, :], PR[s, b]])
        heads = HM3[...]
        every = []
        for q, k, v, g, low_probs in loaded:
            q = jnp.concatenate([q] * 3, axis=0) * heads
            g = jnp.concatenate([g] * 3, axis=0) * heads
            probs = low_probs.astype(F32)
            grad_probs = dot_nt(v, g)
            inner = jnp.sum(grad_probs * probs, axis=0, keepdims=True)
            grad_logits = (probs * (grad_probs - inner)).astype(LOW)
            every.append(
                (
                    (join_heads(dot_tn(grad_logits, k)) * 0.125).astype(LOW),
                    (dot(grad_logits, q) * 0.125).astype(LOW),
                    dot(low_probs, g).astype(LOW),
                )
            )
        for (b, s), grads in zip(places, every):
            at = pl.ds(pl.multiple_of(b * BLOCK, 16), BLOCK)
            for j in range(3):
                QKV[j, s, at, :] = grads[j]

    def attention_back_run(first, count, shards):
        def two(t, carry):
            b = first + 2 * t
            attention_back([(b + x, s) for x in range(2) for s in shards])
            return carry

        lax.fori_loop(0, count // 2, two, 0)
        if count % 2:
            attention_back([(first + count - 1, s) for s in shards])

    def attend_gradient(j):
        def one(i, carry):
            s = m + i * (pair - m)
            IW[i, shard * j : shard * (j + 1), :] = dot_tn(QKV[j, s], N1[...]).astype(LOW)
            return carry

        lax.fori_loop(0, 2, one, 0)

    small_devs = [core_dev, y_dev, x_dev, pair_dev] + [(flip(d, 3 + x), m) for x in range(extra)]
    small = {}

    def small_start(i):
        small[i] = remote(SG.at[i], SGR.at[i], sg_s.at[i], sg_r.at[i], small_devs[i])

    def small_end(i):
        small[i].wait_recv()
        SG[i + 1] = SG[i] + SGR[i]

    small_gain, small_shift = zero8, zero8
    gt_copies = []
    cuts = (0, 4, n_blocks)
    attention_back_run(0, n_blocks, (m, pair))
    back_tick(9)
    attend_gradient(2)
    reduce_start(0, 1)
    attend_gradient(0)
    attend_gradient(1)
    reduce_start(0, 0)
    back_tick(20)
    for r in range(2):
        attention_back_run(cuts[r], cuts[r + 1] - cuts[r], (far, far_pair))
        back_tick(10 + r)
        first, last = cuts[r] * (BLOCK // LEN), cuts[r + 1] * (BLOCK // LEN)
        stripe = pl.ds(first * LEN, (last - first) * LEN)

        def last_norm(t, carry):
            dg, db = carry
            start = pl.multiple_of((first + 7 * t) * LEN, 16)
            rows_here = pl.ds(start, BLOCK)
            e = None
            for s in range(n_mp):
                for j in range(3):
                    term = dot(QKV[j, s, rows_here, :], W[0, s, pl.ds(shard * j, shard), :])
                    e = term if e is None else e + term
            for u in range(BLOCK // LEN):
                at = pl.ds(start + u * LEN, LEN)
                dv, one, two = norm_back(
                    e[u * LEN : (u + 1) * LEN], g1, TOK[first + 7 * t + u].astype(F32)
                )
                GT[at, :] = (RES[at, :] + dv).astype(LOW)
                dg, db = dg + one, db + two
            return dg, db

        small_gain, small_shift = lax.fori_loop(
            0, (last - first) // 7, last_norm, (small_gain, small_shift)
        )
        back_tick(12 + r)
        if r == 1:
            SG[0, 14:15, :] = jnp.sum(small_gain, axis=0, keepdims=True)
            SG[0, 16:17, :] = jnp.sum(small_shift, axis=0, keepdims=True)

            def bias_gradient(s, carry):
                SG[0, pl.ds(s, 1), 0:shard] = dot(ones, QKV[0, s])[0:1]
                SG[0, pl.ds(4 + s, 1), 0:shard] = dot(ones, QKV[2, s])[0:1]
                return carry

            lax.fori_loop(0, n_mp, bias_gradient, 0)
            small_start(0)
            back_tick(16)
            small_end(0)
            small_start(1)
            back_tick(17)
            small_end(1)
            small_start(2)
            back_tick(18)
            small_end(2)
            small_start(3)
        else:
            back_tick(15)
        gt_copies.append(
            remote(GT.at[stripe], gt.at[half, stripe], gt_s.at[r], gt_r.at[r], pair_dev)
        )
    stores.append(local(GT, gt.at[half], out_sem.at[3]))
    back_tick(21)
    small_end(3)
    for i in range(4, 4 + extra):
        small_start(i)
        small_end(i)
    for place in range(22, 28):
        back_tick(place)
    last = SG.shape[0] - 1
    sgo[...] = jnp.zeros_like(sgo)
    sgo[0:1, :] = SG[last, pl.ds(m, 1), :]
    sgo[1:2, :] = SG[last, pl.ds(4 + m, 1), :]
    sgo[2:3, :] = SG[last, pl.ds(8 + m, 1), :]
    sgo[3:10, :] = SG[last, 12:19, :]
    sgo[10:11, :] = jnp.broadcast_to(loss, (1, width))
    back_tick(28)
    for copy in gt_copies:
        copy.wait_recv()
    pltpu.make_async_copy(STATS.at[pl.ds(0, 15)], STATS.at[pl.ds(0, 15)], st_s).wait()
    for copy in sends:
        copy.wait_send()
    for copy in stores:
        copy.wait()


def local_step(
    n_dp,
    n_mp,
    caption_tokens,
    image_tokens,
    image_attend,
    image_output,
    image_expand,
    image_reduce,
    image_gains,
    caption_attend,
    attend_bias,
    caption_output,
    output_bias,
    caption_expand,
    expand_bias,
    caption_reduce,
    reduce_bias,
    norm_gains,
    norm_shifts,
    log_scale,
    caption_image,
):
    captions, length, width = caption_tokens.shape
    images, image_len, _ = image_tokens.shape
    shard = caption_attend.shape[2]
    units = caption_expand.shape[1]
    n_cap = captions // 2
    rows = n_cap * length
    n_blocks = rows // BLOCK
    n_all = n_dp * n_mp
    t_all = n_all * 8
    extra = n_dp.bit_length() - 1 - 3
    assert length == LEN and units == width and shard * n_mp == width and width == 16 * PIECE

    any_space = pl.BlockSpec(memory_space=pl.ANY)
    vmem = pl.BlockSpec(memory_space=pltpu.VMEM)
    nx = max(extra, 1)
    dma = pltpu.SemaphoreType.DMA
    scratch = [
        pltpu.VMEM((3, n_mp, width, width), LOW),
        pltpu.VMEM((8, width, width), LOW),
        pltpu.VMEM((n_cap, length, width), LOW),
        pltpu.VMEM((images, image_len, width), LOW),
        pltpu.VMEM((rows, width), LOW),
        pltpu.VMEM((3, n_mp, rows, shard), LOW),
        pltpu.VMEM((n_mp, n_blocks, BLOCK, 3 * BLOCK), LOW),
        pltpu.VMEM((n_mp, rows, shard), LOW),
        pltpu.VMEM((rows, width), F32),
        pltpu.VMEM((rows, width), LOW),
        pltpu.VMEM((n_mp, rows, width), LOW),
        pltpu.VMEM((n_mp, 64, width), LOW),
        pltpu.VMEM((2, 64, width), LOW),
        pltpu.VMEM((rows, width), F32),
        pltpu.VMEM((rows, width), LOW),
        pltpu.VMEM((rows, width), LOW),
        pltpu.VMEM((16, width), F32),
        pltpu.VMEM((n_all, 8, width), LOW),
        pltpu.VMEM((8, t_all), F32),
        pltpu.VMEM((16, 8, t_all), F32),
        pltpu.VMEM((8, width), F32),
        pltpu.VMEM((n_mp, 8, width), F32),
        pltpu.VMEM((3 * BLOCK, shard), LOW),
        pltpu.VMEM((BLOCK, 3 * BLOCK), F32),
        pltpu.VMEM((256, 256), LOW),
        pltpu.VMEM((64, rows), LOW),
        pltpu.VMEM((64, width), F32),
        pltpu.VMEM((2, 64, width), LOW),
        pltpu.VMEM((n_mp, 64, width), F32),
        pltpu.VMEM((2, 2, 2, 4 * PIECE, width), LOW),
        pltpu.VMEM((2, 2, 2, 2 * PIECE, width), LOW),
        pltpu.VMEM((2, 2, 2, PIECE, width), LOW),
        pltpu.VMEM((3, 2, PIECE, width), LOW),
        pltpu.VMEM((2, nx, 2, PIECE, width), LOW),
        pltpu.VMEM((2, nx, 8, t_all), F32),
        pltpu.VMEM((5 + extra, 24, width), F32),
        pltpu.VMEM((4 + extra, 24, width), F32),
        dma((3, 3, 2)),
        dma((3, 3, 2)),
        dma((3, 3, 3, 2)),
        dma((3, 3, 3, 2)),
        dma((3,)),
        dma((3,)),
        dma((12,)),
        dma,
        dma,
        dma((3,)),
        dma((3,)),
        dma((10 + nx,)),
        dma((10 + nx,)),
        dma,
        dma,
        dma((nx,)),
        dma((nx,)),
        dma((3, 4, 4)),
        dma((3, 4, 4)),
        dma((3, 7, 2)),
        dma((3, 7, 2)),
        dma((3, nx, 2)),
        dma((3, nx, 2)),
        dma((4 + extra,)),
        dma((4 + extra,)),
        dma((3,)),
        dma((3,)),
        dma((4,)),
        dma,
        dma,
    ]
    red, gt, sgo = pl.pallas_call(
        functools.partial(body, n_dp, n_mp),
        out_shape=(
            jax.ShapeDtypeStruct((3, width, width), LOW),
            jax.ShapeDtypeStruct((2, rows, width), LOW),
            jax.ShapeDtypeStruct((16, width), F32),
        ),
        in_specs=[any_space] * 10 + [vmem] * 9,
        out_specs=(any_space, any_space, vmem),
        scratch_shapes=scratch,
        compiler_params=pltpu.CompilerParams(
            collective_id=0, has_side_effects=True, vmem_limit_bytes=66_000_000
        ),
        name="step",
    )(
        caption_tokens,
        image_tokens,
        image_attend,
        image_output,
        image_expand,
        image_reduce,
        jnp.swapaxes(caption_attend, 1, 2),
        caption_output,
        caption_expand,
        caption_reduce,
        image_gains,
        attend_bias,
        output_bias,
        expand_bias,
        reduce_bias,
        norm_gains,
        norm_shifts,
        log_scale,
        caption_image,
    )
    shapes = (
        (1,),
        (captions, length, width),
        (3, shard, width),
        (2, shard),
        (shard, width),
        (width,),
        (width, units),
        (units,),
        (units, width),
        (width,),
        (2, width),
        (2, width),
        (1,),
    )
    large = (1, 2, 4, 6, 8)
    parts = 7
    grads = pl.pallas_call(
        finish,
        out_shape=tuple(jax.ShapeDtypeStruct(shape, F32) for shape in shapes),
        in_specs=[any_space, any_space, vmem],
        out_specs=tuple(any_space if i in large else vmem for i in range(len(shapes))),
        scratch_shapes=[
            pltpu.VMEM((captions, length, width), LOW),
            pltpu.VMEM((captions, length, width), F32),
            pltpu.VMEM((3, width, width), LOW),
            pltpu.VMEM((3, width, width), F32),
            pltpu.VMEM((3, shard, width), F32),
            dma((parts,)),
            dma((parts,)),
            dma((3,)),
            dma((6,)),
        ],
        compiler_params=pltpu.CompilerParams(vmem_limit_bytes=64_000_000),
        name="finish",
    )(red, gt.reshape(captions, length, width), sgo)
    return (*grads[:2], jnp.swapaxes(grads[2], 1, 2), *grads[3:])


def finish(
    red,
    gt,
    small,
    loss,
    tokens,
    attend,
    attend_bias,
    output,
    output_bias,
    expand,
    expand_bias,
    reduce,
    reduce_bias,
    gains,
    shifts,
    log_scale,
    GT,
    TOKENS,
    RED,
    WIDE,
    ATTEND,
    gt_in,
    gt_out,
    red_in,
    red_out,
):
    def copy(src, dst, sem):
        made = pltpu.make_async_copy(src, dst, sem)
        made.start()
        return made

    parts = gt_in.shape[0]
    size = GT.shape[0] // parts
    width = GT.shape[2]
    shard = ATTEND.shape[1]
    order = (0, 1, 2)
    weights = {g: copy(red.at[g], RED.at[g], red_in.at[g]) for g in order}
    pieces = [
        copy(gt.at[pl.ds(i * size, size)], GT.at[pl.ds(i * size, size)], gt_in.at[i])
        for i in range(parts)
    ]
    written = []
    loss[...] = small[10:11, 0:1].reshape(1)
    attend_bias[...] = small[0:2, 0:shard]
    expand_bias[...] = small[2:3, :].reshape(width)
    output_bias[...] = small[3:4, :].reshape(width)
    reduce_bias[...] = small[4:5, :].reshape(width)
    gains[...] = small[5:7, :]
    shifts[...] = small[7:9, :]
    log_scale[...] = small[9:10, 0:1].reshape(1)
    for g in order:
        weights[g].wait()
        if g == 0:
            for j in range(3):
                ATTEND[j] = RED[0, shard * j : shard * (j + 1), :].astype(F32)
                written.append(copy(ATTEND.at[j], attend.at[j], red_out.at[j]))
            WIDE[0, 3 * shard :, :] = RED[0, 3 * shard :, :].astype(F32)
            written.append(copy(WIDE.at[0, pl.ds(3 * shard, shard)], output, red_out.at[3]))
        else:

            def widen(t, carry):
                at = pl.ds(pl.multiple_of(t * 96, 96), 96)
                WIDE[g, at, :] = RED[g, at, :].astype(F32)
                return carry

            lax.fori_loop(0, width // 96, widen, 0)
            written.append(copy(WIDE.at[g], (expand, reduce)[g - 1], red_out.at[3 + g]))
    for i in range(parts):
        pieces[i].wait()
        at = slice(i * size, i * size + size)
        TOKENS[at] = GT[at].astype(F32)
        written.append(
            copy(
                TOKENS.at[pl.ds(i * size, size)], tokens.at[pl.ds(i * size, size)], gt_out.at[i]
            )
        )
    for made in written:
        made.wait()


def solution(mesh):
    in_specs = (
        P("dp", None, None),
        P(("dp", "mp"), None, None),
        P(),
        P(),
        P(),
        P(),
        P(),
        P(None, None, "mp"),
        P(None, "mp"),
        P("mp", None),
        P(),
        P(None, "mp"),
        P("mp"),
        P("mp", None),
        P(),
        P(),
        P(),
        P(),
        P("dp"),
    )
    out_specs = (
        P(),
        P("dp", None, None),
        P(None, None, "mp"),
        P(None, "mp"),
        P("mp", None),
        P(),
        P(None, "mp"),
        P("mp"),
        P("mp", None),
        P(),
        P(),
        P(),
        P(),
    )
    step = functools.partial(local_step, mesh.shape["dp"], mesh.shape["mp"])
    return jax.shard_map(step, mesh=mesh, in_specs=in_specs, out_specs=out_specs, check_vma=False)
```

```python
import functools

import jax
import jax.numpy as jnp
from jax import lax
from jax.experimental import pallas as pl
from jax.experimental.pallas import tpu as pltpu
from jax.sharding import PartitionSpec as P

HEAD_DIM = 64
LEN = 16
PIECE = 48
BLOCK = 112
F32 = jnp.float32
LOW = jnp.bfloat16
FAR = -1e30
ALL_HOPS = (1, 2, 3)
TILES = 7
RPLAN = {
    0: ((2, 0),),
    2: ((2, 1),),
    4: ((1, 0),),
    5: ((2, 2), (1, 1),),
    6: ((2, 3),),
    8: ((2, 4),),
    9: ((1, 2),),
    20: ((1, 3),),
    10: ((0, 1),),
    15: ((1, 4),),
    13: ((2, 5),),
    11: ((0, 2),),
    16: ((0, 3),),
    17: ((2, 6),),
    18: ((1, 5),),
    21: ((0, 4),),
    22: ((1, 6), (2, 7),),
    23: ((0, 5),),
    25: ((1, 7),),
    26: ((0, 6),),
    28: ((0, 7),),
}
PLAN = {
    1: ((0, 0, (1,)),),
    2: ((0, 0, (2, 3)), (1, -1, (1,)), (2, -1, (1,)),),
    3: ((0, 1, (1, 2)), (1, -1, (2, 3)), (2, -1, (2, 3)),),
    4: ((0, 2, (1,)),),
    5: ((0, 1, (3,)),),
    7: ((0, 2, (2,)), (0, 2, (3,)), (1, 0, (1,)), (2, 0, (1,)),),
    10: ((1, 1, (1,)), (2, 1, (1,)),),
    12: ((1, 2, (1,)), (2, 2, (1,)),),
    13: ((1, 0, (2, 3)),),
    14: ((1, 1, (2, 3)),),
    16: ((1, 2, (2, 3)),),
    17: ((2, 0, (2, 3)),),
    20: ((2, 1, (2, 3)),),
    22: ((2, 2, (2, 3)),),
}
GELU_A = 0.7978845608028654
GELU_B = 0.044715


def dot(a, b):
    return lax.dot_general(a, b, (((1,), (0,)), ((), ())), preferred_element_type=F32)


def dot_nt(a, b):
    return lax.dot_general(a, b, (((1,), (1,)), ((), ())), preferred_element_type=F32)


def dot_tn(a, b):
    return lax.dot_general(a, b, (((0,), (0,)), ((), ())), preferred_element_type=F32)


def iota(shape, axis):
    return lax.broadcasted_iota(jnp.int32, shape, axis)


def standard(x):
    width = x.shape[-1]
    centred = x - jnp.sum(x, axis=-1, keepdims=True) * (1.0 / width)
    variance = jnp.sum(centred * centred, axis=-1, keepdims=True) * (1.0 / width)
    scale = lax.rsqrt(variance + 1e-6)
    return centred * scale, scale


def gelu_parts(h):
    square = h * h
    p = 0.5 + 0.5 * jnp.tanh(h * (GELU_A + GELU_A * GELU_B * square))
    inner = h * (2.0 * GELU_A + 6.0 * GELU_A * GELU_B * square)
    return h * p, p * (1.0 + inner * (1.0 - p))


def sum8(x):
    return x[0:8] + x[8:16]


def body(
    n_dp,
    n_mp,
    tok_in,
    imt_in,
    ia_in,
    io_in,
    ie_in,
    ir_in,
    ca_in,
    co_in,
    we_in,
    wr_in,
    image_gains,
    attend_bias,
    output_bias,
    expand_bias,
    reduce_bias,
    norm_gains,
    norm_shifts,
    log_scale,
    cap,
    red,
    gt,
    sgo,
    W,
    IW,
    TOK,
    imt,
    N1,
    QKV,
    PR,
    MIX,
    RES,
    N2,
    GP,
    PA,
    PB,
    ACC,
    GRL,
    GT,
    IP,
    EMB,
    MSG,
    STATS,
    SBL,
    SB,
    HM3,
    BM,
    HM4,
    POOL,
    EL,
    GPL,
    GA,
    RCORE,
    RB1,
    RB2,
    RZ,
    XR,
    XST,
    SG,
    SGR,
    gz_s,
    gz_r,
    ga_s,
    ga_r,
    loc_sem,
    ca_sem,
    iw_sem,
    imt_sem,
    tok_sem,
    sb_s,
    sb_r,
    emb_s,
    emb_r,
    st_s,
    st_r,
    stx_s,
    stx_r,
    rs_s,
    rs_r,
    ag_s,
    ag_r,
    xr_s,
    xr_r,
    sg_s,
    sg_r,
    gt_s,
    gt_r,
    out_sem,
    pb_s,
    pb_r,
):
    d = lax.axis_index("dp")
    m = lax.axis_index("mp")
    n_all = n_dp * n_mp
    me = d * n_mp + m
    bits = n_dp.bit_length() - 1
    extra = bits - 3
    images, image_len = imt.shape[0], imt.shape[1]
    rows = TOK.shape[0] * LEN
    n_cap = TOK.shape[0]
    n_blocks = rows // BLOCK
    width = RES.shape[1]
    shard = QKV.shape[3]
    image_rows = images * 64
    t_all = EMB.shape[0] * 8
    total_images = images * n_all
    total_captions = n_cap * 2 * n_dp

    def bit(v, b):
        return lax.rem(v // (1 << b), 2)

    def flip(v, b):
        return v + (1 - 2 * bit(v, b)) * (1 << b)

    cb, xb, yb = bit(d, 0), bit(d, 1), bit(d, 2)
    half = lax.rem(m, 2)
    pair = flip(m, 0)
    p_a = cb * 4 + yb * 2 + xb
    p_b = 8 + cb * 4 + xb * 2 + yb
    core_dev = (flip(d, 0), m)
    x_dev = (flip(d, 1), m)
    y_dev = (flip(d, 2), m)
    pair_dev = (d, pair)
    sends = []

    def remote(src, dst, ss, rs, dev):
        copy = pltpu.make_async_remote_copy(
            src_ref=src,
            dst_ref=dst,
            send_sem=ss,
            recv_sem=rs,
            device_id=dev,
            device_id_type=pl.DeviceIdType.MESH,
        )
        copy.start()
        sends.append(copy)
        return copy

    def local(src, dst, sem):
        copy = pltpu.make_async_copy(src, dst, sem)
        copy.start()
        return copy

    barrier = pltpu.get_barrier_semaphore()

    low = lax.rem(d, 8)
    slot = low * 2 + half

    def near_device(k):
        q = lax.rem(slot + k, 16)
        return (d - low + q // 2, m - half + lax.rem(q, 2))

    def greet(k, carry):
        pl.semaphore_signal(
            barrier, inc=1, device_id=near_device(k), device_id_type=pl.DeviceIdType.MESH
        )
        return carry

    far = flip(m, 1)
    far_pair = flip(pair, 1)
    others = [(d, far), (d, far_pair)] + [(flip(d, 3 + x), m) for x in range(extra)]
    for dev in others:
        pl.semaphore_signal(barrier, inc=1, device_id=dev, device_id_type=pl.DeviceIdType.MESH)
    lax.fori_loop(1, 16, greet, 0)

    image_loads = {}

    def load_image(i):
        if i < 3:
            src, slot = ia_in.at[i], i
        elif i == 3:
            src, slot = io_in, 3
        elif i < 8:
            src, slot = ie_in.at[:, pl.ds((i - 4) * width, width)], i
        else:
            src, slot = ir_in.at[pl.ds((i - 8) * width, width)], i - 8
        image_loads[i] = local(src, IW.at[slot], iw_sem.at[i])

    ca_copies = [
        local(ca_in.at[j], W.at[0, m, pl.ds(shard * j, shard)], ca_sem.at[j]) for j in range(3)
    ]
    own_loads = [local(co_in, W.at[0, m, pl.ds(3 * shard, shard)], loc_sem.at[0])]
    SBL[...] = jnp.zeros_like(SBL)
    SBL[0:1, 0:shard] = attend_bias[0:1, :]
    SBL[2:3, 0:shard] = attend_bias[1:2, :]
    SBL[3:4, :] = expand_bias[...].reshape(1, width)
    SB[m] = SBL[...]
    for copy in ca_copies + own_loads[0:1]:
        copy.wait()
    pl.semaphore_wait(barrier, 15 + len(others))

    hops = (1, 2, 3)

    def partner(k):
        other = flip(m, 0) if k % 2 else m
        return flip(other, 1) if k >= 2 else other

    zc, ac = {}, {}
    sources = (W.at[0, m], we_in, wr_in)

    def span(p, n):
        return pl.ds(pl.multiple_of(p * PIECE, 16), n * PIECE)

    def gather_z(g, ks=(1, 2, 3)):
        for k in ks:
            dev = (d, partner(k))
            for ab, p in ((0, p_a), (1, p_b)):
                zc[g, k, ab] = remote(
                    sources[g].at[span(p, 1)],
                    W.at[g, m, span(p, 1)],
                    gz_s.at[g, k - 1, ab],
                    gz_r.at[g, k - 1, ab],
                    dev,
                )

    def spread(at, stage, ab, ss, rs):
        if stage == 0:
            p, n, dev = ((p_a, 1, x_dev), (p_b, 1, y_dev))[ab]
        elif stage == 1:
            p, n, dev = ((cb * 4 + yb * 2, 2, y_dev), (8 + cb * 4 + xb * 2, 2, x_dev))[ab]
        else:
            p, n, dev = 8 * ab + cb * 4, 4, core_dev
        return remote(at(p, n), at(p, n), ss.at[stage, ab], rs.at[stage, ab], dev)

    def gather_start(g, stage, ks=(1, 2, 3)):
        for k in ks:
            source = partner(k)
            for ab in range(2):
                (zc[g, k, ab] if stage == 0 else ac[g, stage - 1, k, ab]).wait_recv()
                ac[g, stage, k, ab] = spread(
                    lambda p, n: W.at[g, source, span(p, n)],
                    stage,
                    ab,
                    ga_s.at[g, k - 1],
                    ga_r.at[g, k - 1],
                )

    def gather_end(g, ks=(1, 2, 3)):
        for k in ks:
            for ab in range(2):
                ac[g, 2, k, ab].wait_recv()
        if g > 0 and 1 in ks:
            own_loads[g].wait()

    def tick(place):
        for g, stage, ks in PLAN.get(place, ()):
            if stage < 0:
                gather_z(g, ks)
            else:
                gather_start(g, stage, ks)

    gather_z(0)
    sb_copies = []
    for k in hops:
        sb_copies.append(
            remote(
                SBL,
                SB.at[m],
                sb_s.at[k - 1],
                sb_r.at[k - 1],
                (d, partner(k)),
            )
        )
    imt_copy = local(imt_in, imt, imt_sem)
    for i in range(3):
        load_image(i)
    tok_copy = local(tok_in.at[pl.ds(half * n_cap, n_cap)], TOK, tok_sem)
    for i in range(3, 8):
        load_image(i)
    own_loads.append(local(we_in, W.at[1, m], loc_sem.at[1]))
    own_loads.append(local(wr_in, W.at[2, m], loc_sem.at[2]))
    query = iota((BLOCK, 3 * BLOCK), 1)
    query = query - jnp.where(query >= 2 * BLOCK, 2 * BLOCK, jnp.where(query >= BLOCK, BLOCK, 0))
    BM[...] = jnp.where((iota((BLOCK, 3 * BLOCK), 0) >> 4) == (query >> 4), 0.0, FAR)
    lane_shard = iota((BLOCK, shard), 1) >> 6
    for h in range(3):
        at = slice(h * BLOCK, (h + 1) * BLOCK)
        HM3[at, :] = jnp.where(lane_shard == h, 1.0, 0.0).astype(LOW)
    lane_four = iota((64, 256), 1) >> 6
    for h in range(4):
        HM4[64 * h : 64 * h + 64, :] = jnp.where(lane_four == h, 1.0, 0.0).astype(LOW)
    POOL[...] = jnp.where((iota(POOL.shape, 1) >> 4) == iota(POOL.shape, 0), 1.0, 0.0).astype(LOW)
    RES[pl.ds(0, image_rows), :] = jnp.zeros((image_rows, width), F32)
    GP[3, pl.ds(0, image_rows), :] = jnp.zeros((image_rows, width), LOW)
    gain_one = image_gains[0:1, :]
    gain_two = image_gains[1:2, :]

    def image_norm(i, carry):
        x = imt[i].astype(F32)
        at = pl.multiple_of(i * 64, 64)
        RES[pl.ds(at, image_len), :] = x
        GP[3, pl.ds(at, image_len), :] = (standard(x)[0] * gain_one).astype(LOW)
        return carry

    imt_copy.wait()
    lax.fori_loop(0, images, image_norm, 0)
    for i in range(3):
        image_loads[i].wait()

    def image_qkv(j, carry):
        GP[j, pl.ds(0, image_rows), :] = dot(
            GP[3, pl.ds(0, image_rows), :], IW[j]
        ).astype(LOW)
        return carry

    lax.fori_loop(0, 3, image_qkv, 0)
    for i in range(8, 11):
        load_image(i)
    tick(1)

    key_valid = jnp.where(iota((256, 64), 1) < image_len, 0.0, FAR)
    lane_head = iota((64, 256), 1) >> 6

    def image_attention(i, carry):
        at = pl.multiple_of(i * 64, 64)
        for n in range(width // 256):
            lanes = slice(256 * n, 256 * n + 256)
            q = GP[0, pl.ds(at, 64), lanes]
            k = GP[1, pl.ds(at, 64), lanes]
            v = GP[2, pl.ds(at, 64), lanes]
            logits = dot_nt(jnp.concatenate([q] * 4, axis=0) * HM4[...], k) * 0.125 + key_valid
            expos = jnp.exp(logits - jnp.max(logits, axis=-1, keepdims=True))
            probs = (expos * (1.0 / jnp.sum(expos, axis=-1, keepdims=True))).astype(LOW)
            o = dot(probs, v)
            mix = jnp.where(
                lane_head < 2,
                jnp.where(lane_head == 0, o[0:64], o[64:128]),
                jnp.where(lane_head == 2, o[128:192], o[192:256]),
            )
            N2[pl.ds(at, 64), lanes] = mix.astype(LOW)
        return carry

    lax.fori_loop(0, images, image_attention, 0)
    tick(2)
    image_loads[3].wait()

    def image_out(n, carry):
        lanes = pl.ds(pl.multiple_of(n * 256, 256), 256)
        RES[pl.ds(0, image_rows), lanes] += dot(
            N2[pl.ds(0, image_rows), :], IW[3, :, lanes]
        )
        return carry

    lax.fori_loop(0, width // 256, image_out, 0)
    load_image(11)

    def image_norm_two(t, carry):
        at = pl.ds(pl.multiple_of(t * 16, 16), 16)
        GP[3, at, :] = (standard(RES[at, :])[0] * gain_two).astype(LOW)
        return carry

    lax.fori_loop(0, image_rows // 16, image_norm_two, 0, unroll=4)
    IP[...] = jnp.zeros_like(IP)
    for i in range(images):
        IP[i : i + 1, :] = jnp.sum(RES[64 * i : 64 * i + image_len, :], axis=0, keepdims=True) * (
            1.0 / image_len
        )
    image_pool = jnp.where(
        ((iota((16, image_rows), 1) >> 6) == iota((16, image_rows), 0))
        & ((iota((16, image_rows), 1) & 63) < image_len),
        1.0,
        0.0,
    ).astype(LOW)
    for i in range(4, 12):
        image_loads[i].wait()

    def image_feed(u, carry):
        ACC[pl.ds(0, image_rows), :] = dot(
            GP[3, pl.ds(0, image_rows), :], IW[4 + u]
        )

        def activate(t, inner):
            at = pl.ds(pl.multiple_of(t * 16, 16), 16)
            h = ACC[at, :]
            act = h * (0.5 + 0.5 * jnp.tanh(h * (GELU_A + GELU_A * GELU_B * (h * h))))
            N2[at, :] = act.astype(LOW)
            return inner

        lax.fori_loop(0, image_rows // 16, activate, 0, unroll=4)
        pooled = (dot(image_pool, N2[pl.ds(0, image_rows), :]) * (1.0 / image_len)).astype(LOW)
        IP[...] += dot(pooled, IW[u])
        return carry

    tick(3)
    lax.fori_loop(0, 1, image_feed, 0)
    tick(4)
    lax.fori_loop(1, 2, image_feed, 0)
    tick(5)
    lax.fori_loop(2, 3, image_feed, 0)
    tick(6)
    lax.fori_loop(3, 4, image_feed, 0)
    tick(7)
    pooled_image = IP[0:8]
    EMB[me] = (
        pooled_image
        * lax.rsqrt(jnp.sum(pooled_image * pooled_image, axis=-1, keepdims=True) + 1e-6)
    ).astype(LOW)

    shown = {}

    def show(stage, first, n, dev, at):
        run = EMB.at[pl.ds(first * n_mp, n * n_mp)]
        shown.setdefault(stage, []).append(
            remote(run, run, emb_s.at[at], emb_r.at[at], dev)
        )

    def show_embeds(stage):
        for copy in shown.get(stage - 1, ()):
            copy.wait_recv()
        if stage == 0:
            for k in hops:
                run = EMB.at[me]
                shown.setdefault(0, []).append(
                    remote(run, run, emb_s.at[k - 1], emb_r.at[k - 1], (d, partner(k)))
                )
        elif stage == 1:
            show(1, d, 1, x_dev, 3)
        elif stage == 2:
            for x in range(2):
                show(2, d + 2 * (x - xb), 1, y_dev, 4 + x)
        elif stage == 3:
            for q in range(4):
                show(3, d - low + cb + 2 * q, 1, core_dev, 6 + q)
        else:
            for x in range(extra):
                run = 8 << x
                first = d - lax.rem(d, run)
                show(4 + x, first, run, (flip(d, 3 + x), m), 10 + x)
                for copy in shown[4 + x]:
                    copy.wait_recv()

    show_embeds(0)

    tok_copy.wait()
    g1, g2 = norm_gains[0:1, :], norm_gains[1:2, :]
    b1, b2 = norm_shifts[0:1, :], norm_shifts[1:2, :]

    def norm_one(t, carry):
        at = pl.ds(pl.multiple_of(t * LEN, LEN), LEN)
        N1[at, :] = (standard(TOK[t].astype(F32))[0] * g1 + b1).astype(LOW)
        return carry

    lax.fori_loop(0, n_cap, norm_one, 0, unroll=7)
    tick(8)
    for copy in sb_copies:
        copy.wait_recv()
    gather_end(0, (1,))

    def project(near, distant):
        def one(t, carry):
            s, j = near + (t // 3) * (distant - near), lax.rem(t, 3)
            weight = W[0, s, pl.ds(pl.multiple_of(shard * j, 16), shard), :]
            QKV[j, s] = (dot_nt(N1[...], weight) + SB[s, pl.ds(j, 1), 0:shard]).astype(LOW)
            return carry

        lax.fori_loop(0, 6, one, 0)

    tick(9)
    project(m, pair)
    tick(10)
    gather_end(0, (2, 3))
    project(far, far_pair)
    tick(11)
    lane_three = iota((BLOCK, shard), 1) >> 6

    def join_heads(o):
        return jnp.where(
            lane_three == 0,
            o[0:BLOCK],
            jnp.where(lane_three == 1, o[BLOCK : 2 * BLOCK], o[2 * BLOCK : 3 * BLOCK]),
        )

    def attention(b, carry):
        at = pl.ds(pl.multiple_of(b * BLOCK, 16), BLOCK)
        loaded = [[QKV[j, s, at, :] for j in range(3)] for s in range(n_mp)]
        heads, mask = HM3[...], BM[...]
        every = []
        for q, k, v in loaded:
            logits = dot_nt(k, jnp.concatenate([q] * 3, axis=0) * heads) * 0.125 + mask
            expos = jnp.exp(logits - jnp.max(logits, axis=0, keepdims=True))
            probs = (expos * (1.0 / jnp.sum(expos, axis=0, keepdims=True))).astype(LOW)
            every.append((probs, join_heads(dot_tn(probs, v)).astype(LOW)))
        for s, (probs, mixed) in enumerate(every):
            PR[s, b] = probs
            MIX[s, at, :] = mixed
        return carry

    lax.fori_loop(0, 2, attention, 0)
    tick(12)
    lax.fori_loop(2, 4, attention, 0)
    tick(13)
    lax.fori_loop(4, n_blocks, attention, 0)
    tick(14)

    out_bias = output_bias[...].reshape(1, width)

    def attend_out(t, carry):
        start = pl.multiple_of(t * BLOCK, 16)
        rows_here = pl.ds(start, BLOCK)
        total = dot(MIX[0, rows_here, :], W[0, 0, pl.ds(3 * shard, shard), :])
        for s in range(1, n_mp):
            total += dot(MIX[s, rows_here, :], W[0, s, pl.ds(3 * shard, shard), :])
        for u in range(BLOCK // LEN):
            at = pl.ds(start + u * LEN, LEN)
            x = TOK[7 * t + u].astype(F32) + (total[u * LEN : (u + 1) * LEN] + out_bias)
            RES[at, :] = x
            N2[at, :] = (standard(x)[0] * g2 + b2).astype(LOW)
        return carry

    lax.fori_loop(0, n_blocks, attend_out, 0, unroll=True)
    tick(15)
    show_embeds(1)
    gather_end(1, (1,))

    def feed_one(s):
        bias = SB[s, 3:4, :]

        def tiles(t, carry):
            for x in range(TILES):
                first = pl.multiple_of((TILES * t + x) * BLOCK, 16)
                h = dot(N2[pl.ds(first, BLOCK), :], W[1, s])
                for u in range(BLOCK // LEN):
                    at = pl.ds(first + u * LEN, LEN)
                    act, slope = gelu_parts(h[u * LEN : (u + 1) * LEN] + bias)
                    GT[at, :] = act.astype(LOW)
                    GP[s, at, :] = slope.astype(LOW)
            return carry

        lax.fori_loop(0, n_blocks // TILES, tiles, 0)
        PA[s] = (dot(POOL[...], GT[...]) * (1.0 / LEN)).astype(LOW)

    def feed_near(i, carry):
        feed_one(m + i * (pair - m))
        return carry

    def feed_far(i, carry):
        feed_one(far + i * (far_pair - far))
        return carry

    lax.fori_loop(0, 1, feed_near, 0)
    tick(16)
    show_embeds(2)
    lax.fori_loop(1, 2, feed_near, 0)
    tick(17)
    show_embeds(3)
    gather_end(2, (1,))
    PB[0] = (dot(PA[m], W[2, m]) + dot(PA[pair], W[2, pair])).astype(LOW)
    pooled_copy = remote(PB.at[0], PB.at[1], pb_s, pb_r, (d, far))
    tick(18)

    def pool_residual(n, carry):
        lanes = pl.ds(pl.multiple_of(n * 128, 128), 128)
        res = RES[:, lanes]
        res_high = res.astype(LOW)
        res_low = (res - res_high.astype(F32)).astype(LOW)
        EL[:, lanes] = (dot(POOL[...], res_high) + dot(POOL[...], res_low)) * (1.0 / LEN)
        return carry

    lax.fori_loop(0, width // 128, pool_residual, 0)
    pooled = EL[...] + reduce_bias[...].reshape(1, width)
    pooled_copy.wait_recv()
    pooled += PB[0].astype(F32) + PB[1].astype(F32)
    inverse = lax.rsqrt(jnp.sum(pooled * pooled, axis=-1, keepdims=True) + 1e-6)
    embed = pooled * inverse
    EL[...] = embed

    show_embeds(4)
    group = min(n_all, 32)

    def embeds(c):
        part = EMB[c * group : c * group + group].astype(F32)
        return part.reshape(group * 8, width).astype(LOW)

    scaling = jnp.exp(log_scale[...].reshape(1, 1))
    embed_low = embed.astype(LOW)
    scores = scaling * jnp.concatenate(
        [dot_nt(embed_low, embeds(c)) for c in range(n_all // group)], axis=1
    )
    cap_rows = scores.shape[0]
    column = iota((cap_rows, t_all), 1)
    col_ok = (column & 7) < images
    row_ok = iota((cap_rows, t_all), 0) < n_cap
    image_id = (column >> 3) * images + (column & 7)
    cap_wide = jnp.broadcast_to(cap[...].reshape(1, 2 * n_cap).astype(F32), (cap_rows, 2 * n_cap))
    mine = iota((cap_rows, 2 * n_cap), 1) == iota((cap_rows, 2 * n_cap), 0) + half * n_cap
    cap_column = jnp.sum(jnp.where(mine, cap_wide, 0.0), axis=1, keepdims=True)
    matches = jnp.where((cap_column == image_id.astype(F32)) & col_ok & row_ok, 1.0, 0.0)
    by_row = jnp.where(col_ok, scores, FAR)
    row_top = jnp.max(by_row, axis=1, keepdims=True)
    row_lse = row_top + jnp.log(jnp.sum(jnp.exp(by_row - row_top), axis=1, keepdims=True))
    row_positive = jnp.sum(scores * matches, axis=1, keepdims=True)
    row_part = jnp.sum(
        jnp.where(iota((cap_rows, 1), 0) < n_cap, row_lse - row_positive, 0.0), axis=0, keepdims=True
    )
    by_column = jnp.where(row_ok, scores, FAR)
    top = jnp.max(by_column, axis=0, keepdims=True)
    MSG[...] = jnp.zeros_like(MSG)
    MSG[0:1, :] = top
    MSG[1:2, :] = jnp.sum(jnp.exp(by_column - top), axis=0, keepdims=True)
    MSG[2:3, :] = jnp.sum(scores * matches, axis=0, keepdims=True)
    MSG[3:4, :] = jnp.sum(matches, axis=0, keepdims=True)
    MSG[4:5, :] = jnp.broadcast_to(row_part, (1, t_all))
    STATS[slot] = MSG[...]

    def send_stats(k, carry):
        pltpu.make_async_remote_copy(
            src_ref=MSG,
            dst_ref=STATS.at[slot],
            send_sem=st_s,
            recv_sem=st_r,
            device_id=near_device(k),
            device_id_type=pl.DeviceIdType.MESH,
        ).start()
        return carry

    lax.fori_loop(1, 16, send_stats, 0)
    tick(19)
    gather_end(1, (2, 3))
    lax.fori_loop(0, 1, feed_far, 0)
    tick(20)
    lax.fori_loop(1, 2, feed_far, 0)
    pltpu.make_async_copy(STATS.at[pl.ds(0, 15)], STATS.at[pl.ds(0, 15)], st_r).wait()
    top = jnp.max(STATS[:, 0, :], axis=0, keepdims=True)
    total = jnp.sum(STATS[:, 1, :] * jnp.exp(STATS[:, 0, :] - top), axis=0, keepdims=True)
    positive = jnp.sum(STATS[:, 2, :], axis=0, keepdims=True)
    count = jnp.sum(STATS[:, 3, :], axis=0, keepdims=True)
    row_sum = jnp.sum(STATS[:, 4, :], axis=0, keepdims=True)
    for x in range(extra):
        XST[0, x] = jnp.concatenate(
            [top, total, positive, count, row_sum, jnp.zeros((3, t_all), F32)], axis=0
        )
        remote(
            XST.at[0, x], XST.at[1, x], stx_s.at[x], stx_r.at[x], (flip(d, 3 + x), m)
        ).wait_recv()
        other = XST[1, x]
        joined = jnp.maximum(top, other[0:1])
        total = total * jnp.exp(top - joined) + other[1:2] * jnp.exp(other[0:1] - joined)
        top = joined
        positive = positive + other[2:3]
        count = count + other[3:4]
        row_sum = row_sum + other[4:5]
    ok = col_ok[0:1]
    count = jnp.where(ok, count, 1.0)
    col_lse = top + jnp.log(total)
    column_part = jnp.sum(
        jnp.where(ok, col_lse - positive / count, 0.0), axis=1, keepdims=True
    )
    loss = 0.5 * (row_sum[:, 0:1] * (1.0 / total_captions) + column_part * (1.0 / total_images))
    weight = 0.5 * total_captions / total_images
    grad_scores = 0.5 * (jnp.exp(by_row - row_lse) - matches) + weight * (
        jnp.exp(by_column - col_lse) - matches * (1.0 / count)
    )
    grad_scores = jnp.where(col_ok & row_ok, grad_scores, 0.0)
    grad_log = jnp.sum(
        jnp.sum(grad_scores * scores, axis=1, keepdims=True), axis=0, keepdims=True
    )
    embed = EL[...]
    grad_cosine = (scaling * grad_scores).astype(LOW)
    grad_embed = dot(grad_cosine[:, 0 : group * 8], embeds(0))
    for c in range(1, n_all // group):
        grad_embed += dot(grad_cosine[:, c * group * 8 : (c + 1) * group * 8], embeds(c))
    grad_pooled = (
        grad_embed - embed * jnp.sum(embed * grad_embed, axis=-1, keepdims=True)
    ) * inverse
    SG[0] = jnp.zeros(SG.shape[1:], F32)
    SG[0, 13:14, :] = jnp.sum(grad_pooled, axis=0, keepdims=True)
    SG[0, 18:19, :] = jnp.broadcast_to(grad_log, (1, width))
    GPL[0] = grad_pooled.astype(LOW)
    grad_rows = grad_pooled * (1.0 / LEN)
    EL[...] = grad_rows
    GPL[1] = grad_rows.astype(LOW)

    def part(g, i):
        return IW.at[2 * g + i]

    places = (4, 7, 6)

    def whole(g):
        return IW.at[places[g]]

    def settle(copies):
        for copy in copies:
            copy.wait_send()
        sends[:] = [other for other in sends if all(other is not copy for copy in copies)]

    state = {}
    stores = []
    axis_one = ((yb, y_dev), (xb, x_dev))
    axis_two = ((xb, x_dev), (yb, y_dev))
    own = (p_a, p_b)

    def scatter(g, stage, i, ab):
        bit_one, dev_one = axis_one[ab]
        bit_two, dev_two = axis_two[ab]
        run = 8 * ab + 4 * cb + 2 * bit_one
        if stage == 0:
            p, n, dst, dev = 8 * ab + 4 * (1 - cb), 4, RCORE.at[g % 2, i, ab], core_dev
        elif stage == 1:
            p, n, dst, dev = 8 * ab + 4 * cb + 2 * (1 - bit_one), 2, RB1.at[g % 2, i, ab], dev_one
        elif stage == 2:
            p, n, dst, dev = run + 1 - bit_two, 1, RB2.at[g % 2, i, ab], dev_two
        else:
            p, n, dst, dev = own[ab], 1, RZ.at[g, ab], pair_dev
        k = 2 * i + ab
        state[g, stage, i, ab] = remote(
            part(g, i).at[span(p, n)], dst, rs_s.at[g, stage, k], rs_r.at[g, stage, k], dev
        )

    def add_in(g, stage, i, ab):
        state[g, stage, i, ab].wait_recv()
        run = 8 * ab + 4 * cb
        if stage == 0:
            at, got = span(run, 4), RCORE[g % 2, i, ab]
        elif stage == 1:
            at, got = span(run + 2 * axis_one[ab][0], 2), RB1[g % 2, i, ab]
        else:
            at, got = span(own[ab], 1), RB2[g % 2, i, ab]
        IW[2 * g + i, at, :] = IW[2 * g + i, at, :] + got

    def pass_on(g, ab, k, across_one, across_two, dev):
        bit_one = axis_one[ab][0] + across_one * (1 - 2 * axis_one[ab][0])
        bit_two = axis_two[ab][0] + across_two * (1 - 2 * axis_two[ab][0])
        run = whole(g).at[span(8 * ab + 4 * cb + 2 * bit_one + bit_two, 1)]
        state[g, "back", k, ab] = remote(run, run, ag_s.at[g, k, ab], ag_r.at[g, k, ab], dev)

    def gather_back(g, stage, ab):
        dev_one, dev_two = axis_one[ab][1], axis_two[ab][1]
        if stage == 0:
            pass_on(g, ab, 0, 0, 0, dev_two)
            pass_on(g, ab, 1, 0, 0, dev_one)
            pass_on(g, ab, 2, 0, 0, core_dev)
        elif stage == 1:
            state[g, "back", 0, ab].wait_recv()
            pass_on(g, ab, 3, 0, 1, dev_one)
            pass_on(g, ab, 4, 0, 1, core_dev)
        elif stage == 2:
            state[g, "back", 1, ab].wait_recv()
            pass_on(g, ab, 5, 1, 0, core_dev)
            state[g, "back", 3, ab].wait_recv()
            pass_on(g, ab, 6, 1, 1, core_dev)
        else:
            for k in (2, 4, 5, 6):
                state[g, "back", k, ab].wait_recv()

    def reduce_start(g, ab):
        if g == 0:
            settle([state.pop((2, a, i, ab)) for a in range(4) for i in range(2) if (2, a, i, ab) in state])
        for i in (1, 0):
            scatter(g, 0, i, ab)

    def reduce_step(g, step, half_of=None):
        if step == 0:
            for ab in range(2):
                reduce_start(g, ab)
        elif step < 4:
            halves = (half_of,) if half_of is not None else (0, 1)
            for i in (1, 0):
                for ab in halves:
                    add_in(g, step - 1, i, ab)
                    if step < 3 or i == 1:
                        scatter(g, step, i, ab)
        elif step == 4:
            for ab in range(2):
                state[g, 3, 1, ab].wait_recv()
                at = span(own[ab], 1)
                IW[places[g], at, :] = IW[2 * g, at, :] + RZ[g, ab]
                for x in range(extra):
                    copy = remote(
                        whole(g).at[at],
                        XR.at[g % 2, x, ab],
                        xr_s.at[g, x, ab],
                        xr_r.at[g, x, ab],
                        (flip(d, 3 + x), m),
                    )
                    copy.wait_recv()
                    settle([copy])
                    IW[places[g], at, :] = IW[places[g], at, :] + XR[g % 2, x, ab]
                gather_back(g, 0, ab)
        elif step < 7:
            for ab in range(2):
                gather_back(g, step - 4, ab)
        else:
            for ab in range(2):
                gather_back(g, 3, ab)
            stores.append(local(whole(g), red.at[g], out_sem.at[g]))

    def back_tick(place):
        for entry in RPLAN.get(place, ()):
            reduce_step(*entry)

    shards = (m, pair)
    for i in range(2):
        IW[4 + i] = dot_tn(PA[shards[i]], GPL[0]).astype(LOW)

    back_tick(0)

    def grad_activation(near, distant):
        for s in (near, distant):
            GA[s] = dot_nt(GPL[1], W[2, s])

    ones = jnp.ones((16, rows), LOW)

    def grad_hidden(near, distant):
        def one(k, carry):
            s = near + k * (distant - near)

            def scale(t, total):
                for u in range(7):
                    at = pl.ds(pl.multiple_of((7 * t + u) * LEN, LEN), LEN)
                    low_grad = (GP[s, at, :].astype(F32) * GA[s, pl.ds(7 * t + u, 1), :]).astype(LOW)
                    GP[s, at, :] = low_grad
                    total = total + sum8(low_grad.astype(F32))
                return total

            total = lax.fori_loop(0, n_cap // 7, scale, jnp.zeros((8, width), F32))
            SG[0, pl.ds(8 + s, 1), :] = jnp.sum(total, axis=0, keepdims=True)
            return carry

        lax.fori_loop(0, 2, one, 0)

    grad_activation(m, pair)
    back_tick(1)
    tick(21)
    grad_hidden(m, pair)
    back_tick(2)
    tick(22)

    def expand_gradient(i, carry):
        s = m + i * (pair - m)
        IW[2 + i] = dot_tn(N2[...], GP[s]).astype(LOW)
        return carry

    lax.fori_loop(0, 2, expand_gradient, 0)
    back_tick(4)
    tick(23)
    gather_end(2, (2, 3))
    grad_activation(far, far_pair)
    back_tick(3)
    grad_hidden(far, far_pair)
    back_tick(5)

    def grad_norm_two(n, carry):
        p = pl.ds(pl.multiple_of(n * 384, 128), 384)
        total = dot_nt(
            jnp.concatenate([GP[s] for s in range(n_mp)], axis=1),
            jnp.concatenate([W[1, s, p, :] for s in range(n_mp)], axis=1),
        )
        ACC[:, pl.ds(pl.multiple_of(n * 384, 128), 384)] = total
        return carry

    lax.fori_loop(0, 2, grad_norm_two, 0)
    back_tick(6)

    def norm_back(e, gain, x):
        xhat, scale = standard(x)
        eg = e * gain
        c1 = jnp.sum(eg, axis=-1, keepdims=True) * (1.0 / width)
        c2 = jnp.sum(eg * xhat, axis=-1, keepdims=True) * (1.0 / width)
        return (eg - c1 - xhat * c2) * scale, sum8(e * xhat), sum8(e)

    zero8 = jnp.zeros((8, width), F32)

    def back_two(t, carry):
        dg, db, do = carry
        found = []
        for u in range(7):
            at = pl.ds(pl.multiple_of((7 * t + u) * LEN, LEN), LEN)
            dv, one, two = norm_back(ACC[at, :], g2, RES[at, :])
            g = EL[pl.ds(7 * t + u, 1), :] + dv
            found.append((at, g))
            dg, db, do = dg + one, db + two, do + sum8(g)
        for at, g in found:
            RES[at, :] = g
            GRL[at, :] = g.astype(LOW)
        return dg, db, do

    dg, db, do = lax.fori_loop(0, n_cap // 7, back_two, (zero8, zero8, zero8))
    SG[0, 15:16, :] = jnp.sum(dg, axis=0, keepdims=True)
    SG[0, 17:18, :] = jnp.sum(db, axis=0, keepdims=True)
    SG[0, 12:13, :] = jnp.sum(do, axis=0, keepdims=True)

    back_tick(7)
    for i in range(2):
        IW[i, 3 * shard : 4 * shard, :] = dot_tn(MIX[shards[i]], GRL[...]).astype(LOW)

    def grad_mixture(s, carry):
        MIX[s] = dot_nt(GRL[...], W[0, s, pl.ds(3 * shard, shard), :]).astype(LOW)
        return carry

    lax.fori_loop(0, n_mp, grad_mixture, 0)
    back_tick(8)

    def attention_back(places):
        loaded = []
        for b, s in places:
            at = pl.ds(pl.multiple_of(b * BLOCK, 16), BLOCK)
            loaded.append([QKV[j, s, at, :] for j in range(3)] + [MIX[s, at, :], PR[s, b]])
        heads = HM3[...]
        every = []
        for q, k, v, g, low_probs in loaded:
            q = jnp.concatenate([q] * 3, axis=0) * heads
            g = jnp.concatenate([g] * 3, axis=0) * heads
            probs = low_probs.astype(F32)
            grad_probs = dot_nt(v, g)
            inner = jnp.sum(grad_probs * probs, axis=0, keepdims=True)
            grad_logits = (probs * (grad_probs - inner)).astype(LOW)
            every.append(
                (
                    (join_heads(dot_tn(grad_logits, k)) * 0.125).astype(LOW),
                    (dot(grad_logits, q) * 0.125).astype(LOW),
                    dot(low_probs, g).astype(LOW),
                )
            )
        for (b, s), grads in zip(places, every):
            at = pl.ds(pl.multiple_of(b * BLOCK, 16), BLOCK)
            for j in range(3):
                QKV[j, s, at, :] = grads[j]

    def attention_back_run(first, count, shards):
        def two(t, carry):
            b = first + 2 * t
            attention_back([(b + x, s) for x in range(2) for s in shards])
            return carry

        lax.fori_loop(0, count // 2, two, 0)
        if count % 2:
            attention_back([(first + count - 1, s) for s in shards])

    def attend_gradient(j):
        def one(i, carry):
            s = m + i * (pair - m)
            IW[i, shard * j : shard * (j + 1), :] = dot_tn(QKV[j, s], N1[...]).astype(LOW)
            return carry

        lax.fori_loop(0, 2, one, 0)

    small_devs = [core_dev, y_dev, x_dev, pair_dev] + [(flip(d, 3 + x), m) for x in range(extra)]
    small = {}

    def small_start(i):
        small[i] = remote(SG.at[i], SGR.at[i], sg_s.at[i], sg_r.at[i], small_devs[i])

    def small_end(i):
        small[i].wait_recv()
        SG[i + 1] = SG[i] + SGR[i]

    small_gain, small_shift = zero8, zero8
    gt_copies = []
    cuts = (0, 4, n_blocks)
    attention_back_run(0, n_blocks, (m, pair))
    back_tick(9)
    attend_gradient(2)
    reduce_start(0, 1)
    attend_gradient(0)
    attend_gradient(1)
    reduce_start(0, 0)
    back_tick(20)
    for r in range(2):
        attention_back_run(cuts[r], cuts[r + 1] - cuts[r], (far, far_pair))
        back_tick(10 + r)
        first, last = cuts[r] * (BLOCK // LEN), cuts[r + 1] * (BLOCK // LEN)
        stripe = pl.ds(first * LEN, (last - first) * LEN)

        def last_norm(t, carry):
            dg, db = carry
            start = pl.multiple_of((first + 7 * t) * LEN, 16)
            rows_here = pl.ds(start, BLOCK)
            e = None
            for s in range(n_mp):
                for j in range(3):
                    term = dot(QKV[j, s, rows_here, :], W[0, s, pl.ds(shard * j, shard), :])
                    e = term if e is None else e + term
            for u in range(BLOCK // LEN):
                at = pl.ds(start + u * LEN, LEN)
                dv, one, two = norm_back(
                    e[u * LEN : (u + 1) * LEN], g1, TOK[first + 7 * t + u].astype(F32)
                )
                GT[at, :] = (RES[at, :] + dv).astype(LOW)
                dg, db = dg + one, db + two
            return dg, db

        small_gain, small_shift = lax.fori_loop(
            0, (last - first) // 7, last_norm, (small_gain, small_shift)
        )
        back_tick(12 + r)
        if r == 1:
            SG[0, 14:15, :] = jnp.sum(small_gain, axis=0, keepdims=True)
            SG[0, 16:17, :] = jnp.sum(small_shift, axis=0, keepdims=True)

            def bias_gradient(s, carry):
                SG[0, pl.ds(s, 1), 0:shard] = dot(ones, QKV[0, s])[0:1]
                SG[0, pl.ds(4 + s, 1), 0:shard] = dot(ones, QKV[2, s])[0:1]
                return carry

            lax.fori_loop(0, n_mp, bias_gradient, 0)
            small_start(0)
            back_tick(16)
            small_end(0)
            small_start(1)
            back_tick(17)
            small_end(1)
            small_start(2)
            back_tick(18)
            small_end(2)
            small_start(3)
        else:
            back_tick(15)
        gt_copies.append(
            remote(GT.at[stripe], gt.at[half, stripe], gt_s.at[r], gt_r.at[r], pair_dev)
        )
    stores.append(local(GT, gt.at[half], out_sem.at[3]))
    back_tick(21)
    small_end(3)
    for i in range(4, 4 + extra):
        small_start(i)
        small_end(i)
    for place in range(22, 28):
        back_tick(place)
    last = SG.shape[0] - 1
    sgo[...] = jnp.zeros_like(sgo)
    sgo[0:1, :] = SG[last, pl.ds(m, 1), :]
    sgo[1:2, :] = SG[last, pl.ds(4 + m, 1), :]
    sgo[2:3, :] = SG[last, pl.ds(8 + m, 1), :]
    sgo[3:10, :] = SG[last, 12:19, :]
    sgo[10:11, :] = jnp.broadcast_to(loss, (1, width))
    back_tick(28)
    for copy in gt_copies:
        copy.wait_recv()
    pltpu.make_async_copy(STATS.at[pl.ds(0, 15)], STATS.at[pl.ds(0, 15)], st_s).wait()
    for copy in sends:
        copy.wait_send()
    for copy in stores:
        copy.wait()


def local_step(
    n_dp,
    n_mp,
    caption_tokens,
    image_tokens,
    image_attend,
    image_output,
    image_expand,
    image_reduce,
    image_gains,
    caption_attend,
    attend_bias,
    caption_output,
    output_bias,
    caption_expand,
    expand_bias,
    caption_reduce,
    reduce_bias,
    norm_gains,
    norm_shifts,
    log_scale,
    caption_image,
):
    captions, length, width = caption_tokens.shape
    images, image_len, _ = image_tokens.shape
    shard = caption_attend.shape[2]
    units = caption_expand.shape[1]
    n_cap = captions // 2
    rows = n_cap * length
    n_blocks = rows // BLOCK
    n_all = n_dp * n_mp
    t_all = n_all * 8
    extra = n_dp.bit_length() - 1 - 3
    assert length == LEN and units == width and shard * n_mp == width and width == 16 * PIECE

    any_space = pl.BlockSpec(memory_space=pl.ANY)
    vmem = pl.BlockSpec(memory_space=pltpu.VMEM)
    nx = max(extra, 1)
    dma = pltpu.SemaphoreType.DMA
    scratch = [
        pltpu.VMEM((3, n_mp, width, width), LOW),
        pltpu.VMEM((8, width, width), LOW),
        pltpu.VMEM((n_cap, length, width), LOW),
        pltpu.VMEM((images, image_len, width), LOW),
        pltpu.VMEM((rows, width), LOW),
        pltpu.VMEM((3, n_mp, rows, shard), LOW),
        pltpu.VMEM((n_mp, n_blocks, BLOCK, 3 * BLOCK), LOW),
        pltpu.VMEM((n_mp, rows, shard), LOW),
        pltpu.VMEM((rows, width), F32),
        pltpu.VMEM((rows, width), LOW),
        pltpu.VMEM((n_mp, rows, width), LOW),
        pltpu.VMEM((n_mp, 64, width), LOW),
        pltpu.VMEM((2, 64, width), LOW),
        pltpu.VMEM((rows, width), F32),
        pltpu.VMEM((rows, width), LOW),
        pltpu.VMEM((rows, width), LOW),
        pltpu.VMEM((16, width), F32),
        pltpu.VMEM((n_all, 8, width), LOW),
        pltpu.VMEM((8, t_all), F32),
        pltpu.VMEM((16, 8, t_all), F32),
        pltpu.VMEM((8, width), F32),
        pltpu.VMEM((n_mp, 8, width), F32),
        pltpu.VMEM((3 * BLOCK, shard), LOW),
        pltpu.VMEM((BLOCK, 3 * BLOCK), F32),
        pltpu.VMEM((256, 256), LOW),
        pltpu.VMEM((64, rows), LOW),
        pltpu.VMEM((64, width), F32),
        pltpu.VMEM((2, 64, width), LOW),
        pltpu.VMEM((n_mp, 64, width), F32),
        pltpu.VMEM((2, 2, 2, 4 * PIECE, width), LOW),
        pltpu.VMEM((2, 2, 2, 2 * PIECE, width), LOW),
        pltpu.VMEM((2, 2, 2, PIECE, width), LOW),
        pltpu.VMEM((3, 2, PIECE, width), LOW),
        pltpu.VMEM((2, nx, 2, PIECE, width), LOW),
        pltpu.VMEM((2, nx, 8, t_all), F32),
        pltpu.VMEM((5 + extra, 24, width), F32),
        pltpu.VMEM((4 + extra, 24, width), F32),
        dma((3, 3, 2)),
        dma((3, 3, 2)),
        dma((3, 3, 3, 2)),
        dma((3, 3, 3, 2)),
        dma((3,)),
        dma((3,)),
        dma((12,)),
        dma,
        dma,
        dma((3,)),
        dma((3,)),
        dma((10 + nx,)),
        dma((10 + nx,)),
        dma,
        dma,
        dma((nx,)),
        dma((nx,)),
        dma((3, 4, 4)),
        dma((3, 4, 4)),
        dma((3, 7, 2)),
        dma((3, 7, 2)),
        dma((3, nx, 2)),
        dma((3, nx, 2)),
        dma((4 + extra,)),
        dma((4 + extra,)),
        dma((3,)),
        dma((3,)),
        dma((4,)),
        dma,
        dma,
    ]
    red, gt, sgo = pl.pallas_call(
        functools.partial(body, n_dp, n_mp),
        out_shape=(
            jax.ShapeDtypeStruct((3, width, width), LOW),
            jax.ShapeDtypeStruct((2, rows, width), LOW),
            jax.ShapeDtypeStruct((16, width), F32),
        ),
        in_specs=[any_space] * 10 + [vmem] * 9,
        out_specs=(any_space, any_space, vmem),
        scratch_shapes=scratch,
        compiler_params=pltpu.CompilerParams(
            collective_id=0, has_side_effects=True, vmem_limit_bytes=66_000_000
        ),
        name="step",
    )(
        caption_tokens,
        image_tokens,
        image_attend,
        image_output,
        image_expand,
        image_reduce,
        jnp.swapaxes(caption_attend, 1, 2),
        caption_output,
        caption_expand,
        caption_reduce,
        image_gains,
        attend_bias,
        output_bias,
        expand_bias,
        reduce_bias,
        norm_gains,
        norm_shifts,
        log_scale,
        caption_image,
    )
    shapes = (
        (1,),
        (captions, length, width),
        (3, shard, width),
        (2, shard),
        (shard, width),
        (width,),
        (width, units),
        (units,),
        (units, width),
        (width,),
        (2, width),
        (2, width),
        (1,),
    )
    large = (1, 2, 4, 6, 8)
    parts = 7
    grads = pl.pallas_call(
        finish,
        out_shape=tuple(jax.ShapeDtypeStruct(shape, F32) for shape in shapes),
        in_specs=[any_space, any_space, vmem],
        out_specs=tuple(any_space if i in large else vmem for i in range(len(shapes))),
        scratch_shapes=[
            pltpu.VMEM((captions, length, width), LOW),
            pltpu.VMEM((captions, length, width), F32),
            pltpu.VMEM((3, width, width), LOW),
            pltpu.VMEM((3, width, width), F32),
            pltpu.VMEM((3, shard, width), F32),
            dma((parts,)),
            dma((parts,)),
            dma((3,)),
            dma((6,)),
        ],
        compiler_params=pltpu.CompilerParams(vmem_limit_bytes=64_000_000),
        name="finish",
    )(red, gt.reshape(captions, length, width), sgo)
    return (*grads[:2], jnp.swapaxes(grads[2], 1, 2), *grads[3:])


def finish(
    red,
    gt,
    small,
    loss,
    tokens,
    attend,
    attend_bias,
    output,
    output_bias,
    expand,
    expand_bias,
    reduce,
    reduce_bias,
    gains,
    shifts,
    log_scale,
    GT,
    TOKENS,
    RED,
    WIDE,
    ATTEND,
    gt_in,
    gt_out,
    red_in,
    red_out,
):
    def copy(src, dst, sem):
        made = pltpu.make_async_copy(src, dst, sem)
        made.start()
        return made

    parts = gt_in.shape[0]
    size = GT.shape[0] // parts
    width = GT.shape[2]
    shard = ATTEND.shape[1]
    order = (0, 1, 2)
    weights = {g: copy(red.at[g], RED.at[g], red_in.at[g]) for g in order}
    pieces = [
        copy(gt.at[pl.ds(i * size, size)], GT.at[pl.ds(i * size, size)], gt_in.at[i])
        for i in range(parts)
    ]
    written = []
    loss[...] = small[10:11, 0:1].reshape(1)
    attend_bias[...] = small[0:2, 0:shard]
    expand_bias[...] = small[2:3, :].reshape(width)
    output_bias[...] = small[3:4, :].reshape(width)
    reduce_bias[...] = small[4:5, :].reshape(width)
    gains[...] = small[5:7, :]
    shifts[...] = small[7:9, :]
    log_scale[...] = small[9:10, 0:1].reshape(1)
    for g in order:
        weights[g].wait()
        if g == 0:
            for j in range(3):
                ATTEND[j] = RED[0, shard * j : shard * (j + 1), :].astype(F32)
                written.append(copy(ATTEND.at[j], attend.at[j], red_out.at[j]))
            WIDE[0, 3 * shard :, :] = RED[0, 3 * shard :, :].astype(F32)
            written.append(copy(WIDE.at[0, pl.ds(3 * shard, shard)], output, red_out.at[3]))
        else:

            def widen(t, carry):
                at = pl.ds(pl.multiple_of(t * 96, 96), 96)
                WIDE[g, at, :] = RED[g, at, :].astype(F32)
                return carry

            lax.fori_loop(0, width // 96, widen, 0)
            written.append(copy(WIDE.at[g], (expand, reduce)[g - 1], red_out.at[3 + g]))
    for i in range(parts):
        pieces[i].wait()
        at = slice(i * size, i * size + size)
        TOKENS[at] = GT[at].astype(F32)
        written.append(
            copy(
                TOKENS.at[pl.ds(i * size, size)], tokens.at[pl.ds(i * size, size)], gt_out.at[i]
            )
        )
    for made in written:
        made.wait()


def solution(mesh):
    in_specs = (
        P("dp", None, None),
        P(("dp", "mp"), None, None),
        P(),
        P(),
        P(),
        P(),
        P(),
        P(None, None, "mp"),
        P(None, "mp"),
        P("mp", None),
        P(),
        P(None, "mp"),
        P("mp"),
        P("mp", None),
        P(),
        P(),
        P(),
        P(),
        P("dp"),
    )
    out_specs = (
        P(),
        P("dp", None, None),
        P(None, None, "mp"),
        P(None, "mp"),
        P("mp", None),
        P(),
        P(None, "mp"),
        P("mp"),
        P("mp", None),
        P(),
        P(),
        P(),
        P(),
    )
    step = functools.partial(local_step, mesh.shape["dp"], mesh.shape["mp"])
    return jax.shard_map(step, mesh=mesh, in_specs=in_specs, out_specs=out_specs, check_vma=False)
```
